32 devices in a mesh: dp: 8 (over z, x), wshard: 4 (over y, core).
Axes of the slice: x: 2, y: 2, z: 4, core: 2. Of those that a mesh axis runs over, the one named last changes fastest.
Arguments:
- tokens: bfloat16 [16384, 1024], P(('dp', 'wshard')), may hold values from -6 to 6
- cotangent: bfloat16 [16384, 1024], P(('dp', 'wshard')), may hold values from -6 to 6
- span_starts: int32 [32], P(('dp', 'wshard')), may hold values from 0 to 256
- routes: int32 [16384, 2], P(('dp', 'wshard')), may hold values from 0 to 7, all different within a row; in each aligned block of 512 rows (0 to 511, 512 to 1023, ...) at most 160 rows name the same one
- norm_gains: float32 [2, 1024], replicated, may hold values from 0.5 to 1.5
- bias_table: float32 [32, 16], replicated, may hold values from -4 to 4
- router: bfloat16 [1024, 8], replicated, may hold values from -0.1875 to 0.1875
- attn_qkv: bfloat16 [3, 1024, 1024], P(None, None, 'wshard'), may hold values from -0.1875 to 0.1875
- attn_out: bfloat16 [1024, 1024], P(None, 'wshard'), may hold values from -1.5 to 1.5
- expert_in: bfloat16 [8, 2, 1024, 2816], P('dp', None, None, 'wshard'), may hold values from -0.1875 to 0.1875
- expert_down: bfloat16 [8, 2816, 1024], P('dp', 'wshard'), may hold values from -0.109375 to 0.109375
Outputs:
- output: bfloat16 [16384, 1024], P(('dp', 'wshard'))
- grad_tokens: bfloat16 [16384, 1024], P(('dp', 'wshard'))
- grad_norm_gains: float32 [2, 1024], replicated
- grad_bias_table: float32 [32, 16], replicated
- grad_router: float32 [1024, 8], replicated
- grad_attn_qkv: float32 [3, 1024, 1024], P(None, None, 'wshard')
- grad_attn_out: float32 [1024, 1024], P(None, 'wshard')
- grad_expert_in: float32 [8, 2, 1024, 2816], P('dp', None, None, 'wshard')
- grad_expert_down: float32 [8, 2816, 1024], P('dp', 'wshard')
The draws below stay inside these ranges and needn't reach their ends.
Inputs may be any that keep to these rules, and one draw needn't show every extreme that they name: `routes`: each token names two different experts; among the rows of one device no expert is named more than 160 times, a bound that some block reaches. `span_starts`: the picture span of a sequence covers 256 positions inside it.
All inputs are finite; a program needn't handle non-finite values.
Results may differ from the reference program's by a relative error of at most 0.015.
The reference program's roundings to bfloat16 on the way count: a program that leaves them out, or rounds other values in their place, can miss the bound.
Values may be sent and summed in bfloat16 or wider, within the bound.
A program may use at most 256 MiB of HBM per device.

```python
import math
import jax
import jax.numpy as jnp
import numpy as np
from jax import lax

D = 1024
HEADS = 16
HEAD_DIM = 64
FF = 2816
BUCKETS = 32
SEQ = 512
PIC = 256
TOK_DEV = 512
SEQS = 32
TOKENS = 16384
EXPERTS = 8
CAP = 160
N_DP = 8
N_WSHARD = 4


def place_ends(array, rng, least, top_value):
    extent = array.shape
    spot = [jax.random.randint(jax.random.fold_in(rng, axis), (), 0, extent[axis]) for axis in range(len(extent))]
    array = array.at[tuple(spot)].set(least)
    longest = extent.index(max(extent))
    spot[longest] = (spot[longest] + 1) % extent[longest]
    return array.at[tuple(spot)].set(top_value)


def block_scale(key, extent, cuts, smallest, top_value):
    factor_of = 1.0
    for dim, shards_of in cuts:
        heights = jax.random.uniform(jax.random.fold_in(jax.random.fold_in(key, 6), dim), (shards_of,), jnp.float32, smallest / len(cuts), top_value / len(cuts))
        factor_of = factor_of * jnp.repeat(jnp.exp(heights), extent[dim] // shards_of).reshape((-1,) + (1,) * (len(extent) - 1 - dim))
    return factor_of


def routed_block(stream_key, own, number, rows, amount, top, limit, skew):
    ranking = jax.random.permutation(stream_key, amount)
    heavy_load, ordinary = portions_of(amount, rows * top, limit, skew, True), portions_of(amount, rows * top, limit, skew, False)
    places = jnp.arange(amount)

    def named(tallies, offset_by):
        used = int((tallies > 0).sum())
        fixed = max(1, used // 4)
        shifted = fixed + (places - fixed + offset_by * (used - fixed)) % max(1, amount - fixed)
        return jnp.zeros((amount,), jnp.int32).at[ranking[jnp.where(places < fixed, places, shifted)]].set(jnp.asarray(tallies, jnp.int32))

    tallies = jnp.where(number % 4 == 0, named(heavy_load, number // 4), named(ordinary, number - number // 4 - 1))
    mixed = jax.random.permutation(jax.random.fold_in(own, 3), amount)
    giver, taker = mixed[0:amount // 2 * 2:2], mixed[1:amount // 2 * 2:2]
    margin = jnp.minimum(tallies[giver] - 1, limit - tallies[taker]) // 2
    margin = jnp.where((giver == ranking[0]) | (taker == ranking[0]) | (tallies[taker] == 0), 0, jnp.maximum(margin, 0))
    shifted = jax.random.randint(jax.random.fold_in(own, 4), (amount // 2,), 0, 1 << 20) % (margin + 1)
    tallies = tallies.at[giver].add(-shifted).at[taker].add(shifted)
    members = jnp.searchsorted(jnp.cumsum(tallies), jnp.arange(rows * top), side="right").astype(jnp.int32)
    listing = members.reshape(top, rows).T
    listing = listing[jax.random.permutation(jax.random.fold_in(own, 1), rows)]
    offset_by = jax.random.randint(jax.random.fold_in(own, 2), (rows, 1), 0, top)
    return jnp.take_along_axis(listing, (jnp.arange(top)[None, :] + offset_by) % top, axis=1)


def portions_of(amount, total, limit, lean, full):
    weights = [(1 << 20) // math.isqrt(rank ** lean) + 1 for rank in range(1, amount + 1)]
    largest = limit if full else min(limit, max(-(-total // amount), total * weights[0] // sum(weights)))
    least = 1 if total - largest >= amount - 1 else 0
    holding, spare = [largest] + [least] * (amount - 1), total - largest - least * (amount - 1)
    while spare > 0:
        movable = [i for i in range(1, amount) if holding[i] < largest] or [i for i in range(1, amount) if holding[i] < limit]
        pool, remaining = sum([weights[i] for i in movable]), spare
        for i in movable:
            more = min(limit - holding[i], max(1, remaining * weights[i] // pool), spare)
            holding[i] = holding[i] + more
            spare = spare - more
    return np.array(holding)


def scatter_about(key, shape, deviation, reach, cuts=(), kind=jnp.bfloat16):
    drawn = jax.random.normal(key, shape, jnp.float32) * deviation
    if len(cuts) > 0:
        drawn = block_scale(key, shape, cuts, -0.22, 0.18) * drawn
    return jnp.clip(drawn, min=-reach, max=reach).astype(kind)


def setup_inputs(seed: int = 0) -> dict:
    key_of = jax.random.split(jax.random.key(seed), 12)
    tokens = scatter_about(key_of[0], (TOKENS, D), 1.0, 6.0, ((0, 32),))
    cotangent = scatter_about(key_of[1], (TOKENS, D), 1.0, 6.0, ((0, 32),))
    span_starts = place_ends(jax.random.randint(key_of[2], (SEQS,), 0, SEQ - PIC + 1), jax.random.fold_in(key_of[2], 1), 0, SEQ - PIC).astype(jnp.int32)
    routes_keys = jax.random.split(jax.random.fold_in(key_of[3], 1), TOKENS // TOK_DEV)
    routes_turns = jax.random.permutation(jax.random.fold_in(key_of[3], 3), TOKENS // TOK_DEV)
    routes = jax.vmap(lambda own, number: routed_block(jax.random.fold_in(key_of[3], 2), own, number, TOK_DEV, EXPERTS, 2, CAP, 1))(routes_keys, routes_turns).reshape((TOKENS, 2))
    norm_gains = jnp.clip(1.0 + 0.1 * jax.random.normal(key_of[4], (2, D), jnp.float32), 0.5, 1.5)
    bias_table = scatter_about(key_of[5], (BUCKETS, HEADS), 1.0, 4.0, (), jnp.float32)
    router = scatter_about(key_of[6], (D, EXPERTS), D ** -0.5, 0.1875)
    attn_qkv = scatter_about(key_of[7], (3, D, D), D ** -0.5, 0.1875, ((2, 4),))
    attn_out = scatter_about(key_of[8], (D, D), (max(D // 64, 1)) ** -0.5, 1.5, ((1, 4),))
    expert_in = scatter_about(key_of[9], (EXPERTS, 2, D, FF), D ** -0.5, 0.1875, ((0, 8), (3, 4)))
    expert_down = scatter_about(key_of[10], (EXPERTS, FF, D), FF ** -0.5, 0.109375, ((0, 8), (1, 4)))
    return dict(tokens=tokens, cotangent=cotangent, span_starts=span_starts, routes=routes, norm_gains=norm_gains, bias_table=bias_table, router=router, attn_qkv=attn_qkv, attn_out=attn_out, expert_in=expert_in, expert_down=expert_down)


@jax.custom_vjp
def low(v):
    return lax.optimization_barrier(v.astype(jnp.bfloat16)).astype(jnp.float32)

@jax.custom_vjp
def low_back(v):
    return v

def low_keep(v):
    return (low(v), None)

def low_pass(kept, grad):
    return (grad,)

def back_keep(v):
    return (v, None)

def back_low(kept, grad):
    return (low(grad),)
low.defvjp(low_keep, low_pass)
low_back.defvjp(back_keep, back_low)
PRECISE = lax.Precision.HIGHEST
EPSILON = 1e-06
MASKED_SCORE = -1e+30
BUCKET_EDGES = (8, 11, 16, 23, 32, 45, 64, 91)

def bucket_ones(seq_length, bucket_count):
    positions = jnp.arange(seq_length, dtype=jnp.int32)
    offset = positions[:, None] - positions[None, :]
    magnitude = jnp.abs(offset)
    coarse = 7 + sum(((magnitude >= bound).astype(jnp.int32) for bound in BUCKET_EDGES))
    bucket = jnp.where(magnitude < 8, magnitude, coarse) + 16 * (offset < 0).astype(jnp.int32)
    labels = jnp.arange(bucket_count, dtype=jnp.int32)
    return (bucket.reshape(1, -1) == labels[:, None]).astype(jnp.float32)

def visible_of(span_start, seq_length, span_length):
    positions = jnp.arange(seq_length, dtype=jnp.int32)
    inside = (positions >= span_start) & (positions < span_start + span_length)
    return (positions[None, :] <= positions[:, None]) | inside[:, None] & inside[None, :]

def rms_norm(values, gain):
    recip = lax.rsqrt(lax.optimization_barrier(jnp.mean(values * values, -1, keepdims=True)) + EPSILON)
    return values * recip * gain

def gelu_mix(gate_pre, up_pre):
    inner = 0.7978845608028654 * (gate_pre + 0.044715 * gate_pre * gate_pre * gate_pre)
    return 0.5 * gate_pre * (1.0 + jnp.tanh(inner)) * up_pre

def forward(tokens_f, gains, table, router_f, qkv_f, out_f, in_f, down_f, span_starts, routes):
    bias = jnp.dot(table.T, bucket_ones(SEQ, BUCKETS), precision=PRECISE).reshape(HEADS, SEQ, SEQ)
    group_size = math.gcd(SEQS, max(1, 4096 // SEQ))
    grouped = tokens_f.reshape(SEQS // group_size, group_size, SEQ, D)
    starts = span_starts.reshape(SEQS // group_size, group_size)

    def branch(pieces):
        block, block_starts = pieces
        normed = low(rms_norm(block, gains[0]))
        proj = low_back(low(jnp.einsum('gsd,cde->cgse', normed, qkv_f, precision=PRECISE)))
        proj = proj.reshape(3, group_size, SEQ, HEADS, HEAD_DIM)
        raw_scores = jnp.einsum('gihd,gjhd->ghij', proj[0], proj[1], precision=PRECISE) * 0.125 + bias[None]
        raw_scores = low_back(raw_scores)
        visible = jax.vmap(lambda one: visible_of(one, SEQ, PIC))(block_starts)
        raw_scores = jnp.where(visible[:, None], raw_scores, MASKED_SCORE)
        row_max = lax.optimization_barrier(jnp.max(raw_scores, -1, keepdims=True))
        exps = jnp.exp(raw_scores - row_max)
        soft = low(exps / lax.optimization_barrier(jnp.sum(exps, -1, keepdims=True)))
        mixed = low_back(low(jnp.einsum('ghij,gjhd->gihd', soft, proj[2], precision=PRECISE)))
        result = low_back(jnp.dot(mixed.reshape(group_size * SEQ, D), out_f, precision=PRECISE))
        return result.reshape(group_size, SEQ, D)
    attn = lax.map(jax.checkpoint(branch), (grouped, starts))
    hidden = tokens_f + attn.reshape(TOKENS, D)
    normed = low(rms_norm(hidden, gains[1]))
    logits = jnp.dot(normed, router_f, precision=PRECISE)
    chosen_mask = (routes[:, :, None] == jnp.arange(EXPERTS, dtype=jnp.int32)).astype(jnp.float32)
    chosen = lax.optimization_barrier(jnp.sum(logits[:, None, :] * chosen_mask, -1))
    chosen_max = lax.optimization_barrier(jnp.max(chosen, -1, keepdims=True))
    gate_exp = jnp.exp(chosen - chosen_max)
    gate_probs = gate_exp / lax.optimization_barrier(jnp.sum(gate_exp, -1, keepdims=True))
    blocks = N_DP * N_WSHARD
    flat_routes = routes.reshape(blocks, TOK_DEV * 2)
    hits = (flat_routes[:, :, None] == jnp.arange(EXPERTS, dtype=jnp.int32)).astype(jnp.int32)
    before = jnp.cumsum(hits, 1) - hits
    slot_dest = (flat_routes * CAP + lax.optimization_barrier(jnp.sum(before * hits, -1))).astype(jnp.int32)
    copies = jnp.broadcast_to(normed.reshape(blocks, TOK_DEV, 1, D), (blocks, TOK_DEV, 2, D))
    copies = copies.reshape(blocks, TOK_DEV * 2, D)

    def place(dest_one, copy_one):
        return jnp.zeros((EXPERTS * CAP, D), jnp.float32).at[dest_one].set(copy_one)
    placed = low_back(jax.vmap(place)(slot_dest, copies))
    by_expert = placed.reshape(blocks, EXPERTS, CAP, D).transpose(1, 0, 2, 3).reshape(EXPERTS, blocks * CAP, D)

    def expert(pieces):
        expert_rows, weight_in, weight_down = pieces
        gate_pre = low_back(jnp.dot(expert_rows, weight_in[0], precision=PRECISE))
        up_pre = low_back(jnp.dot(expert_rows, weight_in[1], precision=PRECISE))
        act = low(gelu_mix(gate_pre, up_pre))
        return low_back(low(jnp.dot(act, weight_down, precision=PRECISE)))
    made = lax.map(jax.checkpoint(expert), (by_expert, in_f, down_f))
    made = made.reshape(EXPERTS, blocks, CAP, D).transpose(1, 0, 2, 3).reshape(blocks, EXPERTS * CAP, D)
    picked = jax.vmap(lambda rows_one, dest_one: rows_one[dest_one])(made, slot_dest).reshape(TOKENS, 2, D)
    return hidden + lax.optimization_barrier(jnp.sum(gate_probs[:, :, None] * picked, 1))

def reference(tokens, cotangent, span_starts, routes, norm_gains, bias_table, router, attn_qkv, attn_out, expert_in, expert_down):
    floats = (tokens.astype(jnp.float32), norm_gains, bias_table, router.astype(jnp.float32), attn_qkv.astype(jnp.float32), attn_out.astype(jnp.float32), expert_in.astype(jnp.float32), expert_down.astype(jnp.float32))

    def wrapped(*float_args):
        return forward(*float_args, span_starts, routes)
    result, pull = jax.vjp(wrapped, *floats)
    grads = pull(cotangent.astype(jnp.float32))
    return (result.astype(jnp.bfloat16), grads[0].astype(jnp.bfloat16), grads[1], grads[2], grads[3], grads[4], grads[5], grads[6], grads[7])
```

```python
import functools

import jax
import jax.numpy as jnp
import numpy as np
from jax import lax
from jax.experimental import pallas as pl
from jax.experimental.pallas import tpu as pltpu
from jax.sharding import PartitionSpec as P

PIC = 256
PRECISE = lax.Precision.HIGHEST
EPSILON = 1e-06
MASKED_SCORE = -1e30
BUCKET_EDGES = (8, 11, 16, 23, 32, 45, 64, 91)
TILE = 128
F32 = jnp.float32
BF16 = jnp.bfloat16
I32 = jnp.int32
VMEM = pl.BlockSpec(memory_space=pltpu.VMEM)
SMEM = pl.BlockSpec(memory_space=pltpu.SMEM)
ANY = pl.BlockSpec(memory_space=pl.ANY)
LIGHT = 1024
EXTRA = 8


def dot_nn(a, b):
    return lax.dot_general(a, b, (((1,), (0,)), ((), ())), preferred_element_type=F32)


def dot_nt(a, b):
    return lax.dot_general(a, b, (((1,), (1,)), ((), ())), preferred_element_type=F32)


def dot_tn(a, b):
    return lax.dot_general(a, b, (((0,), (0,)), ((), ())), preferred_element_type=F32)


def iota(shape, axis):
    return lax.broadcasted_iota(I32, shape, axis)


def shape_of(shape, dtype):
    return jax.ShapeDtypeStruct(shape, dtype)


def call(body, out, args, specs, scratch=(), name=None):
    return pl.pallas_call(
        body,
        out_shape=out,
        in_specs=specs,
        out_specs=jax.tree.map(lambda _: VMEM, out),
        scratch_shapes=list(scratch),
        cost_estimate=pl.CostEstimate(flops=LIGHT, bytes_accessed=LIGHT, transcendentals=0),
        name=name,
    )(*args)


def bucket_of(offset):
    magnitude = np.abs(offset)
    coarse = 7 + sum((magnitude >= bound).astype(np.int32) for bound in BUCKET_EDGES)
    return np.where(magnitude < 8, magnitude, coarse) + 16 * (offset < 0)


def diagonal_ones(bucket_count):
    column = np.arange(2 * TILE)
    signed = np.where(column < TILE, column, column - 2 * TILE)
    offsets = np.concatenate([TILE * step - signed for step in (-1, 0, 1)])
    used = np.tile(column != TILE, 3)
    hit = bucket_of(offsets)[None, :] == np.arange(bucket_count)[:, None]
    near = (hit & used[None, :]).astype(np.float32)
    far = np.zeros((bucket_count, 2 * TILE), np.float32)
    far[bucket_of(np.array(TILE)), :TILE] = 1
    far[bucket_of(np.array(-TILE)), TILE:] = 1
    return np.concatenate([near, far], 1)


def onehot_rows(first, count, slots_row):
    index = iota((count, slots_row.shape[1]), 0) + first
    hit = (index == slots_row[0:1, :]) | (index == slots_row[1:2, :])
    return hit.astype(F32).astype(BF16)


def onehot_columns(slots_column, first, count):
    index = iota((slots_column.shape[0], count), 1) + first
    return index == slots_column


def place_rows(slots_row, rows, out_ref):
    total = out_ref.shape[0]
    step = 256
    for first in range(0, total, step):
        size = min(step, total - first)
        hit = onehot_rows(first, size, slots_row)
        out_ref[first : first + size, :] = dot_nn(hit, rows).astype(BF16)


def route_body(experts, capacity, routes_ref, cot_ref, row_ref, col_ref, out_ref):
    tokens = cot_ref.shape[0]
    first, second = iota((tokens, tokens), 0), iota((tokens, tokens), 1)
    routes = routes_ref[...]
    label = iota((experts, tokens), 0)
    hits = ((routes[0:1] == label) | (routes[1:2] == label)).astype(F32).astype(BF16)
    before = dot_nn(hits, (first < second).astype(F32).astype(BF16))
    slots = []
    for k in range(2):
        own = jnp.sum(jnp.where(routes[k : k + 1] == label, before, 0.0), 0, keepdims=True)
        slots.append(own.astype(I32) + routes[k : k + 1] * capacity)
    slots += [slots[k] + routes[k : k + 1] * EXTRA for k in range(2)]
    slots = jnp.concatenate(slots + slots, 0)
    row_ref[...] = slots
    col_ref[...] = slots.astype(F32).T.astype(I32)
    place_rows(slots, cot_ref[...], out_ref)


def route(routes, cotangent, experts, capacity):
    tokens, width = cotangent.shape
    total = experts * capacity
    return call(
        functools.partial(route_body, experts, capacity),
        (
            shape_of((8, tokens), I32),
            shape_of((tokens, 8), I32),
            shape_of((total, width), BF16),
        ),
        (routes.T, cotangent),
        [VMEM] * 2,
        name="route",
    )


def unit_norm(values):
    recip = lax.rsqrt(jnp.mean(values * values, -1, keepdims=True) + EPSILON)
    return values * recip, recip


def fill_mask(mask_ref, span_start):
    size = mask_ref.shape[0]
    i, j = iota((size, size), 0), iota((size, size), 1)

    def inside(p):
        return (p >= span_start) & (p < span_start + PIC)

    visible = (j <= i) | (inside(i) & inside(j))
    mask_ref[...] = jnp.where(visible, 0.0, MASKED_SCORE)


def head_lanes(which, size):
    lane = iota((1, 2 * size), 1)
    return ((lane >= size) == (which == 1)).astype(F32).astype(BF16)


def bias_tiles(diag_row):
    tiles = []
    for step in range(3):
        row = diag_row[:, 2 * TILE * step : 2 * TILE * (step + 1)]
        wide = jnp.broadcast_to(row, (TILE, 2 * TILE))
        tiles.append(pltpu.roll(wide, 0, 1, stride=1, stride_axis=0)[:, :TILE])
    return tiles, (diag_row[:, 6 * TILE : 7 * TILE], diag_row[:, 7 * TILE :])


def score_tiles(block, query, keys, tiles, far, mask_ref):
    raw = dot_nt(query, keys)
    rows = slice(block * TILE, (block + 1) * TILE)
    result = []
    for other in range(keys.shape[0] // TILE):
        piece = raw[:, other * TILE : (other + 1) * TILE]
        step = block - other
        piece = piece + (far[0] if step >= 2 else far[1] if step <= -2 else tiles[step + 1])
        if step <= 0:
            piece = piece + mask_ref[rows, other * TILE : (other + 1) * TILE]
        result.append(piece)
    return result


def softmax_tiles(pieces):
    top = functools.reduce(jnp.maximum, pieces)
    top = jnp.max(top, -1, keepdims=True)
    powers = [jnp.exp(piece - top) for piece in pieces]
    total = jnp.sum(functools.reduce(jnp.add, powers), -1, keepdims=True)
    scale = 1.0 / total
    return [power * scale for power in powers]


def attend_body(
    group, head_size, where_ref, x_ref, gain_ref, diag_ref, w_ref, qkv_ref, mix_ref,
    norm_ref, mask_ref,
):
    count = x_ref.shape[0]
    fill_mask(mask_ref, where_ref[1])
    unit, _ = unit_norm(x_ref[...].astype(F32))
    norm_ref[...] = (unit * gain_ref[0:1, :]).astype(BF16)
    for c in range(3):
        qkv_ref[c] = dot_nn(norm_ref[...], w_ref[c]).astype(BF16)
    width = 2 * head_size
    heads = w_ref.shape[2] // head_size
    first_head = (where_ref[0] ^ group) * heads

    def pair(p, carry):
        lanes = pl.ds(pl.multiple_of(p * width, width), width)
        query, keys, value = qkv_ref[0, :, lanes], qkv_ref[1, :, lanes], qkv_ref[2, :, lanes]
        mixed = [None] * (count // TILE)
        for which in range(2):
            head = first_head + 2 * p + which
            own = head_lanes(which, head_size)
            own_query, own_value = query * (own * 0.125), value * own
            tiles, far = bias_tiles(diag_ref[pl.ds(head, 1), :])
            for block in range(count // TILE):
                rows = slice(block * TILE, (block + 1) * TILE)
                pieces = score_tiles(block, own_query[rows], keys, tiles, far, mask_ref)
                probs = jnp.concatenate([t.astype(BF16) for t in softmax_tiles(pieces)], 1)
                part = dot_nn(probs, own_value)
                mixed[block] = part if which == 0 else mixed[block] + part
        for block in range(count // TILE):
            rows = slice(block * TILE, (block + 1) * TILE)
            mix_ref[rows, lanes] = mixed[block].astype(BF16)
        return carry

    lax.fori_loop(0, heads // 2, pair, 0)


def attend(group, where, tokens, gains, diag, weights, head_size):
    count, width = tokens.shape
    cols = weights.shape[2]
    return call(
        functools.partial(attend_body, group, head_size),
        (shape_of((3, count, cols), BF16), shape_of((count, cols), BF16)),
        (where, tokens, gains, diag, weights),
        [SMEM] + [VMEM] * 4,
        [pltpu.VMEM((count, width), BF16), pltpu.VMEM((count, count), F32)],
        name="attend",
    )


def attend_back_body(
    group, head_size, where_ref, x_ref, gain_ref, diag_ref, w_ref, qkv_ref, mixgrad_ref,
    sum_ref, wgrad_ref, sum_out_ref, diag_out_ref, norm_t_ref, mask_ref, grads_ref, probs_ref,
    scores_ref,
):
    count = x_ref.shape[0]
    blocks = count // TILE
    fill_mask(mask_ref, where_ref[1])
    unit, _ = unit_norm(x_ref[...].astype(F32))
    norm_t_ref[...] = (unit * gain_ref[0:1, :]).astype(BF16).T
    width = 2 * head_size
    cols = w_ref.shape[2]
    heads = cols // head_size
    place = where_ref[0] ^ group

    def pair(p, carry):
        offset = pl.multiple_of(p * width, width)
        lanes = pl.ds(offset, width)
        query, keys, value = qkv_ref[0, :, lanes], qkv_ref[1, :, lanes], qkv_ref[2, :, lanes]
        outer = mixgrad_ref[:, pl.ds(pl.multiple_of(place * cols + offset, width), width)]
        query_sum, key_sum, value_sum = [None] * blocks, None, None
        for which in range(2):
            head = place * heads + 2 * p + which
            own = head_lanes(which, head_size)
            own_query, own_key, own_outer = query * own, keys * own, outer * own
            scaled = own_query * 0.125
            tiles, far = bias_tiles(diag_ref[pl.ds(head, 1), :])
            near_sums, far_sums = [None] * 3, [None] * 2
            for block in range(blocks):
                rows = slice(block * TILE, (block + 1) * TILE)
                probs = softmax_tiles(
                    score_tiles(block, scaled[rows], keys, tiles, far, mask_ref)
                )
                prob_grads = dot_nt(own_outer[rows], value)
                prob_grads = [
                    prob_grads[:, j * TILE : (j + 1) * TILE] for j in range(blocks)
                ]
                delta = functools.reduce(
                    jnp.add, [a * b for a, b in zip(probs, prob_grads)]
                )
                delta = jnp.sum(delta, -1, keepdims=True)
                low = [(a * (b - delta)).astype(BF16) for a, b in zip(probs, prob_grads)]
                for other in range(blocks):
                    step = block - other
                    wide = low[other].astype(F32)
                    if abs(step) >= 2:
                        side = 0 if step > 0 else 1
                        old = far_sums[side]
                        far_sums[side] = wide if old is None else old + wide
                    else:
                        old = near_sums[step + 1]
                        near_sums[step + 1] = wide if old is None else old + wide
                probs_ref[which, rows, :] = jnp.concatenate([t.astype(BF16) for t in probs], 1)
                low = jnp.concatenate(low, 1)
                scores_ref[which, rows, :] = low
                part = dot_nn(low, own_key)
                query_sum[block] = part if which == 0 else query_sum[block] + part
            part = dot_tn(scores_ref[which], own_query)
            key_sum = part if which == 0 else key_sum + part
            part = dot_tn(probs_ref[which], own_outer)
            value_sum = part if which == 0 else value_sum + part
            local = 2 * p + which
            for step in range(3):
                wide = jnp.concatenate([near_sums[step], jnp.zeros((TILE, TILE), F32)], 1)
                half = TILE // 2
                while half:
                    turned = pltpu.roll(wide[half:], 2 * TILE - half, 1)
                    wide = wide[:half] + turned
                    half //= 2
                for side in range(2):
                    spot = 2 * step + side
                    diag_out_ref[local, spot : spot + 1, :] = wide[:, TILE * side : TILE * (side + 1)]
            for side in range(2):
                diag_out_ref[local, 6 + side : 7 + side, :] = jnp.sum(
                    far_sums[side], 0, keepdims=True
                )
        for block in range(blocks):
            rows = slice(block * TILE, (block + 1) * TILE)
            grads_ref[0, rows, lanes] = (query_sum[block] * 0.125).astype(BF16)
        grads_ref[1, :, lanes] = (key_sum * 0.125).astype(BF16)
        grads_ref[2, :, lanes] = value_sum.astype(BF16)
        return carry

    lax.fori_loop(0, heads // 2, pair, 0)
    total = sum_ref[...] if sum_ref is not None else None
    for c in range(3):
        wgrad_ref[c] = dot_nn(norm_t_ref[...], grads_ref[c]).astype(BF16)
        part = dot_nt(grads_ref[c], w_ref[c])
        total = part if total is None else total + part
    sum_out_ref[...] = total


def attend_back(
    group, where, tokens, gains, diag, weights, qkv, mixed_grad, total, head_size
):
    count, width = tokens.shape
    cols = weights.shape[2]
    heads = cols // head_size
    body = functools.partial(attend_back_body, group, head_size)
    args = (where, tokens, gains, diag, weights, qkv, mixed_grad)
    specs = [SMEM] + [VMEM] * 6
    if total is None:
        full = body

        def body(*refs):
            full(*refs[:7], None, *refs[7:])

    else:
        args, specs = args + (total,), specs + [VMEM]
    return call(
        body,
        (
            shape_of((3, width, cols), BF16),
            shape_of((count, width), F32),
            shape_of((heads, 8, TILE), F32),
        ),
        args,
        specs,
        [
            pltpu.VMEM((width, count), BF16),
            pltpu.VMEM((count, count), F32),
            pltpu.VMEM((3, count, cols), BF16),
            pltpu.VMEM((2, count, count), BF16),
            pltpu.VMEM((2, count, count), BF16),
        ],
        name="attend_back",
    )


def gather_lanes(refs, place, out_ref):
    for group, ref in enumerate(refs):
        cols = ref.shape[1]
        spot = pl.multiple_of((place ^ group) * cols, cols)
        out_ref[:, pl.ds(spot, cols)] = ref[...]


def split_three(value):
    high = value.astype(BF16).astype(F32)
    middle = (value - high).astype(BF16).astype(F32)
    return high, middle, value - high - middle


def dispatch_body(
    groups, experts, where_ref, x_ref, gain_ref, router_ref, row_ref, col_ref, *refs
):
    mix_refs, out_refs = refs[:groups], refs[groups : 2 * groups]
    hidden_ref, norm_ref, gate_ref, sent_ref, mixed_ref = refs[2 * groups :]
    place = where_ref[0]
    gather_lanes(mix_refs, place, mixed_ref)
    for group in range(groups):
        cols = out_refs[group].shape[1]
        lanes = pl.ds(pl.multiple_of((place ^ group) * cols, cols), cols)
        branch = dot_nn(mixed_ref[...], out_refs[group][...])
        hidden_ref[:, lanes] = x_ref[:, lanes].astype(F32) + branch
    unit, _ = unit_norm(hidden_ref[...])
    norm_ref[...] = (unit * gain_ref[1:2, :]).astype(BF16)
    place_rows(row_ref[2:4, :], norm_ref[...], sent_ref)
    logits = dot_nt(norm_ref[...], router_ref[...])
    stride = sent_ref.shape[0] // experts
    capacity = stride - EXTRA
    slots = [col_ref[:, k : k + 1] for k in range(2)]
    lane = iota(logits.shape, 1)
    chosen = []
    for k in range(2):
        own = (lane * capacity <= slots[k]) & (slots[k] < (lane + 1) * capacity)
        chosen.append(jnp.sum(jnp.where(own, logits, 0.0), -1, keepdims=True))
    top = jnp.maximum(chosen[0], chosen[1])
    powers = [jnp.exp(c - top) for c in chosen]
    gates = [power / (powers[0] + powers[1]) for power in powers]
    for k in range(2):
        gate_ref[:, k : k + 1] = gates[k]
    span = -(-capacity // TILE) * TILE
    lane = iota((slots[0].shape[0], span), 1)
    below = iota((EXTRA, span), 0)
    for expert in range(experts):
        label = jnp.where(lane < capacity, lane + expert * capacity, -1)
        part = 0.0
        for k in range(2):
            part = part + jnp.where(label == slots[k], gates[k], 0.0)
        high, middle, low = split_three(jnp.sum(part, 0, keepdims=True))
        block = jnp.where(
            below == 0, high, jnp.where(below == 1, middle, jnp.where(below == 2, low, 0.0))
        )
        first = expert * stride + capacity
        sent_ref[first : first + EXTRA, :span] = block.astype(BF16)


def dispatch(where, tokens, gains, router_t, slots_row, slots_col, mixed, out_weights, capacity):
    count, width = tokens.shape
    groups = len(mixed)
    experts = router_t.shape[0]
    return call(
        functools.partial(dispatch_body, groups, experts),
        (
            shape_of((count, width), F32),
            shape_of((count, width), BF16),
            shape_of((count, 2), F32),
            shape_of((experts * (capacity + EXTRA), width), BF16),
        ),
        (where, tokens, gains, router_t, slots_row, slots_col, *mixed, *out_weights),
        [SMEM] + [VMEM] * (5 + 2 * groups),
        [pltpu.VMEM((count, width), BF16)],
        name="dispatch",
    )


def combine_body(hidden_ref, gate_ref, col_ref, rows_ref, out_ref):
    count = out_ref.shape[0]
    total = rows_ref.shape[0]
    step = min(count, 256)
    for first in range(0, count, step):
        part = slice(first, first + step)
        result = hidden_ref[part, :]
        for k in range(2):
            hit = onehot_columns(col_ref[part, k : k + 1], 0, total).astype(F32).astype(BF16)
            result = result + gate_ref[part, k : k + 1] * dot_nn(hit, rows_ref[...])
        out_ref[part, :] = result.astype(BF16)


def combine(hidden, gates, slots_col, rows):
    count, width = hidden.shape
    return call(
        combine_body,
        shape_of((count, width), BF16),
        (hidden, gates, slots_col, rows),
        [VMEM] * 4,
        name="combine",
    )


def undispatch_body(
    groups, experts, where_ref, gain_ref, router_ref, col_ref, gate_ref, gate_grad_ref, hidden_ref,
    norm_ref, cot_ref, rows_ref, *refs
):
    mix_refs, out_refs = refs[:groups], refs[groups : 2 * groups]
    grad_ref, mixgrad_ref, router_grad_ref, gain_grad_ref = refs[2 * groups : 2 * groups + 4]
    wgrad_refs = refs[2 * groups + 4 : 3 * groups + 4]
    mixed_ref, branch_ref = refs[3 * groups + 4 :]
    place = where_ref[0]
    total = rows_ref.shape[0]
    capacity = total // experts - EXTRA
    gates = [gate_ref[:, k : k + 1] for k in range(2)]
    slots = [col_ref[:, k : k + 1] for k in range(2)]
    gate_grads = []
    hits = None
    for k in range(2):
        hit = onehot_columns(slots[k], 0, gate_grad_ref.shape[1])
        picked = jnp.where(hit, gate_grad_ref[...], 0.0)
        gate_grads.append(jnp.sum(picked, -1, keepdims=True))
        hit = onehot_columns(col_ref[:, 2 + k : 3 + k], 0, total)
        hits = hit if hits is None else hits | hit
    hits = hits.astype(F32).astype(BF16)
    mean = gates[0] * gate_grads[0] + gates[1] * gate_grads[1]
    lane = iota((gates[0].shape[0], 3 * experts), 1)
    part = (lane >= experts).astype(I32) + (lane >= 2 * experts).astype(I32)
    label = lane - part * experts
    logit_grads = 0.0
    for k in range(2):
        own = (label * capacity <= slots[k]) & (slots[k] < (label + 1) * capacity)
        logit_grads = logit_grads + jnp.where(own, gates[k] * (gate_grads[k] - mean), 0.0)
    high, middle, low = split_three(logit_grads)
    split = jnp.where(part == 0, high, jnp.where(part == 1, middle, low)).astype(BF16)
    norm_grad = dot_nn(hits, rows_ref[...]) + dot_nn(split, router_ref[...])
    router_grad = dot_tn(split, norm_ref[...])
    router_grad_ref[...] = (
        router_grad[:experts] + router_grad[experts : 2 * experts] + router_grad[2 * experts :]
    )
    unit, recip = unit_norm(hidden_ref[...])
    gain_grad_ref[...] = jnp.sum(norm_grad * unit, 0, keepdims=True)
    scaled = norm_grad * gain_ref[1:2, :]
    back = recip * (scaled - unit * jnp.mean(scaled * unit, -1, keepdims=True))
    grad_ref[...] = cot_ref[...].astype(F32) + back
    branch_ref[...] = grad_ref[...].astype(BF16)
    gather_lanes(mix_refs, place, mixed_ref)
    mixed_t = mixed_ref[...].T
    result = 0.0
    for group in range(groups):
        cols = out_refs[group].shape[1]
        lanes = pl.ds(pl.multiple_of((place ^ group) * cols, cols), cols)
        branch = branch_ref[:, lanes]
        result = result + dot_nt(branch, out_refs[group][...])
        wgrad_refs[group][...] = dot_nn(mixed_t, branch).astype(BF16)
    mixgrad_ref[...] = result.astype(BF16)


def undispatch(
    where, gains, router_t3, slots_col, gates, gate_grads, hidden, normed, cotangent, rows, mixed,
    out_weights,
):
    count, width = hidden.shape
    groups = len(mixed)
    experts = router_t3.shape[0] // 3
    args = (where, gains, router_t3, slots_col, gates, gate_grads, hidden, normed, cotangent, rows)
    result = call(
        functools.partial(undispatch_body, groups, experts),
        (
            shape_of((count, width), F32),
            shape_of((count, width), BF16),
            shape_of((experts, width), F32),
            shape_of((1, width), F32),
        )
        + tuple(shape_of(w.shape, BF16) for w in out_weights),
        (*args, *mixed, *out_weights),
        [SMEM] + [VMEM] * (9 + 2 * groups),
        [pltpu.VMEM((count, width), BF16)] * 2,
        name="undispatch",
    )
    return result[:4], list(result[4:])


def finish_body(x_ref, gain_ref, norm_grad_ref, grad_ref, out_ref, gain_grad_ref):
    unit, recip = unit_norm(x_ref[...].astype(F32))
    norm_grad = norm_grad_ref[...]
    gain_grad_ref[...] = jnp.sum(norm_grad * unit, 0, keepdims=True)
    scaled = norm_grad * gain_ref[0:1, :]
    back = recip * (scaled - unit * jnp.mean(scaled * unit, -1, keepdims=True))
    out_ref[...] = (grad_ref[...] + back).astype(BF16)


def finish(tokens, gains, norm_grad, grad):
    count, width = tokens.shape
    return call(
        finish_body,
        (shape_of((count, width), BF16), shape_of((1, width), F32)),
        (tokens, gains, norm_grad, grad),
        [VMEM] * 4,
        name="finish",
    )


def expert_body(groups, chunk, rows_ref, outer_ref, gate_ref, *refs):
    in_refs, down_refs = refs[:groups], refs[groups : 2 * groups]
    made_ref, back_ref, outer_out_ref, gate_grad_ref = refs[2 * groups : 2 * groups + 4]
    act_ref, low_ref, buf_ref, sems = refs[2 * groups + 4 :]
    share = down_refs[0].shape[0]
    hidden = share * groups

    def copies(group):
        spot = pl.ds(group * share, share)
        return (
            pltpu.make_async_copy(in_refs[group], buf_ref.at[0:2, spot], sems.at[2 * group]),
            pltpu.make_async_copy(down_refs[group], buf_ref.at[2, spot], sems.at[2 * group + 1]),
        )

    @pl.when(pl.program_id(0) == 0)
    def _():
        for group in range(groups):
            for copy in copies(group):
                copy.start()

    rows = rows_ref[...]
    low_outer = (outer_ref[...].astype(F32) * gate_ref[...]).astype(BF16)
    outer_out_ref[...] = low_outer

    @pl.when(pl.program_id(0) == 0)
    def _():
        for group in range(groups):
            for copy in copies(group):
                copy.wait()

    for first in range(0, hidden, chunk):
        part = slice(first, first + chunk)
        gate, up = dot_nt(rows, buf_ref[0, part, :]), dot_nt(rows, buf_ref[1, part, :])
        act_grad = dot_nt(low_outer, buf_ref[2, part, :])
        square = gate * gate
        inner = gate * (0.7978845608028654 + (0.7978845608028654 * 0.044715) * square)
        rise = 0.5 + 0.5 * jnp.tanh(inner)
        bent = gate * rise
        act_ref[:, part] = (bent * up).astype(BF16)
        slope = rise + bent * (1.0 - rise) * (
            2 * 0.7978845608028654 + (6 * 0.7978845608028654 * 0.044715) * square
        )
        low_ref[0, :, part] = (act_grad * up * slope).astype(BF16)
        low_ref[1, :, part] = (act_grad * bent).astype(BF16)
    made = dot_nn(act_ref[...], buf_ref[2]).astype(BF16)
    made_ref[...] = made
    back = dot_nn(low_ref[0], buf_ref[0]) + dot_nn(low_ref[1], buf_ref[1])
    back_ref[...] = back.astype(BF16)
    gate_grad_ref[...] = jnp.sum(
        outer_ref[...].astype(F32) * made.astype(F32), -1, keepdims=True
    )


def experts_pass(rows, outer, gate_column, in_weights, down_weights, block=320, chunk=256):
    total, width = rows.shape
    groups = len(in_weights)
    hidden = down_weights[0].shape[0] * groups
    row_spec = pl.BlockSpec((block, width), lambda i: (i, 0))
    column = pl.BlockSpec((block, 1), lambda i: (i, 0))
    wide = pl.BlockSpec((block, hidden), lambda i: (i, 0))
    both = pl.BlockSpec((2, block, hidden), lambda i: (0, i, 0))
    return pl.pallas_call(
        functools.partial(expert_body, groups, chunk),
        grid=(total // block,),
        out_shape=(
            shape_of((total, width), BF16),
            shape_of((total, width), BF16),
            shape_of((total, width), BF16),
            shape_of((total, 1), F32),
            shape_of((total, hidden), BF16),
            shape_of((2, total, hidden), BF16),
        ),
        in_specs=[row_spec, row_spec, column] + [ANY] * (2 * groups),
        out_specs=(row_spec, row_spec, row_spec, column, wide, both),
        scratch_shapes=[
            pltpu.VMEM((3, hidden, width), BF16),
            pltpu.SemaphoreType.DMA((2 * groups,)),
        ],
        cost_estimate=pl.CostEstimate(flops=LIGHT, bytes_accessed=LIGHT, transcendentals=0),
        name="experts",
    )(rows, outer, gate_column, *in_weights, *down_weights)


def swap(value, axis, bit):
    size = lax.axis_size(axis)
    return lax.ppermute(value, axis, [(i, i ^ bit) for i in range(size)])


def bits_of(axis):
    size = lax.axis_size(axis)
    return [1 << b for b in range(size.bit_length() - 1)]


def after(value, *others):
    return lax.optimization_barrier((value, *others))[0]


def gather_far(shard, axis):
    held = {0: shard}
    for bit in reversed(bits_of(axis)[1:]):
        held.update({place | bit: swap(piece, axis, bit) for place, piece in held.items()})
    return held


def gather_near(held, axis):
    held = dict(held)
    held.update({place | 1: swap(piece, axis, 1) for place, piece in held.items()})
    return [held[place] for place in sorted(held)]


def scatter_sum(parts, axis):
    held = dict(enumerate(parts))
    bits = bits_of(axis)
    for bit in bits:
        last = bit == bits[-1]
        got = {place ^ bit: swap(piece, axis, bit) for place, piece in held.items() if place & bit}
        held = {
            place: (held[place].astype(F32) + piece.astype(F32)).astype(F32 if last else BF16)
            for place, piece in got.items()
        }
    return held[0]


def halve(value, axis, bit):
    upper = (lax.axis_index(axis) // bit) % 2 == 1
    half = value.shape[0] // 2
    low, high = value[:half], value[half:]
    got = swap(jnp.where(upper, low, high), axis, bit)
    kept = jnp.where(upper, high, low)
    return (kept.astype(F32) + got.astype(F32)).astype(BF16)


def double(value, axis, bit):
    upper = (lax.axis_index(axis) // bit) % 2 == 1
    got = swap(value, axis, bit)
    return jnp.where(upper, jnp.concatenate([got, value]), jnp.concatenate([value, got]))


def sum_over(value, axis, bits):
    for bit in bits:
        value = halve(value, axis, bit)
    for bit in reversed(bits):
        value = double(value, axis, bit)
    return value


def sum_small(value, axes):
    value = value.reshape(-1, TILE)
    for axis in axes:
        for bit in bits_of(axis):
            value = value + swap(value, axis, bit)
    return value.reshape(-1)


def exchange(rows, axis):
    size = lax.axis_size(axis)
    total, width = rows.shape
    blocks = rows.reshape(size, total // size, width)
    return lax.all_to_all(blocks, axis, 0, 0, tiled=True)


def per_device(
    tokens,
    cotangent,
    span_starts,
    routes,
    norm_gains,
    bias_table,
    router,
    attn_qkv,
    attn_out,
    expert_in,
    expert_down,
):
    assert span_starts.shape[0] == 1
    tok_count, model_width = tokens.shape
    buckets, head_count = bias_table.shape
    head_size = model_width // head_count
    experts = router.shape[1]
    capacity = (10 * tok_count + 4 * experts - 1) // (4 * experts)
    total = experts * capacity
    place = lax.axis_index("wshard")
    where = jnp.stack([place.astype(I32), span_starts[0]])
    diag = jnp.asarray(diagonal_ones(buckets))
    diag_bias = jnp.dot(bias_table.T, diag, precision=PRECISE)
    router_t = router.T
    expert_in = jnp.swapaxes(expert_in[0], 1, 2)
    expert_down = expert_down[0]

    qkv_far = gather_far(attn_qkv, "wshard")
    slots_row, slots_col, outer_sent = route(routes, cotangent, experts, capacity)
    outer_rows = exchange(outer_sent, "dp").reshape(total, model_width)
    qkv_all = gather_near(qkv_far, "wshard")
    out_far = gather_far(after(attn_out, qkv_far[2]), "wshard")
    out_all = gather_near(out_far, "wshard")
    in_far = gather_far(after(expert_in, out_far[2]), "wshard")
    in_all = gather_near(in_far, "wshard")
    down_far = gather_far(after(expert_down, in_far[2]), "wshard")
    down_all = gather_near(down_far, "wshard")
    groups = len(qkv_all)

    qkv, mixed = [], []
    turn = after(where, slots_row)
    for g in range(groups):
        one = attend(g, turn, tokens, norm_gains, diag_bias, qkv_all[g], head_size)
        qkv.append(one[0])
        mixed.append(one[1])
        turn = after(where, one[1])
    hidden, normed_two, gates, sent = dispatch(
        turn, tokens, norm_gains, router_t, slots_row, slots_col, mixed, out_all, capacity
    )
    arrived = exchange(sent, "dp")
    rows = arrived[:, :capacity].reshape(total, model_width)
    gate_column = jnp.sum(arrived[:, capacity : capacity + 3, :capacity].astype(F32), 1)
    gate_column = gate_column.reshape(total, 1)

    order = [g for g in range(groups) if g % 2 == 0] + [g for g in range(groups) if g % 2]
    made, back, outer_low, gate_grads, act, low = experts_pass(
        rows, outer_rows, gate_column, [in_all[g] for g in order], [down_all[g] for g in order]
    )
    owners = total // capacity
    extra = jnp.stack(split_three(gate_grads.reshape(owners, capacity)), 1).astype(BF16)
    extra = jnp.pad(extra, ((0, 0), (0, EXTRA - 3), (0, model_width - capacity)))
    message = jnp.concatenate([back.reshape(owners, capacity, model_width), extra], 1)
    back_rows = exchange(message.reshape(-1, model_width), "dp")
    gate_grad_row = jnp.sum(back_rows[:, capacity : capacity + 3, :capacity].astype(F32), 1)
    gate_grad_row = gate_grad_row.reshape(1, total)
    back_rows = back_rows.reshape(-1, model_width)

    half = act.shape[1] // 2
    far_part = [low[0, :, half:], low[1, :, half:], act[:, half:]]
    near_part = [low[0, :, :half], low[1, :, :half], act[:, :half]]
    right = [rows, rows, outer_low]
    sums = []
    for far_one, near_one, rows_one in zip(far_part, near_part, right):
        got = swap(dot_tn(far_one, rows_one).astype(BF16), "wshard", 1)
        sums.append((dot_tn(near_one, rows_one) + got.astype(F32)).astype(BF16))
    share = half // 2
    sums = [s[:share].astype(F32) + swap(s[share:], "wshard", 2).astype(F32) for s in sums]
    grad_expert_in = jnp.swapaxes(jnp.stack(sums[:2]), 1, 2)[None]
    grad_expert_down = sums[2][None]

    (grad_hidden, mixed_grad, router_grad, gain_two), out_grads = undispatch(
        where, norm_gains, jnp.concatenate([router_t] * 3, 0), slots_col, gates, gate_grad_row,
        hidden, normed_two, cotangent, back_rows, mixed, out_all,
    )
    made_rows = exchange(after(made, back_rows), "dp").reshape(total, model_width)
    bits = bits_of("dp")
    other_bits = [bits[1], bits[0]] + bits[2:]
    out_sum = scatter_sum(out_grads, "wshard").astype(BF16)
    grad_attn_out = sum_over(out_sum, "dp", bits).astype(F32)
    small = jnp.concatenate([gain_two.reshape(-1), router_grad.reshape(-1)])
    small = sum_small(small, ("wshard", "dp"))
    gain_two, router_grad = small[:model_width], small[model_width:]

    norm_grad = None
    qkv_grads = [None] * groups
    heads = head_count // groups
    diag_all = jnp.zeros((head_count, diag.shape[1]), F32)
    turn = where
    for g in reversed(range(groups)):
        qkv_grads[g], norm_grad, diag_grad = attend_back(
            g, turn, tokens, norm_gains, diag_bias, qkv_all[g], qkv[g], mixed_grad, norm_grad,
            head_size,
        )
        turn = after(where, diag_grad)
        diag_all = lax.dynamic_update_slice_in_dim(
            diag_all, diag_grad.reshape(heads, -1), (place ^ g) * heads, 0
        )
    grad_tokens, gain_one = finish(tokens, norm_gains, norm_grad, grad_hidden)
    table_grad = lax.dot_general(diag, diag_all, (((1,), (1,)), ((), ())), precision=PRECISE)
    small = jnp.concatenate([gain_one.reshape(-1), table_grad.reshape(-1)])
    small = sum_small(small, ("wshard", "dp"))

    qkv_sum = scatter_sum(qkv_grads, "wshard").astype(BF16)
    wide = qkv_sum.shape[2]
    qkv_sum = qkv_sum.reshape(-1, wide)
    middle = qkv_sum.shape[0] // 2
    qkv_sum = jnp.concatenate(
        [
            sum_over(qkv_sum[:middle], "dp", bits).astype(F32),
            sum_over(qkv_sum[middle:], "dp", other_bits).astype(F32),
        ]
    )
    grad_attn_qkv = qkv_sum.reshape(3, model_width, wide)
    output = combine(hidden, after(gates, grad_tokens), slots_col, made_rows)
    return (
        output,
        grad_tokens,
        jnp.stack([small[:model_width], gain_two]),
        small[model_width:].reshape(buckets, head_count),
        router_grad.reshape(experts, model_width).T,
        grad_attn_qkv,
        grad_attn_out,
        grad_expert_in,
        grad_expert_down,
    )


def solution(mesh):
    return jax.shard_map(
        per_device,
        mesh=mesh,
        in_specs=(
            P(("dp", "wshard"), None),
            P(("dp", "wshard"), None),
            P(("dp", "wshard")),
            P(("dp", "wshard"), None),
            P(),
            P(),
            P(),
            P(None, None, "wshard"),
            P(None, "wshard"),
            P("dp", None, None, "wshard"),
            P("dp", "wshard", None),
        ),
        out_specs=(
            P(("dp", "wshard"), None),
            P(("dp", "wshard"), None),
            P(),
            P(),
            P(),
            P(None, None, "wshard"),
            P(None, "wshard"),
            P("dp", None, None, "wshard"),
            P("dp", "wshard", None),
        ),
        check_vma=False,
    )
```

```python
import functools

import jax
import jax.numpy as jnp
import numpy as np
from jax import lax
from jax.experimental import pallas as pl
from jax.experimental.pallas import tpu as pltpu
from jax.sharding import PartitionSpec as P

PIC = 256
PRECISE = lax.Precision.HIGHEST
EPSILON = 1e-06
MASKED_SCORE = -1e30
BUCKET_EDGES = (8, 11, 16, 23, 32, 45, 64, 91)
TILE = 128
F32 = jnp.float32
BF16 = jnp.bfloat16
I32 = jnp.int32
VMEM = pl.BlockSpec(memory_space=pltpu.VMEM)
SMEM = pl.BlockSpec(memory_space=pltpu.SMEM)
ANY = pl.BlockSpec(memory_space=pl.ANY)
LIGHT = 1024
EXTRA = 8


def dot_nn(a, b):
    return lax.dot_general(a, b, (((1,), (0,)), ((), ())), preferred_element_type=F32)


def dot_nt(a, b):
    return lax.dot_general(a, b, (((1,), (1,)), ((), ())), preferred_element_type=F32)


def dot_tn(a, b):
    return lax.dot_general(a, b, (((0,), (0,)), ((), ())), preferred_element_type=F32)


def iota(shape, axis):
    return lax.broadcasted_iota(I32, shape, axis)


def shape_of(shape, dtype):
    return jax.ShapeDtypeStruct(shape, dtype)


def call(body, out, args, specs, scratch=(), name=None):
    return pl.pallas_call(
        body,
        out_shape=out,
        in_specs=specs,
        out_specs=jax.tree.map(lambda _: VMEM, out),
        scratch_shapes=list(scratch),
        cost_estimate=pl.CostEstimate(flops=LIGHT, bytes_accessed=LIGHT, transcendentals=0),
        name=name,
    )(*args)


def bucket_of(offset):
    magnitude = np.abs(offset)
    coarse = 7 + sum((magnitude >= bound).astype(np.int32) for bound in BUCKET_EDGES)
    return np.where(magnitude < 8, magnitude, coarse) + 16 * (offset < 0)


def diagonal_ones(bucket_count):
    column = np.arange(2 * TILE)
    signed = np.where(column < TILE, column, column - 2 * TILE)
    offsets = np.concatenate([TILE * step - signed for step in (-1, 0, 1)])
    used = np.tile(column != TILE, 3)
    hit = bucket_of(offsets)[None, :] == np.arange(bucket_count)[:, None]
    near = (hit & used[None, :]).astype(np.float32)
    far = np.zeros((bucket_count, 2 * TILE), np.float32)
    far[bucket_of(np.array(TILE)), :TILE] = 1
    far[bucket_of(np.array(-TILE)), TILE:] = 1
    return np.concatenate([near, far], 1)


def onehot_rows(first, count, slots_row):
    index = iota((count, slots_row.shape[1]), 0) + first
    hit = (index == slots_row[0:1, :]) | (index == slots_row[1:2, :])
    return hit.astype(F32).astype(BF16)


def onehot_columns(slots_column, first, count):
    index = iota((slots_column.shape[0], count), 1) + first
    return index == slots_column


def place_rows(slots_row, rows, out_ref):
    total = out_ref.shape[0]
    step = 256
    for first in range(0, total, step):
        size = min(step, total - first)
        hit = onehot_rows(first, size, slots_row)
        out_ref[first : first + size, :] = dot_nn(hit, rows).astype(BF16)


def route_body(experts, capacity, routes_ref, cot_ref, row_ref, col_ref, out_ref):
    tokens = cot_ref.shape[0]
    first, second = iota((tokens, tokens), 0), iota((tokens, tokens), 1)
    routes = routes_ref[...]
    label = iota((experts, tokens), 0)
    hits = ((routes[0:1] == label) | (routes[1:2] == label)).astype(F32).astype(BF16)
    before = dot_nn(hits, (first < second).astype(F32).astype(BF16))
    slots = []
    for k in range(2):
        own = jnp.sum(jnp.where(routes[k : k + 1] == label, before, 0.0), 0, keepdims=True)
        slots.append(own.astype(I32) + routes[k : k + 1] * capacity)
    slots = jnp.concatenate(slots * 4, 0)
    row_ref[...] = slots
    col_ref[...] = slots.astype(F32).T.astype(I32)
    place_rows(slots, cot_ref[...], out_ref)


def route(routes, cotangent, experts, capacity):
    tokens, width = cotangent.shape
    total = experts * capacity
    return call(
        functools.partial(route_body, experts, capacity),
        (
            shape_of((8, tokens), I32),
            shape_of((tokens, 8), I32),
            shape_of((total, width), BF16),
        ),
        (routes.T, cotangent),
        [VMEM] * 2,
        name="route",
    )


def unit_norm(values):
    recip = lax.rsqrt(jnp.mean(values * values, -1, keepdims=True) + EPSILON)
    return values * recip, recip


def fill_mask(mask_ref, span_start):
    size = mask_ref.shape[0]
    i, j = iota((size, size), 0), iota((size, size), 1)

    def inside(p):
        return (p >= span_start) & (p < span_start + PIC)

    visible = (j <= i) | (inside(i) & inside(j))
    mask_ref[...] = jnp.where(visible, 0.0, MASKED_SCORE)


def head_lanes(which, size):
    lane = iota((1, 2 * size), 1)
    return ((lane >= size) == (which == 1)).astype(F32).astype(BF16)


def bias_tiles(diag_row):
    tiles = []
    for step in range(3):
        row = diag_row[:, 2 * TILE * step : 2 * TILE * (step + 1)]
        wide = jnp.broadcast_to(row, (TILE, 2 * TILE))
        tiles.append(pltpu.roll(wide, 0, 1, stride=1, stride_axis=0)[:, :TILE])
    return tiles, (diag_row[:, 6 * TILE : 7 * TILE], diag_row[:, 7 * TILE :])


def score_tiles(block, query, keys, tiles, far, mask_ref):
    raw = dot_nt(query, keys)
    rows = slice(block * TILE, (block + 1) * TILE)
    result = []
    for other in range(keys.shape[0] // TILE):
        piece = raw[:, other * TILE : (other + 1) * TILE]
        step = block - other
        piece = piece + (far[0] if step >= 2 else far[1] if step <= -2 else tiles[step + 1])
        if step <= 0:
            piece = piece + mask_ref[rows, other * TILE : (other + 1) * TILE]
        result.append(piece)
    return result


def softmax_tiles(pieces):
    top = functools.reduce(jnp.maximum, pieces)
    top = jnp.max(top, -1, keepdims=True)
    powers = [jnp.exp(piece - top) for piece in pieces]
    total = jnp.sum(functools.reduce(jnp.add, powers), -1, keepdims=True)
    scale = 1.0 / total
    return [power * scale for power in powers]


def attend_body(
    group, head_size, where_ref, x_ref, gain_ref, diag_ref, w_ref, qkv_ref, mix_ref,
    norm_ref, mask_ref,
):
    count = x_ref.shape[0]
    fill_mask(mask_ref, where_ref[1])
    unit, _ = unit_norm(x_ref[...].astype(F32))
    norm_ref[...] = (unit * gain_ref[0:1, :]).astype(BF16)
    for c in range(3):
        qkv_ref[c] = dot_nn(norm_ref[...], w_ref[c]).astype(BF16)
    width = 2 * head_size
    heads = w_ref.shape[2] // head_size
    first_head = (where_ref[0] ^ group) * heads

    def pair(p, carry):
        lanes = pl.ds(pl.multiple_of(p * width, width), width)
        query, keys, value = qkv_ref[0, :, lanes], qkv_ref[1, :, lanes], qkv_ref[2, :, lanes]
        mixed = [None] * (count // TILE)
        for which in range(2):
            head = first_head + 2 * p + which
            own = head_lanes(which, head_size)
            own_query, own_value = query * (own * 0.125), value * own
            tiles, far = bias_tiles(diag_ref[pl.ds(head, 1), :])
            for block in range(count // TILE):
                rows = slice(block * TILE, (block + 1) * TILE)
                pieces = score_tiles(block, own_query[rows], keys, tiles, far, mask_ref)
                probs = jnp.concatenate([t.astype(BF16) for t in softmax_tiles(pieces)], 1)
                part = dot_nn(probs, own_value)
                mixed[block] = part if which == 0 else mixed[block] + part
        for block in range(count // TILE):
            rows = slice(block * TILE, (block + 1) * TILE)
            mix_ref[rows, lanes] = mixed[block].astype(BF16)
        return carry

    lax.fori_loop(0, heads // 2, pair, 0)


def attend(group, where, tokens, gains, diag, weights, head_size):
    count, width = tokens.shape
    cols = weights.shape[2]
    return call(
        functools.partial(attend_body, group, head_size),
        (shape_of((3, count, cols), BF16), shape_of((count, cols), BF16)),
        (where, tokens, gains, diag, weights),
        [SMEM] + [VMEM] * 4,
        [pltpu.VMEM((count, width), BF16), pltpu.VMEM((count, count), F32)],
        name="attend",
    )


def attend_back_body(
    group, head_size, where_ref, x_ref, gain_ref, diag_ref, w_ref, qkv_ref, mixgrad_ref,
    sum_ref, wgrad_ref, sum_out_ref, diag_out_ref, norm_t_ref, mask_ref, grads_ref, probs_ref,
    scores_ref,
):
    count = x_ref.shape[0]
    blocks = count // TILE
    fill_mask(mask_ref, where_ref[1])
    unit, _ = unit_norm(x_ref[...].astype(F32))
    norm_t_ref[...] = (unit * gain_ref[0:1, :]).astype(BF16).T
    width = 2 * head_size
    cols = w_ref.shape[2]
    heads = cols // head_size
    place = where_ref[0] ^ group

    def pair(p, carry):
        offset = pl.multiple_of(p * width, width)
        lanes = pl.ds(offset, width)
        query, keys, value = qkv_ref[0, :, lanes], qkv_ref[1, :, lanes], qkv_ref[2, :, lanes]
        outer = mixgrad_ref[:, pl.ds(pl.multiple_of(place * cols + offset, width), width)]
        query_sum, key_sum, value_sum = [None] * blocks, None, None
        for which in range(2):
            head = place * heads + 2 * p + which
            own = head_lanes(which, head_size)
            own_query, own_key, own_outer = query * own, keys * own, outer * own
            scaled = own_query * 0.125
            tiles, far = bias_tiles(diag_ref[pl.ds(head, 1), :])
            near_sums, far_sums = [None] * 3, [None] * 2
            for block in range(blocks):
                rows = slice(block * TILE, (block + 1) * TILE)
                probs = softmax_tiles(
                    score_tiles(block, scaled[rows], keys, tiles, far, mask_ref)
                )
                prob_grads = dot_nt(own_outer[rows], value)
                prob_grads = [
                    prob_grads[:, j * TILE : (j + 1) * TILE] for j in range(blocks)
                ]
                delta = functools.reduce(
                    jnp.add, [a * b for a, b in zip(probs, prob_grads)]
                )
                delta = jnp.sum(delta, -1, keepdims=True)
                low = [(a * (b - delta)).astype(BF16) for a, b in zip(probs, prob_grads)]
                for other in range(blocks):
                    step = block - other
                    wide = low[other].astype(F32)
                    if abs(step) >= 2:
                        side = 0 if step > 0 else 1
                        old = far_sums[side]
                        far_sums[side] = wide if old is None else old + wide
                    else:
                        old = near_sums[step + 1]
                        near_sums[step + 1] = wide if old is None else old + wide
                probs_ref[which, rows, :] = jnp.concatenate([t.astype(BF16) for t in probs], 1)
                low = jnp.concatenate(low, 1)
                scores_ref[which, rows, :] = low
                part = dot_nn(low, own_key)
                query_sum[block] = part if which == 0 else query_sum[block] + part
            part = dot_tn(scores_ref[which], own_query)
            key_sum = part if which == 0 else key_sum + part
            part = dot_tn(probs_ref[which], own_outer)
            value_sum = part if which == 0 else value_sum + part
            local = 2 * p + which
            for step in range(3):
                wide = jnp.concatenate([near_sums[step], jnp.zeros((TILE, TILE), F32)], 1)
                half = TILE // 2
                while half:
                    turned = pltpu.roll(wide[half:], 2 * TILE - half, 1)
                    wide = wide[:half] + turned
                    half //= 2
                for side in range(2):
                    spot = 2 * step + side
                    diag_out_ref[local, spot : spot + 1, :] = wide[:, TILE * side : TILE * (side + 1)]
            for side in range(2):
                diag_out_ref[local, 6 + side : 7 + side, :] = jnp.sum(
                    far_sums[side], 0, keepdims=True
                )
        for block in range(blocks):
            rows = slice(block * TILE, (block + 1) * TILE)
            grads_ref[0, rows, lanes] = (query_sum[block] * 0.125).astype(BF16)
        grads_ref[1, :, lanes] = (key_sum * 0.125).astype(BF16)
        grads_ref[2, :, lanes] = value_sum.astype(BF16)
        return carry

    lax.fori_loop(0, heads // 2, pair, 0)
    total = sum_ref[...] if sum_ref is not None else None
    for c in range(3):
        wgrad_ref[c] = dot_nn(norm_t_ref[...], grads_ref[c]).astype(BF16)
        part = dot_nt(grads_ref[c], w_ref[c])
        total = part if total is None else total + part
    sum_out_ref[...] = total


def attend_back(
    group, where, tokens, gains, diag, weights, qkv, mixed_grad, total, head_size
):
    count, width = tokens.shape
    cols = weights.shape[2]
    heads = cols // head_size
    body = functools.partial(attend_back_body, group, head_size)
    args = (where, tokens, gains, diag, weights, qkv, mixed_grad)
    specs = [SMEM] + [VMEM] * 6
    if total is None:
        full = body

        def body(*refs):
            full(*refs[:7], None, *refs[7:])

    else:
        args, specs = args + (total,), specs + [VMEM]
    return call(
        body,
        (
            shape_of((3, width, cols), BF16),
            shape_of((count, width), F32),
            shape_of((heads, 8, TILE), F32),
        ),
        args,
        specs,
        [
            pltpu.VMEM((width, count), BF16),
            pltpu.VMEM((count, count), F32),
            pltpu.VMEM((3, count, cols), BF16),
            pltpu.VMEM((2, count, count), BF16),
            pltpu.VMEM((2, count, count), BF16),
        ],
        name="attend_back",
    )


def gather_lanes(refs, place, out_ref):
    for group, ref in enumerate(refs):
        cols = ref.shape[1]
        spot = pl.multiple_of((place ^ group) * cols, cols)
        out_ref[:, pl.ds(spot, cols)] = ref[...]


def split_three(value):
    high = value.astype(BF16).astype(F32)
    middle = (value - high).astype(BF16).astype(F32)
    return high, middle, value - high - middle


def dispatch_body(
    groups, experts, where_ref, x_ref, gain_ref, router_ref, row_ref, col_ref, *refs
):
    mix_refs, out_refs = refs[:groups], refs[groups : 2 * groups]
    hidden_ref, norm_ref, gate_ref, sent_ref, sent_gate_ref, mixed_ref = refs[2 * groups :]
    place = where_ref[0]
    gather_lanes(mix_refs, place, mixed_ref)
    for group in range(groups):
        cols = out_refs[group].shape[1]
        lanes = pl.ds(pl.multiple_of((place ^ group) * cols, cols), cols)
        branch = dot_nn(mixed_ref[...], out_refs[group][...])
        hidden_ref[:, lanes] = x_ref[:, lanes].astype(F32) + branch
    unit, _ = unit_norm(hidden_ref[...])
    norm_ref[...] = (unit * gain_ref[1:2, :]).astype(BF16)
    place_rows(row_ref[...], norm_ref[...], sent_ref)
    logits = dot_nt(norm_ref[...], router_ref[...])
    capacity = sent_ref.shape[0] // experts
    slots = [col_ref[:, k : k + 1] for k in range(2)]
    lane = iota(logits.shape, 1)
    chosen = []
    for k in range(2):
        own = (lane * capacity <= slots[k]) & (slots[k] < (lane + 1) * capacity)
        chosen.append(jnp.sum(jnp.where(own, logits, 0.0), -1, keepdims=True))
    top = jnp.maximum(chosen[0], chosen[1])
    powers = [jnp.exp(c - top) for c in chosen]
    gates = [power / (powers[0] + powers[1]) for power in powers]
    for k in range(2):
        gate_ref[:, k : k + 1] = gates[k]
    lane = iota((slots[0].shape[0], sent_gate_ref.shape[2]), 1)
    for expert in range(experts):
        label = jnp.where(lane < capacity, lane + expert * capacity, -1)
        part = 0.0
        for k in range(2):
            part = part + jnp.where(label == slots[k], gates[k], 0.0)
        line = jnp.sum(part, 0, keepdims=True)
        sent_gate_ref[expert] = jnp.broadcast_to(line, sent_gate_ref.shape[1:])


def dispatch(where, tokens, gains, router_t, slots_row, slots_col, mixed, out_weights, capacity):
    count, width = tokens.shape
    groups = len(mixed)
    experts = router_t.shape[0]
    return call(
        functools.partial(dispatch_body, groups, experts),
        (
            shape_of((count, width), F32),
            shape_of((count, width), BF16),
            shape_of((count, 2), F32),
            shape_of((experts * capacity, width), BF16),
            shape_of((experts, EXTRA, -(-capacity // TILE) * TILE), F32),
        ),
        (where, tokens, gains, router_t, slots_row, slots_col, *mixed, *out_weights),
        [SMEM] + [VMEM] * (5 + 2 * groups),
        [pltpu.VMEM((count, width), BF16)],
        name="dispatch",
    )


def combine_body(hidden_ref, gate_ref, col_ref, rows_ref, out_ref):
    count = out_ref.shape[0]
    total = rows_ref.shape[0]
    step = min(count, 256)
    for first in range(0, count, step):
        part = slice(first, first + step)
        result = hidden_ref[part, :]
        for k in range(2):
            hit = onehot_columns(col_ref[part, k : k + 1], 0, total).astype(F32).astype(BF16)
            result = result + gate_ref[part, k : k + 1] * dot_nn(hit, rows_ref[...])
        out_ref[part, :] = result.astype(BF16)


def combine(hidden, gates, slots_col, rows):
    count, width = hidden.shape
    return call(
        combine_body,
        shape_of((count, width), BF16),
        (hidden, gates, slots_col, rows),
        [VMEM] * 4,
        name="combine",
    )


def undispatch_body(
    groups, experts, where_ref, gain_ref, router_ref, col_ref, gate_ref, gate_grad_ref, hidden_ref,
    norm_ref, cot_ref, rows_ref, *refs
):
    mix_refs, out_refs = refs[:groups], refs[groups : 2 * groups]
    grad_ref, mixgrad_ref, router_grad_ref, gain_grad_ref = refs[2 * groups : 2 * groups + 4]
    wgrad_refs = refs[2 * groups + 4 : 3 * groups + 4]
    mixed_ref, branch_ref = refs[3 * groups + 4 :]
    place = where_ref[0]
    total = rows_ref.shape[0]
    capacity = total // experts
    gates = [gate_ref[:, k : k + 1] for k in range(2)]
    slots = [col_ref[:, k : k + 1] for k in range(2)]
    gate_grads = []
    hits = None
    for k in range(2):
        hit = onehot_columns(slots[k], 0, total)
        picked = jnp.where(hit, gate_grad_ref[...], 0.0)
        gate_grads.append(jnp.sum(picked, -1, keepdims=True))
        hits = hit if hits is None else hits | hit
    hits = hits.astype(F32).astype(BF16)
    mean = gates[0] * gate_grads[0] + gates[1] * gate_grads[1]
    lane = iota((gates[0].shape[0], 3 * experts), 1)
    part = (lane >= experts).astype(I32) + (lane >= 2 * experts).astype(I32)
    label = lane - part * experts
    logit_grads = 0.0
    for k in range(2):
        own = (label * capacity <= slots[k]) & (slots[k] < (label + 1) * capacity)
        logit_grads = logit_grads + jnp.where(own, gates[k] * (gate_grads[k] - mean), 0.0)
    high, middle, low = split_three(logit_grads)
    split = jnp.where(part == 0, high, jnp.where(part == 1, middle, low)).astype(BF16)
    norm_grad = dot_nn(hits, rows_ref[...]) + dot_nn(split, router_ref[...])
    router_grad = dot_tn(split, norm_ref[...])
    router_grad_ref[...] = (
        router_grad[:experts] + router_grad[experts : 2 * experts] + router_grad[2 * experts :]
    )
    unit, recip = unit_norm(hidden_ref[...])
    gain_grad_ref[...] = jnp.sum(norm_grad * unit, 0, keepdims=True)
    scaled = norm_grad * gain_ref[1:2, :]
    back = recip * (scaled - unit * jnp.mean(scaled * unit, -1, keepdims=True))
    grad_ref[...] = cot_ref[...].astype(F32) + back
    branch_ref[...] = grad_ref[...].astype(BF16)
    gather_lanes(mix_refs, place, mixed_ref)
    mixed_t = mixed_ref[...].T
    result = 0.0
    for group in range(groups):
        cols = out_refs[group].shape[1]
        lanes = pl.ds(pl.multiple_of((place ^ group) * cols, cols), cols)
        branch = branch_ref[:, lanes]
        result = result + dot_nt(branch, out_refs[group][...])
        wgrad_refs[group][...] = dot_nn(mixed_t, branch).astype(BF16)
    mixgrad_ref[...] = result.astype(BF16)


def undispatch(
    where, gains, router_t3, slots_col, gates, gate_grads, hidden, normed, cotangent, rows, mixed,
    out_weights,
):
    count, width = hidden.shape
    groups = len(mixed)
    experts = router_t3.shape[0] // 3
    args = (where, gains, router_t3, slots_col, gates, gate_grads, hidden, normed, cotangent, rows)
    result = call(
        functools.partial(undispatch_body, groups, experts),
        (
            shape_of((count, width), F32),
            shape_of((count, width), BF16),
            shape_of((experts, width), F32),
            shape_of((1, width), F32),
        )
        + tuple(shape_of(w.shape, BF16) for w in out_weights),
        (*args, *mixed, *out_weights),
        [SMEM] + [VMEM] * (9 + 2 * groups),
        [pltpu.VMEM((count, width), BF16)] * 2,
        name="undispatch",
    )
    return result[:4], list(result[4:])


def finish_body(x_ref, gain_ref, norm_grad_ref, grad_ref, out_ref, gain_grad_ref):
    unit, recip = unit_norm(x_ref[...].astype(F32))
    norm_grad = norm_grad_ref[...]
    gain_grad_ref[...] = jnp.sum(norm_grad * unit, 0, keepdims=True)
    scaled = norm_grad * gain_ref[0:1, :]
    back = recip * (scaled - unit * jnp.mean(scaled * unit, -1, keepdims=True))
    out_ref[...] = (grad_ref[...] + back).astype(BF16)


def finish(tokens, gains, norm_grad, grad):
    count, width = tokens.shape
    return call(
        finish_body,
        (shape_of((count, width), BF16), shape_of((1, width), F32)),
        (tokens, gains, norm_grad, grad),
        [VMEM] * 4,
        name="finish",
    )


def flip(value, change, size):
    result = 0
    bit = 1
    while bit < size:
        one, two = lax.rem(lax.div(value, bit), 2), lax.rem(lax.div(change, bit), 2)
        result = result + bit * (one + two - 2 * one * two)
        bit *= 2
    return result


def column_of(row, size):
    spot = iota((size, row.shape[1]), 0) == iota((size, row.shape[1]), 1)
    return jnp.sum(jnp.where(spot, row, 0.0), 1, keepdims=True)


def row_of(column, lanes):
    spot = iota((column.shape[0], lanes), 0) == iota((column.shape[0], lanes), 1)
    return jnp.sum(jnp.where(spot, column, 0.0), 0, keepdims=True)


def moe_body(size, groups, chunk, sent_ref, gates_ref, outer_ref, *refs):
    in_refs, down_refs = refs[:groups], refs[groups : 2 * groups]
    refs = refs[2 * groups :]
    back_out, extra_out, made_out = refs[:3]
    grad_outs = refs[3 : 3 + groups]
    (
        buf, rows, gates, outer, low_outer, made_sum, back_sum, act, low, stage, extra_stage,
        made, grad_stage, weight_sems, send_sems, recv_sems, give_sems, take_sems, own_sems,
        save_sems, grad_sems,
    ) = refs[3 + groups :]
    share = down_refs[0].shape[0]
    part_size = share * groups // 2
    capacity, width = outer.shape[1:]
    both = 2 * capacity
    me = lax.axis_index("dp")
    pairs = size // 2
    my_pair = lax.div(me, 2)
    mesh_id = pl.DeviceIdType.MESH

    barrier = pltpu.get_barrier_semaphore()
    for step in range(1, size):
        peer = flip(me, step, size)
        pl.semaphore_signal(barrier, inc=1, device_id={"dp": peer}, device_id_type=mesh_id)
    pl.semaphore_wait(barrier, size - 1)

    def remote(source, target, sent, got, peer):
        return pltpu.make_async_remote_copy(
            src_ref=source, dst_ref=target, send_sem=sent, recv_sem=got,
            device_id={"dp": peer}, device_id_type=mesh_id,
        )

    def forth(source, target, peer):
        return (
            remote(sent_ref.at[source], rows.at[target], send_sems.at[source, 0],
                   recv_sems.at[target, 0], peer),
            remote(gates_ref.at[source], gates.at[target], send_sems.at[source, 1],
                   recv_sems.at[target, 1], peer),
        )

    def back_copies(source, target, peer):
        return (
            remote(stage.at[source], back_out.at[target], give_sems.at[source, 0],
                   take_sems.at[target, 0], peer),
            remote(extra_stage.at[source], extra_out.at[target], give_sems.at[source, 1],
                   take_sems.at[target, 1], peer),
        )

    own = (
        pltpu.make_async_copy(sent_ref.at[me], rows.at[me], own_sems.at[0]),
        pltpu.make_async_copy(gates_ref.at[me], gates.at[me], own_sems.at[1]),
        pltpu.make_async_copy(outer_ref, outer, own_sems.at[2]),
    )
    own_back = (
        pltpu.make_async_copy(stage.at[me], back_out.at[me], own_sems.at[3]),
        pltpu.make_async_copy(extra_stage.at[me], extra_out.at[me], own_sems.at[4]),
    )
    for copy in own:
        copy.start()
    for step in range(1, size):
        peer = flip(me, step, size)
        for copy in forth(peer, me, peer):
            copy.start()

    def weight_copies(group):
        spot = pl.ds(group * share, share)
        return (
            pltpu.make_async_copy(in_refs[group], buf.at[0:2, spot], weight_sems.at[group, 0]),
            pltpu.make_async_copy(down_refs[group], buf.at[2, spot], weight_sems.at[group, 1]),
        )

    for group in range(groups):
        for copy in weight_copies(group):
            copy.start()
    for copy in own:
        copy.wait()

    def hidden_part(pair, base):
        spot = pl.ds(pl.multiple_of(pair * both, both), both)
        two = pl.ds(2 * pair, 2)
        these = rows[two].reshape(both, width)
        outers = low_outer[spot, :]
        for first in range(0, part_size, chunk):
            last = min(first + chunk, part_size)
            part, lanes = slice(base + first, base + last), slice(first, last)
            gate, up = dot_nt(these, buf[0, part, :]), dot_nt(these, buf[1, part, :])
            act_grad = dot_nt(outers, buf[2, part, :])
            square = gate * gate
            inner = gate * (0.7978845608028654 + (0.7978845608028654 * 0.044715) * square)
            rise = 0.5 + 0.5 * jnp.tanh(inner)
            bent = gate * rise
            act[spot, lanes] = (bent * up).astype(BF16)
            slope = rise + bent * (1.0 - rise) * (
                2 * 0.7978845608028654 + (6 * 0.7978845608028654 * 0.044715) * square
            )
            low[0, spot, lanes] = (act_grad * up * slope).astype(BF16)
            low[1, spot, lanes] = (act_grad * bent).astype(BF16)
        whole = slice(base, base + part_size)
        result = dot_nn(act[spot, :], buf[2, whole, :])
        back = dot_nn(low[0, spot, :], buf[0, whole, :]) + dot_nn(low[1, spot, :], buf[1, whole, :])
        return spot, result, back

    def near_step(step, carry):
        pair = flip(my_pair, step, pairs)
        first = 2 * pair

        @pl.when(step == 0)
        def _():
            peer = flip(me, 1, size)
            for copy in forth(me, peer, peer):
                copy.wait_recv()

        @pl.when(step > 0)
        def _():
            for which in range(2):
                for copy in forth(me, first + which, first + which):
                    copy.wait_recv()

        for which in range(2):
            gate = column_of(gates[first + which, 0:1, :], capacity)
            spot = pl.ds(pl.multiple_of((first + which) * capacity, capacity), capacity)
            low_outer[spot, :] = (outer[first + which].astype(F32) * gate).astype(BF16)
        spot, result, back = hidden_part(pair, 0)
        made_sum[spot, :] = result
        back_sum[spot, :] = back
        return carry

    def weight_grads(half):
        every = rows[...].reshape(size * capacity, width)
        outers = low_outer[...]
        count = 0
        base = half * part_size
        waiting = {}
        for c in range(3):
            source = act if c == 2 else low.at[c]
            for first in range(0, part_size, 2 * chunk):
                last = min(first + 2 * chunk, part_size)
                slot = count % 2
                for copy in waiting.pop(slot, ()):
                    copy.wait()
                piece = dot_tn(source[:, first:last], outers if c == 2 else every)
                grad_stage[slot, : last - first, :] = piece.astype(BF16)
                copies = []
                begin = base + first
                while begin < base + last:
                    group = begin // share
                    end = min(base + last, (group + 1) * share)
                    copies.append(
                        pltpu.make_async_copy(
                            grad_stage.at[slot, pl.ds(begin - base - first, end - begin)],
                            grad_outs[group].at[c, pl.ds(begin - group * share, end - begin)],
                            grad_sems.at[slot, len(copies)],
                        )
                    )
                    begin = end
                for copy in copies:
                    copy.start()
                waiting[slot] = copies
                count += 1
        for copies in waiting.values():
            for copy in copies:
                copy.wait()

    for group in range(groups // 2):
        for copy in weight_copies(group):
            copy.wait()
    lax.fori_loop(0, pairs, near_step, 0)
    weight_grads(0)

    def far_step(step, carry):
        pair = flip(my_pair, pairs - 1 - step, pairs)
        first = 2 * pair
        spot, result, back = hidden_part(pair, part_size)
        result = (made_sum[spot, :] + result).astype(BF16)
        back = (back_sum[spot, :] + back).astype(BF16)
        two = pl.ds(first, 2)
        made[two] = result.reshape(2, capacity, width)
        stage[two] = back.reshape(2, capacity, width)
        for which in range(2):
            grads = outer[first + which].astype(F32) * made[first + which].astype(F32)
            line = row_of(jnp.sum(grads, -1, keepdims=True), extra_stage.shape[2])
            extra_stage[first + which] = jnp.broadcast_to(line, extra_stage.shape[1:])
        pltpu.make_async_copy(made.at[two], made_out.at[two], save_sems.at[step]).start()

        @pl.when(step < pairs - 1)
        def _():
            for which in range(2):
                for copy in back_copies(first + which, me, first + which):
                    copy.start()

        @pl.when(step == pairs - 1)
        def _():
            peer = flip(me, 1, size)
            for copy in back_copies(peer, me, peer):
                copy.start()
            for copy in own_back:
                copy.start()

        return carry

    for group in range(groups // 2, groups):
        for copy in weight_copies(group):
            copy.wait()
    lax.fori_loop(0, pairs, far_step, 0)
    weight_grads(1)
    for copy in own_back:
        copy.wait()
    for step in range(pairs):
        two = pl.ds(2 * flip(my_pair, pairs - 1 - step, pairs), 2)
        pltpu.make_async_copy(made.at[two], made_out.at[two], save_sems.at[step]).wait()
    for step in range(1, size):
        peer = flip(me, step, size)
        for copy in forth(peer, me, peer):
            copy.wait_send()
        for copy in back_copies(peer, me, peer):
            copy.wait_send()
        for copy in back_copies(me, peer, peer):
            copy.wait_recv()


def moe(sent, gates, outer, in_weights, down_weights, chunk=256):
    size, capacity, width = sent.shape
    groups = len(in_weights)
    share = down_weights[0].shape[0]
    part = share * groups // 2
    total = size * capacity
    extra = gates.shape[1:]
    dma = pltpu.SemaphoreType.DMA
    result = pl.pallas_call(
        functools.partial(moe_body, size, groups, chunk),
        out_shape=(
            shape_of((size, capacity, width), BF16),
            shape_of((size, *extra), F32),
            shape_of((size, capacity, width), BF16),
        )
        + (shape_of((3, share, width), BF16),) * groups,
        in_specs=[ANY] * (3 + 2 * groups),
        out_specs=(ANY,) * (3 + groups),
        scratch_shapes=[
            pltpu.VMEM((3, share * groups, width), BF16),
            pltpu.VMEM((size, capacity, width), BF16),
            pltpu.VMEM((size, *extra), F32),
            pltpu.VMEM((size, capacity, width), BF16),
            pltpu.VMEM((total, width), BF16),
            pltpu.VMEM((total, width), F32),
            pltpu.VMEM((total, width), F32),
            pltpu.VMEM((total, part), BF16),
            pltpu.VMEM((2, total, part), BF16),
            pltpu.VMEM((size, capacity, width), BF16),
            pltpu.VMEM((size, *extra), F32),
            pltpu.VMEM((size, capacity, width), BF16),
            pltpu.VMEM((2, 2 * chunk, width), BF16),
            dma((groups, 2)),
            dma((size, 2)),
            dma((size, 2)),
            dma((size, 2)),
            dma((size, 2)),
            dma((5,)),
            dma((size // 2,)),
            dma((2, 3)),
        ],
        cost_estimate=pl.CostEstimate(flops=LIGHT, bytes_accessed=LIGHT, transcendentals=0),
        compiler_params=pltpu.CompilerParams(
            collective_id=0, has_side_effects=True, vmem_limit_bytes=66_000_000
        ),
        name="experts",
    )(sent, gates, outer, *in_weights, *down_weights)
    return result[:3], list(result[3:])


def expert_body(groups, chunk, rows_ref, outer_ref, gate_ref, *refs):
    in_refs, down_refs = refs[:groups], refs[groups : 2 * groups]
    made_ref, back_ref, outer_out_ref, gate_grad_ref = refs[2 * groups : 2 * groups + 4]
    act_ref, low_ref, buf_ref, sems = refs[2 * groups + 4 :]
    share = down_refs[0].shape[0]
    hidden = share * groups

    def copies(group):
        spot = pl.ds(group * share, share)
        return (
            pltpu.make_async_copy(in_refs[group], buf_ref.at[0:2, spot], sems.at[2 * group]),
            pltpu.make_async_copy(down_refs[group], buf_ref.at[2, spot], sems.at[2 * group + 1]),
        )

    @pl.when(pl.program_id(0) == 0)
    def _():
        for group in range(groups):
            for copy in copies(group):
                copy.start()

    rows = rows_ref[...]
    low_outer = (outer_ref[...].astype(F32) * gate_ref[...]).astype(BF16)
    outer_out_ref[...] = low_outer

    @pl.when(pl.program_id(0) == 0)
    def _():
        for group in range(groups):
            for copy in copies(group):
                copy.wait()

    for first in range(0, hidden, chunk):
        part = slice(first, first + chunk)
        gate, up = dot_nt(rows, buf_ref[0, part, :]), dot_nt(rows, buf_ref[1, part, :])
        act_grad = dot_nt(low_outer, buf_ref[2, part, :])
        square = gate * gate
        inner = gate * (0.7978845608028654 + (0.7978845608028654 * 0.044715) * square)
        rise = 0.5 + 0.5 * jnp.tanh(inner)
        bent = gate * rise
        act_ref[:, part] = (bent * up).astype(BF16)
        slope = rise + bent * (1.0 - rise) * (
            2 * 0.7978845608028654 + (6 * 0.7978845608028654 * 0.044715) * square
        )
        low_ref[0, :, part] = (act_grad * up * slope).astype(BF16)
        low_ref[1, :, part] = (act_grad * bent).astype(BF16)
    made = dot_nn(act_ref[...], buf_ref[2]).astype(BF16)
    made_ref[...] = made
    back = dot_nn(low_ref[0], buf_ref[0]) + dot_nn(low_ref[1], buf_ref[1])
    back_ref[...] = back.astype(BF16)
    gate_grad_ref[...] = jnp.sum(
        outer_ref[...].astype(F32) * made.astype(F32), -1, keepdims=True
    )


def experts_pass(rows, outer, gate_column, in_weights, down_weights, block=320, chunk=256):
    total, width = rows.shape
    groups = len(in_weights)
    hidden = down_weights[0].shape[0] * groups
    row_spec = pl.BlockSpec((block, width), lambda i: (i, 0))
    column = pl.BlockSpec((block, 1), lambda i: (i, 0))
    wide = pl.BlockSpec((block, hidden), lambda i: (i, 0))
    both = pl.BlockSpec((2, block, hidden), lambda i: (0, i, 0))
    return pl.pallas_call(
        functools.partial(expert_body, groups, chunk),
        grid=(total // block,),
        out_shape=(
            shape_of((total, width), BF16),
            shape_of((total, width), BF16),
            shape_of((total, width), BF16),
            shape_of((total, 1), F32),
            shape_of((total, hidden), BF16),
            shape_of((2, total, hidden), BF16),
        ),
        in_specs=[row_spec, row_spec, column] + [ANY] * (2 * groups),
        out_specs=(row_spec, row_spec, row_spec, column, wide, both),
        scratch_shapes=[
            pltpu.VMEM((3, hidden, width), BF16),
            pltpu.SemaphoreType.DMA((2 * groups,)),
        ],
        cost_estimate=pl.CostEstimate(flops=LIGHT, bytes_accessed=LIGHT, transcendentals=0),
        name="experts",
    )(rows, outer, gate_column, *in_weights, *down_weights)


def moe_plain(sent, gates, outer, in_weights, down_weights):
    size, capacity, width = sent.shape
    total = size * capacity
    rows = exchange(sent.reshape(total, width), "dp").reshape(total, width)
    gate_column = lax.all_to_all(gates, "dp", 0, 0, tiled=True)[:, 0, :capacity].reshape(total, 1)
    made, back, outer_low, gate_grads, act, low = experts_pass(
        rows, outer.reshape(total, width), gate_column, in_weights, down_weights
    )
    extra = jnp.pad(gate_grads.reshape(size, 1, capacity), ((0, 0), (0, EXTRA - 1), (0, 0)))
    extra = lax.all_to_all(extra, "dp", 0, 0, tiled=True)
    share = down_weights[0].shape[0]
    grads = []
    for group in range(len(in_weights)):
        part = slice(group * share, (group + 1) * share)
        pieces = [dot_tn(low[c, :, part], rows) for c in range(2)]
        grads.append(jnp.stack(pieces + [dot_tn(act[:, part], outer_low)]).astype(BF16))
    shape = (size, capacity, width)
    return (exchange(back, "dp"), extra, made.reshape(shape)), grads


def swap(value, axis, bit):
    size = lax.axis_size(axis)
    return lax.ppermute(value, axis, [(i, i ^ bit) for i in range(size)])


def bits_of(axis):
    size = lax.axis_size(axis)
    return [1 << b for b in range(size.bit_length() - 1)]


def after(value, *others):
    return lax.optimization_barrier((value, *others))[0]


def gather_far(shard, axis):
    held = {0: shard}
    for bit in reversed(bits_of(axis)[1:]):
        held.update({place | bit: swap(piece, axis, bit) for place, piece in held.items()})
    return held


def gather_near(held, axis):
    held = dict(held)
    held.update({place | 1: swap(piece, axis, 1) for place, piece in held.items()})
    return [held[place] for place in sorted(held)]


def scatter_sum(parts, axis):
    held = dict(enumerate(parts))
    bits = bits_of(axis)
    for bit in bits:
        last = bit == bits[-1]
        got = {place ^ bit: swap(piece, axis, bit) for place, piece in held.items() if place & bit}
        held = {
            place: (held[place].astype(F32) + piece.astype(F32)).astype(F32 if last else BF16)
            for place, piece in got.items()
        }
    return held[0]


def halve(value, axis, bit):
    upper = (lax.axis_index(axis) // bit) % 2 == 1
    half = value.shape[0] // 2
    low, high = value[:half], value[half:]
    got = swap(jnp.where(upper, low, high), axis, bit)
    kept = jnp.where(upper, high, low)
    return (kept.astype(F32) + got.astype(F32)).astype(BF16)


def double(value, axis, bit):
    upper = (lax.axis_index(axis) // bit) % 2 == 1
    got = swap(value, axis, bit)
    return jnp.where(upper, jnp.concatenate([got, value]), jnp.concatenate([value, got]))


def sum_over(value, axis, bits):
    for bit in bits:
        value = halve(value, axis, bit)
    for bit in reversed(bits):
        value = double(value, axis, bit)
    return value


def sum_small(value, axes):
    value = value.reshape(-1, TILE)
    for axis in axes:
        for bit in bits_of(axis):
            value = value + swap(value, axis, bit)
    return value.reshape(-1)


def exchange(rows, axis):
    size = lax.axis_size(axis)
    total, width = rows.shape
    blocks = rows.reshape(size, total // size, width)
    return lax.all_to_all(blocks, axis, 0, 0, tiled=True)


def per_device(
    tokens,
    cotangent,
    span_starts,
    routes,
    norm_gains,
    bias_table,
    router,
    attn_qkv,
    attn_out,
    expert_in,
    expert_down,
):
    assert span_starts.shape[0] == 1
    tok_count, model_width = tokens.shape
    buckets, head_count = bias_table.shape
    head_size = model_width // head_count
    experts = router.shape[1]
    capacity = (10 * tok_count + 4 * experts - 1) // (4 * experts)
    total = experts * capacity
    place = lax.axis_index("wshard")
    where = jnp.stack([place.astype(I32), span_starts[0]])
    diag = jnp.asarray(diagonal_ones(buckets))
    diag_bias = jnp.dot(bias_table.T, diag, precision=PRECISE)
    router_t = router.T
    expert_in = jnp.swapaxes(expert_in[0], 1, 2)
    expert_down = expert_down[0]

    qkv_far = gather_far(attn_qkv, "wshard")
    slots_row, slots_col, outer_sent = route(routes, cotangent, experts, capacity)
    outer_rows = exchange(outer_sent, "dp")
    qkv_all = gather_near(qkv_far, "wshard")
    out_far = gather_far(after(attn_out, qkv_far[2]), "wshard")
    out_all = gather_near(out_far, "wshard")
    in_far = gather_far(after(expert_in, out_far[2]), "wshard")
    in_all = gather_near(in_far, "wshard")
    down_far = gather_far(after(expert_down, in_far[2]), "wshard")
    down_all = gather_near(down_far, "wshard")
    groups = len(qkv_all)

    qkv, mixed = [], []
    turn = after(where, slots_row)
    for g in range(groups):
        one = attend(g, turn, tokens, norm_gains, diag_bias, qkv_all[g], head_size)
        qkv.append(one[0])
        mixed.append(one[1])
        turn = after(where, one[1])
    hidden, normed_two, gates, sent, sent_gates = dispatch(
        turn, tokens, norm_gains, router_t, slots_row, slots_col, mixed, out_all, capacity
    )

    through = moe if capacity % 16 == 0 else moe_plain
    (back_rows, back_extra, made), expert_grads = through(
        sent.reshape(-1, capacity, model_width), sent_gates, outer_rows, in_all, down_all
    )
    gate_grad_row = back_extra[:, 0, :capacity].reshape(1, total)
    back_rows = back_rows.reshape(total, model_width)
    expert_sum = scatter_sum(expert_grads, "wshard")
    grad_expert_in = jnp.swapaxes(expert_sum[:2], 1, 2)[None]
    grad_expert_down = expert_sum[2][None]

    (grad_hidden, mixed_grad, router_grad, gain_two), out_grads = undispatch(
        where, norm_gains, jnp.concatenate([router_t] * 3, 0), slots_col, gates, gate_grad_row,
        hidden, normed_two, cotangent, back_rows, mixed, out_all,
    )
    made_rows = exchange(made.reshape(total, model_width), "dp").reshape(total, model_width)
    bits = bits_of("dp")
    other_bits = [bits[1], bits[0]] + bits[2:]
    out_sum = scatter_sum(out_grads, "wshard").astype(BF16)
    grad_attn_out = sum_over(out_sum, "dp", bits).astype(F32)
    small = jnp.concatenate([gain_two.reshape(-1), router_grad.reshape(-1)])
    small = sum_small(small, ("wshard", "dp"))
    gain_two, router_grad = small[:model_width], small[model_width:]

    norm_grad = None
    qkv_grads = [None] * groups
    heads = head_count // groups
    diag_all = jnp.zeros((head_count, diag.shape[1]), F32)
    turn = where
    for g in reversed(range(groups)):
        qkv_grads[g], norm_grad, diag_grad = attend_back(
            g, turn, tokens, norm_gains, diag_bias, qkv_all[g], qkv[g], mixed_grad, norm_grad,
            head_size,
        )
        turn = after(where, diag_grad)
        diag_all = lax.dynamic_update_slice_in_dim(
            diag_all, diag_grad.reshape(heads, -1), (place ^ g) * heads, 0
        )
    grad_tokens, gain_one = finish(tokens, norm_gains, norm_grad, grad_hidden)
    table_grad = lax.dot_general(diag, diag_all, (((1,), (1,)), ((), ())), precision=PRECISE)
    small = jnp.concatenate([gain_one.reshape(-1), table_grad.reshape(-1)])
    small = sum_small(small, ("wshard", "dp"))

    qkv_sum = scatter_sum(qkv_grads, "wshard").astype(BF16)
    wide = qkv_sum.shape[2]
    qkv_sum = qkv_sum.reshape(-1, wide)
    middle = qkv_sum.shape[0] // 2
    qkv_sum = jnp.concatenate(
        [
            sum_over(qkv_sum[:middle], "dp", bits).astype(F32),
            sum_over(qkv_sum[middle:], "dp", other_bits).astype(F32),
        ]
    )
    grad_attn_qkv = qkv_sum.reshape(3, model_width, wide)
    output = combine(hidden, after(gates, grad_tokens), slots_col, made_rows)
    return (
        output,
        grad_tokens,
        jnp.stack([small[:model_width], gain_two]),
        small[model_width:].reshape(buckets, head_count),
        router_grad.reshape(experts, model_width).T,
        grad_attn_qkv,
        grad_attn_out,
        grad_expert_in,
        grad_expert_down,
    )


def solution(mesh):
    return jax.shard_map(
        per_device,
        mesh=mesh,
        in_specs=(
            P(("dp", "wshard"), None),
            P(("dp", "wshard"), None),
            P(("dp", "wshard")),
            P(("dp", "wshard"), None),
            P(),
            P(),
            P(),
            P(None, None, "wshard"),
            P(None, "wshard"),
            P("dp", None, None, "wshard"),
            P("dp", "wshard", None),
        ),
        out_specs=(
            P(("dp", "wshard"), None),
            P(("dp", "wshard"), None),
            P(),
            P(),
            P(),
            P(None, None, "wshard"),
            P(None, "wshard"),
            P("dp", None, None, "wshard"),
            P("dp", "wshard", None),
        ),
        check_vma=False,
    )
```

```python
import functools

import jax
import jax.numpy as jnp
import numpy as np
from jax import lax
from jax.experimental import pallas as pl
from jax.experimental.pallas import tpu as pltpu
from jax.sharding import PartitionSpec as P

PIC = 256
PRECISE = lax.Precision.HIGHEST
EPSILON = 1e-06
MASKED_SCORE = -1e30
BUCKET_EDGES = (8, 11, 16, 23, 32, 45, 64, 91)
TILE = 128
F32 = jnp.float32
BF16 = jnp.bfloat16
I32 = jnp.int32
VMEM = pl.BlockSpec(memory_space=pltpu.VMEM)
SMEM = pl.BlockSpec(memory_space=pltpu.SMEM)
ANY = pl.BlockSpec(memory_space=pl.ANY)
LIGHT = 1024
EXTRA = 8


def dot_nn(a, b):
    return lax.dot_general(a, b, (((1,), (0,)), ((), ())), preferred_element_type=F32)


def dot_nt(a, b):
    return lax.dot_general(a, b, (((1,), (1,)), ((), ())), preferred_element_type=F32)


def dot_tn(a, b):
    return lax.dot_general(a, b, (((0,), (0,)), ((), ())), preferred_element_type=F32)


def iota(shape, axis):
    return lax.broadcasted_iota(I32, shape, axis)


def shape_of(shape, dtype):
    return jax.ShapeDtypeStruct(shape, dtype)


def call(body, out, args, specs, scratch=(), name=None):
    return pl.pallas_call(
        body,
        out_shape=out,
        in_specs=specs,
        out_specs=jax.tree.map(lambda _: VMEM, out),
        scratch_shapes=list(scratch),
        cost_estimate=pl.CostEstimate(flops=LIGHT, bytes_accessed=LIGHT, transcendentals=0),
        name=name,
    )(*args)


def bucket_of(offset):
    magnitude = np.abs(offset)
    coarse = 7 + sum((magnitude >= bound).astype(np.int32) for bound in BUCKET_EDGES)
    return np.where(magnitude < 8, magnitude, coarse) + 16 * (offset < 0)


def diagonal_ones(bucket_count):
    column = np.arange(2 * TILE)
    signed = np.where(column < TILE, column, column - 2 * TILE)
    offsets = np.concatenate([TILE * step - signed for step in (-1, 0, 1)])
    used = np.tile(column != TILE, 3)
    hit = bucket_of(offsets)[None, :] == np.arange(bucket_count)[:, None]
    near = (hit & used[None, :]).astype(np.float32)
    far = np.zeros((bucket_count, 2 * TILE), np.float32)
    far[bucket_of(np.array(TILE)), :TILE] = 1
    far[bucket_of(np.array(-TILE)), TILE:] = 1
    return np.concatenate([near, far], 1)


def onehot_rows(first, count, slots_row):
    index = iota((count, slots_row.shape[1]), 0) + first
    hit = (index == slots_row[0:1, :]) | (index == slots_row[1:2, :])
    return hit.astype(F32).astype(BF16)


def onehot_columns(slots_column, first, count):
    index = iota((slots_column.shape[0], count), 1) + first
    return index == slots_column


def route_slots(experts, capacity, routes):
    tokens = routes.shape[1]
    label = iota((experts, tokens), 0)
    hits = ((routes[0:1] == label) | (routes[1:2] == label)).astype(F32).astype(BF16)
    earlier = iota((tokens, tokens), 0) < iota((tokens, tokens), 1)
    before = dot_nn(hits, earlier.astype(F32).astype(BF16))
    slots = []
    for k in range(2):
        own = jnp.sum(jnp.where(routes[k : k + 1] == label, before, 0.0), 0, keepdims=True)
        slots.append(own.astype(I32) + routes[k : k + 1] * capacity)
    return jnp.concatenate(slots * 4, 0)


def unit_norm(values):
    recip = lax.rsqrt(jnp.mean(values * values, -1, keepdims=True) + EPSILON)
    return values * recip, recip


def fill_mask(mask_ref, span_start):
    size = mask_ref.shape[0]
    i, j = iota((size, size), 0), iota((size, size), 1)

    def inside(p):
        return (p >= span_start) & (p < span_start + PIC)

    visible = (j <= i) | (inside(i) & inside(j))
    mask_ref[...] = jnp.where(visible, 0.0, MASKED_SCORE)


def head_lanes(which, size):
    lane = iota((1, 2 * size), 1)
    return ((lane >= size) == (which == 1)).astype(F32).astype(BF16)


def bias_tiles(diag_row):
    tiles = []
    for step in range(3):
        row = diag_row[:, 2 * TILE * step : 2 * TILE * (step + 1)]
        wide = jnp.broadcast_to(row, (TILE, 2 * TILE))
        tiles.append(pltpu.roll(wide, 0, 1, stride=1, stride_axis=0)[:, :TILE])
    return tiles, (diag_row[:, 6 * TILE : 7 * TILE], diag_row[:, 7 * TILE :])


def score_tiles(block, query, keys, tiles, far, mask_ref):
    raw = dot_nt(query, keys)
    rows = slice(block * TILE, (block + 1) * TILE)
    result = []
    for other in range(keys.shape[0] // TILE):
        piece = raw[:, other * TILE : (other + 1) * TILE]
        step = block - other
        piece = piece + (far[0] if step >= 2 else far[1] if step <= -2 else tiles[step + 1])
        if step <= 0:
            piece = piece + mask_ref[rows, other * TILE : (other + 1) * TILE]
        result.append(piece)
    return result


def softmax_tiles(pieces):
    top = functools.reduce(jnp.maximum, pieces)
    top = jnp.max(top, -1, keepdims=True)
    powers = [jnp.exp(piece - top) for piece in pieces]
    total = jnp.sum(functools.reduce(jnp.add, powers), -1, keepdims=True)
    scale = 1.0 / total
    return [power * scale for power in powers]


def split_three(value):
    high = value.astype(BF16).astype(F32)
    middle = (value - high).astype(BF16).astype(F32)
    return high, middle, value - high - middle


def remote_copy(source, target, sent, got, axis, peer):
    return pltpu.make_async_remote_copy(
        src_ref=source,
        dst_ref=target,
        send_sem=sent,
        recv_sem=got,
        device_id={axis: peer},
        device_id_type=pl.DeviceIdType.MESH,
    )


def greet(peers):
    barrier = pltpu.get_barrier_semaphore()
    for axis, peer in peers:
        pl.semaphore_signal(
            barrier, inc=1, device_id={axis: peer}, device_id_type=pl.DeviceIdType.MESH
        )
    pl.semaphore_wait(barrier, len(peers))


def project_and_attend(place, group, groups, head_size, norm, diag_ref, w_ref, qkv_ref, mix_ref, mask):
    count = norm.shape[0]
    cols = w_ref.shape[-1]
    width = 2 * head_size
    owner = flip(place, group, groups)
    for c in range(3):
        qkv_ref[group, c] = dot_nn(norm[...], w_ref[group, c]).astype(BF16)

    def pair(p, carry):
        offset = pl.multiple_of(p * width, width)
        lanes = pl.ds(offset, width)
        query, keys, value = (qkv_ref[group, c, :, lanes] for c in range(3))
        mixed = [None] * (count // TILE)
        for which in range(2):
            head = owner * (cols // head_size) + 2 * p + which
            own = head_lanes(which, head_size)
            own_query, own_value = query * (own * 0.125), value * own
            tiles, far = bias_tiles(diag_ref[pl.ds(head, 1), :])
            for block in range(count // TILE):
                rows = slice(block * TILE, (block + 1) * TILE)
                pieces = score_tiles(block, own_query[rows], keys, tiles, far, mask)
                probs = jnp.concatenate([t.astype(BF16) for t in softmax_tiles(pieces)], 1)
                part = dot_nn(probs, own_value)
                mixed[block] = part if which == 0 else mixed[block] + part
        target = pl.ds(pl.multiple_of(owner * cols + offset, width), width)
        for block in range(count // TILE):
            rows = slice(block * TILE, (block + 1) * TILE)
            mix_ref[rows, target] = mixed[block].astype(BF16)
        return carry

    lax.fori_loop(0, cols // width, pair, 0)


def front_body(
    size, groups, head_size, span_ref, routes_ref, gain_ref, diag_ref, router_ref, tok_hbm, cot_hbm,
    qkv_shard, out_shard, in_shard, down_shard,
    col_ref, gate_ref, sent_gate_ref, qkvw_out, outw_out, qkv_out, mixed_out, hidden_out, norm_out,
    sent_out, outer_out, in_out, down_out,
    tok, cot, qkvw, outw, qkv, mixed, hidden, norm, sent, outer, mask, row, load_sems, save_sems,
    shard_sems, outer_send, outer_got,
):
    me, place = lax.axis_index("dp"), lax.axis_index("wshard")
    near, far = flip(place, 1, groups), flip(place, 2, groups)
    peers = [("dp", flip(me, step, size)) for step in range(1, size)]
    greet(peers + [("wshard", near), ("wshard", far)])

    sources = (qkv_shard, out_shard, in_shard, down_shard)

    def held(item, group):
        if item == 0:
            return qkvw.at[group]
        if item == 1:
            return outw.at[group]
        return (in_out if item == 2 else down_out).at[group - 1]

    def shard_copy(kind, item):
        source = held(item, 2) if kind == 2 else sources[item]
        return remote_copy(
            source, held(item, (1, 2, 3)[kind]), shard_sems.at[kind, item, 0],
            shard_sems.at[kind, item, 1], "wshard", far if kind == 1 else near,
        )

    for item in range(2):
        shard_copy(1, item).start()
        shard_copy(0, item).start()
    loads = [
        pltpu.make_async_copy(source, target, load_sems.at[i])
        for i, (source, target) in enumerate(
            ((cot_hbm, cot), (tok_hbm, tok), (qkv_shard, qkvw.at[0]), (out_shard, outw.at[0]))
        )
    ]
    for copy in loads:
        copy.start()
    for item in range(2, 4):
        shard_copy(1, item).start()
        shard_copy(0, item).start()

    experts, capacity = size, sent.shape[1]
    count = tok.shape[0]
    slots = route_slots(experts, capacity, routes_ref[...])
    row[...] = slots
    col_ref[...] = slots.astype(F32).T.astype(I32)
    loads[0].wait()

    def place_outer(expert, carry):
        outer[expert] = dot_nn(onehot_rows(expert * capacity, capacity, row[...]), cot[...]).astype(BF16)
        return carry

    lax.fori_loop(0, experts, place_outer, 0)
    fill_mask(mask, span_ref[0])
    loads[1].wait()
    unit, _ = unit_norm(tok[...].astype(F32))
    norm[...] = (unit * gain_ref[0:1, :]).astype(BF16)
    loads[2].wait()

    def outer_copy(source, target, peer):
        return remote_copy(
            outer.at[source], outer_out.at[target], outer_send.at[source], outer_got.at[target],
            "dp", peer,
        )

    own_outer = pltpu.make_async_copy(outer.at[me], outer_out.at[me], load_sems.at[4])
    own_outer.start()
    for _, peer in peers:
        outer_copy(peer, me, peer).start()

    def one_group(group, carry):
        @pl.when(group == 1)
        def _():
            shard_copy(0, 0).wait_recv()

        @pl.when(group == 2)
        def _():
            shard_copy(1, 0).wait_recv()
            shard_copy(2, 0).start()

        @pl.when(group == 3)
        def _():
            shard_copy(2, 0).wait_recv()

        project_and_attend(
            place, group, groups, head_size, norm, diag_ref, qkvw, qkv, mixed, mask
        )
        return carry

    lax.fori_loop(0, groups, one_group, 0)
    saves = [
        pltpu.make_async_copy(source, target, save_sems.at[i])
        for i, (source, target) in enumerate(
            (
                (qkvw, qkvw_out), (qkv, qkv_out), (mixed, mixed_out), (outw, outw_out),
                (hidden, hidden_out), (norm, norm_out), (sent, sent_out),
            )
        )
    ]
    for copy in saves[:3]:
        copy.start()
    loads[3].wait()
    shard_copy(0, 1).wait_recv()
    shard_copy(1, 1).wait_recv()
    shard_copy(2, 1).start()

    shard_copy(2, 1).wait_recv()
    saves[3].start()
    for group in range(groups):
        cols = outw.shape[2]
        lanes = pl.ds(pl.multiple_of(flip(place, group, groups) * cols, cols), cols)
        hidden[:, lanes] = tok[:, lanes].astype(F32) + dot_nn(mixed[...], outw[group])
    saves[4].start()
    unit, _ = unit_norm(hidden[...])
    norm[...] = (unit * gain_ref[1:2, :]).astype(BF16)
    saves[5].start()

    def place_sent(expert, carry):
        sent[expert] = dot_nn(onehot_rows(expert * capacity, capacity, row[...]), norm[...]).astype(BF16)
        return carry

    lax.fori_loop(0, experts, place_sent, 0)
    saves[6].start()
    logits = dot_nt(norm[...], router_ref[...])
    slots = [col_ref[:, k : k + 1] for k in range(2)]
    lane = iota(logits.shape, 1)
    chosen = []
    for k in range(2):
        own = (lane * capacity <= slots[k]) & (slots[k] < (lane + 1) * capacity)
        chosen.append(jnp.sum(jnp.where(own, logits, 0.0), -1, keepdims=True))
    top = jnp.maximum(chosen[0], chosen[1])
    powers = [jnp.exp(c - top) for c in chosen]
    gates = [power / (powers[0] + powers[1]) for power in powers]
    for k in range(2):
        gate_ref[:, k : k + 1] = gates[k]
    lane = iota((count, sent_gate_ref.shape[2]), 1)
    for expert in range(experts):
        label = jnp.where(lane < capacity, lane + expert * capacity, -1)
        part = 0.0
        for k in range(2):
            part = part + jnp.where(label == slots[k], gates[k], 0.0)
        line = jnp.sum(part, 0, keepdims=True)
        sent_gate_ref[expert] = jnp.broadcast_to(line, sent_gate_ref.shape[1:])

    for item in range(2, 4):
        shard_copy(1, item).wait_recv()
        shard_copy(2, item).start()
    own_outer.wait()
    for copy in saves:
        copy.wait()
    for _, peer in peers:
        outer_copy(peer, me, peer).wait_send()
        outer_copy(me, peer, peer).wait_recv()
    for item in range(4):
        for kind in range(3):
            shard_copy(kind, item).wait_send()
    for item in range(2, 4):
        shard_copy(0, item).wait_recv()
        shard_copy(2, item).wait_recv()


def front(span, routes, gains, diag, router_t, tokens, cotangent, shards, head_size, capacity):
    count, width = tokens.shape
    size, groups = lax.axis_size("dp"), lax.axis_size("wshard")
    qkv_shard, out_shard, in_shard, down_shard = shards
    cols = out_shard.shape[1]
    lanes = -(-capacity // TILE) * TILE
    dma = pltpu.SemaphoreType.DMA
    block = (size, capacity, width)
    return pl.pallas_call(
        functools.partial(front_body, size, groups, head_size),
        out_shape=(
            shape_of((count, 8), I32),
            shape_of((count, 2), F32),
            shape_of((size, EXTRA, lanes), F32),
            shape_of((groups, *qkv_shard.shape), BF16),
            shape_of((groups, *out_shard.shape), BF16),
            shape_of((groups, 3, count, cols), BF16),
            shape_of((count, width), BF16),
            shape_of((count, width), F32),
            shape_of((count, width), BF16),
            shape_of(block, BF16),
            shape_of(block, BF16),
            shape_of((groups - 1, *in_shard.shape), BF16),
            shape_of((groups - 1, *down_shard.shape), BF16),
        ),
        in_specs=[SMEM] + [VMEM] * 4 + [ANY] * 6,
        out_specs=(VMEM,) * 3 + (ANY,) * 10,
        scratch_shapes=[
            pltpu.VMEM((count, width), BF16),
            pltpu.VMEM((count, width), BF16),
            pltpu.VMEM((groups, *qkv_shard.shape), BF16),
            pltpu.VMEM((groups, *out_shard.shape), BF16),
            pltpu.VMEM((groups, 3, count, cols), BF16),
            pltpu.VMEM((count, width), BF16),
            pltpu.VMEM((count, width), F32),
            pltpu.VMEM((count, width), BF16),
            pltpu.VMEM(block, BF16),
            pltpu.VMEM(block, BF16),
            pltpu.VMEM((count, count), F32),
            pltpu.VMEM((8, count), I32),
            dma((5,)),
            dma((7,)),
            dma((3, 4, 2)),
            dma((size,)),
            dma((size,)),
        ],
        cost_estimate=pl.CostEstimate(flops=LIGHT, bytes_accessed=LIGHT, transcendentals=0),
        compiler_params=pltpu.CompilerParams(
            collective_id=1, has_side_effects=True, vmem_limit_bytes=60_000_000
        ),
        name="front",
    )(span, routes.T, gains, diag, router_t, tokens, cotangent, *shards)


def flip(value, change, size):
    result = 0
    bit = 1
    while bit < size:
        one, two = lax.rem(lax.div(value, bit), 2), lax.rem(lax.div(change, bit), 2)
        result = result + bit * (one + two - 2 * one * two)
        bit *= 2
    return result


def column_of(row, size):
    spot = iota((size, row.shape[1]), 0) == iota((size, row.shape[1]), 1)
    return jnp.sum(jnp.where(spot, row, 0.0), 1, keepdims=True)


def row_of(column, lanes):
    spot = iota((column.shape[0], lanes), 0) == iota((column.shape[0], lanes), 1)
    return jnp.sum(jnp.where(spot, column, 0.0), 0, keepdims=True)


def moe_body(
    size, groups, chunk, sent_ref, gates_ref, outer_ref, own_in, own_down, other_in, other_down, *refs
):
    in_refs = [own_in] + [other_in.at[g] for g in range(groups - 1)]
    down_refs = [own_down] + [other_down.at[g] for g in range(groups - 1)]
    back_out, extra_out, made_out, grad_out, moved_out = refs[:5]
    (
        buf, rows, gates, outer, low_outer, made_sum, back_sum, act, low, stage, extra_stage,
        made, grad_stage, weight_sems, send_sems, recv_sems, give_sems, take_sems, own_sems,
        save_sems, grad_sems, moved_sem,
    ) = refs[5:]
    share = down_refs[0].shape[0]
    part_size = share * groups // 2
    capacity, width = outer.shape[1:]
    both = 2 * capacity
    me = lax.axis_index("dp")
    pairs = size // 2
    my_pair = lax.div(me, 2)
    mesh_id = pl.DeviceIdType.MESH

    place = lax.axis_index("wshard")
    near = flip(place, 1, groups)
    greet([("dp", flip(me, step, size)) for step in range(1, size)] + [("wshard", near)])

    def remote(source, target, sent, got, peer):
        return pltpu.make_async_remote_copy(
            src_ref=source, dst_ref=target, send_sem=sent, recv_sem=got,
            device_id={"dp": peer}, device_id_type=mesh_id,
        )

    def forth(source, target, peer):
        return (
            remote(sent_ref.at[source], rows.at[target], send_sems.at[source, 0],
                   recv_sems.at[target, 0], peer),
            remote(gates_ref.at[source], gates.at[target], send_sems.at[source, 1],
                   recv_sems.at[target, 1], peer),
        )

    def back_copies(source, target, peer):
        return (
            remote(stage.at[source], back_out.at[target], give_sems.at[source, 0],
                   take_sems.at[target, 0], peer),
            remote(extra_stage.at[source], extra_out.at[target], give_sems.at[source, 1],
                   take_sems.at[target, 1], peer),
        )

    own = (
        pltpu.make_async_copy(sent_ref.at[me], rows.at[me], own_sems.at[0]),
        pltpu.make_async_copy(gates_ref.at[me], gates.at[me], own_sems.at[1]),
        pltpu.make_async_copy(outer_ref, outer, own_sems.at[2]),
    )
    own_back = (
        pltpu.make_async_copy(stage.at[me], back_out.at[me], own_sems.at[3]),
        pltpu.make_async_copy(extra_stage.at[me], extra_out.at[me], own_sems.at[4]),
    )
    for copy in own:
        copy.start()
    for step in range(1, size):
        peer = flip(me, step, size)
        for copy in forth(peer, me, peer):
            copy.start()

    def weight_copies(group):
        spot = pl.ds(group * share, share)
        return (
            pltpu.make_async_copy(in_refs[group], buf.at[0:2, spot], weight_sems.at[group, 0]),
            pltpu.make_async_copy(down_refs[group], buf.at[2, spot], weight_sems.at[group, 1]),
        )

    for group in range(groups):
        for copy in weight_copies(group):
            copy.start()
    for copy in own:
        copy.wait()

    def hidden_part(pair, base):
        spot = pl.ds(pl.multiple_of(pair * both, both), both)
        two = pl.ds(2 * pair, 2)
        these = rows[two].reshape(both, width)
        outers = low_outer[spot, :]
        for first in range(0, part_size, chunk):
            last = min(first + chunk, part_size)
            part, lanes = slice(base + first, base + last), slice(first, last)
            gate, up = dot_nt(these, buf[0, part, :]), dot_nt(these, buf[1, part, :])
            act_grad = dot_nt(outers, buf[2, part, :])
            square = gate * gate
            inner = gate * (0.7978845608028654 + (0.7978845608028654 * 0.044715) * square)
            rise = 0.5 + 0.5 * jnp.tanh(inner)
            bent = gate * rise
            act[spot, lanes] = (bent * up).astype(BF16)
            slope = rise + bent * (1.0 - rise) * (
                2 * 0.7978845608028654 + (6 * 0.7978845608028654 * 0.044715) * square
            )
            low[0, spot, lanes] = (act_grad * up * slope).astype(BF16)
            low[1, spot, lanes] = (act_grad * bent).astype(BF16)
        whole = slice(base, base + part_size)
        result = dot_nn(act[spot, :], buf[2, whole, :])
        back = dot_nn(low[0, spot, :], buf[0, whole, :]) + dot_nn(low[1, spot, :], buf[1, whole, :])
        return spot, result, back

    def near_step(step, carry):
        pair = flip(my_pair, step, pairs)
        first = 2 * pair

        @pl.when(step == 0)
        def _():
            peer = flip(me, 1, size)
            for copy in forth(me, peer, peer):
                copy.wait_recv()

        @pl.when(step > 0)
        def _():
            for which in range(2):
                for copy in forth(me, first + which, first + which):
                    copy.wait_recv()

        for which in range(2):
            gate = column_of(gates[first + which, 0:1, :], capacity)
            spot = pl.ds(pl.multiple_of((first + which) * capacity, capacity), capacity)
            low_outer[spot, :] = (outer[first + which].astype(F32) * gate).astype(BF16)
        spot, result, back = hidden_part(pair, 0)
        made_sum[spot, :] = result
        back_sum[spot, :] = back
        return carry

    def sent_all(copies):
        for remote_one, copy in copies:
            if remote_one:
                copy.wait_send()
            else:
                copy.wait()

    def weight_grads(half):
        every = rows[...].reshape(size * capacity, width)
        outers = low_outer[...]
        count = 0
        base = half * part_size
        waiting = {}
        for c in range(3):
            left = act if c == 2 else low.at[c]
            for first in range(0, part_size, 2 * chunk):
                last = min(first + 2 * chunk, part_size)
                slot = count % 2
                sent_all(waiting.pop(slot, ()))
                piece = dot_tn(left[:, first:last], outers if c == 2 else every)
                grad_stage[slot, : last - first, :] = piece.astype(BF16)
                copies = []
                begin = base + first
                while begin < base + last:
                    group = begin // share
                    end = min(base + last, (group + 1) * share)
                    source = grad_stage.at[slot, pl.ds(begin - base - first, end - begin)]
                    spot = pl.ds(begin - group * share, end - begin)
                    sem = grad_sems.at[slot, len(copies)]
                    if group % 2:
                        target = moved_out.at[group // 2, c, spot]
                        copies.append((True, remote_copy(source, target, sem, moved_sem, "wshard", near)))
                    else:
                        target = grad_out.at[group // 2, c, spot]
                        copies.append((False, pltpu.make_async_copy(source, target, sem)))
                    begin = end
                for _, copy in copies:
                    copy.start()
                waiting[slot] = copies
                count += 1
        for copies in waiting.values():
            sent_all(copies)

    for group in range(groups // 2):
        for copy in weight_copies(group):
            copy.wait()
    lax.fori_loop(0, pairs, near_step, 0)
    weight_grads(0)

    def far_step(step, carry):
        pair = flip(my_pair, pairs - 1 - step, pairs)
        first = 2 * pair
        spot, result, back = hidden_part(pair, part_size)
        result = (made_sum[spot, :] + result).astype(BF16)
        back = (back_sum[spot, :] + back).astype(BF16)
        two = pl.ds(first, 2)
        made[two] = result.reshape(2, capacity, width)
        stage[two] = back.reshape(2, capacity, width)
        for which in range(2):
            grads = outer[first + which].astype(F32) * made[first + which].astype(F32)
            line = row_of(jnp.sum(grads, -1, keepdims=True), extra_stage.shape[2])
            extra_stage[first + which] = jnp.broadcast_to(line, extra_stage.shape[1:])
        pltpu.make_async_copy(made.at[two], made_out.at[two], save_sems.at[step]).start()

        @pl.when(step < pairs - 1)
        def _():
            for which in range(2):
                for copy in back_copies(first + which, me, first + which):
                    copy.start()

        @pl.when(step == pairs - 1)
        def _():
            peer = flip(me, 1, size)
            for copy in back_copies(peer, me, peer):
                copy.start()
            for copy in own_back:
                copy.start()

        return carry

    for group in range(groups // 2, groups):
        for copy in weight_copies(group):
            copy.wait()
    lax.fori_loop(0, pairs, far_step, 0)
    weight_grads(1)
    for copy in own_back:
        copy.wait()
    remote_copy(moved_out, moved_out, moved_sem, moved_sem, "wshard", near).wait_recv()
    for step in range(pairs):
        two = pl.ds(2 * flip(my_pair, pairs - 1 - step, pairs), 2)
        pltpu.make_async_copy(made.at[two], made_out.at[two], save_sems.at[step]).wait()
    for step in range(1, size):
        peer = flip(me, step, size)
        for copy in forth(peer, me, peer):
            copy.wait_send()
        for copy in back_copies(peer, me, peer):
            copy.wait_send()
        for copy in back_copies(me, peer, peer):
            copy.wait_recv()


def moe(sent, gates, outer, own_in, own_down, other_in, other_down, chunk=256):
    size, capacity, width = sent.shape
    groups = 1 + other_in.shape[0]
    share = own_down.shape[0]
    part = share * groups // 2
    total = size * capacity
    extra = gates.shape[1:]
    dma = pltpu.SemaphoreType.DMA
    result = pl.pallas_call(
        functools.partial(moe_body, size, groups, chunk),
        out_shape=(
            shape_of((size, capacity, width), BF16),
            shape_of((size, *extra), F32),
            shape_of((size, capacity, width), BF16),
        )
        + (shape_of((2, 3, share, width), BF16),) * 2,
        in_specs=[ANY] * 7,
        out_specs=(ANY,) * 5,
        scratch_shapes=[
            pltpu.VMEM((3, share * groups, width), BF16),
            pltpu.VMEM((size, capacity, width), BF16),
            pltpu.VMEM((size, *extra), F32),
            pltpu.VMEM((size, capacity, width), BF16),
            pltpu.VMEM((total, width), BF16),
            pltpu.VMEM((total, width), F32),
            pltpu.VMEM((total, width), F32),
            pltpu.VMEM((total, part), BF16),
            pltpu.VMEM((2, total, part), BF16),
            pltpu.VMEM((size, capacity, width), BF16),
            pltpu.VMEM((size, *extra), F32),
            pltpu.VMEM((size, capacity, width), BF16),
            pltpu.VMEM((2, 2 * chunk, width), BF16),
            dma((groups, 2)),
            dma((size, 2)),
            dma((size, 2)),
            dma((size, 2)),
            dma((size, 2)),
            dma((5,)),
            dma((size // 2,)),
            dma((2, 3)),
            dma,
        ],
        cost_estimate=pl.CostEstimate(flops=LIGHT, bytes_accessed=LIGHT, transcendentals=0),
        compiler_params=pltpu.CompilerParams(
            collective_id=0, has_side_effects=True, vmem_limit_bytes=66_000_000
        ),
        name="experts",
    )(sent, gates, outer, own_in, own_down, other_in, other_down)
    return result


def expert_body(groups, chunk, rows_ref, outer_ref, gate_ref, *refs):
    in_refs, down_refs = refs[:groups], refs[groups : 2 * groups]
    made_ref, back_ref, outer_out_ref, gate_grad_ref = refs[2 * groups : 2 * groups + 4]
    act_ref, low_ref, buf_ref, sems = refs[2 * groups + 4 :]
    share = down_refs[0].shape[0]
    hidden = share * groups

    def copies(group):
        spot = pl.ds(group * share, share)
        return (
            pltpu.make_async_copy(in_refs[group], buf_ref.at[0:2, spot], sems.at[2 * group]),
            pltpu.make_async_copy(down_refs[group], buf_ref.at[2, spot], sems.at[2 * group + 1]),
        )

    @pl.when(pl.program_id(0) == 0)
    def _():
        for group in range(groups):
            for copy in copies(group):
                copy.start()

    rows = rows_ref[...]
    low_outer = (outer_ref[...].astype(F32) * gate_ref[...]).astype(BF16)
    outer_out_ref[...] = low_outer

    @pl.when(pl.program_id(0) == 0)
    def _():
        for group in range(groups):
            for copy in copies(group):
                copy.wait()

    for first in range(0, hidden, chunk):
        part = slice(first, first + chunk)
        gate, up = dot_nt(rows, buf_ref[0, part, :]), dot_nt(rows, buf_ref[1, part, :])
        act_grad = dot_nt(low_outer, buf_ref[2, part, :])
        square = gate * gate
        inner = gate * (0.7978845608028654 + (0.7978845608028654 * 0.044715) * square)
        rise = 0.5 + 0.5 * jnp.tanh(inner)
        bent = gate * rise
        act_ref[:, part] = (bent * up).astype(BF16)
        slope = rise + bent * (1.0 - rise) * (
            2 * 0.7978845608028654 + (6 * 0.7978845608028654 * 0.044715) * square
        )
        low_ref[0, :, part] = (act_grad * up * slope).astype(BF16)
        low_ref[1, :, part] = (act_grad * bent).astype(BF16)
    made = dot_nn(act_ref[...], buf_ref[2]).astype(BF16)
    made_ref[...] = made
    back = dot_nn(low_ref[0], buf_ref[0]) + dot_nn(low_ref[1], buf_ref[1])
    back_ref[...] = back.astype(BF16)
    gate_grad_ref[...] = jnp.sum(
        outer_ref[...].astype(F32) * made.astype(F32), -1, keepdims=True
    )


def experts_pass(rows, outer, gate_column, in_weights, down_weights, block=320, chunk=256):
    total, width = rows.shape
    groups = len(in_weights)
    hidden = down_weights[0].shape[0] * groups
    row_spec = pl.BlockSpec((block, width), lambda i: (i, 0))
    column = pl.BlockSpec((block, 1), lambda i: (i, 0))
    wide = pl.BlockSpec((block, hidden), lambda i: (i, 0))
    both = pl.BlockSpec((2, block, hidden), lambda i: (0, i, 0))
    return pl.pallas_call(
        functools.partial(expert_body, groups, chunk),
        grid=(total // block,),
        out_shape=(
            shape_of((total, width), BF16),
            shape_of((total, width), BF16),
            shape_of((total, width), BF16),
            shape_of((total, 1), F32),
            shape_of((total, hidden), BF16),
            shape_of((2, total, hidden), BF16),
        ),
        in_specs=[row_spec, row_spec, column] + [ANY] * (2 * groups),
        out_specs=(row_spec, row_spec, row_spec, column, wide, both),
        scratch_shapes=[
            pltpu.VMEM((3, hidden, width), BF16),
            pltpu.SemaphoreType.DMA((2 * groups,)),
        ],
        cost_estimate=pl.CostEstimate(flops=LIGHT, bytes_accessed=LIGHT, transcendentals=0),
        name="experts",
    )(rows, outer, gate_column, *in_weights, *down_weights)


def moe_plain(sent, gates, outer, own_in, own_down, other_in, other_down):
    in_weights, down_weights = [own_in, *other_in], [own_down, *other_down]
    size, capacity, width = sent.shape
    total = size * capacity
    rows = exchange(sent.reshape(total, width), "dp").reshape(total, width)
    gate_column = lax.all_to_all(gates, "dp", 0, 0, tiled=True)[:, 0, :capacity].reshape(total, 1)
    made, back, outer_low, gate_grads, act, low = experts_pass(
        rows, outer.reshape(total, width), gate_column, in_weights, down_weights
    )
    extra = jnp.pad(gate_grads.reshape(size, 1, capacity), ((0, 0), (0, EXTRA - 1), (0, 0)))
    extra = lax.all_to_all(extra, "dp", 0, 0, tiled=True)
    share = down_weights[0].shape[0]
    grads = []
    for group in range(len(in_weights)):
        part = slice(group * share, (group + 1) * share)
        pieces = [dot_tn(low[c, :, part], rows) for c in range(2)]
        grads.append(jnp.stack(pieces + [dot_tn(act[:, part], outer_low)]).astype(BF16))
    shape = (size, capacity, width)
    moved = jnp.stack([swap(grads[g], "wshard", 1) for g in (1, 3)])
    return exchange(back, "dp"), extra, made.reshape(shape), jnp.stack(grads[::2]), moved


def rear_body(
    size, groups, head_size, remote_made, span_ref, gain_ref, diag_ref, ones_ref, router_ref, col_ref, gate_ref,
    extra_ref, tok_hbm, cot_hbm, hidden_hbm, norm_hbm, mixed_hbm, rows_hbm, made_hbm, outw_hbm,
    qkvw_hbm, qkv_hbm, far_hbm,
    output_ref, grad_ref, early_out, late_out, sum_out, far_out,
    tok, cot, hidden, norm, mixed, rows, made, outw, qkvw, qkv, norm_t, mask, grad_hidden,
    grads, probs_ref, scores_ref, diag_sums, wo, wo_got, wg, wg_got, total,
    total_got, sum_ref, early_ref, early_got, late_ref, late_got,
    load_sems, weight_sems, made_send, made_got, part_sems, total_sems, small_sems, far_sems,
):
    me, place = lax.axis_index("dp"), lax.axis_index("wshard")
    near, far = flip(place, 1, groups), flip(place, 2, groups)
    dp_bits, shard_bits = bits_below(size), bits_below(groups)
    peers = [("dp", flip(me, step, size)) for step in range(1, size)]
    greet(peers + [("wshard", near), ("wshard", far)])
    count, width = tok.shape
    blocks = count // TILE
    experts = size
    capacity = rows.shape[0] // experts
    cols = outw.shape[2]
    two_heads = 2 * head_size
    branch, mixgrad, norm_grad = cot, norm, hidden

    loads = [
        pltpu.make_async_copy(source, target, load_sems.at[i])
        for i, (source, target) in enumerate(
            (
                (rows_hbm, rows), (norm_hbm, norm), (hidden_hbm, hidden), (cot_hbm, cot),
                (mixed_hbm, mixed), (outw_hbm, outw), (tok_hbm, tok), (qkv_hbm, qkv),
                (made_hbm.at[me], made.at[me]) if remote_made else (made_hbm, rows),
            )
        )
    ]
    for copy in loads[: 9 if remote_made else 8]:
        copy.start()

    def far_copy(piece):
        return remote_copy(
            far_hbm.at[piece], far_out.at[piece], far_sems.at[piece, 0], far_sems.at[piece, 1],
            "wshard", far,
        )

    far_copy(0).start()

    def weight_load(step):
        slot = lax.rem(step, 2)
        return pltpu.make_async_copy(
            qkvw_hbm.at[groups - 1 - step], qkvw.at[slot], weight_sems.at[slot]
        )

    hidden_again = pltpu.make_async_copy(hidden_hbm, hidden, load_sems.at[9])

    def made_copy(source, target, peer):
        return remote_copy(
            made_hbm.at[source], made.at[target], made_send.at[source], made_got.at[target], "dp",
            peer,
        )

    if remote_made:
        for _, peer in peers:
            made_copy(peer, me, peer).start()

    exchanges = [("wshard", place, bit, groups) for bit in shard_bits]
    exchanges += [("dp", me, bit, size) for bit in dp_bits]

    def small_copy(kind, ref, got, step):
        axis, index, bit, length = exchanges[step]
        return remote_copy(
            ref, got.at[step], small_sems.at[kind, step, 0], small_sems.at[kind, step, 1], axis,
            flip(index, bit, length),
        )

    def small_step(kind, ref, got, step):
        now, before = step % 2, (step + 1) % 2
        if step > 0:
            small_copy(kind, ref.at[before], got, step - 1).wait()
            ref[now] = ref[before] + got[step - 1]
        if step < len(exchanges):
            small_copy(kind, ref.at[now], got, step).start()

    slots = [col_ref[:, k : k + 1] for k in range(2)]
    gates = [gate_ref[:, k : k + 1] for k in range(2)]
    lane = iota((count, extra_ref.shape[2]), 1)
    picked = [0.0, 0.0]
    for copy in loads[:1]:
        copy.wait()
    grads_in = 0.0
    for expert in range(experts):
        label = jnp.where(lane < capacity, lane + expert * capacity, -1)
        for k in range(2):
            picked[k] = picked[k] + jnp.where(label == slots[k], extra_ref[expert, 0:1, :], 0.0)
    gate_grads = [jnp.sum(p, -1, keepdims=True) for p in picked]
    mean = gates[0] * gate_grads[0] + gates[1] * gate_grads[1]
    lane = iota((count, 3 * experts), 1)
    part = (lane >= experts).astype(I32) + (lane >= 2 * experts).astype(I32)
    label = lane - part * experts
    logit_grads = 0.0
    for k in range(2):
        own = (label * capacity <= slots[k]) & (slots[k] < (label + 1) * capacity)
        logit_grads = logit_grads + jnp.where(own, gates[k] * (gate_grads[k] - mean), 0.0)
    high, middle, low = split_three(logit_grads)
    split = jnp.where(part == 0, high, jnp.where(part == 1, middle, low)).astype(BF16)
    hits = [onehot_columns(slots[k], 0, experts * capacity) for k in range(2)]
    hits = (hits[0] | hits[1]).astype(F32).astype(BF16)
    for copy in loads[1:4]:
        copy.wait()
    normed_grad = dot_nn(hits, rows[...])
    normed_grad = normed_grad + dot_nn(split, router_ref[...])
    router_grad = dot_tn(split, norm[...])
    early_ref[0, :experts, :] = (
        router_grad[:experts] + router_grad[experts : 2 * experts] + router_grad[2 * experts :]
    )
    unit, recip = unit_norm(hidden[...])
    early_ref[0, experts:, :] = jnp.broadcast_to(
        jnp.sum(normed_grad * unit, 0, keepdims=True), (EXTRA, width)
    )
    small_step(0, early_ref, early_got, 0)
    scaled = normed_grad * gain_ref[1:2, :]
    back = recip * (scaled - unit * jnp.mean(scaled * unit, -1, keepdims=True))
    grad_hidden[...] = cot[...].astype(F32) + back
    branch[...] = grad_hidden[...].astype(BF16)
    for copy in loads[4:6]:
        copy.wait()
    mixed_t = mixed[...].T
    result = 0.0

    def part_copy(item, source, target, kind, axis, peer):
        return remote_copy(
            source, target, part_sems.at[item, kind, 0], part_sems.at[item, kind, 1], axis, peer
        )

    def out_copy(kind):
        return part_copy(
            0, wo.at[(3, 1, 2)[kind]], wo_got.at[kind], kind, "wshard", far if kind == 2 else near
        )

    def qkv_copy(kind):
        return part_copy(
            1, wg.at[(2, 0, 1)[kind]], wg_got.at[kind], kind, "wshard", far if kind == 2 else near
        )

    for group in reversed(range(groups)):
        lanes = pl.ds(pl.multiple_of(flip(place, group, groups) * cols, cols), cols)
        piece = branch[:, lanes]
        result = result + dot_nt(piece, outw[group])
        wo[group] = dot_nn(mixed_t, piece).astype(BF16)
        if group == 3:
            out_copy(0).start()
        if group == 1:
            out_copy(1).start()
    mixgrad[...] = result.astype(BF16)
    for copy in loads[6:8]:
        copy.wait()
    weight_load(0).start()
    unit, _ = unit_norm(tok[...].astype(F32))
    norm_t[...] = (unit * gain_ref[0:1, :]).astype(BF16).T
    fill_mask(mask, span_ref[0])
    norm_grad[...] = jnp.zeros_like(norm_grad)

    def attend_group(step):
        group = groups - 1 - step
        slot = lax.rem(step, 2)
        weight_load(step).wait()

        @pl.when(step < groups - 1)
        def _():
            weight_load(step + 1).start()

        owner = flip(place, group, groups)
        heads = cols // head_size

        def pair(p, carry):
            offset = pl.multiple_of(p * two_heads, two_heads)
            lanes = pl.ds(offset, two_heads)
            query, keys, value = (qkv[group, c, :, lanes] for c in range(3))
            outer = mixgrad[:, pl.ds(pl.multiple_of(owner * cols + offset, two_heads), two_heads)]
            query_sum, key_sum, value_sum = [None] * blocks, None, None
            for which in range(2):
                head = owner * heads + 2 * p + which
                own = head_lanes(which, head_size)
                own_query, own_key, own_outer = query * own, keys * own, outer * own
                shrunk = own_query * 0.125
                tiles, far_bias = bias_tiles(diag_ref[pl.ds(head, 1), :])
                near_sums, far_sums = [None] * 3, [None] * 2
                for block in range(blocks):
                    piece = slice(block * TILE, (block + 1) * TILE)
                    probs = softmax_tiles(
                        score_tiles(block, shrunk[piece], keys, tiles, far_bias, mask)
                    )
                    prob_grads = dot_nt(own_outer[piece], value)
                    prob_grads = [prob_grads[:, j * TILE : (j + 1) * TILE] for j in range(blocks)]
                    delta = functools.reduce(jnp.add, [a * b for a, b in zip(probs, prob_grads)])
                    delta = jnp.sum(delta, -1, keepdims=True)
                    lows = [(a * (b - delta)).astype(BF16) for a, b in zip(probs, prob_grads)]
                    for other in range(blocks):
                        step = block - other
                        wide = lows[other].astype(F32)
                        if abs(step) >= 2:
                            side = 0 if step > 0 else 1
                            old = far_sums[side]
                            far_sums[side] = wide if old is None else old + wide
                        else:
                            old = near_sums[step + 1]
                            near_sums[step + 1] = wide if old is None else old + wide
                    probs_ref[which, piece, :] = jnp.concatenate([t.astype(BF16) for t in probs], 1)
                    lows = jnp.concatenate(lows, 1)
                    scores_ref[which, piece, :] = lows
                    more = dot_nn(lows, own_key)
                    query_sum[block] = more if which == 0 else query_sum[block] + more
                more = dot_tn(scores_ref[which], own_query)
                key_sum = more if which == 0 else key_sum + more
                more = dot_tn(probs_ref[which], own_outer)
                value_sum = more if which == 0 else value_sum + more
                for step in range(3):
                    wide = jnp.concatenate([near_sums[step], jnp.zeros((TILE, TILE), F32)], 1)
                    half = TILE // 2
                    while half:
                        turned = pltpu.roll(wide[half:], 2 * TILE - half, 1)
                        wide = wide[:half] + turned
                        half //= 2
                    for side in range(2):
                        spot = 2 * step + side
                        diag_sums[head, spot : spot + 1, :] = wide[:, TILE * side : TILE * (side + 1)]
                for side in range(2):
                    diag_sums[head, 6 + side : 7 + side, :] = jnp.sum(far_sums[side], 0, keepdims=True)
            for block in range(blocks):
                piece = slice(block * TILE, (block + 1) * TILE)
                grads[0, piece, lanes] = (query_sum[block] * 0.125).astype(BF16)
            grads[1, :, lanes] = (key_sum * 0.125).astype(BF16)
            grads[2, :, lanes] = value_sum.astype(BF16)
            return carry

        lax.fori_loop(0, cols // two_heads, pair, 0)
        for c in range(3):
            weight_grad = dot_nn(norm_t[...], grads[c]).astype(BF16)

            @pl.when(group > 0)
            def _():
                wg[group - 1, c] = weight_grad

            @pl.when(group == 0)
            def _():
                total[c * width : (c + 1) * width, :] = weight_grad

            norm_grad[...] += dot_nt(grads[c], qkvw[slot, c])

    def add_into(target, *others):
        for first in range(0, target.shape[0], 256):
            spot = slice(first, first + 256)
            value = target[spot].astype(F32)
            for other in others:
                value = value + other[spot].astype(F32)
            target[spot] = value.astype(BF16)

    def group_step(step, carry):
        attend_group(step)

        @pl.when(step == 0)
        def _():
            qkv_copy(0).start()
            small_step(0, early_ref, early_got, 1)
            out_copy(0).wait_recv()
            add_into(wo.at[2], wo_got.at[0])
            out_copy(2).start()

        @pl.when(step == 1)
        def _():
            qkv_copy(0).wait_recv()
            for c in range(3):
                add_into(wg.at[1, c], wg_got.at[0, c])
            qkv_copy(2).start()
            far_copy(1).start()
            far_copy(2).start()
            small_step(0, early_ref, early_got, 2)

        @pl.when(step == 2)
        def _():
            qkv_copy(1).start()
            small_step(0, early_ref, early_got, 3)

        return carry

    lax.fori_loop(0, groups, group_step, 0)

    small_step(0, early_ref, early_got, 4)
    unit, recip = unit_norm(tok[...].astype(F32))
    gain_grad = jnp.sum(norm_grad[...] * unit, 0, keepdims=True)
    table_grad = 0.0
    for k in range(8):
        for piece in split_three(diag_sums[:, k, :]):
            table_grad = table_grad + dot_nt(piece.astype(BF16), ones_ref[:, k * TILE : (k + 1) * TILE])
    late_ref[0] = jnp.zeros(late_ref.shape[1:], F32)
    for k in range(width // TILE):
        late_ref[0, k : k + 1, :] = gain_grad[:, k * TILE : (k + 1) * TILE]
    heads, buckets = table_grad.shape
    late_ref[0, 8 : 8 + heads, :buckets] = table_grad
    small_step(1, late_ref, late_got, 0)

    qkv_copy(1).wait_recv()
    out_copy(1).wait_recv()
    out_copy(2).wait_recv()
    qkv_copy(2).wait_recv()
    third = outw.shape[1]
    for c in range(3):
        add_into(total.at[c * third : (c + 1) * third], wg_got.at[1, c], wg_got.at[2, c])
    add_into(wo.at[0], wo_got.at[1], wo_got.at[2])
    total[3 * third :, :] = wo[0]
    parts = 2
    length = total.shape[0] // parts
    stages = len(dp_bits)

    def bit_of(step):
        return lax.rem(lax.div(me, dp_bits[step]), 2)

    def segment(part, step):
        first, size_of = part * length, length
        for s in range(step):
            size_of //= 2
            first = first + bit_of(s) * size_of
        return first, size_of

    def halving(part, step):
        first, size_of = segment(part, step)
        half = size_of // 2
        away = pl.multiple_of(first + (1 - bit_of(step)) * half, half)
        return remote_copy(
            total.at[pl.ds(away, half)],
            total_got.at[pl.ds(part * length + length - size_of, half)],
            total_sems.at[part, 0, step, 0], total_sems.at[part, 0, step, 1], "dp",
            flip(me, dp_bits[step], size),
        )

    def add_half(part, step):
        first, half = segment(part, step + 1)
        first = pl.multiple_of(first, half)
        got = part * length + length - 2 * half
        value = total[pl.ds(first, half), :].astype(F32) + total_got[got : got + half, :].astype(F32)
        total[pl.ds(first, half), :] = value.astype(BF16)
        if step == stages - 1:
            sum_ref[pl.ds(first, half), :] = value.astype(BF16)

    def doubling(part, step):
        first, size_of = segment(part, step + 1)
        spot = pl.ds(pl.multiple_of(first, size_of), size_of)
        return remote_copy(
            sum_ref.at[spot], sum_ref.at[spot],
            total_sems.at[part, 1, step, 0], total_sems.at[part, 1, step, 1], "dp",
            flip(me, dp_bits[step], size),
        )

    def sum_stage(part, stage):
        if 0 < stage <= stages:
            halving(part, stage - 1).wait()
            add_half(part, stage - 1)
        elif stage > stages:
            doubling(part, 2 * stages - stage).wait()
        if stage < stages:
            halving(part, stage).start()
        elif stage < 2 * stages:
            doubling(part, 2 * stages - 1 - stage).start()

    def finish_tokens():
        scaled = norm_grad[...] * gain_ref[0:1, :]
        back = recip * (scaled - unit * jnp.mean(scaled * unit, -1, keepdims=True))
        grad_ref[...] = (grad_hidden[...] + back).astype(BF16)
        hidden_again.start()
        if not remote_made:
            loads[8].start()

    def finish_output():
        loads[8].wait()
        hidden_again.wait()
        if remote_made:
            for _, peer in peers:
                made_copy(me, peer, peer).wait_recv()
        values = made[...].reshape(experts * capacity, width) if remote_made else rows[...]
        for first in range(0, count, 256):
            spot = slice(first, first + 256)
            value = hidden[spot, :]
            for k in range(2):
                hit = onehot_columns(slots[k][spot], 0, experts * capacity)
                value = value + gates[k][spot] * dot_nn(hit.astype(F32).astype(BF16), values)
            output_ref[spot, :] = value.astype(BF16)

    rest_early = list(range(groups + 1, len(exchanges) + 1))
    rest_late = list(range(1, len(exchanges) + 1))

    def next_small():
        if rest_early:
            small_step(0, early_ref, early_got, rest_early.pop(0))
        if rest_late:
            small_step(1, late_ref, late_got, rest_late.pop(0))

    sum_stage(0, 0)
    sum_stage(1, 0)
    finish_tokens()
    next_small()
    sum_stage(0, 1)
    finish_output()
    next_small()
    sum_stage(1, 1)
    for stage in range(2, 2 * stages + 1):
        next_small()
        for part in range(parts):
            sum_stage(part, stage)
    while rest_early or rest_late:
        next_small()
    early_out[...] = early_ref[len(exchanges) % 2]
    late_out[...] = late_ref[len(exchanges) % 2]
    save = pltpu.make_async_copy(sum_ref, sum_out, load_sems.at[10])
    save.start()
    save.wait()
    for piece in range(3):
        far_copy(piece).wait()
    if remote_made:
        for _, peer in peers:
            made_copy(peer, me, peer).wait_send()
    for kind in range(3):
        out_copy(kind).wait_send()
        qkv_copy(kind).wait_send()


def bits_below(size):
    return [1 << b for b in range(size.bit_length() - 1)]


def rear(
    span, gains, diag, ones, router_t3, slots_col, gates, extra, tokens, cotangent, hidden, normed,
    mixed, rows, made, out_weights, qkv_weights, qkv, far_sum, head_size,
):
    count, width = tokens.shape
    size, groups = lax.axis_size("dp"), lax.axis_size("wshard")
    heads, buckets = width // head_size, ones.shape[0]
    experts = router_t3.shape[0] // 3
    cols = out_weights.shape[2]
    exchanges = len(bits_below(size)) + len(bits_below(groups))
    dma = pltpu.SemaphoreType.DMA
    wide, small = (count, width), (experts + EXTRA, width)
    late = (8 + heads, TILE)
    total = (4 * width, cols)
    vmem = pltpu.VMEM
    return pl.pallas_call(
        functools.partial(rear_body, size, groups, head_size, made.ndim == 3),
        out_shape=(
            shape_of(wide, BF16),
            shape_of(wide, BF16),
            shape_of(small, F32),
            shape_of(late, F32),
            shape_of(total, BF16),
            shape_of(far_sum.shape, BF16),
        ),
        in_specs=[SMEM] + [VMEM] * 7 + [ANY] * 11,
        out_specs=(VMEM,) * 4 + (ANY,) * 2,
        scratch_shapes=[
            vmem(wide, BF16),
            vmem(wide, BF16),
            vmem(wide, F32),
            vmem(wide, BF16),
            vmem(wide, BF16),
            vmem(rows.shape, BF16),
            vmem(made.shape if made.ndim == 3 else (16, TILE), BF16),
            vmem(out_weights.shape, BF16),
            vmem((2, *qkv_weights.shape[1:]), BF16),
            vmem(qkv.shape, BF16),
            vmem((width, count), BF16),
            vmem((count, count), F32),
            vmem(wide, F32),
            vmem((3, count, cols), BF16),
            vmem((2, count, count), BF16),
            vmem((2, count, count), BF16),
            vmem((heads, 8, TILE), F32),
            vmem((groups, width, cols), BF16),
            vmem((3, width, cols), BF16),
            vmem((groups - 1, 3, width, cols), BF16),
            vmem((3, 3, width, cols), BF16),
            vmem(total, BF16),
            vmem(total, BF16),
            vmem(total, BF16),
            vmem((2, *small), F32),
            vmem((exchanges, *small), F32),
            vmem((2, *late), F32),
            vmem((exchanges, *late), F32),
            dma((11,)),
            dma((2,)),
            dma((size,)),
            dma((size,)),
            dma((2, 3, 2)),
            dma((2, 2, len(bits_below(size)), 2)),
            dma((2, exchanges, 2)),
            dma((3, 2)),
        ],
        cost_estimate=pl.CostEstimate(flops=LIGHT, bytes_accessed=LIGHT, transcendentals=0),
        compiler_params=pltpu.CompilerParams(
            collective_id=2, has_side_effects=True, vmem_limit_bytes=66_000_000
        ),
        name="rear",
    )(
        span, gains, diag, ones, router_t3, slots_col, gates, extra, tokens, cotangent, hidden,
        normed, mixed, rows, made, out_weights, qkv_weights, qkv, far_sum,
    )


def swap(value, axis, bit):
    size = lax.axis_size(axis)
    return lax.ppermute(value, axis, [(i, i ^ bit) for i in range(size)])


def bits_of(axis):
    size = lax.axis_size(axis)
    return [1 << b for b in range(size.bit_length() - 1)]


def after(value, *others):
    return lax.optimization_barrier((value, *others))[0]


def exchange(rows, axis):
    size = lax.axis_size(axis)
    total, width = rows.shape
    blocks = rows.reshape(size, total // size, width)
    return lax.all_to_all(blocks, axis, 0, 0, tiled=True)


def per_device(
    tokens,
    cotangent,
    span_starts,
    routes,
    norm_gains,
    bias_table,
    router,
    attn_qkv,
    attn_out,
    expert_in,
    expert_down,
):
    assert span_starts.shape[0] == 1
    tok_count, model_width = tokens.shape
    buckets, head_count = bias_table.shape
    head_size = model_width // head_count
    experts = router.shape[1]
    capacity = (10 * tok_count + 4 * experts - 1) // (4 * experts)
    total = experts * capacity
    place = lax.axis_index("wshard")
    where = jnp.stack([place.astype(I32), span_starts[0]])
    diag = jnp.asarray(diagonal_ones(buckets))
    diag_bias = jnp.dot(bias_table.T, diag, precision=PRECISE)
    router_t = router.T
    expert_in = jnp.swapaxes(expert_in[0], 1, 2)
    expert_down = expert_down[0]

    shards = (attn_qkv, attn_out, expert_in, expert_down)
    (
        slots_col, gates, sent_gates, qkv_all, out_all, qkv, mixed, hidden, normed_two, sent,
        outer_rows, in_other, down_other,
    ) = front(
        span_starts, routes, norm_gains, diag_bias, router_t, tokens, cotangent, shards, head_size,
        capacity,
    )
    groups = out_all.shape[0]
    through = moe if capacity % 16 == 0 else moe_plain
    back_rows, back_extra, made, expert_grads, moved = through(
        sent, sent_gates, outer_rows, expert_in, expert_down, in_other, down_other
    )
    far_sum = (expert_grads[1].astype(F32) + moved[1].astype(F32)).astype(BF16)
    if through is moe_plain:
        made = exchange(made.reshape(total, model_width), "dp").reshape(total, model_width)

    output, grad_tokens, early, late, attn_sum, far_got = rear(
        span_starts, norm_gains, diag_bias, diag.astype(BF16), jnp.concatenate([router_t] * 3, 0),
        slots_col, gates, back_extra, tokens, cotangent, hidden, normed_two,
        mixed, back_rows.reshape(total, model_width), made, out_all, qkv_all, qkv, far_sum, head_size,
    )

    def expert_sum(part):
        pieces = (expert_grads[0, part], moved[0, part], far_got[part])
        return functools.reduce(jnp.add, [piece.astype(F32) for piece in pieces])

    grad_expert_in = jnp.swapaxes(expert_sum(slice(0, 2)), 1, 2)[None]
    grad_expert_down = expert_sum(2)[None]
    cols = out_all.shape[2]
    grad_attn_qkv = attn_sum[: 3 * model_width].astype(F32).reshape(3, model_width, cols)
    grad_attn_out = attn_sum[3 * model_width :].astype(F32)
    gain_rows = model_width // TILE
    gain_one = late[:gain_rows].reshape(model_width)
    return (
        output,
        grad_tokens,
        jnp.stack([gain_one, early[experts]]),
        late[gain_rows:, :buckets].T,
        early[:experts].T,
        grad_attn_qkv,
        grad_attn_out,
        grad_expert_in,
        grad_expert_down,
    )


def solution(mesh):
    return jax.shard_map(
        per_device,
        mesh=mesh,
        in_specs=(
            P(("dp", "wshard"), None),
            P(("dp", "wshard"), None),
            P(("dp", "wshard")),
            P(("dp", "wshard"), None),
            P(),
            P(),
            P(),
            P(None, None, "wshard"),
            P(None, "wshard"),
            P("dp", None, None, "wshard"),
            P("dp", "wshard", None),
        ),
        out_specs=(
            P(("dp", "wshard"), None),
            P(("dp", "wshard"), None),
            P(),
            P(),
            P(),
            P(None, None, "wshard"),
            P(None, "wshard"),
            P("dp", None, None, "wshard"),
            P("dp", "wshard", None),
        ),
        check_vma=False,
    )
```

```python
import functools

import jax
import jax.numpy as jnp
import numpy as np
from jax import lax
from jax.experimental import pallas as pl
from jax.experimental.pallas import tpu as pltpu
from jax.sharding import PartitionSpec as P

PIC = 256
PRECISE = lax.Precision.HIGHEST
EPSILON = 1e-06
MASKED_SCORE = -1e30
BUCKET_EDGES = (8, 11, 16, 23, 32, 45, 64, 91)
TILE = 128
F32 = jnp.float32
BF16 = jnp.bfloat16
I32 = jnp.int32
VMEM = pl.BlockSpec(memory_space=pltpu.VMEM)
SMEM = pl.BlockSpec(memory_space=pltpu.SMEM)
ANY = pl.BlockSpec(memory_space=pl.ANY)
LIGHT = 1024
EXTRA = 8


def dot_nn(a, b):
    return lax.dot_general(a, b, (((1,), (0,)), ((), ())), preferred_element_type=F32)


def dot_nt(a, b):
    return lax.dot_general(a, b, (((1,), (1,)), ((), ())), preferred_element_type=F32)


def dot_tn(a, b):
    return lax.dot_general(a, b, (((0,), (0,)), ((), ())), preferred_element_type=F32)


def iota(shape, axis):
    return lax.broadcasted_iota(I32, shape, axis)


def shape_of(shape, dtype):
    return jax.ShapeDtypeStruct(shape, dtype)


def call(body, out, args, specs, scratch=(), name=None):
    return pl.pallas_call(
        body,
        out_shape=out,
        in_specs=specs,
        out_specs=jax.tree.map(lambda _: VMEM, out),
        scratch_shapes=list(scratch),
        cost_estimate=pl.CostEstimate(flops=LIGHT, bytes_accessed=LIGHT, transcendentals=0),
        name=name,
    )(*args)


def bucket_of(offset):
    magnitude = np.abs(offset)
    coarse = 7 + sum((magnitude >= bound).astype(np.int32) for bound in BUCKET_EDGES)
    return np.where(magnitude < 8, magnitude, coarse) + 16 * (offset < 0)


def diagonal_ones(bucket_count):
    column = np.arange(2 * TILE)
    signed = np.where(column < TILE, column, column - 2 * TILE)
    offsets = np.concatenate([TILE * step - signed for step in (-1, 0, 1)])
    used = np.tile(column != TILE, 3)
    hit = bucket_of(offsets)[None, :] == np.arange(bucket_count)[:, None]
    near = (hit & used[None, :]).astype(np.float32)
    far = np.zeros((bucket_count, 2 * TILE), np.float32)
    far[bucket_of(np.array(TILE)), :TILE] = 1
    far[bucket_of(np.array(-TILE)), TILE:] = 1
    return np.concatenate([near, far], 1)


def onehot_rows(first, count, slots_row):
    index = iota((count, slots_row.shape[1]), 0) + first
    hit = (index == slots_row[0:1, :]) | (index == slots_row[1:2, :])
    return hit.astype(F32).astype(BF16)


def onehot_columns(slots_column, first, count):
    index = iota((slots_column.shape[0], count), 1) + first
    return index == slots_column


def route_slots(experts, capacity, routes):
    tokens = routes.shape[1]
    label = iota((experts, tokens), 0)
    hits = ((routes[0:1] == label) | (routes[1:2] == label)).astype(F32).astype(BF16)
    earlier = iota((tokens, tokens), 0) < iota((tokens, tokens), 1)
    before = dot_nn(hits, earlier.astype(F32).astype(BF16))
    slots = []
    for k in range(2):
        own = jnp.sum(jnp.where(routes[k : k + 1] == label, before, 0.0), 0, keepdims=True)
        slots.append(own.astype(I32) + routes[k : k + 1] * capacity)
    return jnp.concatenate(slots * 4, 0)


def unit_norm(values):
    recip = lax.rsqrt(jnp.mean(values * values, -1, keepdims=True) + EPSILON)
    return values * recip, recip


def fill_mask(mask_ref, span_start):
    size = mask_ref.shape[0]
    i, j = iota((size, size), 0), iota((size, size), 1)

    def inside(p):
        return (p >= span_start) & (p < span_start + PIC)

    visible = (j <= i) | (inside(i) & inside(j))
    mask_ref[...] = jnp.where(visible, 0.0, MASKED_SCORE)


def head_lanes(which, size):
    lane = iota((1, 2 * size), 1)
    return ((lane >= size) == (which == 1)).astype(F32).astype(BF16)


def bias_tiles(diag_row):
    tiles = []
    for step in range(3):
        row = diag_row[:, 2 * TILE * step : 2 * TILE * (step + 1)]
        wide = jnp.broadcast_to(row, (TILE, 2 * TILE))
        tiles.append(pltpu.roll(wide, 0, 1, stride=1, stride_axis=0)[:, :TILE])
    return tiles, (diag_row[:, 6 * TILE : 7 * TILE], diag_row[:, 7 * TILE :])


def score_tiles(block, query, keys, tiles, far, mask_ref):
    raw = dot_nt(query, keys)
    rows = slice(block * TILE, (block + 1) * TILE)
    result = []
    for other in range(keys.shape[0] // TILE):
        piece = raw[:, other * TILE : (other + 1) * TILE]
        step = block - other
        piece = piece + (far[0] if step >= 2 else far[1] if step <= -2 else tiles[step + 1])
        if step <= 0:
            piece = piece + mask_ref[rows, other * TILE : (other + 1) * TILE]
        result.append(piece)
    return result


def softmax_tiles(pieces):
    top = functools.reduce(jnp.maximum, pieces)
    top = jnp.max(top, -1, keepdims=True)
    powers = [jnp.exp(piece - top) for piece in pieces]
    total = jnp.sum(functools.reduce(jnp.add, powers), -1, keepdims=True)
    scale = 1.0 / total
    return [power * scale for power in powers]


def split_three(value):
    high = value.astype(BF16).astype(F32)
    middle = (value - high).astype(BF16).astype(F32)
    return high, middle, value - high - middle


def remote_copy(source, target, sent, got, axis, peer):
    return pltpu.make_async_remote_copy(
        src_ref=source,
        dst_ref=target,
        send_sem=sent,
        recv_sem=got,
        device_id={axis: peer},
        device_id_type=pl.DeviceIdType.MESH,
    )


def turns_of(size):
    half, quarter = size // 2, size // 4
    return range(half, half + quarter), range(half + quarter, size), range(1, half)


def greet(peers):
    barrier = pltpu.get_barrier_semaphore()
    for axis, peer in peers:
        pl.semaphore_signal(
            barrier, inc=1, device_id={axis: peer}, device_id_type=pl.DeviceIdType.MESH
        )
    pl.semaphore_wait(barrier, len(peers))


def project_and_attend(place, group, groups, head_size, norm, diag_ref, w_ref, qkv_ref, mix_ref, mask):
    count = norm.shape[0]
    cols = w_ref.shape[-1]
    width = 2 * head_size
    owner = flip(place, group, groups)
    for c in range(3):
        qkv_ref[group, c] = dot_nn(norm[...], w_ref[group, c]).astype(BF16)

    def pair(p, carry):
        offset = pl.multiple_of(p * width, width)
        lanes = pl.ds(offset, width)
        query, keys, value = (qkv_ref[group, c, :, lanes] for c in range(3))
        mixed = [None] * (count // TILE)
        for which in range(2):
            head = owner * (cols // head_size) + 2 * p + which
            own = head_lanes(which, head_size)
            own_query, own_value = query * (own * 0.125), value * own
            tiles, far = bias_tiles(diag_ref[pl.ds(head, 1), :])
            for block in range(count // TILE):
                rows = slice(block * TILE, (block + 1) * TILE)
                pieces = score_tiles(block, own_query[rows], keys, tiles, far, mask)
                probs = jnp.concatenate([t.astype(BF16) for t in softmax_tiles(pieces)], 1)
                part = dot_nn(probs, own_value)
                mixed[block] = part if which == 0 else mixed[block] + part
        target = pl.ds(pl.multiple_of(owner * cols + offset, width), width)
        for block in range(count // TILE):
            rows = slice(block * TILE, (block + 1) * TILE)
            mix_ref[rows, target] = mixed[block].astype(BF16)
        return carry

    lax.fori_loop(0, cols // width, pair, 0)


def front_body(
    size, groups, head_size, span_ref, routes_ref, gain_ref, diag_ref, router_ref, tok_hbm, cot_hbm,
    qkv_shard, out_shard, in_shard,
    col_ref, gate_ref, sent_gate_ref, qkvw_out, outw_out, qkv_out, mixed_out, hidden_out, norm_out,
    sent_out, outer_out, gate_out,
    tok, cot, qkvw, outw, qkv, mixed, hidden, norm, sent, outer, mask, row, load_sems, save_sems,
    shard_sems, outer_send, outer_got,
):
    me, place = lax.axis_index("dp"), lax.axis_index("wshard")
    near, far = flip(place, 1, groups), flip(place, 2, groups)
    peers = [("dp", flip(me, step, size)) for step in range(1, size)]
    greet(peers + [("wshard", near), ("wshard", far)])

    sources = (qkv_shard, out_shard, in_shard.at[0, : gate_out.shape[1]])

    def held(item, group):
        if item == 0:
            return qkvw.at[group]
        if item == 1:
            return outw.at[group]
        return gate_out.at[group - 2]

    def shard_copy(kind, item):
        source = held(item, 2) if kind == 2 else sources[item]
        return remote_copy(
            source, held(item, (1, 2, 3)[kind]), shard_sems.at[kind, item, 0],
            shard_sems.at[kind, item, 1], "wshard", far if kind == 1 else near,
        )

    shard_copy(1, 0).start()
    for item in range(2):
        shard_copy(0, item).start()
    loads = [
        pltpu.make_async_copy(source, target, load_sems.at[i])
        for i, (source, target) in enumerate(
            ((cot_hbm, cot), (tok_hbm, tok), (qkv_shard, qkvw.at[0]), (out_shard, outw.at[0]))
        )
    ]
    for copy in loads:
        copy.start()

    experts, capacity = size, sent.shape[1]
    count = tok.shape[0]
    slots = route_slots(experts, capacity, routes_ref[...])
    row[...] = slots
    col_ref[...] = slots.astype(F32).T.astype(I32)
    loads[0].wait()

    def place_outer(expert, carry):
        outer[expert] = dot_nn(onehot_rows(expert * capacity, capacity, row[...]), cot[...]).astype(BF16)
        return carry

    lax.fori_loop(0, experts, place_outer, 0)
    fill_mask(mask, span_ref[0])
    loads[1].wait()
    unit, _ = unit_norm(tok[...].astype(F32))
    norm[...] = (unit * gain_ref[0:1, :]).astype(BF16)
    loads[2].wait()

    def outer_copy(source, target, peer):
        return remote_copy(
            outer.at[source], outer_out.at[target], outer_send.at[source], outer_got.at[target],
            "dp", peer,
        )

    own_outer = pltpu.make_async_copy(outer.at[me], outer_out.at[me], load_sems.at[4])
    own_outer.start()
    turns = turns_of(size)

    def send_outer(turn):
        for step in turns[turn]:
            peer = flip(me, step, size)
            outer_copy(peer, me, peer).start()

    send_outer(0)

    def one_group(group, carry):
        @pl.when(group == 1)
        def _():
            send_outer(1)
            shard_copy(0, 0).wait_recv()

        @pl.when(group == 2)
        def _():
            shard_copy(1, 0).wait()
            shard_copy(2, 0).start()
            shard_copy(1, 1).start()

        @pl.when(group == 3)
        def _():
            send_outer(2)
            shard_copy(2, 0).wait_recv()

        project_and_attend(
            place, group, groups, head_size, norm, diag_ref, qkvw, qkv, mixed, mask
        )
        return carry

    lax.fori_loop(0, groups, one_group, 0)
    saves = [
        pltpu.make_async_copy(source, target, save_sems.at[i])
        for i, (source, target) in enumerate(
            (
                (qkvw, qkvw_out), (qkv, qkv_out), (mixed, mixed_out), (outw, outw_out),
                (hidden, hidden_out), (norm, norm_out), (sent, sent_out),
            )
        )
    ]
    for copy in saves[:3]:
        copy.start()
    loads[3].wait()
    shard_copy(0, 1).wait_recv()
    shard_copy(1, 1).wait()
    shard_copy(2, 1).start()
    shard_copy(1, 2).start()

    shard_copy(2, 1).wait_recv()
    saves[3].start()
    for group in range(groups):
        cols = outw.shape[2]
        lanes = pl.ds(pl.multiple_of(flip(place, group, groups) * cols, cols), cols)
        hidden[:, lanes] = tok[:, lanes].astype(F32) + dot_nn(mixed[...], outw[group])
    saves[4].start()
    unit, _ = unit_norm(hidden[...])
    norm[...] = (unit * gain_ref[1:2, :]).astype(BF16)
    saves[5].start()

    def place_sent(expert, carry):
        sent[expert] = dot_nn(onehot_rows(expert * capacity, capacity, row[...]), norm[...]).astype(BF16)
        return carry

    lax.fori_loop(0, experts, place_sent, 0)
    saves[6].start()
    logits = dot_nt(norm[...], router_ref[...])
    slots = [col_ref[:, k : k + 1] for k in range(2)]
    lane = iota(logits.shape, 1)
    chosen = []
    for k in range(2):
        own = (lane * capacity <= slots[k]) & (slots[k] < (lane + 1) * capacity)
        chosen.append(jnp.sum(jnp.where(own, logits, 0.0), -1, keepdims=True))
    top = jnp.maximum(chosen[0], chosen[1])
    powers = [jnp.exp(c - top) for c in chosen]
    gates = [power / (powers[0] + powers[1]) for power in powers]
    for k in range(2):
        gate_ref[:, k : k + 1] = gates[k]
    lane = iota((count, sent_gate_ref.shape[2]), 1)
    for expert in range(experts):
        label = jnp.where(lane < capacity, lane + expert * capacity, -1)
        part = 0.0
        for k in range(2):
            part = part + jnp.where(label == slots[k], gates[k], 0.0)
        line = jnp.sum(part, 0, keepdims=True)
        sent_gate_ref[expert] = jnp.broadcast_to(line, sent_gate_ref.shape[1:])

    shard_copy(1, 2).wait()
    shard_copy(2, 2).start()
    own_outer.wait()
    for copy in saves:
        copy.wait()
    for _, peer in peers:
        outer_copy(peer, me, peer).wait_send()
        outer_copy(me, peer, peer).wait_recv()
    for item in range(2):
        shard_copy(0, item).wait_send()
        shard_copy(2, item).wait_send()
    shard_copy(2, 2).wait()


def front(span, routes, gains, diag, router_t, tokens, cotangent, shards, head_size, capacity):
    count, width = tokens.shape
    size, groups = lax.axis_size("dp"), lax.axis_size("wshard")
    qkv_shard, out_shard, in_shard = shards
    cols = out_shard.shape[1]
    lanes = -(-capacity // TILE) * TILE
    dma = pltpu.SemaphoreType.DMA
    block = (size, capacity, width)
    return pl.pallas_call(
        functools.partial(front_body, size, groups, head_size),
        out_shape=(
            shape_of((count, 8), I32),
            shape_of((count, 2), F32),
            shape_of((size, EXTRA, lanes), F32),
            shape_of((groups, *qkv_shard.shape), BF16),
            shape_of((groups, *out_shard.shape), BF16),
            shape_of((groups, 3, count, cols), BF16),
            shape_of((count, width), BF16),
            shape_of((count, width), F32),
            shape_of((count, width), BF16),
            shape_of(block, BF16),
            shape_of(block, BF16),
            shape_of((2, in_shard.shape[1] // 32 * 16, width), BF16),
        ),
        in_specs=[SMEM] + [VMEM] * 4 + [ANY] * 5,
        out_specs=(VMEM,) * 3 + (ANY,) * 9,
        scratch_shapes=[
            pltpu.VMEM((count, width), BF16),
            pltpu.VMEM((count, width), BF16),
            pltpu.VMEM((groups, *qkv_shard.shape), BF16),
            pltpu.VMEM((groups, *out_shard.shape), BF16),
            pltpu.VMEM((groups, 3, count, cols), BF16),
            pltpu.VMEM((count, width), BF16),
            pltpu.VMEM((count, width), F32),
            pltpu.VMEM((count, width), BF16),
            pltpu.VMEM(block, BF16),
            pltpu.VMEM(block, BF16),
            pltpu.VMEM((count, count), F32),
            pltpu.VMEM((8, count), I32),
            dma((5,)),
            dma((7,)),
            dma((3, 3, 2)),
            dma((size,)),
            dma((size,)),
        ],
        cost_estimate=pl.CostEstimate(flops=LIGHT, bytes_accessed=LIGHT, transcendentals=0),
        compiler_params=pltpu.CompilerParams(
            collective_id=1, has_side_effects=True, vmem_limit_bytes=60_000_000
        ),
        name="front",
    )(span, routes.T, gains, diag, router_t, tokens, cotangent, *shards)


def flip(value, change, size):
    result = 0
    bit = 1
    while bit < size:
        one, two = lax.rem(lax.div(value, bit), 2), lax.rem(lax.div(change, bit), 2)
        result = result + bit * (one + two - 2 * one * two)
        bit *= 2
    return result


def column_of(row, size):
    spot = iota((size, row.shape[1]), 0) == iota((size, row.shape[1]), 1)
    return jnp.sum(jnp.where(spot, row, 0.0), 1, keepdims=True)


def row_of(column, lanes):
    spot = iota((column.shape[0], lanes), 0) == iota((column.shape[0], lanes), 1)
    return jnp.sum(jnp.where(spot, column, 0.0), 0, keepdims=True)


def moe_body(
    size, groups, chunk, sent_ref, gates_ref, outer_ref, own_in, own_down, far_gate, *refs
):
    back_out, extra_out, made_out, grad_out, moved_out = refs[:5]
    (
        buf, rows, gates, outer, low_outer, made_sum, back_sum, act, low, stage, extra_stage,
        made, grad_stage, weight_sems, shard_sems, send_sems, recv_sems, give_sems, take_sems, own_sems,
        save_sems, grad_sems, moved_sem,
    ) = refs[5:]
    share = own_down.shape[0]
    part_size = share * groups // 2
    capacity, width = outer.shape[1:]
    both = 2 * capacity
    me = lax.axis_index("dp")
    pairs = size // 2
    my_pair = lax.div(me, 2)
    mesh_id = pl.DeviceIdType.MESH

    place = lax.axis_index("wshard")
    near, far = flip(place, 1, groups), flip(place, 2, groups)
    peers = [("dp", flip(me, step, size)) for step in range(1, size)]
    greet(peers + [("wshard", near), ("wshard", far)])

    def remote(source, target, sent, got, peer):
        return pltpu.make_async_remote_copy(
            src_ref=source, dst_ref=target, send_sem=sent, recv_sem=got,
            device_id={"dp": peer}, device_id_type=mesh_id,
        )

    def forth(source, target, peer):
        return (
            remote(sent_ref.at[source], rows.at[target], send_sems.at[source, 0],
                   recv_sems.at[target, 0], peer),
            remote(gates_ref.at[source], gates.at[target], send_sems.at[source, 1],
                   recv_sems.at[target, 1], peer),
        )

    def back_copies(source, target, peer):
        return (
            remote(stage.at[source], back_out.at[target], give_sems.at[source, 0],
                   take_sems.at[target, 0], peer),
            remote(extra_stage.at[source], extra_out.at[target], give_sems.at[source, 1],
                   take_sems.at[target, 1], peer),
        )

    own = (
        pltpu.make_async_copy(sent_ref.at[me], rows.at[me], own_sems.at[0]),
        pltpu.make_async_copy(gates_ref.at[me], gates.at[me], own_sems.at[1]),
        pltpu.make_async_copy(outer_ref, outer, own_sems.at[2]),
    )
    own_back = (
        pltpu.make_async_copy(stage.at[me], back_out.at[me], own_sems.at[3]),
        pltpu.make_async_copy(extra_stage.at[me], extra_out.at[me], own_sems.at[4]),
    )
    for copy in own:
        copy.start()
    turns = turns_of(size)

    def send_rows(steps):
        for step in steps:
            peer = flip(me, step, size)
            for copy in forth(peer, me, peer):
                copy.start()

    send_rows(turns[2])
    send_rows(turns[0])

    begun = far_gate.shape[1]

    def home(c, group, first, count):
        return buf.at[c, pl.ds(group * share + first, count)]

    loads = [
        pltpu.make_async_copy(own_in, buf.at[0:2, pl.ds(0, share)], weight_sems.at[0]),
        pltpu.make_async_copy(own_down, home(2, 0, 0, share), weight_sems.at[1]),
    ]
    loads += [
        pltpu.make_async_copy(far_gate.at[i], home(0, 2 + i, 0, begun), weight_sems.at[2 + i])
        for i in range(2)
    ]
    near_copies = [
        remote_copy(own_in, buf.at[0:2, pl.ds(share, share)], shard_sems.at[0, 0, 0],
                    shard_sems.at[0, 0, 1], "wshard", near),
        remote_copy(own_down, home(2, 1, 0, share), shard_sems.at[0, 1, 0],
                    shard_sems.at[0, 1, 1], "wshard", near),
    ]
    rest = ((0, begun, share - begun), (1, 0, share), (2, 0, share))

    def far_copy(c):
        _, first, count = rest[c]
        source = own_down if c == 2 else own_in.at[c]
        return remote_copy(source.at[pl.ds(first, count)], home(c, 2, first, count),
                           shard_sems.at[1, c, 0], shard_sems.at[1, c, 1], "wshard", far)

    def onward_copy(c):
        _, first, count = rest[c]
        return remote_copy(home(c, 2, first, count), home(c, 3, first, count),
                           shard_sems.at[2, c, 0], shard_sems.at[2, c, 1], "wshard", near)

    far_copy(0).start()
    for copy in loads + near_copies:
        copy.start()
    for copy in own:
        copy.wait()

    def hidden_part(pair, base):
        spot = pl.ds(pl.multiple_of(pair * both, both), both)
        two = pl.ds(2 * pair, 2)
        these = rows[two].reshape(both, width)
        outers = low_outer[spot, :]
        for first in range(0, part_size, chunk):
            last = min(first + chunk, part_size)
            part, lanes = slice(base + first, base + last), slice(first, last)
            gate, up = dot_nt(these, buf[0, part, :]), dot_nt(these, buf[1, part, :])
            act_grad = dot_nt(outers, buf[2, part, :])
            square = gate * gate
            inner = gate * (0.7978845608028654 + (0.7978845608028654 * 0.044715) * square)
            rise = 0.5 + 0.5 * jnp.tanh(inner)
            bent = gate * rise
            act[spot, lanes] = (bent * up).astype(BF16)
            slope = rise + bent * (1.0 - rise) * (
                2 * 0.7978845608028654 + (6 * 0.7978845608028654 * 0.044715) * square
            )
            low[0, spot, lanes] = (act_grad * up * slope).astype(BF16)
            low[1, spot, lanes] = (act_grad * bent).astype(BF16)
        whole = slice(base, base + part_size)
        result = dot_nn(act[spot, :], buf[2, whole, :])
        back = dot_nn(low[0, spot, :], buf[0, whole, :]) + dot_nn(low[1, spot, :], buf[1, whole, :])
        return spot, result, back

    def near_step(step, carry):
        pair = flip(my_pair, step, pairs)
        first = 2 * pair

        @pl.when(step == 1)
        def _():
            send_rows(turns[1])
            far_copy(0).wait()
            onward_copy(0).start()
            far_copy(1).start()

        @pl.when(step == pairs - 1)
        def _():
            far_copy(1).wait()
            onward_copy(1).start()
            far_copy(2).start()

        @pl.when(step == 0)
        def _():
            peer = flip(me, 1, size)
            for copy in forth(me, peer, peer):
                copy.wait_recv()

        @pl.when(step > 0)
        def _():
            for which in range(2):
                for copy in forth(me, first + which, first + which):
                    copy.wait_recv()

        for which in range(2):
            gate = column_of(gates[first + which, 0:1, :], capacity)
            spot = pl.ds(pl.multiple_of((first + which) * capacity, capacity), capacity)
            low_outer[spot, :] = (outer[first + which].astype(F32) * gate).astype(BF16)
        spot, result, back = hidden_part(pair, 0)
        made_sum[spot, :] = result
        back_sum[spot, :] = back
        return carry

    def sent_all(copies):
        for remote_one, copy in copies:
            if remote_one:
                copy.wait_send()
            else:
                copy.wait()

    def weight_grads(half):
        every = rows[...].reshape(size * capacity, width)
        outers = low_outer[...]
        count = 0
        base = half * part_size
        waiting = {}
        for c in range(3):
            left = act if c == 2 else low.at[c]
            for first in range(0, part_size, 2 * chunk):
                last = min(first + 2 * chunk, part_size)
                slot = count % 2
                sent_all(waiting.pop(slot, ()))
                piece = dot_tn(left[:, first:last], outers if c == 2 else every)
                grad_stage[slot, : last - first, :] = piece.astype(BF16)
                copies = []
                begin = base + first
                while begin < base + last:
                    group = begin // share
                    end = min(base + last, (group + 1) * share)
                    source = grad_stage.at[slot, pl.ds(begin - base - first, end - begin)]
                    spot = pl.ds(begin - group * share, end - begin)
                    sem = grad_sems.at[slot, len(copies)]
                    if group % 2:
                        target = moved_out.at[group // 2, c, spot]
                        copies.append((True, remote_copy(source, target, sem, moved_sem, "wshard", near)))
                    else:
                        target = grad_out.at[group // 2, c, spot]
                        copies.append((False, pltpu.make_async_copy(source, target, sem)))
                    begin = end
                for _, copy in copies:
                    copy.start()
                waiting[slot] = copies
                count += 1
        for copies in waiting.values():
            sent_all(copies)

    for copy in loads[:2]:
        copy.wait()
    for copy in near_copies:
        copy.wait_recv()
    lax.fori_loop(0, pairs, near_step, 0)
    weight_grads(0)

    def far_step(step, carry):
        pair = flip(my_pair, pairs - 1 - step, pairs)
        first = 2 * pair
        spot, result, back = hidden_part(pair, part_size)
        result = (made_sum[spot, :] + result).astype(BF16)
        back = (back_sum[spot, :] + back).astype(BF16)
        two = pl.ds(first, 2)
        made[two] = result.reshape(2, capacity, width)
        stage[two] = back.reshape(2, capacity, width)
        for which in range(2):
            grads = outer[first + which].astype(F32) * made[first + which].astype(F32)
            line = row_of(jnp.sum(grads, -1, keepdims=True), extra_stage.shape[2])
            extra_stage[first + which] = jnp.broadcast_to(line, extra_stage.shape[1:])
        pltpu.make_async_copy(made.at[two], made_out.at[two], save_sems.at[step]).start()

        @pl.when(step < pairs - 1)
        def _():
            for which in range(2):
                for copy in back_copies(first + which, me, first + which):
                    copy.start()

        @pl.when(step == pairs - 1)
        def _():
            peer = flip(me, 1, size)
            for copy in back_copies(peer, me, peer):
                copy.start()
            for copy in own_back:
                copy.start()

        return carry

    far_copy(2).wait()
    onward_copy(2).start()
    for copy in loads[2:]:
        copy.wait()
    for c in range(3):
        onward_copy(c).wait_recv()
    lax.fori_loop(0, pairs, far_step, 0)
    weight_grads(1)
    for copy in own_back:
        copy.wait()
    remote_copy(moved_out, moved_out, moved_sem, moved_sem, "wshard", near).wait_recv()
    for copy in near_copies:
        copy.wait_send()
    for c in range(3):
        onward_copy(c).wait_send()
    for step in range(pairs):
        two = pl.ds(2 * flip(my_pair, pairs - 1 - step, pairs), 2)
        pltpu.make_async_copy(made.at[two], made_out.at[two], save_sems.at[step]).wait()
    for step in range(1, size):
        peer = flip(me, step, size)
        for copy in forth(peer, me, peer):
            copy.wait_send()
        for copy in back_copies(peer, me, peer):
            copy.wait_send()
        for copy in back_copies(me, peer, peer):
            copy.wait_recv()


def moe(sent, gates, outer, own_in, own_down, far_gate, chunk=256):
    size, capacity, width = sent.shape
    groups = lax.axis_size("wshard")
    share = own_down.shape[0]
    part = share * groups // 2
    total = size * capacity
    extra = gates.shape[1:]
    dma = pltpu.SemaphoreType.DMA
    result = pl.pallas_call(
        functools.partial(moe_body, size, groups, chunk),
        out_shape=(
            shape_of((size, capacity, width), BF16),
            shape_of((size, *extra), F32),
            shape_of((size, capacity, width), BF16),
        )
        + (shape_of((2, 3, share, width), BF16),) * 2,
        in_specs=[ANY] * 6,
        out_specs=(ANY,) * 5,
        scratch_shapes=[
            pltpu.VMEM((3, share * groups, width), BF16),
            pltpu.VMEM((size, capacity, width), BF16),
            pltpu.VMEM((size, *extra), F32),
            pltpu.VMEM((size, capacity, width), BF16),
            pltpu.VMEM((total, width), BF16),
            pltpu.VMEM((total, width), F32),
            pltpu.VMEM((total, width), F32),
            pltpu.VMEM((total, part), BF16),
            pltpu.VMEM((2, total, part), BF16),
            pltpu.VMEM((size, capacity, width), BF16),
            pltpu.VMEM((size, *extra), F32),
            pltpu.VMEM((size, capacity, width), BF16),
            pltpu.VMEM((2, 2 * chunk, width), BF16),
            dma((4,)),
            dma((3, 3, 2)),
            dma((size, 2)),
            dma((size, 2)),
            dma((size, 2)),
            dma((size, 2)),
            dma((5,)),
            dma((size // 2,)),
            dma((2, 3)),
            dma,
        ],
        cost_estimate=pl.CostEstimate(flops=LIGHT, bytes_accessed=LIGHT, transcendentals=0),
        compiler_params=pltpu.CompilerParams(
            collective_id=0, has_side_effects=True, vmem_limit_bytes=66_000_000
        ),
        name="experts",
    )(sent, gates, outer, own_in, own_down, far_gate)
    return result


def expert_body(groups, chunk, rows_ref, outer_ref, gate_ref, *refs):
    in_refs, down_refs = refs[:groups], refs[groups : 2 * groups]
    made_ref, back_ref, outer_out_ref, gate_grad_ref = refs[2 * groups : 2 * groups + 4]
    act_ref, low_ref, buf_ref, sems = refs[2 * groups + 4 :]
    share = down_refs[0].shape[0]
    hidden = share * groups

    def copies(group):
        spot = pl.ds(group * share, share)
        return (
            pltpu.make_async_copy(in_refs[group], buf_ref.at[0:2, spot], sems.at[2 * group]),
            pltpu.make_async_copy(down_refs[group], buf_ref.at[2, spot], sems.at[2 * group + 1]),
        )

    @pl.when(pl.program_id(0) == 0)
    def _():
        for group in range(groups):
            for copy in copies(group):
                copy.start()

    rows = rows_ref[...]
    low_outer = (outer_ref[...].astype(F32) * gate_ref[...]).astype(BF16)
    outer_out_ref[...] = low_outer

    @pl.when(pl.program_id(0) == 0)
    def _():
        for group in range(groups):
            for copy in copies(group):
                copy.wait()

    for first in range(0, hidden, chunk):
        part = slice(first, first + chunk)
        gate, up = dot_nt(rows, buf_ref[0, part, :]), dot_nt(rows, buf_ref[1, part, :])
        act_grad = dot_nt(low_outer, buf_ref[2, part, :])
        square = gate * gate
        inner = gate * (0.7978845608028654 + (0.7978845608028654 * 0.044715) * square)
        rise = 0.5 + 0.5 * jnp.tanh(inner)
        bent = gate * rise
        act_ref[:, part] = (bent * up).astype(BF16)
        slope = rise + bent * (1.0 - rise) * (
            2 * 0.7978845608028654 + (6 * 0.7978845608028654 * 0.044715) * square
        )
        low_ref[0, :, part] = (act_grad * up * slope).astype(BF16)
        low_ref[1, :, part] = (act_grad * bent).astype(BF16)
    made = dot_nn(act_ref[...], buf_ref[2]).astype(BF16)
    made_ref[...] = made
    back = dot_nn(low_ref[0], buf_ref[0]) + dot_nn(low_ref[1], buf_ref[1])
    back_ref[...] = back.astype(BF16)
    gate_grad_ref[...] = jnp.sum(
        outer_ref[...].astype(F32) * made.astype(F32), -1, keepdims=True
    )


def experts_pass(rows, outer, gate_column, in_weights, down_weights, block=320, chunk=256):
    total, width = rows.shape
    groups = len(in_weights)
    hidden = down_weights[0].shape[0] * groups
    row_spec = pl.BlockSpec((block, width), lambda i: (i, 0))
    column = pl.BlockSpec((block, 1), lambda i: (i, 0))
    wide = pl.BlockSpec((block, hidden), lambda i: (i, 0))
    both = pl.BlockSpec((2, block, hidden), lambda i: (0, i, 0))
    return pl.pallas_call(
        functools.partial(expert_body, groups, chunk),
        grid=(total // block,),
        out_shape=(
            shape_of((total, width), BF16),
            shape_of((total, width), BF16),
            shape_of((total, width), BF16),
            shape_of((total, 1), F32),
            shape_of((total, hidden), BF16),
            shape_of((2, total, hidden), BF16),
        ),
        in_specs=[row_spec, row_spec, column] + [ANY] * (2 * groups),
        out_specs=(row_spec, row_spec, row_spec, column, wide, both),
        scratch_shapes=[
            pltpu.VMEM((3, hidden, width), BF16),
            pltpu.SemaphoreType.DMA((2 * groups,)),
        ],
        cost_estimate=pl.CostEstimate(flops=LIGHT, bytes_accessed=LIGHT, transcendentals=0),
        name="experts",
    )(rows, outer, gate_column, *in_weights, *down_weights)


def moe_plain(sent, gates, outer, own_in, own_down, far_gate):
    in_weights, down_weights = [own_in], [own_down]
    for bit in (1, 2):
        in_weights += [swap(w, "wshard", bit) for w in in_weights]
        down_weights += [swap(w, "wshard", bit) for w in down_weights]
    size, capacity, width = sent.shape
    total = size * capacity
    rows = exchange(sent.reshape(total, width), "dp").reshape(total, width)
    gate_column = lax.all_to_all(gates, "dp", 0, 0, tiled=True)[:, 0, :capacity].reshape(total, 1)
    made, back, outer_low, gate_grads, act, low = experts_pass(
        rows, outer.reshape(total, width), gate_column, in_weights, down_weights
    )
    extra = jnp.pad(gate_grads.reshape(size, 1, capacity), ((0, 0), (0, EXTRA - 1), (0, 0)))
    extra = lax.all_to_all(extra, "dp", 0, 0, tiled=True)
    share = down_weights[0].shape[0]
    grads = []
    for group in range(len(in_weights)):
        part = slice(group * share, (group + 1) * share)
        pieces = [dot_tn(low[c, :, part], rows) for c in range(2)]
        grads.append(jnp.stack(pieces + [dot_tn(act[:, part], outer_low)]).astype(BF16))
    shape = (size, capacity, width)
    moved = jnp.stack([swap(grads[g], "wshard", 1) for g in (1, 3)])
    return exchange(back, "dp"), extra, made.reshape(shape), jnp.stack(grads[::2]), moved


def rear_body(
    size, groups, head_size, remote_made, span_ref, gain_ref, diag_ref, ones_ref, router_ref, col_ref, gate_ref,
    extra_ref, tok_hbm, cot_hbm, hidden_hbm, norm_hbm, mixed_hbm, rows_hbm, made_hbm, outw_hbm,
    qkvw_hbm, qkv_hbm, far_hbm,
    output_ref, grad_ref, early_out, late_out, sum_out, far_out,
    tok, cot, hidden, norm, mixed, rows, made, outw, qkvw, qkv, norm_t, mask, grad_hidden,
    grads, probs_ref, scores_ref, diag_sums, wo, wo_got, wg, wg_got, total,
    total_got, sum_ref, early_ref, early_got, late_ref, late_got,
    load_sems, weight_sems, made_send, made_got, part_sems, total_sems, small_sems, far_sems,
):
    me, place = lax.axis_index("dp"), lax.axis_index("wshard")
    near, far = flip(place, 1, groups), flip(place, 2, groups)
    dp_bits, shard_bits = bits_below(size), bits_below(groups)
    peers = [("dp", flip(me, step, size)) for step in range(1, size)]
    greet(peers + [("wshard", near), ("wshard", far)])
    count, width = tok.shape
    blocks = count // TILE
    experts = size
    capacity = rows.shape[0] // experts
    cols = outw.shape[2]
    two_heads = 2 * head_size
    branch, mixgrad, norm_grad = cot, norm, hidden

    loads = [
        pltpu.make_async_copy(source, target, load_sems.at[i])
        for i, (source, target) in enumerate(
            (
                (rows_hbm, rows), (norm_hbm, norm), (hidden_hbm, hidden), (cot_hbm, cot),
                (mixed_hbm, mixed), (outw_hbm, outw), (tok_hbm, tok), (qkv_hbm, qkv),
                (made_hbm.at[me], made.at[me]) if remote_made else (made_hbm, rows),
            )
        )
    ]
    for copy in loads[: 9 if remote_made else 8]:
        copy.start()

    def far_copy(piece):
        return remote_copy(
            far_hbm.at[piece], far_out.at[piece], far_sems.at[piece, 0], far_sems.at[piece, 1],
            "wshard", far,
        )

    far_copy(0).start()

    def weight_load(step):
        slot = lax.rem(step, 2)
        return pltpu.make_async_copy(
            qkvw_hbm.at[groups - 1 - step], qkvw.at[slot], weight_sems.at[slot]
        )

    hidden_again = pltpu.make_async_copy(hidden_hbm, hidden, load_sems.at[9])

    def made_copy(source, target, peer):
        return remote_copy(
            made_hbm.at[source], made.at[target], made_send.at[source], made_got.at[target], "dp",
            peer,
        )

    turns = turns_of(size)

    def send_made(turn):
        if remote_made:
            for step in turns[turn]:
                peer = flip(me, step, size)
                made_copy(peer, me, peer).start()

    send_made(0)

    exchanges = [("wshard", place, bit, groups) for bit in shard_bits]
    exchanges += [("dp", me, bit, size) for bit in dp_bits]

    def small_copy(kind, ref, got, step):
        axis, index, bit, length = exchanges[step]
        return remote_copy(
            ref, got.at[step], small_sems.at[kind, step, 0], small_sems.at[kind, step, 1], axis,
            flip(index, bit, length),
        )

    def small_step(kind, ref, got, step):
        now, before = step % 2, (step + 1) % 2
        if step > 0:
            small_copy(kind, ref.at[before], got, step - 1).wait()
            ref[now] = ref[before] + got[step - 1]
        if step < len(exchanges):
            small_copy(kind, ref.at[now], got, step).start()

    slots = [col_ref[:, k : k + 1] for k in range(2)]
    gates = [gate_ref[:, k : k + 1] for k in range(2)]
    lane = iota((count, extra_ref.shape[2]), 1)
    picked = [0.0, 0.0]
    for copy in loads[:1]:
        copy.wait()
    grads_in = 0.0
    for expert in range(experts):
        label = jnp.where(lane < capacity, lane + expert * capacity, -1)
        for k in range(2):
            picked[k] = picked[k] + jnp.where(label == slots[k], extra_ref[expert, 0:1, :], 0.0)
    gate_grads = [jnp.sum(p, -1, keepdims=True) for p in picked]
    mean = gates[0] * gate_grads[0] + gates[1] * gate_grads[1]
    lane = iota((count, 3 * experts), 1)
    part = (lane >= experts).astype(I32) + (lane >= 2 * experts).astype(I32)
    label = lane - part * experts
    logit_grads = 0.0
    for k in range(2):
        own = (label * capacity <= slots[k]) & (slots[k] < (label + 1) * capacity)
        logit_grads = logit_grads + jnp.where(own, gates[k] * (gate_grads[k] - mean), 0.0)
    high, middle, low = split_three(logit_grads)
    split = jnp.where(part == 0, high, jnp.where(part == 1, middle, low)).astype(BF16)
    hits = [onehot_columns(slots[k], 0, experts * capacity) for k in range(2)]
    hits = (hits[0] | hits[1]).astype(F32).astype(BF16)
    for copy in loads[1:4]:
        copy.wait()
    normed_grad = dot_nn(hits, rows[...])
    normed_grad = normed_grad + dot_nn(split, router_ref[...])
    router_grad = dot_tn(split, norm[...])
    early_ref[0, :experts, :] = (
        router_grad[:experts] + router_grad[experts : 2 * experts] + router_grad[2 * experts :]
    )
    unit, recip = unit_norm(hidden[...])
    early_ref[0, experts:, :] = jnp.broadcast_to(
        jnp.sum(normed_grad * unit, 0, keepdims=True), (EXTRA, width)
    )
    small_step(0, early_ref, early_got, 0)
    scaled = normed_grad * gain_ref[1:2, :]
    back = recip * (scaled - unit * jnp.mean(scaled * unit, -1, keepdims=True))
    grad_hidden[...] = cot[...].astype(F32) + back
    branch[...] = grad_hidden[...].astype(BF16)
    for copy in loads[4:6]:
        copy.wait()
    mixed_t = mixed[...].T
    result = 0.0

    def part_copy(item, source, target, kind, axis, peer):
        return remote_copy(
            source, target, part_sems.at[item, kind, 0], part_sems.at[item, kind, 1], axis, peer
        )

    def out_copy(kind):
        return part_copy(
            0, wo.at[(3, 1, 2)[kind]], wo_got.at[kind], kind, "wshard", far if kind == 2 else near
        )

    def qkv_copy(kind):
        return part_copy(
            1, wg.at[(2, 0, 1)[kind]], wg_got.at[kind], kind, "wshard", far if kind == 2 else near
        )

    for group in reversed(range(groups)):
        lanes = pl.ds(pl.multiple_of(flip(place, group, groups) * cols, cols), cols)
        piece = branch[:, lanes]
        result = result + dot_nt(piece, outw[group])
        wo[group] = dot_nn(mixed_t, piece).astype(BF16)
        if group == 3:
            out_copy(0).start()
        if group == 1:
            out_copy(1).start()
    mixgrad[...] = result.astype(BF16)
    for copy in loads[6:8]:
        copy.wait()
    weight_load(0).start()
    unit, _ = unit_norm(tok[...].astype(F32))
    norm_t[...] = (unit * gain_ref[0:1, :]).astype(BF16).T
    fill_mask(mask, span_ref[0])
    norm_grad[...] = jnp.zeros_like(norm_grad)

    def attend_group(step):
        group = groups - 1 - step
        slot = lax.rem(step, 2)
        weight_load(step).wait()

        @pl.when(step < groups - 1)
        def _():
            weight_load(step + 1).start()

        owner = flip(place, group, groups)
        heads = cols // head_size

        def pair(p, carry):
            offset = pl.multiple_of(p * two_heads, two_heads)
            lanes = pl.ds(offset, two_heads)
            query, keys, value = (qkv[group, c, :, lanes] for c in range(3))
            outer = mixgrad[:, pl.ds(pl.multiple_of(owner * cols + offset, two_heads), two_heads)]
            query_sum, key_sum, value_sum = [None] * blocks, None, None
            for which in range(2):
                head = owner * heads + 2 * p + which
                own = head_lanes(which, head_size)
                own_query, own_key, own_outer = query * own, keys * own, outer * own
                shrunk = own_query * 0.125
                tiles, far_bias = bias_tiles(diag_ref[pl.ds(head, 1), :])
                near_sums, far_sums = [None] * 3, [None] * 2
                for block in range(blocks):
                    piece = slice(block * TILE, (block + 1) * TILE)
                    probs = softmax_tiles(
                        score_tiles(block, shrunk[piece], keys, tiles, far_bias, mask)
                    )
                    prob_grads = dot_nt(own_outer[piece], value)
                    prob_grads = [prob_grads[:, j * TILE : (j + 1) * TILE] for j in range(blocks)]
                    delta = functools.reduce(jnp.add, [a * b for a, b in zip(probs, prob_grads)])
                    delta = jnp.sum(delta, -1, keepdims=True)
                    lows = [(a * (b - delta)).astype(BF16) for a, b in zip(probs, prob_grads)]
                    for other in range(blocks):
                        step = block - other
                        wide = lows[other].astype(F32)
                        if abs(step) >= 2:
                            side = 0 if step > 0 else 1
                            old = far_sums[side]
                            far_sums[side] = wide if old is None else old + wide
                        else:
                            old = near_sums[step + 1]
                            near_sums[step + 1] = wide if old is None else old + wide
                    probs_ref[which, piece, :] = jnp.concatenate([t.astype(BF16) for t in probs], 1)
                    lows = jnp.concatenate(lows, 1)
                    scores_ref[which, piece, :] = lows
                    more = dot_nn(lows, own_key)
                    query_sum[block] = more if which == 0 else query_sum[block] + more
                more = dot_tn(scores_ref[which], own_query)
                key_sum = more if which == 0 else key_sum + more
                more = dot_tn(probs_ref[which], own_outer)
                value_sum = more if which == 0 else value_sum + more
                for step in range(3):
                    wide = jnp.concatenate([near_sums[step], jnp.zeros((TILE, TILE), F32)], 1)
                    half = TILE // 2
                    while half:
                        turned = pltpu.roll(wide[half:], 2 * TILE - half, 1)
                        wide = wide[:half] + turned
                        half //= 2
                    for side in range(2):
                        spot = 2 * step + side
                        diag_sums[head, spot : spot + 1, :] = wide[:, TILE * side : TILE * (side + 1)]
                for side in range(2):
                    diag_sums[head, 6 + side : 7 + side, :] = jnp.sum(far_sums[side], 0, keepdims=True)
            for block in range(blocks):
                piece = slice(block * TILE, (block + 1) * TILE)
                grads[0, piece, lanes] = (query_sum[block] * 0.125).astype(BF16)
            grads[1, :, lanes] = (key_sum * 0.125).astype(BF16)
            grads[2, :, lanes] = value_sum.astype(BF16)
            return carry

        lax.fori_loop(0, cols // two_heads, pair, 0)
        for c in range(3):
            weight_grad = dot_nn(norm_t[...], grads[c]).astype(BF16)

            @pl.when(group > 0)
            def _():
                wg[group - 1, c] = weight_grad

            @pl.when(group == 0)
            def _():
                total[c * width : (c + 1) * width, :] = weight_grad

            norm_grad[...] += dot_nt(grads[c], qkvw[slot, c])

    def add_into(target, *others):
        for first in range(0, target.shape[0], 256):
            spot = slice(first, first + 256)
            value = target[spot].astype(F32)
            for other in others:
                value = value + other[spot].astype(F32)
            target[spot] = value.astype(BF16)

    def group_step(step, carry):
        attend_group(step)

        @pl.when(step == 0)
        def _():
            send_made(1)
            qkv_copy(0).start()
            small_step(0, early_ref, early_got, 1)
            out_copy(0).wait_recv()
            add_into(wo.at[2], wo_got.at[0])
            out_copy(2).start()

        @pl.when(step == 1)
        def _():
            send_made(2)
            qkv_copy(0).wait_recv()
            for c in range(3):
                add_into(wg.at[1, c], wg_got.at[0, c])
            qkv_copy(2).start()
            small_step(0, early_ref, early_got, 2)

        @pl.when(step == 2)
        def _():
            qkv_copy(1).start()
            small_step(0, early_ref, early_got, 3)

        return carry

    lax.fori_loop(0, groups, group_step, 0)

    small_step(0, early_ref, early_got, 4)
    unit, recip = unit_norm(tok[...].astype(F32))
    gain_grad = jnp.sum(norm_grad[...] * unit, 0, keepdims=True)
    table_grad = 0.0
    for k in range(8):
        for piece in split_three(diag_sums[:, k, :]):
            table_grad = table_grad + dot_nt(piece.astype(BF16), ones_ref[:, k * TILE : (k + 1) * TILE])
    late_ref[0] = jnp.zeros(late_ref.shape[1:], F32)
    for k in range(width // TILE):
        late_ref[0, k : k + 1, :] = gain_grad[:, k * TILE : (k + 1) * TILE]
    heads, buckets = table_grad.shape
    late_ref[0, 8 : 8 + heads, :buckets] = table_grad
    small_step(1, late_ref, late_got, 0)

    qkv_copy(1).wait_recv()
    out_copy(1).wait_recv()
    out_copy(2).wait_recv()
    qkv_copy(2).wait()
    far_copy(1).start()
    third = outw.shape[1]
    for c in range(3):
        add_into(total.at[c * third : (c + 1) * third], wg_got.at[1, c], wg_got.at[2, c])
    add_into(wo.at[0], wo_got.at[1], wo_got.at[2])
    total[3 * third :, :] = wo[0]
    parts = 4
    length = total.shape[0] // parts
    stages = len(dp_bits)

    def bit_of(step):
        return lax.rem(lax.div(me, dp_bits[step]), 2)

    def segment(part, step):
        first, size_of = part * length, length
        for s in range(step):
            size_of //= 2
            first = first + bit_of(s) * size_of
        return first, size_of

    def halving(part, step):
        first, size_of = segment(part, step)
        half = size_of // 2
        away = pl.multiple_of(first + (1 - bit_of(step)) * half, half)
        return remote_copy(
            total.at[pl.ds(away, half)],
            total_got.at[pl.ds(part * length + length - size_of, half)],
            total_sems.at[part, 0, step, 0], total_sems.at[part, 0, step, 1], "dp",
            flip(me, dp_bits[step], size),
        )

    def add_half(part, step):
        first, half = segment(part, step + 1)
        first = pl.multiple_of(first, half)
        got = part * length + length - 2 * half
        value = total[pl.ds(first, half), :].astype(F32) + total_got[got : got + half, :].astype(F32)
        total[pl.ds(first, half), :] = value.astype(BF16)
        if step == stages - 1:
            sum_ref[pl.ds(first, half), :] = value.astype(BF16)

    def doubling(part, step):
        first, size_of = segment(part, step + 1)
        spot = pl.ds(pl.multiple_of(first, size_of), size_of)
        return remote_copy(
            sum_ref.at[spot], sum_ref.at[spot],
            total_sems.at[part, 1, step, 0], total_sems.at[part, 1, step, 1], "dp",
            flip(me, dp_bits[step], size),
        )

    def sum_stage(part, stage):
        if 0 < stage <= stages:
            halving(part, stage - 1).wait()
            add_half(part, stage - 1)
        elif stage > stages:
            doubling(part, 2 * stages - stage).wait()
        if stage < stages:
            halving(part, stage).start()
        elif stage < 2 * stages:
            doubling(part, 2 * stages - 1 - stage).start()

    def finish_tokens():
        scaled = norm_grad[...] * gain_ref[0:1, :]
        back = recip * (scaled - unit * jnp.mean(scaled * unit, -1, keepdims=True))
        grad_ref[...] = (grad_hidden[...] + back).astype(BF16)
        hidden_again.start()
        if not remote_made:
            loads[8].start()

    def finish_output():
        loads[8].wait()
        hidden_again.wait()
        if remote_made:
            for _, peer in peers:
                made_copy(me, peer, peer).wait_recv()
        values = made[...].reshape(experts * capacity, width) if remote_made else rows[...]
        for first in range(0, count, 256):
            spot = slice(first, first + 256)
            value = hidden[spot, :]
            for k in range(2):
                hit = onehot_columns(slots[k][spot], 0, experts * capacity)
                value = value + gates[k][spot] * dot_nn(hit.astype(F32).astype(BF16), values)
            output_ref[spot, :] = value.astype(BF16)

    rest_early = list(range(groups + 1, len(exchanges) + 1))
    rest_late = list(range(1, len(exchanges) + 1))

    def next_small():
        if rest_early:
            small_step(0, early_ref, early_got, rest_early.pop(0))
        if rest_late:
            small_step(1, late_ref, late_got, rest_late.pop(0))

    for time in range(parts + 2 * stages):
        for part in range(min(parts, time + 1)):
            if time - part <= 2 * stages:
                sum_stage(part, time - part)
        if time == 0:
            finish_tokens()
        elif time == 1:
            finish_output()
        elif time == 5:
            far_copy(1).wait()
            far_copy(2).start()
        next_small()
    while rest_early or rest_late:
        next_small()
    early_out[...] = early_ref[len(exchanges) % 2]
    late_out[...] = late_ref[len(exchanges) % 2]
    save = pltpu.make_async_copy(sum_ref, sum_out, load_sems.at[10])
    save.start()
    save.wait()
    far_copy(0).wait()
    far_copy(2).wait()
    if remote_made:
        for _, peer in peers:
            made_copy(peer, me, peer).wait_send()
    for kind in range(3):
        out_copy(kind).wait_send()
    for kind in range(2):
        qkv_copy(kind).wait_send()


def bits_below(size):
    return [1 << b for b in range(size.bit_length() - 1)]


def rear(
    span, gains, diag, ones, router_t3, slots_col, gates, extra, tokens, cotangent, hidden, normed,
    mixed, rows, made, out_weights, qkv_weights, qkv, far_sum, head_size,
):
    count, width = tokens.shape
    size, groups = lax.axis_size("dp"), lax.axis_size("wshard")
    heads, buckets = width // head_size, ones.shape[0]
    experts = router_t3.shape[0] // 3
    cols = out_weights.shape[2]
    exchanges = len(bits_below(size)) + len(bits_below(groups))
    dma = pltpu.SemaphoreType.DMA
    wide, small = (count, width), (experts + EXTRA, width)
    late = (8 + heads, TILE)
    total = (4 * width, cols)
    vmem = pltpu.VMEM
    return pl.pallas_call(
        functools.partial(rear_body, size, groups, head_size, made.ndim == 3),
        out_shape=(
            shape_of(wide, BF16),
            shape_of(wide, BF16),
            shape_of(small, F32),
            shape_of(late, F32),
            shape_of(total, BF16),
            shape_of(far_sum.shape, BF16),
        ),
        in_specs=[SMEM] + [VMEM] * 7 + [ANY] * 11,
        out_specs=(VMEM,) * 4 + (ANY,) * 2,
        scratch_shapes=[
            vmem(wide, BF16),
            vmem(wide, BF16),
            vmem(wide, F32),
            vmem(wide, BF16),
            vmem(wide, BF16),
            vmem(rows.shape, BF16),
            vmem(made.shape if made.ndim == 3 else (16, TILE), BF16),
            vmem(out_weights.shape, BF16),
            vmem((2, *qkv_weights.shape[1:]), BF16),
            vmem(qkv.shape, BF16),
            vmem((width, count), BF16),
            vmem((count, count), F32),
            vmem(wide, F32),
            vmem((3, count, cols), BF16),
            vmem((2, count, count), BF16),
            vmem((2, count, count), BF16),
            vmem((heads, 8, TILE), F32),
            vmem((groups, width, cols), BF16),
            vmem((3, width, cols), BF16),
            vmem((groups - 1, 3, width, cols), BF16),
            vmem((3, 3, width, cols), BF16),
            vmem(total, BF16),
            vmem(total, BF16),
            vmem(total, BF16),
            vmem((2, *small), F32),
            vmem((exchanges, *small), F32),
            vmem((2, *late), F32),
            vmem((exchanges, *late), F32),
            dma((11,)),
            dma((2,)),
            dma((size,)),
            dma((size,)),
            dma((2, 3, 2)),
            dma((4, 2, len(bits_below(size)), 2)),
            dma((2, exchanges, 2)),
            dma((3, 2)),
        ],
        cost_estimate=pl.CostEstimate(flops=LIGHT, bytes_accessed=LIGHT, transcendentals=0),
        compiler_params=pltpu.CompilerParams(
            collective_id=2, has_side_effects=True, vmem_limit_bytes=66_000_000
        ),
        name="rear",
    )(
        span, gains, diag, ones, router_t3, slots_col, gates, extra, tokens, cotangent, hidden,
        normed, mixed, rows, made, out_weights, qkv_weights, qkv, far_sum,
    )


def swap(value, axis, bit):
    size = lax.axis_size(axis)
    return lax.ppermute(value, axis, [(i, i ^ bit) for i in range(size)])


def bits_of(axis):
    size = lax.axis_size(axis)
    return [1 << b for b in range(size.bit_length() - 1)]


def after(value, *others):
    return lax.optimization_barrier((value, *others))[0]


def exchange(rows, axis):
    size = lax.axis_size(axis)
    total, width = rows.shape
    blocks = rows.reshape(size, total // size, width)
    return lax.all_to_all(blocks, axis, 0, 0, tiled=True)


def per_device(
    tokens,
    cotangent,
    span_starts,
    routes,
    norm_gains,
    bias_table,
    router,
    attn_qkv,
    attn_out,
    expert_in,
    expert_down,
):
    assert span_starts.shape[0] == 1
    tok_count, model_width = tokens.shape
    buckets, head_count = bias_table.shape
    head_size = model_width // head_count
    experts = router.shape[1]
    capacity = (10 * tok_count + 4 * experts - 1) // (4 * experts)
    total = experts * capacity
    place = lax.axis_index("wshard")
    where = jnp.stack([place.astype(I32), span_starts[0]])
    diag = jnp.asarray(diagonal_ones(buckets))
    diag_bias = jnp.dot(bias_table.T, diag, precision=PRECISE)
    router_t = router.T
    expert_in = jnp.swapaxes(expert_in[0], 1, 2)
    expert_down = expert_down[0]

    shards = (attn_qkv, attn_out, expert_in)
    (
        slots_col, gates, sent_gates, qkv_all, out_all, qkv, mixed, hidden, normed_two, sent,
        outer_rows, far_gate,
    ) = front(
        span_starts, routes, norm_gains, diag_bias, router_t, tokens, cotangent, shards, head_size,
        capacity,
    )
    groups = out_all.shape[0]
    through = moe if capacity % 16 == 0 else moe_plain
    back_rows, back_extra, made, expert_grads, moved = through(
        sent, sent_gates, outer_rows, expert_in, expert_down, far_gate
    )
    far_sum = (expert_grads[1].astype(F32) + moved[1].astype(F32)).astype(BF16)
    if through is moe_plain:
        made = exchange(made.reshape(total, model_width), "dp").reshape(total, model_width)

    output, grad_tokens, early, late, attn_sum, far_got = rear(
        span_starts, norm_gains, diag_bias, diag.astype(BF16), jnp.concatenate([router_t] * 3, 0),
        slots_col, gates, back_extra, tokens, cotangent, hidden, normed_two,
        mixed, back_rows.reshape(total, model_width), made, out_all, qkv_all, qkv, far_sum, head_size,
    )

    def expert_sum(part):
        pieces = (expert_grads[0, part], moved[0, part], far_got[part])
        return functools.reduce(jnp.add, [piece.astype(F32) for piece in pieces])

    grad_expert_in = jnp.swapaxes(expert_sum(slice(0, 2)), 1, 2)[None]
    grad_expert_down = expert_sum(2)[None]
    cols = out_all.shape[2]
    grad_attn_qkv = attn_sum[: 3 * model_width].astype(F32).reshape(3, model_width, cols)
    grad_attn_out = attn_sum[3 * model_width :].astype(F32)
    gain_rows = model_width // TILE
    gain_one = late[:gain_rows].reshape(model_width)
    return (
        output,
        grad_tokens,
        jnp.stack([gain_one, early[experts]]),
        late[gain_rows:, :buckets].T,
        early[:experts].T,
        grad_attn_qkv,
        grad_attn_out,
        grad_expert_in,
        grad_expert_down,
    )


def solution(mesh):
    return jax.shard_map(
        per_device,
        mesh=mesh,
        in_specs=(
            P(("dp", "wshard"), None),
            P(("dp", "wshard"), None),
            P(("dp", "wshard")),
            P(("dp", "wshard"), None),
            P(),
            P(),
            P(),
            P(None, None, "wshard"),
            P(None, "wshard"),
            P("dp", None, None, "wshard"),
            P("dp", "wshard", None),
        ),
        out_specs=(
            P(("dp", "wshard"), None),
            P(("dp", "wshard"), None),
            P(),
            P(),
            P(),
            P(None, None, "wshard"),
            P(None, "wshard"),
            P("dp", None, None, "wshard"),
            P("dp", "wshard", None),
        ),
        check_vma=False,
    )
```

```python
import functools

import jax
import jax.numpy as jnp
import numpy as np
from jax import lax
from jax.experimental import pallas as pl
from jax.experimental.pallas import tpu as pltpu
from jax.sharding import PartitionSpec as P

PIC = 256
PRECISE = lax.Precision.HIGHEST
EPSILON = 1e-06
MASKED_SCORE = -1e30
BUCKET_EDGES = (8, 11, 16, 23, 32, 45, 64, 91)
TILE = 128
F32 = jnp.float32
BF16 = jnp.bfloat16
I32 = jnp.int32
VMEM = pl.BlockSpec(memory_space=pltpu.VMEM)
SMEM = pl.BlockSpec(memory_space=pltpu.SMEM)
ANY = pl.BlockSpec(memory_space=pl.ANY)
LIGHT = 1024
EXTRA = 8


def dot_nn(a, b):
    return lax.dot_general(a, b, (((1,), (0,)), ((), ())), preferred_element_type=F32)


def dot_nt(a, b):
    return lax.dot_general(a, b, (((1,), (1,)), ((), ())), preferred_element_type=F32)


def dot_tn(a, b):
    return lax.dot_general(a, b, (((0,), (0,)), ((), ())), preferred_element_type=F32)


def iota(shape, axis):
    return lax.broadcasted_iota(I32, shape, axis)


def shape_of(shape, dtype):
    return jax.ShapeDtypeStruct(shape, dtype)


def call(body, out, args, specs, scratch=(), name=None):
    return pl.pallas_call(
        body,
        out_shape=out,
        in_specs=specs,
        out_specs=jax.tree.map(lambda _: VMEM, out),
        scratch_shapes=list(scratch),
        cost_estimate=pl.CostEstimate(flops=LIGHT, bytes_accessed=LIGHT, transcendentals=0),
        name=name,
    )(*args)


def bucket_of(offset):
    magnitude = np.abs(offset)
    coarse = 7 + sum((magnitude >= bound).astype(np.int32) for bound in BUCKET_EDGES)
    return np.where(magnitude < 8, magnitude, coarse) + 16 * (offset < 0)


def diagonal_ones(bucket_count):
    column = np.arange(2 * TILE)
    signed = np.where(column < TILE, column, column - 2 * TILE)
    offsets = np.concatenate([TILE * step - signed for step in (-1, 0, 1)])
    used = np.tile(column != TILE, 3)
    hit = bucket_of(offsets)[None, :] == np.arange(bucket_count)[:, None]
    near = (hit & used[None, :]).astype(np.float32)
    far = np.zeros((bucket_count, 2 * TILE), np.float32)
    far[bucket_of(np.array(TILE)), :TILE] = 1
    far[bucket_of(np.array(-TILE)), TILE:] = 1
    return np.concatenate([near, far], 1)


def onehot_rows(first, count, slots_row):
    index = iota((count, slots_row.shape[1]), 0) + first
    hit = (index == slots_row[0:1, :]) | (index == slots_row[1:2, :])
    return hit.astype(F32).astype(BF16)


def onehot_columns(slots_column, first, count):
    index = iota((slots_column.shape[0], count), 1) + first
    return index == slots_column


def route_slots(experts, capacity, routes):
    tokens = routes.shape[1]
    label = iota((experts, tokens), 0)
    hits = ((routes[0:1] == label) | (routes[1:2] == label)).astype(F32).astype(BF16)
    earlier = iota((tokens, tokens), 0) < iota((tokens, tokens), 1)
    before = dot_nn(hits, earlier.astype(F32).astype(BF16))
    slots = []
    for k in range(2):
        own = jnp.sum(jnp.where(routes[k : k + 1] == label, before, 0.0), 0, keepdims=True)
        slots.append(own.astype(I32) + routes[k : k + 1] * capacity)
    return jnp.concatenate(slots * 4, 0)


def unit_norm(values):
    recip = lax.rsqrt(jnp.mean(values * values, -1, keepdims=True) + EPSILON)
    return values * recip, recip


def fill_mask(mask_ref, span_start):
    size = mask_ref.shape[0]
    i, j = iota((size, size), 0), iota((size, size), 1)

    def inside(p):
        return (p >= span_start) & (p < span_start + PIC)

    visible = (j <= i) | (inside(i) & inside(j))
    mask_ref[...] = jnp.where(visible, 0.0, MASKED_SCORE)


def head_lanes(which, size):
    lane = iota((1, 2 * size), 1)
    return ((lane >= size) == (which == 1)).astype(F32).astype(BF16)


def bias_tiles(diag_row):
    tiles = []
    for step in range(3):
        row = diag_row[:, 2 * TILE * step : 2 * TILE * (step + 1)]
        wide = jnp.broadcast_to(row, (TILE, 2 * TILE))
        tiles.append(pltpu.roll(wide, 0, 1, stride=1, stride_axis=0)[:, :TILE])
    return tiles, (diag_row[:, 6 * TILE : 7 * TILE], diag_row[:, 7 * TILE :])


def score_tiles(block, query, keys, tiles, far, mask_ref):
    raw = dot_nt(query, keys)
    rows = slice(block * TILE, (block + 1) * TILE)
    result = []
    for other in range(keys.shape[0] // TILE):
        piece = raw[:, other * TILE : (other + 1) * TILE]
        step = block - other
        piece = piece + (far[0] if step >= 2 else far[1] if step <= -2 else tiles[step + 1])
        if step <= 0:
            piece = piece + mask_ref[rows, other * TILE : (other + 1) * TILE]
        result.append(piece)
    return result


def softmax_tiles(pieces):
    top = functools.reduce(jnp.maximum, pieces)
    top = jnp.max(top, -1, keepdims=True)
    powers = [jnp.exp(piece - top) for piece in pieces]
    total = jnp.sum(functools.reduce(jnp.add, powers), -1, keepdims=True)
    scale = 1.0 / total
    return [power * scale for power in powers]


def split_three(value):
    high = value.astype(BF16).astype(F32)
    middle = (value - high).astype(BF16).astype(F32)
    return high, middle, value - high - middle


def remote_copy(source, target, sent, got, axis, peer):
    return pltpu.make_async_remote_copy(
        src_ref=source,
        dst_ref=target,
        send_sem=sent,
        recv_sem=got,
        device_id={axis: peer},
        device_id_type=pl.DeviceIdType.MESH,
    )


def turns_of(size):
    half, quarter = size // 2, size // 4
    return range(half, half + quarter), range(half + quarter, size), range(1, half)


def greet(peers):
    barrier = pltpu.get_barrier_semaphore()
    for axis, peer in peers:
        pl.semaphore_signal(
            barrier, inc=1, device_id={axis: peer}, device_id_type=pl.DeviceIdType.MESH
        )
    pl.semaphore_wait(barrier, len(peers))


def project_and_attend(place, group, groups, head_size, norm, diag_ref, w_ref, qkv_ref, mix_ref, mask):
    count = norm.shape[0]
    cols = w_ref.shape[-1]
    width = 2 * head_size
    owner = flip(place, group, groups)
    for c in range(3):
        qkv_ref[group, c] = dot_nn(norm[...], w_ref[group, c]).astype(BF16)

    def pair(p, carry):
        offset = pl.multiple_of(p * width, width)
        lanes = pl.ds(offset, width)
        query, keys, value = (qkv_ref[group, c, :, lanes] for c in range(3))
        mixed = [None] * (count // TILE)
        for which in range(2):
            head = owner * (cols // head_size) + 2 * p + which
            own = head_lanes(which, head_size)
            own_query, own_value = query * (own * 0.125), value * own
            tiles, far = bias_tiles(diag_ref[pl.ds(head, 1), :])
            for block in range(count // TILE):
                rows = slice(block * TILE, (block + 1) * TILE)
                pieces = score_tiles(block, own_query[rows], keys, tiles, far, mask)
                probs = jnp.concatenate([t.astype(BF16) for t in softmax_tiles(pieces)], 1)
                part = dot_nn(probs, own_value)
                mixed[block] = part if which == 0 else mixed[block] + part
        target = pl.ds(pl.multiple_of(owner * cols + offset, width), width)
        for block in range(count // TILE):
            rows = slice(block * TILE, (block + 1) * TILE)
            mix_ref[rows, target] = mixed[block].astype(BF16)
        return carry

    lax.fori_loop(0, cols // width, pair, 0)


def front_body(
    size, groups, head_size, span_ref, routes_ref, gain_ref, diag_ref, router_ref, tok_hbm, cot_hbm,
    qkv_shard, out_shard, in_shard,
    col_ref, gate_ref, sent_gate_ref, qkvw_out, outw_out, qkv_out, mixed_out, hidden_out, norm_out,
    sent_out, outer_out, gate_out,
    tok, cot, qkvw, outw, qkv, mixed, hidden, norm, sent, outer, mask, row, load_sems, save_sems,
    shard_sems, outer_send, outer_got,
):
    me, place = lax.axis_index("dp"), lax.axis_index("wshard")
    near, far = flip(place, 1, groups), flip(place, 2, groups)
    peers = [("dp", flip(me, step, size)) for step in range(1, size)]
    greet(peers + [("wshard", near), ("wshard", far)])

    sources = (qkv_shard, out_shard, in_shard.at[0, : gate_out.shape[1]])

    def held(item, group):
        if item == 0:
            return qkvw.at[group]
        if item == 1:
            return outw.at[group]
        return gate_out.at[group - 2]

    def shard_copy(kind, item):
        source = held(item, 2) if kind == 2 else sources[item]
        return remote_copy(
            source, held(item, (1, 2, 3)[kind]), shard_sems.at[kind, item, 0],
            shard_sems.at[kind, item, 1], "wshard", far if kind == 1 else near,
        )

    shard_copy(1, 0).start()
    for item in range(2):
        shard_copy(0, item).start()
    loads = [
        pltpu.make_async_copy(source, target, load_sems.at[i])
        for i, (source, target) in enumerate(
            ((cot_hbm, cot), (tok_hbm, tok), (qkv_shard, qkvw.at[0]), (out_shard, outw.at[0]))
        )
    ]
    for copy in loads:
        copy.start()

    experts, capacity = size, sent.shape[1]
    count = tok.shape[0]
    slots = route_slots(experts, capacity, routes_ref[...])
    row[...] = slots
    col_ref[...] = slots.astype(F32).T.astype(I32)
    loads[0].wait()

    def place_outer(expert, carry):
        outer[expert] = dot_nn(onehot_rows(expert * capacity, capacity, row[...]), cot[...]).astype(BF16)
        return carry

    lax.fori_loop(0, experts, place_outer, 0)
    fill_mask(mask, span_ref[0])
    loads[1].wait()
    unit, _ = unit_norm(tok[...].astype(F32))
    norm[...] = (unit * gain_ref[0:1, :]).astype(BF16)
    loads[2].wait()

    def outer_copy(source, target, peer):
        return remote_copy(
            outer.at[source], outer_out.at[target], outer_send.at[source], outer_got.at[target],
            "dp", peer,
        )

    own_outer = pltpu.make_async_copy(outer.at[me], outer_out.at[me], load_sems.at[4])
    own_outer.start()
    turns = turns_of(size)

    def send_outer(turn):
        for step in turns[turn]:
            peer = flip(me, step, size)
            outer_copy(peer, me, peer).start()

    send_outer(0)

    def one_group(group, carry):
        @pl.when(group == 1)
        def _():
            send_outer(1)
            shard_copy(0, 0).wait_recv()

        @pl.when(group == 2)
        def _():
            shard_copy(1, 0).wait()
            shard_copy(2, 0).start()
            shard_copy(1, 1).start()

        @pl.when(group == 3)
        def _():
            send_outer(2)
            shard_copy(2, 0).wait_recv()

        project_and_attend(
            place, group, groups, head_size, norm, diag_ref, qkvw, qkv, mixed, mask
        )
        return carry

    lax.fori_loop(0, groups, one_group, 0)
    saves = [
        pltpu.make_async_copy(source, target, save_sems.at[i])
        for i, (source, target) in enumerate(
            (
                (qkvw, qkvw_out), (qkv, qkv_out), (mixed, mixed_out), (outw, outw_out),
                (hidden, hidden_out), (norm, norm_out), (sent, sent_out),
            )
        )
    ]
    for copy in saves[:3]:
        copy.start()
    loads[3].wait()
    shard_copy(0, 1).wait_recv()
    shard_copy(1, 1).wait()
    shard_copy(2, 1).start()
    shard_copy(1, 2).start()

    shard_copy(2, 1).wait_recv()
    saves[3].start()
    for group in range(groups):
        cols = outw.shape[2]
        lanes = pl.ds(pl.multiple_of(flip(place, group, groups) * cols, cols), cols)
        hidden[:, lanes] = tok[:, lanes].astype(F32) + dot_nn(mixed[...], outw[group])
    saves[4].start()
    unit, _ = unit_norm(hidden[...])
    norm[...] = (unit * gain_ref[1:2, :]).astype(BF16)
    saves[5].start()

    def place_sent(expert, carry):
        sent[expert] = dot_nn(onehot_rows(expert * capacity, capacity, row[...]), norm[...]).astype(BF16)
        return carry

    lax.fori_loop(0, experts, place_sent, 0)
    saves[6].start()
    logits = dot_nt(norm[...], router_ref[...])
    slots = [col_ref[:, k : k + 1] for k in range(2)]
    lane = iota(logits.shape, 1)
    chosen = []
    for k in range(2):
        own = (lane * capacity <= slots[k]) & (slots[k] < (lane + 1) * capacity)
        chosen.append(jnp.sum(jnp.where(own, logits, 0.0), -1, keepdims=True))
    top = jnp.maximum(chosen[0], chosen[1])
    powers = [jnp.exp(c - top) for c in chosen]
    gates = [power / (powers[0] + powers[1]) for power in powers]
    for k in range(2):
        gate_ref[:, k : k + 1] = gates[k]
    lane = iota((count, sent_gate_ref.shape[2]), 1)
    for expert in range(experts):
        label = jnp.where(lane < capacity, lane + expert * capacity, -1)
        part = 0.0
        for k in range(2):
            part = part + jnp.where(label == slots[k], gates[k], 0.0)
        line = jnp.sum(part, 0, keepdims=True)
        sent_gate_ref[expert] = jnp.broadcast_to(line, sent_gate_ref.shape[1:])

    shard_copy(1, 2).wait()
    shard_copy(2, 2).start()
    own_outer.wait()
    for copy in saves:
        copy.wait()
    for _, peer in peers:
        outer_copy(peer, me, peer).wait_send()
        outer_copy(me, peer, peer).wait_recv()
    for item in range(2):
        shard_copy(0, item).wait_send()
        shard_copy(2, item).wait_send()
    shard_copy(2, 2).wait()


def front(span, routes, gains, diag, router_t, tokens, cotangent, shards, head_size, capacity):
    count, width = tokens.shape
    size, groups = lax.axis_size("dp"), lax.axis_size("wshard")
    qkv_shard, out_shard, in_shard = shards
    cols = out_shard.shape[1]
    lanes = -(-capacity // TILE) * TILE
    dma = pltpu.SemaphoreType.DMA
    block = (size, capacity, width)
    return pl.pallas_call(
        functools.partial(front_body, size, groups, head_size),
        out_shape=(
            shape_of((count, 8), I32),
            shape_of((count, 2), F32),
            shape_of((size, EXTRA, lanes), F32),
            shape_of((groups, *qkv_shard.shape), BF16),
            shape_of((groups, *out_shard.shape), BF16),
            shape_of((groups, 3, count, cols), BF16),
            shape_of((count, width), BF16),
            shape_of((count, width), F32),
            shape_of((count, width), BF16),
            shape_of(block, BF16),
            shape_of(block, BF16),
            shape_of((2, in_shard.shape[1] // 32 * 16, width), BF16),
        ),
        in_specs=[SMEM] + [VMEM] * 4 + [ANY] * 5,
        out_specs=(VMEM,) * 3 + (ANY,) * 9,
        scratch_shapes=[
            pltpu.VMEM((count, width), BF16),
            pltpu.VMEM((count, width), BF16),
            pltpu.VMEM((groups, *qkv_shard.shape), BF16),
            pltpu.VMEM((groups, *out_shard.shape), BF16),
            pltpu.VMEM((groups, 3, count, cols), BF16),
            pltpu.VMEM((count, width), BF16),
            pltpu.VMEM((count, width), F32),
            pltpu.VMEM((count, width), BF16),
            pltpu.VMEM(block, BF16),
            pltpu.VMEM(block, BF16),
            pltpu.VMEM((count, count), F32),
            pltpu.VMEM((8, count), I32),
            dma((5,)),
            dma((7,)),
            dma((3, 3, 2)),
            dma((size,)),
            dma((size,)),
        ],
        cost_estimate=pl.CostEstimate(flops=LIGHT, bytes_accessed=LIGHT, transcendentals=0),
        compiler_params=pltpu.CompilerParams(
            collective_id=1, has_side_effects=True, vmem_limit_bytes=60_000_000
        ),
        name="front",
    )(span, routes.T, gains, diag, router_t, tokens, cotangent, *shards)


def flip(value, change, size):
    result = 0
    bit = 1
    while bit < size:
        one, two = lax.rem(lax.div(value, bit), 2), lax.rem(lax.div(change, bit), 2)
        result = result + bit * (one + two - 2 * one * two)
        bit *= 2
    return result


def column_of(row, size):
    spot = iota((size, row.shape[1]), 0) == iota((size, row.shape[1]), 1)
    return jnp.sum(jnp.where(spot, row, 0.0), 1, keepdims=True)


def row_of(column, lanes):
    spot = iota((column.shape[0], lanes), 0) == iota((column.shape[0], lanes), 1)
    return jnp.sum(jnp.where(spot, column, 0.0), 0, keepdims=True)


def moe_body(
    size, groups, chunk, sent_ref, gates_ref, outer_ref, own_in, own_down, far_gate, *refs
):
    back_out, extra_out, made_out, grad_out, moved_out = refs[:5]
    (
        buf, rows, gates, outer, low_outer, made_sum, back_sum, act, low, stage, extra_stage,
        made, grad_stage, weight_sems, shard_sems, send_sems, recv_sems, give_sems, take_sems, own_sems,
        save_sems, grad_sems, moved_sem, sum_sems,
    ) = refs[5:]
    share = own_down.shape[0]
    part_size = share * groups // 2
    capacity, width = outer.shape[1:]
    both = 2 * capacity
    me = lax.axis_index("dp")
    pairs = size // 2
    my_pair = lax.div(me, 2)
    mesh_id = pl.DeviceIdType.MESH

    place = lax.axis_index("wshard")
    near, far = flip(place, 1, groups), flip(place, 2, groups)
    peers = [("dp", flip(me, step, size)) for step in range(1, size)]
    greet(peers + [("wshard", near), ("wshard", far)])

    def remote(source, target, sent, got, peer):
        return pltpu.make_async_remote_copy(
            src_ref=source, dst_ref=target, send_sem=sent, recv_sem=got,
            device_id={"dp": peer}, device_id_type=mesh_id,
        )

    def forth(source, target, peer):
        return (
            remote(sent_ref.at[source], rows.at[target], send_sems.at[source, 0],
                   recv_sems.at[target, 0], peer),
            remote(gates_ref.at[source], gates.at[target], send_sems.at[source, 1],
                   recv_sems.at[target, 1], peer),
        )

    def back_copies(source, target, peer):
        return (
            remote(stage.at[source], back_out.at[target], give_sems.at[source, 0],
                   take_sems.at[target, 0], peer),
            remote(extra_stage.at[source], extra_out.at[target], give_sems.at[source, 1],
                   take_sems.at[target, 1], peer),
        )

    own = (
        pltpu.make_async_copy(sent_ref.at[me], rows.at[me], own_sems.at[0]),
        pltpu.make_async_copy(gates_ref.at[me], gates.at[me], own_sems.at[1]),
        pltpu.make_async_copy(outer_ref, outer, own_sems.at[2]),
    )
    own_back = (
        pltpu.make_async_copy(stage.at[me], back_out.at[me], own_sems.at[3]),
        pltpu.make_async_copy(extra_stage.at[me], extra_out.at[me], own_sems.at[4]),
    )
    for copy in own:
        copy.start()
    turns = turns_of(size)

    def send_rows(steps):
        for step in steps:
            peer = flip(me, step, size)
            for copy in forth(peer, me, peer):
                copy.start()

    send_rows(turns[2])
    send_rows(turns[0])

    begun = far_gate.shape[1]

    def home(c, group, first, count):
        return buf.at[c, pl.ds(group * share + first, count)]

    loads = [
        pltpu.make_async_copy(own_in, buf.at[0:2, pl.ds(0, share)], weight_sems.at[0]),
        pltpu.make_async_copy(own_down, home(2, 0, 0, share), weight_sems.at[1]),
    ]
    loads += [
        pltpu.make_async_copy(far_gate.at[i], home(0, 2 + i, 0, begun), weight_sems.at[2 + i])
        for i in range(2)
    ]
    near_copies = [
        remote_copy(own_in, buf.at[0:2, pl.ds(share, share)], shard_sems.at[0, 0, 0],
                    shard_sems.at[0, 0, 1], "wshard", near),
        remote_copy(own_down, home(2, 1, 0, share), shard_sems.at[0, 1, 0],
                    shard_sems.at[0, 1, 1], "wshard", near),
    ]
    rest = ((0, begun, share - begun), (1, 0, share), (2, 0, share))

    def far_copy(c):
        _, first, count = rest[c]
        source = own_down if c == 2 else own_in.at[c]
        return remote_copy(source.at[pl.ds(first, count)], home(c, 2, first, count),
                           shard_sems.at[1, c, 0], shard_sems.at[1, c, 1], "wshard", far)

    def onward_copy(c):
        _, first, count = rest[c]
        return remote_copy(home(c, 2, first, count), home(c, 3, first, count),
                           shard_sems.at[2, c, 0], shard_sems.at[2, c, 1], "wshard", near)

    far_copy(0).start()
    far_copy(1).start()
    for copy in loads + near_copies:
        copy.start()
    for copy in own:
        copy.wait()

    def hidden_part(pair, base):
        spot = pl.ds(pl.multiple_of(pair * both, both), both)
        two = pl.ds(2 * pair, 2)
        these = rows[two].reshape(both, width)
        outers = low_outer[spot, :]
        for first in range(0, part_size, chunk):
            last = min(first + chunk, part_size)
            part, lanes = slice(base + first, base + last), slice(first, last)
            gate, up = dot_nt(these, buf[0, part, :]), dot_nt(these, buf[1, part, :])
            act_grad = dot_nt(outers, buf[2, part, :])
            square = gate * gate
            inner = gate * (0.7978845608028654 + (0.7978845608028654 * 0.044715) * square)
            rise = 0.5 + 0.5 * jnp.tanh(inner)
            bent = gate * rise
            act[spot, lanes] = (bent * up).astype(BF16)
            slope = rise + bent * (1.0 - rise) * (
                2 * 0.7978845608028654 + (6 * 0.7978845608028654 * 0.044715) * square
            )
            low[0, spot, lanes] = (act_grad * up * slope).astype(BF16)
            low[1, spot, lanes] = (act_grad * bent).astype(BF16)
        whole = slice(base, base + part_size)
        result = dot_nn(act[spot, :], buf[2, whole, :])
        back = dot_nn(low[0, spot, :], buf[0, whole, :]) + dot_nn(low[1, spot, :], buf[1, whole, :])
        return spot, result, back

    def near_step(step, carry):
        pair = flip(my_pair, step, pairs)
        first = 2 * pair

        @pl.when(step == 1)
        def _():
            send_rows(turns[1])

        @pl.when(step == pairs // 2)
        def _():
            for c in range(2):
                far_copy(c).wait()
                onward_copy(c).start()
            far_copy(2).start()

        @pl.when(step == 0)
        def _():
            peer = flip(me, 1, size)
            for copy in forth(me, peer, peer):
                copy.wait_recv()

        @pl.when(step > 0)
        def _():
            for which in range(2):
                for copy in forth(me, first + which, first + which):
                    copy.wait_recv()

        for which in range(2):
            gate = column_of(gates[first + which, 0:1, :], capacity)
            spot = pl.ds(pl.multiple_of((first + which) * capacity, capacity), capacity)
            low_outer[spot, :] = (outer[first + which].astype(F32) * gate).astype(BF16)
        spot, result, back = hidden_part(pair, 0)
        made_sum[spot, :] = result
        back_sum[spot, :] = back
        return carry

    def sent_all(copies):
        for remote_one, copy in copies:
            if remote_one:
                copy.wait_send()
            else:
                copy.wait()

    def weight_grads(half):
        every = rows[...].reshape(size * capacity, width)
        outers = low_outer[...]
        count = 0
        base = half * part_size
        waiting = {}
        for c in range(3):
            left = act if c == 2 else low.at[c]
            for first in range(0, part_size, 2 * chunk):
                last = min(first + 2 * chunk, part_size)
                slot = count % 2
                sent_all(waiting.pop(slot, ()))
                piece = dot_tn(left[:, first:last], outers if c == 2 else every)
                grad_stage[slot, : last - first, :] = piece.astype(BF16)
                copies = []
                begin = base + first
                while begin < base + last:
                    group = begin // share
                    end = min(base + last, (group + 1) * share)
                    source = grad_stage.at[slot, pl.ds(begin - base - first, end - begin)]
                    spot = pl.ds(begin - group * share, end - begin)
                    sem = grad_sems.at[slot, len(copies)]
                    if group % 2:
                        target = moved_out.at[group // 2, c, spot]
                        copies.append((True, remote_copy(source, target, sem, moved_sem, "wshard", near)))
                    else:
                        target = grad_out.at[group // 2, c, spot]
                        copies.append((False, pltpu.make_async_copy(source, target, sem)))
                    begin = end
                for _, copy in copies:
                    copy.start()
                waiting[slot] = copies
                count += 1
        for copies in waiting.values():
            sent_all(copies)

    for copy in loads[:2]:
        copy.wait()
    for copy in near_copies:
        copy.wait_recv()
    lax.fori_loop(0, pairs, near_step, 0)
    weight_grads(0)

    def far_step(step, carry):
        pair = flip(my_pair, pairs - 1 - step, pairs)
        first = 2 * pair
        spot, result, back = hidden_part(pair, part_size)
        result = (made_sum[spot, :] + result).astype(BF16)
        back = (back_sum[spot, :] + back).astype(BF16)
        two = pl.ds(first, 2)
        made[two] = result.reshape(2, capacity, width)
        stage[two] = back.reshape(2, capacity, width)
        for which in range(2):
            grads = outer[first + which].astype(F32) * made[first + which].astype(F32)
            line = row_of(jnp.sum(grads, -1, keepdims=True), extra_stage.shape[2])
            extra_stage[first + which] = jnp.broadcast_to(line, extra_stage.shape[1:])
        pltpu.make_async_copy(made.at[two], made_out.at[two], save_sems.at[step]).start()

        @pl.when(step < pairs - 1)
        def _():
            for which in range(2):
                for copy in back_copies(first + which, me, first + which):
                    copy.start()

        @pl.when(step == pairs - 1)
        def _():
            peer = flip(me, 1, size)
            for copy in back_copies(peer, me, peer):
                copy.start()
            for copy in own_back:
                copy.start()

        return carry

    far_copy(2).wait()
    onward_copy(2).start()
    for copy in loads[2:]:
        copy.wait()
    for c in range(3):
        onward_copy(c).wait_recv()
    lax.fori_loop(0, pairs, far_step, 0)
    weight_grads(1)
    remote_copy(moved_out, moved_out, moved_sem, moved_sem, "wshard", near).wait_recv()

    corner = (pl.ds(0, share), pl.ds(0, width))
    rooms = ((low.at[0], act), (low.at[1], low_outer))
    pieces = [(g, c) for g in (1, 0) for c in range(3)]

    def fetch(i):
        slot = i % 2
        return [
            pltpu.make_async_copy(source.at[pieces[i]], room.at[corner], sum_sems.at[slot, k])
            for k, (source, room) in enumerate(zip((grad_out, moved_out), rooms[slot]))
        ]

    def put(i):
        slot = i % 2
        return pltpu.make_async_copy(
            rooms[slot][0].at[corner], grad_out.at[pieces[i]], sum_sems.at[slot, 2]
        )

    for i in range(2):
        for copy in fetch(i):
            copy.start()
    for i in range(len(pieces)):
        for copy in fetch(i):
            copy.wait()
        one, other = rooms[i % 2]

        def add_rows(block, carry):
            spot = (pl.ds(pl.multiple_of(block * 64, 64), 64), slice(0, width))
            one[spot] = (one[spot].astype(F32) + other[spot].astype(F32)).astype(BF16)
            return carry

        lax.fori_loop(0, share // 64, add_rows, 0)
        put(i).start()
        if i + 2 < len(pieces):
            put(i).wait()
            for copy in fetch(i + 2):
                copy.start()
    for i in range(len(pieces) - 2, len(pieces)):
        put(i).wait()
    for copy in own_back:
        copy.wait()
    for copy in near_copies:
        copy.wait_send()
    for c in range(3):
        onward_copy(c).wait_send()
    for step in range(pairs):
        two = pl.ds(2 * flip(my_pair, pairs - 1 - step, pairs), 2)
        pltpu.make_async_copy(made.at[two], made_out.at[two], save_sems.at[step]).wait()
    for step in range(1, size):
        peer = flip(me, step, size)
        for copy in forth(peer, me, peer):
            copy.wait_send()
        for copy in back_copies(peer, me, peer):
            copy.wait_send()
        for copy in back_copies(me, peer, peer):
            copy.wait_recv()


def moe(sent, gates, outer, own_in, own_down, far_gate, chunk=256):
    size, capacity, width = sent.shape
    groups = lax.axis_size("wshard")
    share = own_down.shape[0]
    part = share * groups // 2
    total = size * capacity
    extra = gates.shape[1:]
    dma = pltpu.SemaphoreType.DMA
    result = pl.pallas_call(
        functools.partial(moe_body, size, groups, chunk),
        out_shape=(
            shape_of((size, capacity, width), BF16),
            shape_of((size, *extra), F32),
            shape_of((size, capacity, width), BF16),
        )
        + (shape_of((2, 3, share, width), BF16),) * 2,
        in_specs=[ANY] * 6,
        out_specs=(ANY,) * 5,
        scratch_shapes=[
            pltpu.VMEM((3, share * groups, width), BF16),
            pltpu.VMEM((size, capacity, width), BF16),
            pltpu.VMEM((size, *extra), F32),
            pltpu.VMEM((size, capacity, width), BF16),
            pltpu.VMEM((total, width), BF16),
            pltpu.VMEM((total, width), F32),
            pltpu.VMEM((total, width), F32),
            pltpu.VMEM((total, part), BF16),
            pltpu.VMEM((2, total, part), BF16),
            pltpu.VMEM((size, capacity, width), BF16),
            pltpu.VMEM((size, *extra), F32),
            pltpu.VMEM((size, capacity, width), BF16),
            pltpu.VMEM((2, 2 * chunk, width), BF16),
            dma((4,)),
            dma((3, 3, 2)),
            dma((size, 2)),
            dma((size, 2)),
            dma((size, 2)),
            dma((size, 2)),
            dma((5,)),
            dma((size // 2,)),
            dma((2, 3)),
            dma,
            dma((2, 3)),
        ],
        cost_estimate=pl.CostEstimate(flops=LIGHT, bytes_accessed=LIGHT, transcendentals=0),
        compiler_params=pltpu.CompilerParams(
            collective_id=0, has_side_effects=True, vmem_limit_bytes=66_000_000
        ),
        name="experts",
    )(sent, gates, outer, own_in, own_down, far_gate)
    return result[:4]


def expert_body(groups, chunk, rows_ref, outer_ref, gate_ref, *refs):
    in_refs, down_refs = refs[:groups], refs[groups : 2 * groups]
    made_ref, back_ref, outer_out_ref, gate_grad_ref = refs[2 * groups : 2 * groups + 4]
    act_ref, low_ref, buf_ref, sems = refs[2 * groups + 4 :]
    share = down_refs[0].shape[0]
    hidden = share * groups

    def copies(group):
        spot = pl.ds(group * share, share)
        return (
            pltpu.make_async_copy(in_refs[group], buf_ref.at[0:2, spot], sems.at[2 * group]),
            pltpu.make_async_copy(down_refs[group], buf_ref.at[2, spot], sems.at[2 * group + 1]),
        )

    @pl.when(pl.program_id(0) == 0)
    def _():
        for group in range(groups):
            for copy in copies(group):
                copy.start()

    rows = rows_ref[...]
    low_outer = (outer_ref[...].astype(F32) * gate_ref[...]).astype(BF16)
    outer_out_ref[...] = low_outer

    @pl.when(pl.program_id(0) == 0)
    def _():
        for group in range(groups):
            for copy in copies(group):
                copy.wait()

    for first in range(0, hidden, chunk):
        part = slice(first, first + chunk)
        gate, up = dot_nt(rows, buf_ref[0, part, :]), dot_nt(rows, buf_ref[1, part, :])
        act_grad = dot_nt(low_outer, buf_ref[2, part, :])
        square = gate * gate
        inner = gate * (0.7978845608028654 + (0.7978845608028654 * 0.044715) * square)
        rise = 0.5 + 0.5 * jnp.tanh(inner)
        bent = gate * rise
        act_ref[:, part] = (bent * up).astype(BF16)
        slope = rise + bent * (1.0 - rise) * (
            2 * 0.7978845608028654 + (6 * 0.7978845608028654 * 0.044715) * square
        )
        low_ref[0, :, part] = (act_grad * up * slope).astype(BF16)
        low_ref[1, :, part] = (act_grad * bent).astype(BF16)
    made = dot_nn(act_ref[...], buf_ref[2]).astype(BF16)
    made_ref[...] = made
    back = dot_nn(low_ref[0], buf_ref[0]) + dot_nn(low_ref[1], buf_ref[1])
    back_ref[...] = back.astype(BF16)
    gate_grad_ref[...] = jnp.sum(
        outer_ref[...].astype(F32) * made.astype(F32), -1, keepdims=True
    )


def experts_pass(rows, outer, gate_column, in_weights, down_weights, block=320, chunk=256):
    total, width = rows.shape
    groups = len(in_weights)
    hidden = down_weights[0].shape[0] * groups
    row_spec = pl.BlockSpec((block, width), lambda i: (i, 0))
    column = pl.BlockSpec((block, 1), lambda i: (i, 0))
    wide = pl.BlockSpec((block, hidden), lambda i: (i, 0))
    both = pl.BlockSpec((2, block, hidden), lambda i: (0, i, 0))
    return pl.pallas_call(
        functools.partial(expert_body, groups, chunk),
        grid=(total // block,),
        out_shape=(
            shape_of((total, width), BF16),
            shape_of((total, width), BF16),
            shape_of((total, width), BF16),
            shape_of((total, 1), F32),
            shape_of((total, hidden), BF16),
            shape_of((2, total, hidden), BF16),
        ),
        in_specs=[row_spec, row_spec, column] + [ANY] * (2 * groups),
        out_specs=(row_spec, row_spec, row_spec, column, wide, both),
        scratch_shapes=[
            pltpu.VMEM((3, hidden, width), BF16),
            pltpu.SemaphoreType.DMA((2 * groups,)),
        ],
        cost_estimate=pl.CostEstimate(flops=LIGHT, bytes_accessed=LIGHT, transcendentals=0),
        name="experts",
    )(rows, outer, gate_column, *in_weights, *down_weights)


def moe_plain(sent, gates, outer, own_in, own_down, far_gate):
    in_weights, down_weights = [own_in], [own_down]
    for bit in (1, 2):
        in_weights += [swap(w, "wshard", bit) for w in in_weights]
        down_weights += [swap(w, "wshard", bit) for w in down_weights]
    size, capacity, width = sent.shape
    total = size * capacity
    rows = exchange(sent.reshape(total, width), "dp").reshape(total, width)
    gate_column = lax.all_to_all(gates, "dp", 0, 0, tiled=True)[:, 0, :capacity].reshape(total, 1)
    made, back, outer_low, gate_grads, act, low = experts_pass(
        rows, outer.reshape(total, width), gate_column, in_weights, down_weights
    )
    extra = jnp.pad(gate_grads.reshape(size, 1, capacity), ((0, 0), (0, EXTRA - 1), (0, 0)))
    extra = lax.all_to_all(extra, "dp", 0, 0, tiled=True)
    share = down_weights[0].shape[0]
    grads = []
    for group in range(len(in_weights)):
        part = slice(group * share, (group + 1) * share)
        pieces = [dot_tn(low[c, :, part], rows) for c in range(2)]
        grads.append(jnp.stack(pieces + [dot_tn(act[:, part], outer_low)]).astype(BF16))
    shape = (size, capacity, width)
    moved = jnp.stack([swap(grads[g], "wshard", 1) for g in (1, 3)])
    sums = (jnp.stack(grads[::2]).astype(F32) + moved.astype(F32)).astype(BF16)
    return exchange(back, "dp"), extra, made.reshape(shape), sums


def rear_body(
    size, groups, head_size, remote_made, span_ref, gain_ref, diag_ref, ones_ref, router_ref, col_ref, gate_ref,
    extra_ref, tok_hbm, cot_hbm, hidden_hbm, norm_hbm, mixed_hbm, rows_hbm, made_hbm, outw_hbm,
    qkvw_hbm, qkv_hbm, far_hbm,
    output_ref, grad_ref, gains_out, table_out, router_out, sum_out, sum_out_two, far_out,
    tok, cot, hidden, norm, mixed, rows, made, outw, qkvw, qkv, norm_t, mask, grad_hidden,
    grads, probs_ref, scores_ref, diag_sums, wo, wo_got, wg, wg_got, total,
    total_got, sum_ref, early_ref, early_got, late_ref, late_got,
    load_sems, weight_sems, made_send, made_got, part_sems, total_sems, small_sems, far_sems,
):
    me, place = lax.axis_index("dp"), lax.axis_index("wshard")
    near, far = flip(place, 1, groups), flip(place, 2, groups)
    dp_bits, shard_bits = bits_below(size), bits_below(groups)
    peers = [("dp", flip(me, step, size)) for step in range(1, size)]
    greet(peers + [("wshard", near), ("wshard", far)])
    count, width = tok.shape
    blocks = count // TILE
    experts = size
    capacity = rows.shape[0] // experts
    cols = outw.shape[2]
    two_heads = 2 * head_size
    branch, mixgrad, norm_grad = cot, norm, hidden

    loads = [
        pltpu.make_async_copy(source, target, load_sems.at[i])
        for i, (source, target) in enumerate(
            (
                (rows_hbm, rows), (norm_hbm, norm), (hidden_hbm, hidden), (cot_hbm, cot),
                (mixed_hbm, mixed), (outw_hbm, outw), (tok_hbm, tok), (qkv_hbm, qkv),
                (made_hbm.at[me], made.at[me]) if remote_made else (made_hbm, rows),
            )
        )
    ]
    for copy in loads[: 9 if remote_made else 8]:
        copy.start()

    def far_copy(piece):
        return remote_copy(
            far_hbm.at[1, piece], far_out.at[piece], far_sems.at[piece, 0], far_sems.at[piece, 1],
            "wshard", far,
        )

    far_copy(0).start()

    def weight_load(step):
        slot = lax.rem(step, 2)
        return pltpu.make_async_copy(
            qkvw_hbm.at[groups - 1 - step], qkvw.at[slot], weight_sems.at[slot]
        )

    hidden_again = pltpu.make_async_copy(hidden_hbm, hidden, load_sems.at[9])

    def made_copy(source, target, peer):
        return remote_copy(
            made_hbm.at[source], made.at[target], made_send.at[source], made_got.at[target], "dp",
            peer,
        )

    turns = turns_of(size)

    def send_made(turn):
        if remote_made:
            for step in turns[turn]:
                peer = flip(me, step, size)
                made_copy(peer, me, peer).start()

    send_made(0)

    exchanges = [("wshard", place, bit, groups) for bit in shard_bits]
    exchanges += [("dp", me, bit, size) for bit in dp_bits]

    def small_copy(kind, ref, got, step):
        axis, index, bit, length = exchanges[step]
        return remote_copy(
            ref, got.at[step], small_sems.at[kind, step, 0], small_sems.at[kind, step, 1], axis,
            flip(index, bit, length),
        )

    def small_step(kind, ref, got, step):
        now, before = step % 2, (step + 1) % 2
        if step > 0:
            small_copy(kind, ref.at[before], got, step - 1).wait()
            ref[now] = ref[before] + got[step - 1]
        if step < len(exchanges):
            small_copy(kind, ref.at[now], got, step).start()

    slots = [col_ref[:, k : k + 1] for k in range(2)]
    gates = [gate_ref[:, k : k + 1] for k in range(2)]
    lane = iota((count, extra_ref.shape[2]), 1)
    picked = [0.0, 0.0]
    for copy in loads[:1]:
        copy.wait()
    grads_in = 0.0
    for expert in range(experts):
        label = jnp.where(lane < capacity, lane + expert * capacity, -1)
        for k in range(2):
            picked[k] = picked[k] + jnp.where(label == slots[k], extra_ref[expert, 0:1, :], 0.0)
    gate_grads = [jnp.sum(p, -1, keepdims=True) for p in picked]
    mean = gates[0] * gate_grads[0] + gates[1] * gate_grads[1]
    lane = iota((count, 3 * experts), 1)
    part = (lane >= experts).astype(I32) + (lane >= 2 * experts).astype(I32)
    label = lane - part * experts
    logit_grads = 0.0
    for k in range(2):
        own = (label * capacity <= slots[k]) & (slots[k] < (label + 1) * capacity)
        logit_grads = logit_grads + jnp.where(own, gates[k] * (gate_grads[k] - mean), 0.0)
    high, middle, low = split_three(logit_grads)
    split = jnp.where(part == 0, high, jnp.where(part == 1, middle, low)).astype(BF16)
    hits = [onehot_columns(slots[k], 0, experts * capacity) for k in range(2)]
    hits = (hits[0] | hits[1]).astype(F32).astype(BF16)
    for copy in loads[1:4]:
        copy.wait()
    normed_grad = dot_nn(hits, rows[...])
    normed_grad = normed_grad + dot_nn(split, router_ref[...])
    router_grad = dot_tn(split, norm[...])
    early_ref[0, :experts, :] = (
        router_grad[:experts] + router_grad[experts : 2 * experts] + router_grad[2 * experts :]
    )
    unit, recip = unit_norm(hidden[...])
    early_ref[0, experts:, :] = jnp.broadcast_to(
        jnp.sum(normed_grad * unit, 0, keepdims=True), (EXTRA, width)
    )
    small_step(0, early_ref, early_got, 0)
    scaled = normed_grad * gain_ref[1:2, :]
    back = recip * (scaled - unit * jnp.mean(scaled * unit, -1, keepdims=True))
    grad_hidden[...] = cot[...].astype(F32) + back
    branch[...] = grad_hidden[...].astype(BF16)
    for copy in loads[4:6]:
        copy.wait()
    mixed_t = mixed[...].T
    result = 0.0

    def part_copy(item, source, target, kind, axis, peer):
        return remote_copy(
            source, target, part_sems.at[item, kind, 0], part_sems.at[item, kind, 1], axis, peer
        )

    def out_copy(kind):
        return part_copy(
            0, wo.at[(3, 1, 2)[kind]], wo_got.at[kind], kind, "wshard", far if kind == 2 else near
        )

    def qkv_copy(kind):
        return part_copy(
            1, wg.at[(2, 0, 1)[kind]], wg_got.at[kind], kind, "wshard", far if kind == 2 else near
        )

    for group in reversed(range(groups)):
        lanes = pl.ds(pl.multiple_of(flip(place, group, groups) * cols, cols), cols)
        piece = branch[:, lanes]
        result = result + dot_nt(piece, outw[group])
        wo[group] = dot_nn(mixed_t, piece).astype(BF16)
        if group == 3:
            out_copy(0).start()
        if group == 1:
            out_copy(1).start()
    mixgrad[...] = result.astype(BF16)
    for copy in loads[6:8]:
        copy.wait()
    weight_load(0).start()
    unit, _ = unit_norm(tok[...].astype(F32))
    norm_t[...] = (unit * gain_ref[0:1, :]).astype(BF16).T
    fill_mask(mask, span_ref[0])
    norm_grad[...] = jnp.zeros_like(norm_grad)

    def attend_group(step):
        group = groups - 1 - step
        slot = lax.rem(step, 2)
        weight_load(step).wait()

        @pl.when(step < groups - 1)
        def _():
            weight_load(step + 1).start()

        owner = flip(place, group, groups)
        heads = cols // head_size

        def pair(p, carry):
            offset = pl.multiple_of(p * two_heads, two_heads)
            lanes = pl.ds(offset, two_heads)
            query, keys, value = (qkv[group, c, :, lanes] for c in range(3))
            outer = mixgrad[:, pl.ds(pl.multiple_of(owner * cols + offset, two_heads), two_heads)]
            query_sum, key_sum, value_sum = [None] * blocks, None, None
            for which in range(2):
                head = owner * heads + 2 * p + which
                own = head_lanes(which, head_size)
                own_query, own_key, own_outer = query * own, keys * own, outer * own
                shrunk = own_query * 0.125
                tiles, far_bias = bias_tiles(diag_ref[pl.ds(head, 1), :])
                near_sums, far_sums = [None] * 3, [None] * 2
                for block in range(blocks):
                    piece = slice(block * TILE, (block + 1) * TILE)
                    probs = softmax_tiles(
                        score_tiles(block, shrunk[piece], keys, tiles, far_bias, mask)
                    )
                    prob_grads = dot_nt(own_outer[piece], value)
                    prob_grads = [prob_grads[:, j * TILE : (j + 1) * TILE] for j in range(blocks)]
                    delta = functools.reduce(jnp.add, [a * b for a, b in zip(probs, prob_grads)])
                    delta = jnp.sum(delta, -1, keepdims=True)
                    lows = [(a * (b - delta)).astype(BF16) for a, b in zip(probs, prob_grads)]
                    for other in range(blocks):
                        step = block - other
                        wide = lows[other].astype(F32)
                        if abs(step) >= 2:
                            side = 0 if step > 0 else 1
                            old = far_sums[side]
                            far_sums[side] = wide if old is None else old + wide
                        else:
                            old = near_sums[step + 1]
                            near_sums[step + 1] = wide if old is None else old + wide
                    probs_ref[which, piece, :] = jnp.concatenate([t.astype(BF16) for t in probs], 1)
                    lows = jnp.concatenate(lows, 1)
                    scores_ref[which, piece, :] = lows
                    more = dot_nn(lows, own_key)
                    query_sum[block] = more if which == 0 else query_sum[block] + more
                more = dot_tn(scores_ref[which], own_query)
                key_sum = more if which == 0 else key_sum + more
                more = dot_tn(probs_ref[which], own_outer)
                value_sum = more if which == 0 else value_sum + more
                for step in range(3):
                    wide = jnp.concatenate([near_sums[step], jnp.zeros((TILE, TILE), F32)], 1)
                    half = TILE // 2
                    while half:
                        turned = pltpu.roll(wide[half:], 2 * TILE - half, 1)
                        wide = wide[:half] + turned
                        half //= 2
                    for side in range(2):
                        spot = 2 * step + side
                        diag_sums[head, spot : spot + 1, :] = wide[:, TILE * side : TILE * (side + 1)]
                for side in range(2):
                    diag_sums[head, 6 + side : 7 + side, :] = jnp.sum(far_sums[side], 0, keepdims=True)
            for block in range(blocks):
                piece = slice(block * TILE, (block + 1) * TILE)
                grads[0, piece, lanes] = (query_sum[block] * 0.125).astype(BF16)
            grads[1, :, lanes] = (key_sum * 0.125).astype(BF16)
            grads[2, :, lanes] = value_sum.astype(BF16)
            return carry

        lax.fori_loop(0, cols // two_heads, pair, 0)
        for c in range(3):
            weight_grad = dot_nn(norm_t[...], grads[c]).astype(BF16)

            @pl.when(group > 0)
            def _():
                wg[group - 1, c] = weight_grad

            @pl.when(group == 0)
            def _():
                total[c * width : (c + 1) * width, :] = weight_grad

            norm_grad[...] += dot_nt(grads[c], qkvw[slot, c])

    def add_into(target, *others):
        for first in range(0, target.shape[0], 256):
            spot = slice(first, first + 256)
            value = target[spot].astype(F32)
            for other in others:
                value = value + other[spot].astype(F32)
            target[spot] = value.astype(BF16)

    third = outw.shape[1]
    parts = 4
    length = total.shape[0] // parts
    stages = len(dp_bits)

    def bit_of(step):
        return lax.rem(lax.div(me, dp_bits[step]), 2)

    def segment(part, step):
        first, size_of = part * length, length
        for s in range(step):
            size_of //= 2
            first = first + bit_of(s) * size_of
        return first, size_of

    def halving(part, step):
        first, size_of = segment(part, step)
        half = size_of // 2
        away = pl.multiple_of(first + (1 - bit_of(step)) * half, half)
        return remote_copy(
            total.at[pl.ds(away, half)],
            total_got.at[pl.ds(part * length + length - size_of, half)],
            total_sems.at[part, 0, step, 0], total_sems.at[part, 0, step, 1], "dp",
            flip(me, dp_bits[step], size),
        )

    def add_half(part, step):
        first, half = segment(part, step + 1)
        first = pl.multiple_of(first, half)
        got = part * length + length - 2 * half
        value = total[pl.ds(first, half), :].astype(F32) + total_got[got : got + half, :].astype(F32)
        total[pl.ds(first, half), :] = value.astype(BF16)
        if step == stages - 1:
            sum_ref[pl.ds(first, half), :] = value.astype(BF16)

    def doubling(part, step):
        first, size_of = segment(part, step + 1)
        spot = pl.ds(pl.multiple_of(first, size_of), size_of)
        return remote_copy(
            sum_ref.at[spot], sum_ref.at[spot],
            total_sems.at[part, 1, step, 0], total_sems.at[part, 1, step, 1], "dp",
            flip(me, dp_bits[step], size),
        )

    def sum_stage(part, stage):
        if 0 < stage <= stages:
            halving(part, stage - 1).wait()
            add_half(part, stage - 1)
        elif stage > stages:
            doubling(part, 2 * stages - stage).wait()
        if stage < stages:
            halving(part, stage).start()
        elif stage < 2 * stages:
            doubling(part, 2 * stages - 1 - stage).start()

    def group_step(step, carry):
        @pl.when(step == groups - 1)
        def _():
            far_copy(1).start()

        attend_group(step)

        @pl.when(step == 0)
        def _():
            send_made(1)
            qkv_copy(0).start()
            small_step(0, early_ref, early_got, 1)
            out_copy(0).wait_recv()
            add_into(wo.at[2], wo_got.at[0])
            out_copy(2).start()

        @pl.when(step == 1)
        def _():
            send_made(2)
            qkv_copy(0).wait_recv()
            for c in range(3):
                add_into(wg.at[1, c], wg_got.at[0, c])
            qkv_copy(2).start()
            small_step(0, early_ref, early_got, 2)

        @pl.when(step == 2)
        def _():
            qkv_copy(1).start()
            small_step(0, early_ref, early_got, 3)
            out_copy(1).wait_recv()
            out_copy(2).wait_recv()
            add_into(wo.at[0], wo_got.at[1], wo_got.at[2])
            total[3 * third :, :] = wo[0]
            sum_stage(3, 0)

        return carry

    lax.fori_loop(0, groups, group_step, 0)
    sum_stage(3, 1)

    small_step(0, early_ref, early_got, 4)
    unit, recip = unit_norm(tok[...].astype(F32))
    gain_grad = jnp.sum(norm_grad[...] * unit, 0, keepdims=True)
    table_grad = 0.0
    for k in range(8):
        for piece in split_three(diag_sums[:, k, :]):
            table_grad = table_grad + dot_nt(piece.astype(BF16), ones_ref[:, k * TILE : (k + 1) * TILE])
    late_ref[0] = jnp.zeros(late_ref.shape[1:], F32)
    for k in range(width // TILE):
        late_ref[0, k : k + 1, :] = gain_grad[:, k * TILE : (k + 1) * TILE]
    heads, buckets = table_grad.shape
    late_ref[0, 8 : 8 + heads, :buckets] = table_grad
    small_step(1, late_ref, late_got, 0)

    qkv_copy(1).wait_recv()
    qkv_copy(2).wait()
    def finish_tokens():
        scaled = norm_grad[...] * gain_ref[0:1, :]
        back = recip * (scaled - unit * jnp.mean(scaled * unit, -1, keepdims=True))
        grad_ref[...] = (grad_hidden[...] + back).astype(BF16)
        hidden_again.start()
        if not remote_made:
            loads[8].start()

    def finish_output():
        loads[8].wait()
        hidden_again.wait()
        if remote_made:
            for _, peer in peers:
                made_copy(me, peer, peer).wait_recv()
        values = made[...].reshape(experts * capacity, width) if remote_made else rows[...]
        for first in range(0, count, 256):
            spot = slice(first, first + 256)
            value = hidden[spot, :]
            for k in range(2):
                hit = onehot_columns(slots[k][spot], 0, experts * capacity)
                value = value + gates[k][spot] * dot_nn(hit.astype(F32).astype(BF16), values)
            output_ref[spot, :] = value.astype(BF16)

    rest_early = list(range(groups + 1, len(exchanges) + 1))
    rest_late = list(range(1, len(exchanges) + 1))

    def next_small():
        if rest_early:
            small_step(0, early_ref, early_got, rest_early.pop(0))
        if rest_late:
            small_step(1, late_ref, late_got, rest_late.pop(0))

    for time in range(3 + 2 * stages):
        for part in range(min(3, time + 1)):
            if time == part:
                add_into(
                    total.at[part * third : (part + 1) * third], wg_got.at[1, part], wg_got.at[2, part]
                )
            if time - part <= 2 * stages:
                sum_stage(part, time - part)
        if time + 2 <= 2 * stages:
            sum_stage(3, time + 2)
        if time == 0:
            finish_tokens()
        elif time == 1:
            finish_output()
        elif time == 2:
            far_copy(1).wait()
            far_copy(2).start()
        next_small()
    while rest_early or rest_late:
        next_small()
    saves = [
        pltpu.make_async_copy(sum_ref.at[pl.ds(0, 3 * third)], sum_out, load_sems.at[10]),
        pltpu.make_async_copy(sum_ref.at[pl.ds(3 * third, third)], sum_out_two, load_sems.at[11]),
    ]
    for copy in saves:
        copy.start()
    last = len(exchanges) % 2
    router_out[...] = early_ref[last, :experts, :]
    gains_out[1:2, :] = early_ref[last, experts : experts + 1, :]
    for k in range(width // TILE):
        gains_out[0:1, k * TILE : (k + 1) * TILE] = late_ref[last, k : k + 1, :]
    table_out[...] = late_ref[last, 8 : 8 + heads, :buckets]
    for copy in saves:
        copy.wait()
    far_copy(0).wait()
    far_copy(2).wait()
    if remote_made:
        for _, peer in peers:
            made_copy(peer, me, peer).wait_send()
    for kind in range(3):
        out_copy(kind).wait_send()
    for kind in range(2):
        qkv_copy(kind).wait_send()


def bits_below(size):
    return [1 << b for b in range(size.bit_length() - 1)]


def rear(
    span, gains, diag, ones, router_t3, slots_col, gates, extra, tokens, cotangent, hidden, normed,
    mixed, rows, made, out_weights, qkv_weights, qkv, expert_sums, head_size,
):
    count, width = tokens.shape
    size, groups = lax.axis_size("dp"), lax.axis_size("wshard")
    heads, buckets = width // head_size, ones.shape[0]
    experts = router_t3.shape[0] // 3
    cols = out_weights.shape[2]
    exchanges = len(bits_below(size)) + len(bits_below(groups))
    dma = pltpu.SemaphoreType.DMA
    wide, small = (count, width), (experts + EXTRA, width)
    late = (8 + heads, TILE)
    total = (4 * width, cols)
    vmem = pltpu.VMEM
    return pl.pallas_call(
        functools.partial(rear_body, size, groups, head_size, made.ndim == 3),
        out_shape=(
            shape_of(wide, BF16),
            shape_of(wide, BF16),
            shape_of((2, width), F32),
            shape_of((heads, buckets), F32),
            shape_of((experts, width), F32),
            shape_of((3 * width, cols), BF16),
            shape_of((width, cols), BF16),
            shape_of(expert_sums.shape[1:], BF16),
        ),
        in_specs=[SMEM] + [VMEM] * 7 + [ANY] * 11,
        out_specs=(VMEM,) * 5 + (ANY,) * 3,
        scratch_shapes=[
            vmem(wide, BF16),
            vmem(wide, BF16),
            vmem(wide, F32),
            vmem(wide, BF16),
            vmem(wide, BF16),
            vmem(rows.shape, BF16),
            vmem(made.shape if made.ndim == 3 else (16, TILE), BF16),
            vmem(out_weights.shape, BF16),
            vmem((2, *qkv_weights.shape[1:]), BF16),
            vmem(qkv.shape, BF16),
            vmem((width, count), BF16),
            vmem((count, count), F32),
            vmem(wide, F32),
            vmem((3, count, cols), BF16),
            vmem((2, count, count), BF16),
            vmem((2, count, count), BF16),
            vmem((heads, 8, TILE), F32),
            vmem((groups, width, cols), BF16),
            vmem((3, width, cols), BF16),
            vmem((groups - 1, 3, width, cols), BF16),
            vmem((3, 3, width, cols), BF16),
            vmem(total, BF16),
            vmem(total, BF16),
            vmem(total, BF16),
            vmem((2, *small), F32),
            vmem((exchanges, *small), F32),
            vmem((2, *late), F32),
            vmem((exchanges, *late), F32),
            dma((12,)),
            dma((2,)),
            dma((size,)),
            dma((size,)),
            dma((2, 3, 2)),
            dma((4, 2, len(bits_below(size)), 2)),
            dma((2, exchanges, 2)),
            dma((3, 2)),
        ],
        cost_estimate=pl.CostEstimate(flops=LIGHT, bytes_accessed=LIGHT, transcendentals=0),
        compiler_params=pltpu.CompilerParams(
            collective_id=2, has_side_effects=True, vmem_limit_bytes=66_000_000
        ),
        name="rear",
    )(
        span, gains, diag, ones, router_t3, slots_col, gates, extra, tokens, cotangent, hidden,
        normed, mixed, rows, made, out_weights, qkv_weights, qkv, expert_sums,
    )


def swap(value, axis, bit):
    size = lax.axis_size(axis)
    return lax.ppermute(value, axis, [(i, i ^ bit) for i in range(size)])


def bits_of(axis):
    size = lax.axis_size(axis)
    return [1 << b for b in range(size.bit_length() - 1)]


def after(value, *others):
    return lax.optimization_barrier((value, *others))[0]


def exchange(rows, axis):
    size = lax.axis_size(axis)
    total, width = rows.shape
    blocks = rows.reshape(size, total // size, width)
    return lax.all_to_all(blocks, axis, 0, 0, tiled=True)


def per_device(
    tokens,
    cotangent,
    span_starts,
    routes,
    norm_gains,
    bias_table,
    router,
    attn_qkv,
    attn_out,
    expert_in,
    expert_down,
):
    assert span_starts.shape[0] == 1
    tok_count, model_width = tokens.shape
    buckets, head_count = bias_table.shape
    head_size = model_width // head_count
    experts = router.shape[1]
    capacity = (10 * tok_count + 4 * experts - 1) // (4 * experts)
    total = experts * capacity
    place = lax.axis_index("wshard")
    where = jnp.stack([place.astype(I32), span_starts[0]])
    diag = jnp.asarray(diagonal_ones(buckets))
    diag_bias = jnp.dot(bias_table.T, diag, precision=PRECISE)
    router_t = router.T
    expert_in = jnp.swapaxes(expert_in[0], 1, 2)
    expert_down = expert_down[0]

    shards = (attn_qkv, attn_out, expert_in)
    (
        slots_col, gates, sent_gates, qkv_all, out_all, qkv, mixed, hidden, normed_two, sent,
        outer_rows, far_gate,
    ) = front(
        span_starts, routes, norm_gains, diag_bias, router_t, tokens, cotangent, shards, head_size,
        capacity,
    )
    groups = out_all.shape[0]
    through = moe if capacity % 16 == 0 else moe_plain
    back_rows, back_extra, made, expert_grads = through(
        sent, sent_gates, outer_rows, expert_in, expert_down, far_gate
    )
    if through is moe_plain:
        made = exchange(made.reshape(total, model_width), "dp").reshape(total, model_width)

    output, grad_tokens, grad_gains, table_grad, router_grad, qkv_sum, out_sum, far_got = rear(
        span_starts, norm_gains, diag_bias, diag.astype(BF16), jnp.concatenate([router_t] * 3, 0),
        slots_col, gates, back_extra, tokens, cotangent, hidden, normed_two,
        mixed, back_rows.reshape(total, model_width), made, out_all, qkv_all, qkv, expert_grads,
        head_size,
    )

    def expert_sum(part):
        return expert_grads[0, part].astype(F32) + far_got[part].astype(F32)

    grad_expert_in = jnp.swapaxes(expert_sum(slice(0, 2)), 1, 2)[None]
    grad_expert_down = expert_sum(2)[None]
    cols = out_all.shape[2]
    return (
        output,
        grad_tokens,
        grad_gains,
        table_grad.T,
        router_grad.T,
        qkv_sum.astype(F32).reshape(3, model_width, cols),
        out_sum.astype(F32),
        grad_expert_in,
        grad_expert_down,
    )


def solution(mesh):
    return jax.shard_map(
        per_device,
        mesh=mesh,
        in_specs=(
            P(("dp", "wshard"), None),
            P(("dp", "wshard"), None),
            P(("dp", "wshard")),
            P(("dp", "wshard"), None),
            P(),
            P(),
            P(),
            P(None, None, "wshard"),
            P(None, "wshard"),
            P("dp", None, None, "wshard"),
            P("dp", "wshard", None),
        ),
        out_specs=(
            P(("dp", "wshard"), None),
            P(("dp", "wshard"), None),
            P(),
            P(),
            P(),
            P(None, None, "wshard"),
            P(None, "wshard"),
            P("dp", None, None, "wshard"),
            P("dp", "wshard", None),
        ),
        check_vma=False,
    )
```

```python
import functools

import jax
import jax.numpy as jnp
import numpy as np
from jax import lax
from jax.experimental import pallas as pl
from jax.experimental.pallas import tpu as pltpu
from jax.sharding import PartitionSpec as P

PIC = 256
PRECISE = lax.Precision.HIGHEST
EPSILON = 1e-06
MASKED_SCORE = -1e30
BUCKET_EDGES = (8, 11, 16, 23, 32, 45, 64, 91)
TILE = 128
F32 = jnp.float32
BF16 = jnp.bfloat16
I32 = jnp.int32
VMEM = pl.BlockSpec(memory_space=pltpu.VMEM)
SMEM = pl.BlockSpec(memory_space=pltpu.SMEM)
ANY = pl.BlockSpec(memory_space=pl.ANY)
LIGHT = 1024
EXTRA = 8


def dot_nn(a, b):
    return lax.dot_general(a, b, (((1,), (0,)), ((), ())), preferred_element_type=F32)


def dot_nt(a, b):
    return lax.dot_general(a, b, (((1,), (1,)), ((), ())), preferred_element_type=F32)


def dot_tn(a, b):
    return lax.dot_general(a, b, (((0,), (0,)), ((), ())), preferred_element_type=F32)


def iota(shape, axis):
    return lax.broadcasted_iota(I32, shape, axis)


def shape_of(shape, dtype):
    return jax.ShapeDtypeStruct(shape, dtype)


def call(body, out, args, specs, scratch=(), name=None):
    return pl.pallas_call(
        body,
        out_shape=out,
        in_specs=specs,
        out_specs=jax.tree.map(lambda _: VMEM, out),
        scratch_shapes=list(scratch),
        cost_estimate=pl.CostEstimate(flops=LIGHT, bytes_accessed=LIGHT, transcendentals=0),
        name=name,
    )(*args)


def bucket_of(offset):
    magnitude = np.abs(offset)
    coarse = 7 + sum((magnitude >= bound).astype(np.int32) for bound in BUCKET_EDGES)
    return np.where(magnitude < 8, magnitude, coarse) + 16 * (offset < 0)


def diagonal_ones(bucket_count):
    column = np.arange(2 * TILE)
    signed = np.where(column < TILE, column, column - 2 * TILE)
    offsets = np.concatenate([TILE * step - signed for step in (-1, 0, 1)])
    used = np.tile(column != TILE, 3)
    hit = bucket_of(offsets)[None, :] == np.arange(bucket_count)[:, None]
    near = (hit & used[None, :]).astype(np.float32)
    far = np.zeros((bucket_count, 2 * TILE), np.float32)
    far[bucket_of(np.array(TILE)), :TILE] = 1
    far[bucket_of(np.array(-TILE)), TILE:] = 1
    return np.concatenate([near, far], 1)


def onehot_rows(first, count, slots_row):
    index = iota((count, slots_row.shape[1]), 0) + first
    hit = (index == slots_row[0:1, :]) | (index == slots_row[1:2, :])
    return hit.astype(F32).astype(BF16)


def onehot_columns(slots_column, first, count):
    index = iota((slots_column.shape[0], count), 1) + first
    return index == slots_column


def route_slots(experts, capacity, routes):
    tokens = routes.shape[1]
    label = iota((experts, tokens), 0)
    hits = ((routes[0:1] == label) | (routes[1:2] == label)).astype(F32).astype(BF16)
    earlier = iota((tokens, tokens), 0) < iota((tokens, tokens), 1)
    before = dot_nn(hits, earlier.astype(F32).astype(BF16))
    slots = []
    for k in range(2):
        own = jnp.sum(jnp.where(routes[k : k + 1] == label, before, 0.0), 0, keepdims=True)
        slots.append(own.astype(I32) + routes[k : k + 1] * capacity)
    return jnp.concatenate(slots * 4, 0)


def unit_norm(values):
    recip = lax.rsqrt(jnp.mean(values * values, -1, keepdims=True) + EPSILON)
    return values * recip, recip


def fill_mask(mask_ref, span_start):
    size = mask_ref.shape[0]
    i, j = iota((size, size), 0), iota((size, size), 1)

    def inside(p):
        return (p >= span_start) & (p < span_start + PIC)

    visible = (j <= i) | (inside(i) & inside(j))
    mask_ref[...] = jnp.where(visible, 0.0, MASKED_SCORE)


def head_lanes(which, size):
    lane = iota((1, 2 * size), 1)
    return ((lane >= size) == (which == 1)).astype(F32).astype(BF16)


def spread_bias(table_ref, ones_ref):
    pieces = [dot_nn(piece.astype(BF16), ones_ref[...]) for piece in split_three(table_ref[...])]
    return pieces[0] + pieces[1] + pieces[2]


def bias_tiles(diag_row):
    tiles = []
    for step in range(3):
        row = diag_row[:, 2 * TILE * step : 2 * TILE * (step + 1)]
        wide = jnp.broadcast_to(row, (TILE, 2 * TILE))
        tiles.append(pltpu.roll(wide, 0, 1, stride=1, stride_axis=0)[:, :TILE])
    return tiles, (diag_row[:, 6 * TILE : 7 * TILE], diag_row[:, 7 * TILE :])


def score_tiles(block, query, keys, tiles, far, mask_ref):
    raw = dot_nt(query, keys)
    rows = slice(block * TILE, (block + 1) * TILE)
    result = []
    for other in range(keys.shape[0] // TILE):
        piece = raw[:, other * TILE : (other + 1) * TILE]
        step = block - other
        piece = piece + (far[0] if step >= 2 else far[1] if step <= -2 else tiles[step + 1])
        if step <= 0:
            piece = piece + mask_ref[rows, other * TILE : (other + 1) * TILE]
        result.append(piece)
    return result


def softmax_tiles(pieces):
    top = functools.reduce(jnp.maximum, pieces)
    top = jnp.max(top, -1, keepdims=True)
    powers = [jnp.exp(piece - top) for piece in pieces]
    total = jnp.sum(functools.reduce(jnp.add, powers), -1, keepdims=True)
    scale = 1.0 / total
    return [power * scale for power in powers]


def split_three(value):
    high = value.astype(BF16).astype(F32)
    middle = (value - high).astype(BF16).astype(F32)
    return high, middle, value - high - middle


def remote_copy(source, target, sent, got, axis, peer):
    return pltpu.make_async_remote_copy(
        src_ref=source,
        dst_ref=target,
        send_sem=sent,
        recv_sem=got,
        device_id={axis: peer},
        device_id_type=pl.DeviceIdType.MESH,
    )


def turns_of(size):
    half, quarter = size // 2, size // 4
    return range(half, half + quarter), range(half + quarter, size), range(1, half)


def greet(peers):
    barrier = pltpu.get_barrier_semaphore()
    for axis, peer in peers:
        pl.semaphore_signal(
            barrier, inc=1, device_id={axis: peer}, device_id_type=pl.DeviceIdType.MESH
        )
    pl.semaphore_wait(barrier, len(peers))


def project_and_attend(place, group, groups, head_size, norm, diag_ref, w_ref, qkv_ref, mix_ref, mask):
    count = norm.shape[0]
    cols = w_ref.shape[-1]
    width = 2 * head_size
    owner = flip(place, group, groups)
    for c in range(3):
        qkv_ref[group, c] = dot_nn(norm[...], w_ref[group, c]).astype(BF16)

    def pair(p, carry):
        offset = pl.multiple_of(p * width, width)
        lanes = pl.ds(offset, width)
        query, keys, value = (qkv_ref[group, c, :, lanes] for c in range(3))
        mixed = [None] * (count // TILE)
        for which in range(2):
            head = owner * (cols // head_size) + 2 * p + which
            own = head_lanes(which, head_size)
            own_query, own_value = query * (own * 0.125), value * own
            tiles, far = bias_tiles(diag_ref[pl.ds(head, 1), :])
            for block in range(count // TILE):
                rows = slice(block * TILE, (block + 1) * TILE)
                pieces = score_tiles(block, own_query[rows], keys, tiles, far, mask)
                probs = jnp.concatenate([t.astype(BF16) for t in softmax_tiles(pieces)], 1)
                part = dot_nn(probs, own_value)
                mixed[block] = part if which == 0 else mixed[block] + part
        target = pl.ds(pl.multiple_of(owner * cols + offset, width), width)
        for block in range(count // TILE):
            rows = slice(block * TILE, (block + 1) * TILE)
            mix_ref[rows, target] = mixed[block].astype(BF16)
        return carry

    lax.fori_loop(0, cols // width, pair, 0)


def front_body(
    size, groups, head_size, span_ref, routes_ref, gain_ref, table_ref, ones_ref, router_ref, tok_hbm,
    cot_hbm,
    qkv_shard, out_shard, in_shard,
    col_ref, gate_ref, sent_gate_ref, qkvw_out, outw_out, qkv_out, mixed_out, hidden_out, norm_out,
    sent_out, outer_out, gate_out,
    tok, cot, qkvw, outw, qkv, mixed, hidden, norm, sent, outer, mask, row, diag_ref, load_sems, save_sems,
    shard_sems, outer_send, outer_got,
):
    me, place = lax.axis_index("dp"), lax.axis_index("wshard")
    near, far = flip(place, 1, groups), flip(place, 2, groups)
    peers = [("dp", flip(me, step, size)) for step in range(1, size)]
    greet(peers + [("wshard", near), ("wshard", far)])

    sources = (qkv_shard, out_shard, in_shard.at[0, : gate_out.shape[1]])

    def held(item, group):
        if item == 0:
            return qkvw.at[group]
        if item == 1:
            return outw.at[group]
        return gate_out.at[group - 2]

    def shard_copy(kind, item):
        source = held(item, 2) if kind == 2 else sources[item]
        return remote_copy(
            source, held(item, (1, 2, 3)[kind]), shard_sems.at[kind, item, 0],
            shard_sems.at[kind, item, 1], "wshard", far if kind == 1 else near,
        )

    shard_copy(1, 0).start()
    for item in range(2):
        shard_copy(0, item).start()
    loads = [
        pltpu.make_async_copy(source, target, load_sems.at[i])
        for i, (source, target) in enumerate(
            ((cot_hbm, cot), (tok_hbm, tok), (qkv_shard, qkvw.at[0]), (out_shard, outw.at[0]))
        )
    ]
    for copy in loads:
        copy.start()

    experts, capacity = size, sent.shape[1]
    count = tok.shape[0]
    slots = route_slots(experts, capacity, routes_ref[...])
    row[...] = slots
    col_ref[...] = slots.astype(F32).T.astype(I32)
    loads[0].wait()

    def place_outer(expert, carry):
        outer[expert] = dot_nn(onehot_rows(expert * capacity, capacity, row[...]), cot[...]).astype(BF16)
        return carry

    lax.fori_loop(0, experts, place_outer, 0)
    fill_mask(mask, span_ref[0])
    diag_ref[...] = spread_bias(table_ref, ones_ref)
    loads[1].wait()
    unit, _ = unit_norm(tok[...].astype(F32))
    norm[...] = (unit * gain_ref[0:1, :]).astype(BF16)
    loads[2].wait()

    def outer_copy(source, target, peer):
        return remote_copy(
            outer.at[source], outer_out.at[target], outer_send.at[source], outer_got.at[target],
            "dp", peer,
        )

    own_outer = pltpu.make_async_copy(outer.at[me], outer_out.at[me], load_sems.at[4])
    own_outer.start()
    turns = turns_of(size)

    def send_outer(turn):
        for step in turns[turn]:
            peer = flip(me, step, size)
            outer_copy(peer, me, peer).start()

    send_outer(0)

    def one_group(group, carry):
        @pl.when(group == 1)
        def _():
            send_outer(1)
            shard_copy(0, 0).wait_recv()

        @pl.when(group == 2)
        def _():
            shard_copy(1, 0).wait()
            shard_copy(2, 0).start()
            shard_copy(1, 1).start()

        @pl.when(group == 3)
        def _():
            send_outer(2)
            shard_copy(2, 0).wait_recv()

        project_and_attend(
            place, group, groups, head_size, norm, diag_ref, qkvw, qkv, mixed, mask
        )
        return carry

    lax.fori_loop(0, groups, one_group, 0)
    saves = [
        pltpu.make_async_copy(source, target, save_sems.at[i])
        for i, (source, target) in enumerate(
            (
                (qkvw, qkvw_out), (qkv, qkv_out), (mixed, mixed_out), (outw, outw_out),
                (hidden, hidden_out), (norm, norm_out), (sent, sent_out),
            )
        )
    ]
    for copy in saves[:3]:
        copy.start()
    loads[3].wait()
    shard_copy(0, 1).wait_recv()
    shard_copy(1, 1).wait()
    shard_copy(2, 1).start()
    shard_copy(1, 2).start()

    shard_copy(2, 1).wait_recv()
    saves[3].start()
    for group in range(groups):
        cols = outw.shape[2]
        lanes = pl.ds(pl.multiple_of(flip(place, group, groups) * cols, cols), cols)
        hidden[:, lanes] = tok[:, lanes].astype(F32) + dot_nn(mixed[...], outw[group])
    saves[4].start()
    unit, _ = unit_norm(hidden[...])
    norm[...] = (unit * gain_ref[1:2, :]).astype(BF16)
    saves[5].start()

    def place_sent(expert, carry):
        sent[expert] = dot_nn(onehot_rows(expert * capacity, capacity, row[...]), norm[...]).astype(BF16)
        return carry

    lax.fori_loop(0, experts, place_sent, 0)
    saves[6].start()
    logits = dot_nt(norm[...], router_ref[...])
    slots = [col_ref[:, k : k + 1] for k in range(2)]
    lane = iota(logits.shape, 1)
    chosen = []
    for k in range(2):
        own = (lane * capacity <= slots[k]) & (slots[k] < (lane + 1) * capacity)
        chosen.append(jnp.sum(jnp.where(own, logits, 0.0), -1, keepdims=True))
    top = jnp.maximum(chosen[0], chosen[1])
    powers = [jnp.exp(c - top) for c in chosen]
    gates = [power / (powers[0] + powers[1]) for power in powers]
    for k in range(2):
        gate_ref[:, k : k + 1] = gates[k]
    lane = iota((count, sent_gate_ref.shape[2]), 1)
    for expert in range(experts):
        label = jnp.where(lane < capacity, lane + expert * capacity, -1)
        part = 0.0
        for k in range(2):
            part = part + jnp.where(label == slots[k], gates[k], 0.0)
        line = jnp.sum(part, 0, keepdims=True)
        sent_gate_ref[expert] = jnp.broadcast_to(line, sent_gate_ref.shape[1:])

    shard_copy(1, 2).wait()
    shard_copy(2, 2).start()
    own_outer.wait()
    for copy in saves:
        copy.wait()
    for _, peer in peers:
        outer_copy(peer, me, peer).wait_send()
        outer_copy(me, peer, peer).wait_recv()
    for item in range(2):
        shard_copy(0, item).wait_send()
        shard_copy(2, item).wait_send()
    shard_copy(2, 2).wait()


def front(
    span, routes, gains, table_t, ones, router_t, tokens, cotangent, shards, head_size, capacity
):
    count, width = tokens.shape
    size, groups = lax.axis_size("dp"), lax.axis_size("wshard")
    qkv_shard, out_shard, in_shard = shards
    cols = out_shard.shape[1]
    lanes = -(-capacity // TILE) * TILE
    dma = pltpu.SemaphoreType.DMA
    block = (size, capacity, width)
    return pl.pallas_call(
        functools.partial(front_body, size, groups, head_size),
        out_shape=(
            shape_of((count, 8), I32),
            shape_of((count, 2), F32),
            shape_of((size, EXTRA, lanes), F32),
            shape_of((groups, *qkv_shard.shape), BF16),
            shape_of((groups, *out_shard.shape), BF16),
            shape_of((groups, 3, count, cols), BF16),
            shape_of((count, width), BF16),
            shape_of((count, width), F32),
            shape_of((count, width), BF16),
            shape_of(block, BF16),
            shape_of(block, BF16),
            shape_of((2, in_shard.shape[1] // 32 * 16, width), BF16),
        ),
        in_specs=[SMEM] + [VMEM] * 5 + [ANY] * 5,
        out_specs=(VMEM,) * 3 + (ANY,) * 9,
        scratch_shapes=[
            pltpu.VMEM((count, width), BF16),
            pltpu.VMEM((count, width), BF16),
            pltpu.VMEM((groups, *qkv_shard.shape), BF16),
            pltpu.VMEM((groups, *out_shard.shape), BF16),
            pltpu.VMEM((groups, 3, count, cols), BF16),
            pltpu.VMEM((count, width), BF16),
            pltpu.VMEM((count, width), F32),
            pltpu.VMEM((count, width), BF16),
            pltpu.VMEM(block, BF16),
            pltpu.VMEM(block, BF16),
            pltpu.VMEM((count, count), F32),
            pltpu.VMEM((8, count), I32),
            pltpu.VMEM((table_t.shape[0], ones.shape[1]), F32),
            dma((5,)),
            dma((7,)),
            dma((3, 3, 2)),
            dma((size,)),
            dma((size,)),
        ],
        cost_estimate=pl.CostEstimate(flops=LIGHT, bytes_accessed=LIGHT, transcendentals=0),
        compiler_params=pltpu.CompilerParams(
            collective_id=1, has_side_effects=True, vmem_limit_bytes=60_000_000
        ),
        name="front",
    )(span, routes.T, gains, table_t, ones, router_t, tokens, cotangent, *shards)


def flip(value, change, size):
    result = 0
    bit = 1
    while bit < size:
        one, two = lax.rem(lax.div(value, bit), 2), lax.rem(lax.div(change, bit), 2)
        result = result + bit * (one + two - 2 * one * two)
        bit *= 2
    return result


def column_of(row, size):
    spot = iota((size, row.shape[1]), 0) == iota((size, row.shape[1]), 1)
    return jnp.sum(jnp.where(spot, row, 0.0), 1, keepdims=True)


def row_of(column, lanes):
    spot = iota((column.shape[0], lanes), 0) == iota((column.shape[0], lanes), 1)
    return jnp.sum(jnp.where(spot, column, 0.0), 0, keepdims=True)


def moe_body(
    size, groups, chunk, sent_ref, gates_ref, outer_ref, own_in, own_down, far_gate, *refs
):
    back_out, extra_out, made_out, grad_out, moved_out = refs[:5]
    (
        buf, rows, gates, outer, low_outer, made_sum, back_sum, act, low, stage, extra_stage,
        made, grad_stage, weight_sems, shard_sems, send_sems, recv_sems, give_sems, take_sems, own_sems,
        save_sems, grad_sems, moved_sem, sum_sems,
    ) = refs[5:]
    share = own_down.shape[0]
    part_size = share * groups // 2
    capacity, width = outer.shape[1:]
    both = 2 * capacity
    me = lax.axis_index("dp")
    pairs = size // 2
    my_pair = lax.div(me, 2)
    mesh_id = pl.DeviceIdType.MESH

    place = lax.axis_index("wshard")
    near, far = flip(place, 1, groups), flip(place, 2, groups)
    peers = [("dp", flip(me, step, size)) for step in range(1, size)]
    greet(peers + [("wshard", near), ("wshard", far)])

    def remote(source, target, sent, got, peer):
        return pltpu.make_async_remote_copy(
            src_ref=source, dst_ref=target, send_sem=sent, recv_sem=got,
            device_id={"dp": peer}, device_id_type=mesh_id,
        )

    def forth(source, target, peer):
        return (
            remote(sent_ref.at[source], rows.at[target], send_sems.at[source, 0],
                   recv_sems.at[target, 0], peer),
            remote(gates_ref.at[source], gates.at[target], send_sems.at[source, 1],
                   recv_sems.at[target, 1], peer),
        )

    def back_copies(source, target, peer):
        return (
            remote(stage.at[source], back_out.at[target], give_sems.at[source, 0],
                   take_sems.at[target, 0], peer),
            remote(extra_stage.at[source], extra_out.at[target], give_sems.at[source, 1],
                   take_sems.at[target, 1], peer),
        )

    own = (
        pltpu.make_async_copy(sent_ref.at[me], rows.at[me], own_sems.at[0]),
        pltpu.make_async_copy(gates_ref.at[me], gates.at[me], own_sems.at[1]),
        pltpu.make_async_copy(outer_ref, outer, own_sems.at[2]),
    )
    own_back = (
        pltpu.make_async_copy(stage.at[me], back_out.at[me], own_sems.at[3]),
        pltpu.make_async_copy(extra_stage.at[me], extra_out.at[me], own_sems.at[4]),
    )
    for copy in own:
        copy.start()
    turns = turns_of(size)

    def send_rows(steps):
        for step in steps:
            peer = flip(me, step, size)
            for copy in forth(peer, me, peer):
                copy.start()

    send_rows(turns[2])
    send_rows(turns[0])

    begun = far_gate.shape[1]

    def home(c, group, first, count):
        return buf.at[c, pl.ds(group * share + first, count)]

    loads = [
        pltpu.make_async_copy(own_in, buf.at[0:2, pl.ds(0, share)], weight_sems.at[0]),
        pltpu.make_async_copy(own_down, home(2, 0, 0, share), weight_sems.at[1]),
    ]
    loads += [
        pltpu.make_async_copy(far_gate.at[i], home(0, 2 + i, 0, begun), weight_sems.at[2 + i])
        for i in range(2)
    ]
    near_copies = [
        remote_copy(own_in, buf.at[0:2, pl.ds(share, share)], shard_sems.at[0, 0, 0],
                    shard_sems.at[0, 0, 1], "wshard", near),
        remote_copy(own_down, home(2, 1, 0, share), shard_sems.at[0, 1, 0],
                    shard_sems.at[0, 1, 1], "wshard", near),
    ]
    rest = ((0, begun, share - begun), (1, 0, share), (2, 0, share))

    def far_copy(c):
        _, first, count = rest[c]
        source = own_down if c == 2 else own_in.at[c]
        return remote_copy(source.at[pl.ds(first, count)], home(c, 2, first, count),
                           shard_sems.at[1, c, 0], shard_sems.at[1, c, 1], "wshard", far)

    def onward_copy(c):
        _, first, count = rest[c]
        return remote_copy(home(c, 2, first, count), home(c, 3, first, count),
                           shard_sems.at[2, c, 0], shard_sems.at[2, c, 1], "wshard", near)

    far_copy(0).start()
    far_copy(1).start()
    for copy in loads + near_copies:
        copy.start()
    for copy in own:
        copy.wait()

    def hidden_part(pair, base):
        spot = pl.ds(pl.multiple_of(pair * both, both), both)
        two = pl.ds(2 * pair, 2)
        these = rows[two].reshape(both, width)
        outers = low_outer[spot, :]
        for first in range(0, part_size, chunk):
            last = min(first + chunk, part_size)
            part, lanes = slice(base + first, base + last), slice(first, last)
            gate, up = dot_nt(these, buf[0, part, :]), dot_nt(these, buf[1, part, :])
            act_grad = dot_nt(outers, buf[2, part, :])
            square = gate * gate
            inner = gate * (0.7978845608028654 + (0.7978845608028654 * 0.044715) * square)
            rise = 0.5 + 0.5 * jnp.tanh(inner)
            bent = gate * rise
            act[spot, lanes] = (bent * up).astype(BF16)
            slope = rise + bent * (1.0 - rise) * (
                2 * 0.7978845608028654 + (6 * 0.7978845608028654 * 0.044715) * square
            )
            low[0, spot, lanes] = (act_grad * up * slope).astype(BF16)
            low[1, spot, lanes] = (act_grad * bent).astype(BF16)
        whole = slice(base, base + part_size)
        result = dot_nn(act[spot, :], buf[2, whole, :])
        back = dot_nn(low[0, spot, :], buf[0, whole, :]) + dot_nn(low[1, spot, :], buf[1, whole, :])
        return spot, result, back

    def near_step(step, carry):
        pair = flip(my_pair, step, pairs)
        first = 2 * pair

        @pl.when(step == 1)
        def _():
            send_rows(turns[1])

        @pl.when(step == pairs // 2)
        def _():
            for c in range(2):
                far_copy(c).wait()
                onward_copy(c).start()
            far_copy(2).start()

        @pl.when(step == 0)
        def _():
            peer = flip(me, 1, size)
            for copy in forth(me, peer, peer):
                copy.wait_recv()

        @pl.when(step > 0)
        def _():
            for which in range(2):
                for copy in forth(me, first + which, first + which):
                    copy.wait_recv()

        for which in range(2):
            gate = column_of(gates[first + which, 0:1, :], capacity)
            spot = pl.ds(pl.multiple_of((first + which) * capacity, capacity), capacity)
            low_outer[spot, :] = (outer[first + which].astype(F32) * gate).astype(BF16)
        spot, result, back = hidden_part(pair, 0)
        made_sum[spot, :] = result
        back_sum[spot, :] = back
        return carry

    def sent_all(copies):
        for remote_one, copy in copies:
            if remote_one:
                copy.wait_send()
            else:
                copy.wait()

    def weight_grads(half):
        every = rows[...].reshape(size * capacity, width)
        outers = low_outer[...]
        count = 0
        base = half * part_size
        waiting = {}
        for c in range(3):
            left = act if c == 2 else low.at[c]
            for first in range(0, part_size, 2 * chunk):
                last = min(first + 2 * chunk, part_size)
                slot = count % 2
                sent_all(waiting.pop(slot, ()))
                piece = dot_tn(left[:, first:last], outers if c == 2 else every)
                grad_stage[slot, : last - first, :] = piece.astype(BF16)
                copies = []
                begin = base + first
                while begin < base + last:
                    group = begin // share
                    end = min(base + last, (group + 1) * share)
                    source = grad_stage.at[slot, pl.ds(begin - base - first, end - begin)]
                    spot = pl.ds(begin - group * share, end - begin)
                    sem = grad_sems.at[slot, len(copies)]
                    if group % 2:
                        target = moved_out.at[group // 2, c, spot]
                        copies.append((True, remote_copy(source, target, sem, moved_sem, "wshard", near)))
                    else:
                        target = grad_out.at[group // 2, c, spot]
                        copies.append((False, pltpu.make_async_copy(source, target, sem)))
                    begin = end
                for _, copy in copies:
                    copy.start()
                waiting[slot] = copies
                count += 1
        for copies in waiting.values():
            sent_all(copies)

    for copy in loads[:2]:
        copy.wait()
    for copy in near_copies:
        copy.wait_recv()
    lax.fori_loop(0, pairs, near_step, 0)
    weight_grads(0)

    def far_step(step, carry):
        pair = flip(my_pair, pairs - 1 - step, pairs)
        first = 2 * pair
        spot, result, back = hidden_part(pair, part_size)
        result = (made_sum[spot, :] + result).astype(BF16)
        back = (back_sum[spot, :] + back).astype(BF16)
        two = pl.ds(first, 2)
        made[two] = result.reshape(2, capacity, width)
        stage[two] = back.reshape(2, capacity, width)
        for which in range(2):
            grads = outer[first + which].astype(F32) * made[first + which].astype(F32)
            line = row_of(jnp.sum(grads, -1, keepdims=True), extra_stage.shape[2])
            extra_stage[first + which] = jnp.broadcast_to(line, extra_stage.shape[1:])
        pltpu.make_async_copy(made.at[two], made_out.at[two], save_sems.at[step]).start()

        @pl.when(step < pairs - 1)
        def _():
            for which in range(2):
                for copy in back_copies(first + which, me, first + which):
                    copy.start()

        @pl.when(step == pairs - 1)
        def _():
            peer = flip(me, 1, size)
            for copy in back_copies(peer, me, peer):
                copy.start()
            for copy in own_back:
                copy.start()

        return carry

    far_copy(2).wait()
    onward_copy(2).start()
    for copy in loads[2:]:
        copy.wait()
    for c in range(3):
        onward_copy(c).wait_recv()
    lax.fori_loop(0, pairs, far_step, 0)
    weight_grads(1)
    remote_copy(moved_out, moved_out, moved_sem, moved_sem, "wshard", near).wait_recv()

    corner = (pl.ds(0, share), pl.ds(0, width))
    rooms = ((low.at[0], act), (low.at[1], low_outer))
    pieces = [(g, c) for g in (1, 0) for c in range(3)]

    def fetch(i):
        slot = i % 2
        return [
            pltpu.make_async_copy(source.at[pieces[i]], room.at[corner], sum_sems.at[slot, k])
            for k, (source, room) in enumerate(zip((grad_out, moved_out), rooms[slot]))
        ]

    def put(i):
        slot = i % 2
        return pltpu.make_async_copy(
            rooms[slot][0].at[corner], grad_out.at[pieces[i]], sum_sems.at[slot, 2]
        )

    for i in range(2):
        for copy in fetch(i):
            copy.start()
    for i in range(len(pieces)):
        for copy in fetch(i):
            copy.wait()
        one, other = rooms[i % 2]

        def add_rows(block, carry):
            spot = (pl.ds(pl.multiple_of(block * 64, 64), 64), slice(0, width))
            one[spot] = (one[spot].astype(F32) + other[spot].astype(F32)).astype(BF16)
            return carry

        lax.fori_loop(0, share // 64, add_rows, 0)
        put(i).start()
        if i + 2 < len(pieces):
            put(i).wait()
            for copy in fetch(i + 2):
                copy.start()
    for i in range(len(pieces) - 2, len(pieces)):
        put(i).wait()
    for copy in own_back:
        copy.wait()
    for copy in near_copies:
        copy.wait_send()
    for c in range(3):
        onward_copy(c).wait_send()
    for step in range(pairs):
        two = pl.ds(2 * flip(my_pair, pairs - 1 - step, pairs), 2)
        pltpu.make_async_copy(made.at[two], made_out.at[two], save_sems.at[step]).wait()
    for step in range(1, size):
        peer = flip(me, step, size)
        for copy in forth(peer, me, peer):
            copy.wait_send()
        for copy in back_copies(peer, me, peer):
            copy.wait_send()
        for copy in back_copies(me, peer, peer):
            copy.wait_recv()


def moe(sent, gates, outer, own_in, own_down, far_gate, chunk=256):
    size, capacity, width = sent.shape
    groups = lax.axis_size("wshard")
    share = own_down.shape[0]
    part = share * groups // 2
    total = size * capacity
    extra = gates.shape[1:]
    dma = pltpu.SemaphoreType.DMA
    result = pl.pallas_call(
        functools.partial(moe_body, size, groups, chunk),
        out_shape=(
            shape_of((size, capacity, width), BF16),
            shape_of((size, *extra), F32),
            shape_of((size, capacity, width), BF16),
        )
        + (shape_of((2, 3, share, width), BF16),) * 2,
        in_specs=[ANY] * 6,
        out_specs=(ANY,) * 5,
        scratch_shapes=[
            pltpu.VMEM((3, share * groups, width), BF16),
            pltpu.VMEM((size, capacity, width), BF16),
            pltpu.VMEM((size, *extra), F32),
            pltpu.VMEM((size, capacity, width), BF16),
            pltpu.VMEM((total, width), BF16),
            pltpu.VMEM((total, width), F32),
            pltpu.VMEM((total, width), F32),
            pltpu.VMEM((total, part), BF16),
            pltpu.VMEM((2, total, part), BF16),
            pltpu.VMEM((size, capacity, width), BF16),
            pltpu.VMEM((size, *extra), F32),
            pltpu.VMEM((size, capacity, width), BF16),
            pltpu.VMEM((2, 2 * chunk, width), BF16),
            dma((4,)),
            dma((3, 3, 2)),
            dma((size, 2)),
            dma((size, 2)),
            dma((size, 2)),
            dma((size, 2)),
            dma((5,)),
            dma((size // 2,)),
            dma((2, 3)),
            dma,
            dma((2, 3)),
        ],
        cost_estimate=pl.CostEstimate(flops=LIGHT, bytes_accessed=LIGHT, transcendentals=0),
        compiler_params=pltpu.CompilerParams(
            collective_id=0, has_side_effects=True, vmem_limit_bytes=66_000_000
        ),
        name="experts",
    )(sent, gates, outer, own_in, own_down, far_gate)
    return result[:4]


def expert_body(groups, chunk, rows_ref, outer_ref, gate_ref, *refs):
    in_refs, down_refs = refs[:groups], refs[groups : 2 * groups]
    made_ref, back_ref, outer_out_ref, gate_grad_ref = refs[2 * groups : 2 * groups + 4]
    act_ref, low_ref, buf_ref, sems = refs[2 * groups + 4 :]
    share = down_refs[0].shape[0]
    hidden = share * groups

    def copies(group):
        spot = pl.ds(group * share, share)
        return (
            pltpu.make_async_copy(in_refs[group], buf_ref.at[0:2, spot], sems.at[2 * group]),
            pltpu.make_async_copy(down_refs[group], buf_ref.at[2, spot], sems.at[2 * group + 1]),
        )

    @pl.when(pl.program_id(0) == 0)
    def _():
        for group in range(groups):
            for copy in copies(group):
                copy.start()

    rows = rows_ref[...]
    low_outer = (outer_ref[...].astype(F32) * gate_ref[...]).astype(BF16)
    outer_out_ref[...] = low_outer

    @pl.when(pl.program_id(0) == 0)
    def _():
        for group in range(groups):
            for copy in copies(group):
                copy.wait()

    for first in range(0, hidden, chunk):
        part = slice(first, first + chunk)
        gate, up = dot_nt(rows, buf_ref[0, part, :]), dot_nt(rows, buf_ref[1, part, :])
        act_grad = dot_nt(low_outer, buf_ref[2, part, :])
        square = gate * gate
        inner = gate * (0.7978845608028654 + (0.7978845608028654 * 0.044715) * square)
        rise = 0.5 + 0.5 * jnp.tanh(inner)
        bent = gate * rise
        act_ref[:, part] = (bent * up).astype(BF16)
        slope = rise + bent * (1.0 - rise) * (
            2 * 0.7978845608028654 + (6 * 0.7978845608028654 * 0.044715) * square
        )
        low_ref[0, :, part] = (act_grad * up * slope).astype(BF16)
        low_ref[1, :, part] = (act_grad * bent).astype(BF16)
    made = dot_nn(act_ref[...], buf_ref[2]).astype(BF16)
    made_ref[...] = made
    back = dot_nn(low_ref[0], buf_ref[0]) + dot_nn(low_ref[1], buf_ref[1])
    back_ref[...] = back.astype(BF16)
    gate_grad_ref[...] = jnp.sum(
        outer_ref[...].astype(F32) * made.astype(F32), -1, keepdims=True
    )


def experts_pass(rows, outer, gate_column, in_weights, down_weights, block=320, chunk=256):
    total, width = rows.shape
    groups = len(in_weights)
    hidden = down_weights[0].shape[0] * groups
    row_spec = pl.BlockSpec((block, width), lambda i: (i, 0))
    column = pl.BlockSpec((block, 1), lambda i: (i, 0))
    wide = pl.BlockSpec((block, hidden), lambda i: (i, 0))
    both = pl.BlockSpec((2, block, hidden), lambda i: (0, i, 0))
    return pl.pallas_call(
        functools.partial(expert_body, groups, chunk),
        grid=(total // block,),
        out_shape=(
            shape_of((total, width), BF16),
            shape_of((total, width), BF16),
            shape_of((total, width), BF16),
            shape_of((total, 1), F32),
            shape_of((total, hidden), BF16),
            shape_of((2, total, hidden), BF16),
        ),
        in_specs=[row_spec, row_spec, column] + [ANY] * (2 * groups),
        out_specs=(row_spec, row_spec, row_spec, column, wide, both),
        scratch_shapes=[
            pltpu.VMEM((3, hidden, width), BF16),
            pltpu.SemaphoreType.DMA((2 * groups,)),
        ],
        cost_estimate=pl.CostEstimate(flops=LIGHT, bytes_accessed=LIGHT, transcendentals=0),
        name="experts",
    )(rows, outer, gate_column, *in_weights, *down_weights)


def moe_plain(sent, gates, outer, own_in, own_down, far_gate):
    in_weights, down_weights = [own_in], [own_down]
    for bit in (1, 2):
        in_weights += [swap(w, "wshard", bit) for w in in_weights]
        down_weights += [swap(w, "wshard", bit) for w in down_weights]
    size, capacity, width = sent.shape
    total = size * capacity
    rows = exchange(sent.reshape(total, width), "dp").reshape(total, width)
    gate_column = lax.all_to_all(gates, "dp", 0, 0, tiled=True)[:, 0, :capacity].reshape(total, 1)
    made, back, outer_low, gate_grads, act, low = experts_pass(
        rows, outer.reshape(total, width), gate_column, in_weights, down_weights
    )
    extra = jnp.pad(gate_grads.reshape(size, 1, capacity), ((0, 0), (0, EXTRA - 1), (0, 0)))
    extra = lax.all_to_all(extra, "dp", 0, 0, tiled=True)
    share = down_weights[0].shape[0]
    grads = []
    for group in range(len(in_weights)):
        part = slice(group * share, (group + 1) * share)
        pieces = [dot_tn(low[c, :, part], rows) for c in range(2)]
        grads.append(jnp.stack(pieces + [dot_tn(act[:, part], outer_low)]).astype(BF16))
    shape = (size, capacity, width)
    moved = jnp.stack([swap(grads[g], "wshard", 1) for g in (1, 3)])
    sums = (jnp.stack(grads[::2]).astype(F32) + moved.astype(F32)).astype(BF16)
    return exchange(back, "dp"), extra, made.reshape(shape), sums


def rear_body(
    size, groups, head_size, remote_made, span_ref, gain_ref, table_ref, ones_ref, router_ref, col_ref, gate_ref,
    extra_ref, tok_hbm, cot_hbm, hidden_hbm, norm_hbm, mixed_hbm, rows_hbm, made_hbm, outw_hbm,
    qkvw_hbm, qkv_hbm, far_hbm,
    output_ref, grad_ref, gains_out, table_out, router_out, sum_out, sum_out_two, far_out,
    tok, cot, hidden, norm, mixed, rows, made, outw, qkvw, qkv, norm_t, mask, grad_hidden,
    grads, probs_ref, scores_ref, diag_sums, wo, wo_got, wg, wg_got, total,
    total_got, sum_ref, early_ref, early_got, late_ref, late_got, diag_ref,
    load_sems, weight_sems, made_send, made_got, part_sems, total_sems, small_sems, far_sems,
):
    me, place = lax.axis_index("dp"), lax.axis_index("wshard")
    near, far = flip(place, 1, groups), flip(place, 2, groups)
    dp_bits, shard_bits = bits_below(size), bits_below(groups)
    peers = [("dp", flip(me, step, size)) for step in range(1, size)]
    greet(peers + [("wshard", near), ("wshard", far)])
    count, width = tok.shape
    blocks = count // TILE
    experts = size
    capacity = rows.shape[0] // experts
    cols = outw.shape[2]
    two_heads = 2 * head_size
    branch, mixgrad, norm_grad = cot, norm, hidden

    loads = [
        pltpu.make_async_copy(source, target, load_sems.at[i])
        for i, (source, target) in enumerate(
            (
                (rows_hbm, rows), (norm_hbm, norm), (hidden_hbm, hidden), (cot_hbm, cot),
                (mixed_hbm, mixed), (outw_hbm, outw), (tok_hbm, tok), (qkv_hbm, qkv),
                (made_hbm.at[me], made.at[me]) if remote_made else (made_hbm, rows),
            )
        )
    ]
    for copy in loads[: 9 if remote_made else 8]:
        copy.start()

    def far_copy(piece):
        return remote_copy(
            far_hbm.at[1, piece], far_out.at[piece], far_sems.at[piece, 0], far_sems.at[piece, 1],
            "wshard", far,
        )

    far_copy(0).start()

    def weight_load(step):
        slot = lax.rem(step, 2)
        return pltpu.make_async_copy(
            qkvw_hbm.at[groups - 1 - step], qkvw.at[slot], weight_sems.at[slot]
        )

    hidden_again = pltpu.make_async_copy(hidden_hbm, hidden, load_sems.at[9])

    def made_copy(source, target, peer):
        return remote_copy(
            made_hbm.at[source], made.at[target], made_send.at[source], made_got.at[target], "dp",
            peer,
        )

    turns = turns_of(size)

    def send_made(turn):
        if remote_made:
            for step in turns[turn]:
                peer = flip(me, step, size)
                made_copy(peer, me, peer).start()

    send_made(0)

    exchanges = [("wshard", place, bit, groups) for bit in shard_bits]
    exchanges += [("dp", me, bit, size) for bit in dp_bits]

    def small_copy(kind, ref, got, step):
        axis, index, bit, length = exchanges[step]
        return remote_copy(
            ref, got.at[step], small_sems.at[kind, step, 0], small_sems.at[kind, step, 1], axis,
            flip(index, bit, length),
        )

    def small_step(kind, ref, got, step):
        now, before = step % 2, (step + 1) % 2
        if step > 0:
            small_copy(kind, ref.at[before], got, step - 1).wait()
            ref[now] = ref[before] + got[step - 1]
        if step < len(exchanges):
            small_copy(kind, ref.at[now], got, step).start()

    slots = [col_ref[:, k : k + 1] for k in range(2)]
    gates = [gate_ref[:, k : k + 1] for k in range(2)]
    lane = iota((count, extra_ref.shape[2]), 1)
    picked = [0.0, 0.0]
    for copy in loads[:1]:
        copy.wait()
    grads_in = 0.0
    for expert in range(experts):
        label = jnp.where(lane < capacity, lane + expert * capacity, -1)
        for k in range(2):
            picked[k] = picked[k] + jnp.where(label == slots[k], extra_ref[expert, 0:1, :], 0.0)
    gate_grads = [jnp.sum(p, -1, keepdims=True) for p in picked]
    mean = gates[0] * gate_grads[0] + gates[1] * gate_grads[1]
    lane = iota((count, 3 * experts), 1)
    part = (lane >= experts).astype(I32) + (lane >= 2 * experts).astype(I32)
    label = lane - part * experts
    logit_grads = 0.0
    for k in range(2):
        own = (label * capacity <= slots[k]) & (slots[k] < (label + 1) * capacity)
        logit_grads = logit_grads + jnp.where(own, gates[k] * (gate_grads[k] - mean), 0.0)
    high, middle, low = split_three(logit_grads)
    split = jnp.where(part == 0, high, jnp.where(part == 1, middle, low)).astype(BF16)
    hits = [onehot_columns(slots[k], 0, experts * capacity) for k in range(2)]
    hits = (hits[0] | hits[1]).astype(F32).astype(BF16)
    for copy in loads[1:4]:
        copy.wait()
    normed_grad = dot_nn(hits, rows[...])
    normed_grad = normed_grad + dot_nn(split, router_ref[...])
    router_grad = dot_tn(split, norm[...])
    early_ref[0, :experts, :] = (
        router_grad[:experts] + router_grad[experts : 2 * experts] + router_grad[2 * experts :]
    )
    unit, recip = unit_norm(hidden[...])
    early_ref[0, experts:, :] = jnp.broadcast_to(
        jnp.sum(normed_grad * unit, 0, keepdims=True), (EXTRA, width)
    )
    small_step(0, early_ref, early_got, 0)
    scaled = normed_grad * gain_ref[1:2, :]
    back = recip * (scaled - unit * jnp.mean(scaled * unit, -1, keepdims=True))
    grad_hidden[...] = cot[...].astype(F32) + back
    branch[...] = grad_hidden[...].astype(BF16)
    for copy in loads[4:6]:
        copy.wait()
    mixed_t = mixed[...].T
    result = 0.0

    def part_copy(item, source, target, kind, axis, peer):
        return remote_copy(
            source, target, part_sems.at[item, kind, 0], part_sems.at[item, kind, 1], axis, peer
        )

    def out_copy(kind):
        return part_copy(
            0, wo.at[(3, 1, 2)[kind]], wo_got.at[kind], kind, "wshard", far if kind == 2 else near
        )

    def qkv_copy(kind):
        return part_copy(
            1, wg.at[(2, 0, 1)[kind]], wg_got.at[kind], kind, "wshard", far if kind == 2 else near
        )

    for group in reversed(range(groups)):
        lanes = pl.ds(pl.multiple_of(flip(place, group, groups) * cols, cols), cols)
        piece = branch[:, lanes]
        result = result + dot_nt(piece, outw[group])
        wo[group] = dot_nn(mixed_t, piece).astype(BF16)
        if group == 3:
            out_copy(0).start()
        if group == 1:
            out_copy(1).start()
    mixgrad[...] = result.astype(BF16)
    for copy in loads[6:8]:
        copy.wait()
    weight_load(0).start()
    unit, _ = unit_norm(tok[...].astype(F32))
    norm_t[...] = (unit * gain_ref[0:1, :]).astype(BF16).T
    fill_mask(mask, span_ref[0])
    diag_ref[...] = spread_bias(table_ref, ones_ref)
    norm_grad[...] = jnp.zeros_like(norm_grad)

    def attend_group(step):
        group = groups - 1 - step
        slot = lax.rem(step, 2)
        weight_load(step).wait()

        @pl.when(step < groups - 1)
        def _():
            weight_load(step + 1).start()

        owner = flip(place, group, groups)
        heads = cols // head_size

        def pair(p, carry):
            offset = pl.multiple_of(p * two_heads, two_heads)
            lanes = pl.ds(offset, two_heads)
            query, keys, value = (qkv[group, c, :, lanes] for c in range(3))
            outer = mixgrad[:, pl.ds(pl.multiple_of(owner * cols + offset, two_heads), two_heads)]
            query_sum, key_sum, value_sum = [None] * blocks, None, None
            for which in range(2):
                head = owner * heads + 2 * p + which
                own = head_lanes(which, head_size)
                own_query, own_key, own_outer = query * own, keys * own, outer * own
                shrunk = own_query * 0.125
                tiles, far_bias = bias_tiles(diag_ref[pl.ds(head, 1), :])
                near_sums, far_sums = [None] * 3, [None] * 2
                for block in range(blocks):
                    piece = slice(block * TILE, (block + 1) * TILE)
                    probs = softmax_tiles(
                        score_tiles(block, shrunk[piece], keys, tiles, far_bias, mask)
                    )
                    prob_grads = dot_nt(own_outer[piece], value)
                    prob_grads = [prob_grads[:, j * TILE : (j + 1) * TILE] for j in range(blocks)]
                    delta = functools.reduce(jnp.add, [a * b for a, b in zip(probs, prob_grads)])
                    delta = jnp.sum(delta, -1, keepdims=True)
                    lows = [(a * (b - delta)).astype(BF16) for a, b in zip(probs, prob_grads)]
                    for other in range(blocks):
                        step = block - other
                        wide = lows[other].astype(F32)
                        if abs(step) >= 2:
                            side = 0 if step > 0 else 1
                            old = far_sums[side]
                            far_sums[side] = wide if old is None else old + wide
                        else:
                            old = near_sums[step + 1]
                            near_sums[step + 1] = wide if old is None else old + wide
                    probs_ref[which, piece, :] = jnp.concatenate([t.astype(BF16) for t in probs], 1)
                    lows = jnp.concatenate(lows, 1)
                    scores_ref[which, piece, :] = lows
                    more = dot_nn(lows, own_key)
                    query_sum[block] = more if which == 0 else query_sum[block] + more
                more = dot_tn(scores_ref[which], own_query)
                key_sum = more if which == 0 else key_sum + more
                more = dot_tn(probs_ref[which], own_outer)
                value_sum = more if which == 0 else value_sum + more
                for step in range(3):
                    wide = jnp.concatenate([near_sums[step], jnp.zeros((TILE, TILE), F32)], 1)
                    half = TILE // 2
                    while half:
                        turned = pltpu.roll(wide[half:], 2 * TILE - half, 1)
                        wide = wide[:half] + turned
                        half //= 2
                    for side in range(2):
                        spot = 2 * step + side
                        diag_sums[head, spot : spot + 1, :] = wide[:, TILE * side : TILE * (side + 1)]
                for side in range(2):
                    diag_sums[head, 6 + side : 7 + side, :] = jnp.sum(far_sums[side], 0, keepdims=True)
            for block in range(blocks):
                piece = slice(block * TILE, (block + 1) * TILE)
                grads[0, piece, lanes] = (query_sum[block] * 0.125).astype(BF16)
            grads[1, :, lanes] = (key_sum * 0.125).astype(BF16)
            grads[2, :, lanes] = value_sum.astype(BF16)
            return carry

        lax.fori_loop(0, cols // two_heads, pair, 0)
        for c in range(3):
            weight_grad = dot_nn(norm_t[...], grads[c]).astype(BF16)

            @pl.when(group > 0)
            def _():
                wg[group - 1, c] = weight_grad

            @pl.when(group == 0)
            def _():
                total[c * width : (c + 1) * width, :] = weight_grad

            norm_grad[...] += dot_nt(grads[c], qkvw[slot, c])

    def add_into(target, *others):
        for first in range(0, target.shape[0], 256):
            spot = slice(first, first + 256)
            value = target[spot].astype(F32)
            for other in others:
                value = value + other[spot].astype(F32)
            target[spot] = value.astype(BF16)

    third = outw.shape[1]
    parts = 4
    length = total.shape[0] // parts
    stages = len(dp_bits)

    def bit_of(step):
        return lax.rem(lax.div(me, dp_bits[step]), 2)

    def segment(part, step):
        first, size_of = part * length, length
        for s in range(step):
            size_of //= 2
            first = first + bit_of(s) * size_of
        return first, size_of

    def halving(part, step):
        first, size_of = segment(part, step)
        half = size_of // 2
        away = pl.multiple_of(first + (1 - bit_of(step)) * half, half)
        return remote_copy(
            total.at[pl.ds(away, half)],
            total_got.at[pl.ds(part * length + length - size_of, half)],
            total_sems.at[part, 0, step, 0], total_sems.at[part, 0, step, 1], "dp",
            flip(me, dp_bits[step], size),
        )

    def add_half(part, step):
        first, half = segment(part, step + 1)
        first = pl.multiple_of(first, half)
        got = part * length + length - 2 * half
        value = total[pl.ds(first, half), :].astype(F32) + total_got[got : got + half, :].astype(F32)
        total[pl.ds(first, half), :] = value.astype(BF16)
        if step == stages - 1:
            sum_ref[pl.ds(first, half), :] = value.astype(BF16)

    def doubling(part, step):
        first, size_of = segment(part, step + 1)
        spot = pl.ds(pl.multiple_of(first, size_of), size_of)
        return remote_copy(
            sum_ref.at[spot], sum_ref.at[spot],
            total_sems.at[part, 1, step, 0], total_sems.at[part, 1, step, 1], "dp",
            flip(me, dp_bits[step], size),
        )

    def sum_stage(part, stage):
        if 0 < stage <= stages:
            halving(part, stage - 1).wait()
            add_half(part, stage - 1)
        elif stage > stages:
            doubling(part, 2 * stages - stage).wait()
        if stage < stages:
            halving(part, stage).start()
        elif stage < 2 * stages:
            doubling(part, 2 * stages - 1 - stage).start()

    def group_step(step, carry):
        @pl.when(step == groups - 1)
        def _():
            far_copy(1).start()

        attend_group(step)

        @pl.when(step == 0)
        def _():
            send_made(1)
            qkv_copy(0).start()
            small_step(0, early_ref, early_got, 1)
            out_copy(0).wait_recv()
            add_into(wo.at[2], wo_got.at[0])
            out_copy(2).start()

        @pl.when(step == 1)
        def _():
            send_made(2)
            qkv_copy(0).wait_recv()
            for c in range(3):
                add_into(wg.at[1, c], wg_got.at[0, c])
            qkv_copy(2).start()
            small_step(0, early_ref, early_got, 2)

        @pl.when(step == 2)
        def _():
            qkv_copy(1).start()
            small_step(0, early_ref, early_got, 3)
            out_copy(1).wait_recv()
            out_copy(2).wait_recv()
            add_into(wo.at[0], wo_got.at[1], wo_got.at[2])
            total[3 * third :, :] = wo[0]
            sum_stage(3, 0)

        return carry

    lax.fori_loop(0, groups, group_step, 0)
    sum_stage(3, 1)

    small_step(0, early_ref, early_got, 4)
    unit, recip = unit_norm(tok[...].astype(F32))
    gain_grad = jnp.sum(norm_grad[...] * unit, 0, keepdims=True)
    table_grad = 0.0
    for k in range(8):
        for piece in split_three(diag_sums[:, k, :]):
            table_grad = table_grad + dot_nt(piece.astype(BF16), ones_ref[:, k * TILE : (k + 1) * TILE])
    late_ref[0] = jnp.zeros(late_ref.shape[1:], F32)
    for k in range(width // TILE):
        late_ref[0, k : k + 1, :] = gain_grad[:, k * TILE : (k + 1) * TILE]
    heads, buckets = table_grad.shape
    late_ref[0, 8 : 8 + heads, :buckets] = table_grad
    small_step(1, late_ref, late_got, 0)

    qkv_copy(1).wait_recv()
    qkv_copy(2).wait()
    def finish_tokens():
        scaled = norm_grad[...] * gain_ref[0:1, :]
        back = recip * (scaled - unit * jnp.mean(scaled * unit, -1, keepdims=True))
        grad_ref[...] = (grad_hidden[...] + back).astype(BF16)
        hidden_again.start()
        if not remote_made:
            loads[8].start()

    def finish_output():
        loads[8].wait()
        hidden_again.wait()
        if remote_made:
            for _, peer in peers:
                made_copy(me, peer, peer).wait_recv()
        values = made[...].reshape(experts * capacity, width) if remote_made else rows[...]
        for first in range(0, count, 256):
            spot = slice(first, first + 256)
            value = hidden[spot, :]
            for k in range(2):
                hit = onehot_columns(slots[k][spot], 0, experts * capacity)
                value = value + gates[k][spot] * dot_nn(hit.astype(F32).astype(BF16), values)
            output_ref[spot, :] = value.astype(BF16)

    rest_early = list(range(groups + 1, len(exchanges) + 1))
    rest_late = list(range(1, len(exchanges) + 1))

    def next_small():
        if rest_early:
            small_step(0, early_ref, early_got, rest_early.pop(0))
        if rest_late:
            small_step(1, late_ref, late_got, rest_late.pop(0))

    for time in range(3 + 2 * stages):
        for part in range(min(3, time + 1)):
            if time == part:
                add_into(
                    total.at[part * third : (part + 1) * third], wg_got.at[1, part], wg_got.at[2, part]
                )
            if time - part <= 2 * stages:
                sum_stage(part, time - part)
        if time + 2 <= 2 * stages:
            sum_stage(3, time + 2)
        if time == 0:
            finish_tokens()
        elif time == 1:
            finish_output()
        elif time == 2:
            far_copy(1).wait()
            far_copy(2).start()
        next_small()
    while rest_early or rest_late:
        next_small()
    saves = [
        pltpu.make_async_copy(sum_ref.at[pl.ds(0, 3 * third)], sum_out, load_sems.at[10]),
        pltpu.make_async_copy(sum_ref.at[pl.ds(3 * third, third)], sum_out_two, load_sems.at[11]),
    ]
    for copy in saves:
        copy.start()
    last = len(exchanges) % 2
    router_out[...] = early_ref[last, :experts, :]
    gains_out[1:2, :] = early_ref[last, experts : experts + 1, :]
    for k in range(width // TILE):
        gains_out[0:1, k * TILE : (k + 1) * TILE] = late_ref[last, k : k + 1, :]
    table_out[...] = late_ref[last, 8 : 8 + heads, :buckets]
    for copy in saves:
        copy.wait()
    far_copy(0).wait()
    far_copy(2).wait()
    if remote_made:
        for _, peer in peers:
            made_copy(peer, me, peer).wait_send()
    for kind in range(3):
        out_copy(kind).wait_send()
    for kind in range(2):
        qkv_copy(kind).wait_send()


def bits_below(size):
    return [1 << b for b in range(size.bit_length() - 1)]


def rear(
    span, gains, table_t, ones, router_t3, slots_col, gates, extra, tokens, cotangent, hidden, normed,
    mixed, rows, made, out_weights, qkv_weights, qkv, expert_sums, head_size,
):
    count, width = tokens.shape
    size, groups = lax.axis_size("dp"), lax.axis_size("wshard")
    heads, buckets = width // head_size, ones.shape[0]
    experts = router_t3.shape[0] // 3
    cols = out_weights.shape[2]
    exchanges = len(bits_below(size)) + len(bits_below(groups))
    dma = pltpu.SemaphoreType.DMA
    wide, small = (count, width), (experts + EXTRA, width)
    late = (8 + heads, TILE)
    total = (4 * width, cols)
    vmem = pltpu.VMEM
    return pl.pallas_call(
        functools.partial(rear_body, size, groups, head_size, made.ndim == 3),
        out_shape=(
            shape_of(wide, BF16),
            shape_of(wide, BF16),
            shape_of((2, width), F32),
            shape_of((heads, buckets), F32),
            shape_of((experts, width), F32),
            shape_of((3 * width, cols), BF16),
            shape_of((width, cols), BF16),
            shape_of(expert_sums.shape[1:], BF16),
        ),
        in_specs=[SMEM] + [VMEM] * 7 + [ANY] * 11,
        out_specs=(VMEM,) * 5 + (ANY,) * 3,
        scratch_shapes=[
            vmem(wide, BF16),
            vmem(wide, BF16),
            vmem(wide, F32),
            vmem(wide, BF16),
            vmem(wide, BF16),
            vmem(rows.shape, BF16),
            vmem(made.shape if made.ndim == 3 else (16, TILE), BF16),
            vmem(out_weights.shape, BF16),
            vmem((2, *qkv_weights.shape[1:]), BF16),
            vmem(qkv.shape, BF16),
            vmem((width, count), BF16),
            vmem((count, count), F32),
            vmem(wide, F32),
            vmem((3, count, cols), BF16),
            vmem((2, count, count), BF16),
            vmem((2, count, count), BF16),
            vmem((heads, 8, TILE), F32),
            vmem((groups, width, cols), BF16),
            vmem((3, width, cols), BF16),
            vmem((groups - 1, 3, width, cols), BF16),
            vmem((3, 3, width, cols), BF16),
            vmem(total, BF16),
            vmem(total, BF16),
            vmem(total, BF16),
            vmem((2, *small), F32),
            vmem((exchanges, *small), F32),
            vmem((2, *late), F32),
            vmem((exchanges, *late), F32),
            vmem((heads, ones.shape[1]), F32),
            dma((12,)),
            dma((2,)),
            dma((size,)),
            dma((size,)),
            dma((2, 3, 2)),
            dma((4, 2, len(bits_below(size)), 2)),
            dma((2, exchanges, 2)),
            dma((3, 2)),
        ],
        cost_estimate=pl.CostEstimate(flops=LIGHT, bytes_accessed=LIGHT, transcendentals=0),
        compiler_params=pltpu.CompilerParams(
            collective_id=2, has_side_effects=True, vmem_limit_bytes=66_000_000
        ),
        name="rear",
    )(
        span, gains, table_t, ones, router_t3, slots_col, gates, extra, tokens, cotangent, hidden,
        normed, mixed, rows, made, out_weights, qkv_weights, qkv, expert_sums,
    )


def result_body(
    in_ref, far_in_ref, down_ref, far_down_ref, qkv_ref, out_ref, output_ref, tokens_ref, gains_ref,
    table_ref, router_ref,
    in_out, down_out, qkv_out, out_out, output_out, tokens_out, gains_out, table_out, router_out,
):
    for c in range(2):
        in_out[c] = in_ref[0, c].astype(F32) + far_in_ref[c].astype(F32)
    down_out[...] = down_ref[0, 0].astype(F32) + far_down_ref[0].astype(F32)
    qkv_out[...] = qkv_ref[...].astype(F32)
    out_out[...] = out_ref[...].astype(F32)
    output_out[...] = output_ref[...]
    tokens_out[...] = tokens_ref[...]
    gains_out[...] = gains_ref[...]
    table_out[...] = table_ref[...]
    router_out[...] = router_ref[...]


def results(expert_sums, far_got, qkv_sum, out_sum, output, grad_tokens, *small, steps=4):
    share, width = far_got.shape[1:]
    part = share // steps

    def rows_of(array):
        return pl.BlockSpec((array.shape[0] // steps, array.shape[1]), lambda i: (i, 0))

    def whole(array):
        return pl.BlockSpec(array.shape, lambda i: (0, 0))

    tall = (qkv_sum, out_sum, output, grad_tokens)
    return pl.pallas_call(
        result_body,
        grid=(steps,),
        out_shape=(
            shape_of((2, share, width), F32),
            shape_of((share, width), F32),
            shape_of(qkv_sum.shape, F32),
            shape_of(out_sum.shape, F32),
            shape_of(output.shape, BF16),
            shape_of(grad_tokens.shape, BF16),
        )
        + tuple(shape_of(a.shape, F32) for a in small),
        in_specs=[
            pl.BlockSpec((1, 2, part, width), lambda i: (0, 0, i, 0)),
            pl.BlockSpec((2, part, width), lambda i: (0, i, 0)),
            pl.BlockSpec((1, 1, part, width), lambda i: (0, 2, i, 0)),
            pl.BlockSpec((1, part, width), lambda i: (2, i, 0)),
        ]
        + [rows_of(a) for a in tall]
        + [whole(a) for a in small],
        out_specs=(
            pl.BlockSpec((2, part, width), lambda i: (0, i, 0)),
            pl.BlockSpec((part, width), lambda i: (i, 0)),
        )
        + tuple(rows_of(a) for a in tall)
        + tuple(whole(a) for a in small),
        cost_estimate=pl.CostEstimate(flops=LIGHT, bytes_accessed=LIGHT, transcendentals=0),
        name="results",
    )(expert_sums, far_got, expert_sums, far_got, *tall, *small)


def swap(value, axis, bit):
    size = lax.axis_size(axis)
    return lax.ppermute(value, axis, [(i, i ^ bit) for i in range(size)])


def bits_of(axis):
    size = lax.axis_size(axis)
    return [1 << b for b in range(size.bit_length() - 1)]


def after(value, *others):
    return lax.optimization_barrier((value, *others))[0]


def exchange(rows, axis):
    size = lax.axis_size(axis)
    total, width = rows.shape
    blocks = rows.reshape(size, total // size, width)
    return lax.all_to_all(blocks, axis, 0, 0, tiled=True)


def per_device(
    tokens,
    cotangent,
    span_starts,
    routes,
    norm_gains,
    bias_table,
    router,
    attn_qkv,
    attn_out,
    expert_in,
    expert_down,
):
    assert span_starts.shape[0] == 1
    tok_count, model_width = tokens.shape
    buckets, head_count = bias_table.shape
    head_size = model_width // head_count
    experts = router.shape[1]
    capacity = (10 * tok_count + 4 * experts - 1) // (4 * experts)
    total = experts * capacity
    place = lax.axis_index("wshard")
    where = jnp.stack([place.astype(I32), span_starts[0]])
    ones = jnp.asarray(diagonal_ones(buckets), BF16)
    table_t = bias_table.T
    router_t = router.T
    expert_in = jnp.swapaxes(expert_in[0], 1, 2)
    expert_down = expert_down[0]

    shards = (attn_qkv, attn_out, expert_in)
    (
        slots_col, gates, sent_gates, qkv_all, out_all, qkv, mixed, hidden, normed_two, sent,
        outer_rows, far_gate,
    ) = front(
        span_starts, routes, norm_gains, table_t, ones, router_t, tokens, cotangent, shards, head_size,
        capacity,
    )
    groups = out_all.shape[0]
    through = moe if capacity % 16 == 0 else moe_plain
    back_rows, back_extra, made, expert_grads = through(
        sent, sent_gates, outer_rows, expert_in, expert_down, far_gate
    )
    if through is moe_plain:
        made = exchange(made.reshape(total, model_width), "dp").reshape(total, model_width)

    output, grad_tokens, grad_gains, table_grad, router_grad, qkv_sum, out_sum, far_got = rear(
        span_starts, norm_gains, table_t, ones, jnp.concatenate([router_t] * 3, 0),
        slots_col, gates, back_extra, tokens, cotangent, hidden, normed_two,
        mixed, back_rows.reshape(total, model_width), made, out_all, qkv_all, qkv, expert_grads,
        head_size,
    )

    (
        in_grad, down_grad, qkv_sum, out_sum, output, grad_tokens, grad_gains, table_grad, router_grad,
    ) = results(
        expert_grads, far_got, qkv_sum, out_sum, output, grad_tokens, grad_gains, table_grad,
        router_grad,
    )
    return (
        output,
        grad_tokens,
        grad_gains,
        table_grad.T,
        router_grad.T,
        qkv_sum.reshape(3, model_width, out_sum.shape[1]),
        out_sum,
        jnp.swapaxes(in_grad, 1, 2)[None],
        down_grad[None],
    )


def solution(mesh):
    return jax.shard_map(
        per_device,
        mesh=mesh,
        in_specs=(
            P(("dp", "wshard"), None),
            P(("dp", "wshard"), None),
            P(("dp", "wshard")),
            P(("dp", "wshard"), None),
            P(),
            P(),
            P(),
            P(None, None, "wshard"),
            P(None, "wshard"),
            P("dp", None, None, "wshard"),
            P("dp", "wshard", None),
        ),
        out_specs=(
            P(("dp", "wshard"), None),
            P(("dp", "wshard"), None),
            P(),
            P(),
            P(),
            P(None, None, "wshard"),
            P(None, "wshard"),
            P("dp", None, None, "wshard"),
            P("dp", "wshard", None),
        ),
        check_vma=False,
    )
```

```python
import functools

import jax
import jax.numpy as jnp
import numpy as np
from jax import lax
from jax.experimental import pallas as pl
from jax.experimental.pallas import tpu as pltpu
from jax.sharding import PartitionSpec as P

PIC = 256
PRECISE = lax.Precision.HIGHEST
EPSILON = 1e-06
MASKED_SCORE = -1e30
BUCKET_EDGES = (8, 11, 16, 23, 32, 45, 64, 91)
TILE = 128
F32 = jnp.float32
BF16 = jnp.bfloat16
I32 = jnp.int32
VMEM = pl.BlockSpec(memory_space=pltpu.VMEM)
SMEM = pl.BlockSpec(memory_space=pltpu.SMEM)
ANY = pl.BlockSpec(memory_space=pl.ANY)
LIGHT = 1024
EXTRA = 8


def dot_nn(a, b):
    return lax.dot_general(a, b, (((1,), (0,)), ((), ())), preferred_element_type=F32)


def dot_nt(a, b):
    return lax.dot_general(a, b, (((1,), (1,)), ((), ())), preferred_element_type=F32)


def dot_tn(a, b):
    return lax.dot_general(a, b, (((0,), (0,)), ((), ())), preferred_element_type=F32)


def iota(shape, axis):
    return lax.broadcasted_iota(I32, shape, axis)


def shape_of(shape, dtype):
    return jax.ShapeDtypeStruct(shape, dtype)


def call(body, out, args, specs, scratch=(), name=None):
    return pl.pallas_call(
        body,
        out_shape=out,
        in_specs=specs,
        out_specs=jax.tree.map(lambda _: VMEM, out),
        scratch_shapes=list(scratch),
        cost_estimate=pl.CostEstimate(flops=LIGHT, bytes_accessed=LIGHT, transcendentals=0),
        name=name,
    )(*args)


def bucket_of(offset):
    magnitude = np.abs(offset)
    coarse = 7 + sum((magnitude >= bound).astype(np.int32) for bound in BUCKET_EDGES)
    return np.where(magnitude < 8, magnitude, coarse) + 16 * (offset < 0)


def diagonal_ones(bucket_count):
    column = np.arange(2 * TILE)
    signed = np.where(column < TILE, column, column - 2 * TILE)
    offsets = np.concatenate([TILE * step - signed for step in (-1, 0, 1)])
    used = np.tile(column != TILE, 3)
    hit = bucket_of(offsets)[None, :] == np.arange(bucket_count)[:, None]
    near = (hit & used[None, :]).astype(np.float32)
    far = np.zeros((bucket_count, 2 * TILE), np.float32)
    far[bucket_of(np.array(TILE)), :TILE] = 1
    far[bucket_of(np.array(-TILE)), TILE:] = 1
    return np.concatenate([near, far], 1)


def onehot_rows(first, count, slots_row):
    index = iota((count, slots_row.shape[1]), 0) + first
    hit = (index == slots_row[0:1, :]) | (index == slots_row[1:2, :])
    return hit.astype(F32).astype(BF16)


def onehot_columns(slots_column, first, count):
    index = iota((slots_column.shape[0], count), 1) + first
    return index == slots_column


def route_slots(experts, capacity, routes):
    tokens = routes.shape[1]
    label = iota((experts, tokens), 0)
    hits = ((routes[0:1] == label) | (routes[1:2] == label)).astype(F32).astype(BF16)
    earlier = iota((tokens, tokens), 0) < iota((tokens, tokens), 1)
    before = dot_nn(hits, earlier.astype(F32).astype(BF16))
    slots = []
    for k in range(2):
        own = jnp.sum(jnp.where(routes[k : k + 1] == label, before, 0.0), 0, keepdims=True)
        slots.append(own.astype(I32) + routes[k : k + 1] * capacity)
    return jnp.concatenate(slots * 4, 0)


def unit_norm(values):
    recip = lax.rsqrt(jnp.mean(values * values, -1, keepdims=True) + EPSILON)
    return values * recip, recip


def fill_mask(mask_ref, span_start):
    size = mask_ref.shape[0]
    i, j = iota((size, size), 0), iota((size, size), 1)

    def inside(p):
        return (p >= span_start) & (p < span_start + PIC)

    visible = (j <= i) | (inside(i) & inside(j))
    mask_ref[...] = jnp.where(visible, 0.0, MASKED_SCORE)


def head_lanes(which, size):
    lane = iota((1, 2 * size), 1)
    return ((lane >= size) == (which == 1)).astype(F32).astype(BF16)


def spread_bias(table_ref, ones_ref):
    pieces = [dot_nn(piece.astype(BF16), ones_ref[...]) for piece in split_three(table_ref[...])]
    return pieces[0] + pieces[1] + pieces[2]


def bias_tiles(diag_row):
    tiles = []
    for step in range(3):
        row = diag_row[:, 2 * TILE * step : 2 * TILE * (step + 1)]
        wide = jnp.broadcast_to(row, (TILE, 2 * TILE))
        tiles.append(pltpu.roll(wide, 0, 1, stride=1, stride_axis=0)[:, :TILE])
    return tiles, (diag_row[:, 6 * TILE : 7 * TILE], diag_row[:, 7 * TILE :])


def score_tiles(block, query, keys, tiles, far, mask_ref):
    raw = dot_nt(query, keys)
    rows = slice(block * TILE, (block + 1) * TILE)
    result = []
    for other in range(keys.shape[0] // TILE):
        piece = raw[:, other * TILE : (other + 1) * TILE]
        step = block - other
        piece = piece + (far[0] if step >= 2 else far[1] if step <= -2 else tiles[step + 1])
        if step <= 0:
            piece = piece + mask_ref[rows, other * TILE : (other + 1) * TILE]
        result.append(piece)
    return result


def softmax_tiles(pieces):
    top = functools.reduce(jnp.maximum, pieces)
    top = jnp.max(top, -1, keepdims=True)
    powers = [jnp.exp(piece - top) for piece in pieces]
    total = jnp.sum(functools.reduce(jnp.add, powers), -1, keepdims=True)
    scale = 1.0 / total
    return [power * scale for power in powers]


def split_three(value):
    high = value.astype(BF16).astype(F32)
    middle = (value - high).astype(BF16).astype(F32)
    return high, middle, value - high - middle


def remote_copy(source, target, sent, got, axis, peer):
    return pltpu.make_async_remote_copy(
        src_ref=source,
        dst_ref=target,
        send_sem=sent,
        recv_sem=got,
        device_id={axis: peer},
        device_id_type=pl.DeviceIdType.MESH,
    )


def turns_of(size):
    half, quarter = size // 2, size // 4
    return range(half, half + quarter), range(half + quarter, size), range(1, half)


def greet(peers):
    barrier = pltpu.get_barrier_semaphore()
    for axis, peer in peers:
        pl.semaphore_signal(
            barrier, inc=1, device_id={axis: peer}, device_id_type=pl.DeviceIdType.MESH
        )
    pl.semaphore_wait(barrier, len(peers))


def project_and_attend(place, group, groups, head_size, norm, diag_ref, w_ref, qkv_ref, mix_ref, mask):
    count = norm.shape[0]
    cols = w_ref.shape[-1]
    width = 2 * head_size
    owner = flip(place, group, groups)
    for c in range(3):
        qkv_ref[group, c] = dot_nn(norm[...], w_ref[group, c]).astype(BF16)

    def pair(p, carry):
        offset = pl.multiple_of(p * width, width)
        lanes = pl.ds(offset, width)
        query, keys, value = (qkv_ref[group, c, :, lanes] for c in range(3))
        mixed = [None] * (count // TILE)
        for which in range(2):
            head = owner * (cols // head_size) + 2 * p + which
            own = head_lanes(which, head_size)
            own_query, own_value = query * (own * 0.125), value * own
            tiles, far = bias_tiles(diag_ref[pl.ds(head, 1), :])
            for block in range(count // TILE):
                rows = slice(block * TILE, (block + 1) * TILE)
                pieces = score_tiles(block, own_query[rows], keys, tiles, far, mask)
                probs = jnp.concatenate([t.astype(BF16) for t in softmax_tiles(pieces)], 1)
                part = dot_nn(probs, own_value)
                mixed[block] = part if which == 0 else mixed[block] + part
        target = pl.ds(pl.multiple_of(owner * cols + offset, width), width)
        for block in range(count // TILE):
            rows = slice(block * TILE, (block + 1) * TILE)
            mix_ref[rows, target] = mixed[block].astype(BF16)
        return carry

    lax.fori_loop(0, cols // width, pair, 0)


def front_body(
    size, groups, head_size, span_ref, routes_ref, gain_ref, table_ref, ones_ref, router_ref, tok_hbm,
    cot_hbm,
    qkv_shard, out_shard, in_shard,
    col_ref, gate_ref, sent_gate_ref, qkvw_out, outw_out, qkv_out, mixed_out, hidden_out, norm_out,
    sent_out, outer_out, gate_out,
    tok, cot, qkvw, outw, qkv, mixed, hidden, norm, sent, outer, mask, row, diag_ref, load_sems, save_sems,
    shard_sems, outer_send, outer_got,
):
    me, place = lax.axis_index("dp"), lax.axis_index("wshard")
    near, far = flip(place, 1, groups), flip(place, 2, groups)
    peers = [("dp", flip(me, step, size)) for step in range(1, size)]
    greet(peers + [("wshard", near), ("wshard", far)])

    sources = (qkv_shard, out_shard, in_shard.at[0, : gate_out.shape[1]])

    def held(item, group):
        if item == 0:
            return qkvw.at[group]
        if item == 1:
            return outw.at[group]
        return gate_out.at[group - 2]

    def shard_copy(kind, item):
        source = held(item, 2) if kind == 2 else sources[item]
        return remote_copy(
            source, held(item, (1, 2, 3)[kind]), shard_sems.at[kind, item, 0],
            shard_sems.at[kind, item, 1], "wshard", far if kind == 1 else near,
        )

    shard_copy(1, 0).start()
    for item in range(2):
        shard_copy(0, item).start()
    loads = [
        pltpu.make_async_copy(source, target, load_sems.at[i])
        for i, (source, target) in enumerate(
            ((cot_hbm, cot), (tok_hbm, tok), (qkv_shard, qkvw.at[0]), (out_shard, outw.at[0]))
        )
    ]
    for copy in loads:
        copy.start()

    experts, capacity = size, sent.shape[1]
    count = tok.shape[0]
    slots = route_slots(experts, capacity, routes_ref[...])
    row[...] = slots
    col_ref[...] = slots.astype(F32).T.astype(I32)
    loads[0].wait()

    def place_outer(expert, carry):
        outer[expert] = dot_nn(onehot_rows(expert * capacity, capacity, row[...]), cot[...]).astype(BF16)
        return carry

    lax.fori_loop(0, experts, place_outer, 0)
    fill_mask(mask, span_ref[0])
    diag_ref[...] = spread_bias(table_ref, ones_ref)
    loads[1].wait()
    unit, _ = unit_norm(tok[...].astype(F32))
    norm[...] = (unit * gain_ref[0:1, :]).astype(BF16)
    loads[2].wait()

    def outer_copy(source, target, peer):
        return remote_copy(
            outer.at[source], outer_out.at[target], outer_send.at[source], outer_got.at[target],
            "dp", peer,
        )

    own_outer = pltpu.make_async_copy(outer.at[me], outer_out.at[me], load_sems.at[4])
    own_outer.start()
    turns = turns_of(size)

    def send_outer(turn):
        for step in turns[turn]:
            peer = flip(me, step, size)
            outer_copy(peer, me, peer).start()

    send_outer(0)

    def one_group(group, carry):
        @pl.when(group == 1)
        def _():
            send_outer(1)
            shard_copy(0, 0).wait_recv()

        @pl.when(group == 2)
        def _():
            shard_copy(1, 0).wait()
            shard_copy(2, 0).start()
            shard_copy(1, 1).start()

        @pl.when(group == 3)
        def _():
            send_outer(2)
            shard_copy(2, 0).wait_recv()

        project_and_attend(
            place, group, groups, head_size, norm, diag_ref, qkvw, qkv, mixed, mask
        )
        return carry

    lax.fori_loop(0, groups, one_group, 0)
    saves = [
        pltpu.make_async_copy(source, target, save_sems.at[i])
        for i, (source, target) in enumerate(
            (
                (qkvw, qkvw_out), (qkv, qkv_out), (mixed, mixed_out), (outw, outw_out),
                (hidden, hidden_out), (norm, norm_out), (sent, sent_out),
            )
        )
    ]
    for copy in saves[:3]:
        copy.start()
    loads[3].wait()
    shard_copy(0, 1).wait_recv()
    shard_copy(1, 1).wait()
    shard_copy(2, 1).start()
    shard_copy(1, 2).start()

    shard_copy(2, 1).wait_recv()
    saves[3].start()
    for group in range(groups):
        cols = outw.shape[2]
        lanes = pl.ds(pl.multiple_of(flip(place, group, groups) * cols, cols), cols)
        hidden[:, lanes] = tok[:, lanes].astype(F32) + dot_nn(mixed[...], outw[group])
    saves[4].start()
    unit, _ = unit_norm(hidden[...])
    norm[...] = (unit * gain_ref[1:2, :]).astype(BF16)
    saves[5].start()

    def place_sent(expert, carry):
        sent[expert] = dot_nn(onehot_rows(expert * capacity, capacity, row[...]), norm[...]).astype(BF16)
        return carry

    lax.fori_loop(0, experts, place_sent, 0)
    saves[6].start()
    logits = dot_nt(norm[...], router_ref[...])
    slots = [col_ref[:, k : k + 1] for k in range(2)]
    lane = iota(logits.shape, 1)
    chosen = []
    for k in range(2):
        own = (lane * capacity <= slots[k]) & (slots[k] < (lane + 1) * capacity)
        chosen.append(jnp.sum(jnp.where(own, logits, 0.0), -1, keepdims=True))
    top = jnp.maximum(chosen[0], chosen[1])
    powers = [jnp.exp(c - top) for c in chosen]
    gates = [power / (powers[0] + powers[1]) for power in powers]
    for k in range(2):
        gate_ref[:, k : k + 1] = gates[k]
    lane = iota((count, sent_gate_ref.shape[2]), 1)
    for expert in range(experts):
        label = jnp.where(lane < capacity, lane + expert * capacity, -1)
        part = 0.0
        for k in range(2):
            part = part + jnp.where(label == slots[k], gates[k], 0.0)
        line = jnp.sum(part, 0, keepdims=True)
        sent_gate_ref[expert] = jnp.broadcast_to(line, sent_gate_ref.shape[1:])

    shard_copy(1, 2).wait()
    shard_copy(2, 2).start()
    own_outer.wait()
    for copy in saves:
        copy.wait()
    for _, peer in peers:
        outer_copy(peer, me, peer).wait_send()
        outer_copy(me, peer, peer).wait_recv()
    for item in range(2):
        shard_copy(0, item).wait_send()
        shard_copy(2, item).wait_send()
    shard_copy(2, 2).wait()


def front(
    span, routes, gains, table_t, ones, router_t, tokens, cotangent, shards, head_size, capacity
):
    count, width = tokens.shape
    size, groups = lax.axis_size("dp"), lax.axis_size("wshard")
    qkv_shard, out_shard, in_shard = shards
    cols = out_shard.shape[1]
    lanes = -(-capacity // TILE) * TILE
    dma = pltpu.SemaphoreType.DMA
    block = (size, capacity, width)
    return pl.pallas_call(
        functools.partial(front_body, size, groups, head_size),
        out_shape=(
            shape_of((count, 8), I32),
            shape_of((count, 2), F32),
            shape_of((size, EXTRA, lanes), F32),
            shape_of((groups, *qkv_shard.shape), BF16),
            shape_of((groups, *out_shard.shape), BF16),
            shape_of((groups, 3, count, cols), BF16),
            shape_of((count, width), BF16),
            shape_of((count, width), F32),
            shape_of((count, width), BF16),
            shape_of(block, BF16),
            shape_of(block, BF16),
            shape_of((2, in_shard.shape[1] // 32 * 16, width), BF16),
        ),
        in_specs=[SMEM] + [VMEM] * 5 + [ANY] * 5,
        out_specs=(VMEM,) * 3 + (ANY,) * 9,
        scratch_shapes=[
            pltpu.VMEM((count, width), BF16),
            pltpu.VMEM((count, width), BF16),
            pltpu.VMEM((groups, *qkv_shard.shape), BF16),
            pltpu.VMEM((groups, *out_shard.shape), BF16),
            pltpu.VMEM((groups, 3, count, cols), BF16),
            pltpu.VMEM((count, width), BF16),
            pltpu.VMEM((count, width), F32),
            pltpu.VMEM((count, width), BF16),
            pltpu.VMEM(block, BF16),
            pltpu.VMEM(block, BF16),
            pltpu.VMEM((count, count), F32),
            pltpu.VMEM((8, count), I32),
            pltpu.VMEM((table_t.shape[0], ones.shape[1]), F32),
            dma((5,)),
            dma((7,)),
            dma((3, 3, 2)),
            dma((size,)),
            dma((size,)),
        ],
        cost_estimate=pl.CostEstimate(flops=LIGHT, bytes_accessed=LIGHT, transcendentals=0),
        compiler_params=pltpu.CompilerParams(
            collective_id=1, has_side_effects=True, vmem_limit_bytes=60_000_000
        ),
        name="front",
    )(span, routes.T, gains, table_t, ones, router_t, tokens, cotangent, *shards)


def flip(value, change, size):
    result = 0
    bit = 1
    while bit < size:
        one, two = lax.rem(lax.div(value, bit), 2), lax.rem(lax.div(change, bit), 2)
        result = result + bit * (one + two - 2 * one * two)
        bit *= 2
    return result


def column_of(row, size):
    spot = iota((size, row.shape[1]), 0) == iota((size, row.shape[1]), 1)
    return jnp.sum(jnp.where(spot, row, 0.0), 1, keepdims=True)


def row_of(column, lanes):
    spot = iota((column.shape[0], lanes), 0) == iota((column.shape[0], lanes), 1)
    return jnp.sum(jnp.where(spot, column, 0.0), 0, keepdims=True)


def moe_body(
    size, groups, chunk, sent_ref, gates_ref, outer_ref, own_in, own_down, far_gate, *refs
):
    back_out, extra_out, made_out, grad_out, moved_out = refs[:5]
    (
        buf, rows, gates, outer, low_outer, made_sum, back_sum, act, low, stage, extra_stage,
        made, grad_stage, weight_sems, shard_sems, send_sems, recv_sems, give_sems, take_sems, own_sems,
        save_sems, grad_sems, moved_sem, sum_sems,
    ) = refs[5:]
    share = own_down.shape[0]
    part_size = share * groups // 2
    capacity, width = outer.shape[1:]
    both = 2 * capacity
    me = lax.axis_index("dp")
    pairs = size // 2
    my_pair = lax.div(me, 2)
    mesh_id = pl.DeviceIdType.MESH

    place = lax.axis_index("wshard")
    near, far = flip(place, 1, groups), flip(place, 2, groups)
    peers = [("dp", flip(me, step, size)) for step in range(1, size)]
    greet(peers + [("wshard", near), ("wshard", far)])

    def remote(source, target, sent, got, peer):
        return pltpu.make_async_remote_copy(
            src_ref=source, dst_ref=target, send_sem=sent, recv_sem=got,
            device_id={"dp": peer}, device_id_type=mesh_id,
        )

    def forth(source, target, peer):
        return (
            remote(sent_ref.at[source], rows.at[target], send_sems.at[source, 0],
                   recv_sems.at[target, 0], peer),
            remote(gates_ref.at[source], gates.at[target], send_sems.at[source, 1],
                   recv_sems.at[target, 1], peer),
        )

    def back_copies(source, target, peer):
        return (
            remote(stage.at[source], back_out.at[target], give_sems.at[source, 0],
                   take_sems.at[target, 0], peer),
            remote(extra_stage.at[source], extra_out.at[target], give_sems.at[source, 1],
                   take_sems.at[target, 1], peer),
        )

    own = (
        pltpu.make_async_copy(sent_ref.at[me], rows.at[me], own_sems.at[0]),
        pltpu.make_async_copy(gates_ref.at[me], gates.at[me], own_sems.at[1]),
        pltpu.make_async_copy(outer_ref, outer, own_sems.at[2]),
    )
    own_back = (
        pltpu.make_async_copy(stage.at[me], back_out.at[me], own_sems.at[3]),
        pltpu.make_async_copy(extra_stage.at[me], extra_out.at[me], own_sems.at[4]),
    )
    for copy in own:
        copy.start()
    turns = turns_of(size)

    def send_rows(steps):
        for step in steps:
            peer = flip(me, step, size)
            for copy in forth(peer, me, peer):
                copy.start()

    send_rows(turns[2])
    send_rows(turns[0])

    begun = far_gate.shape[1]

    def home(c, group, first, count):
        return buf.at[c, pl.ds(group * share + first, count)]

    loads = [
        pltpu.make_async_copy(own_in, buf.at[0:2, pl.ds(0, share)], weight_sems.at[0]),
        pltpu.make_async_copy(own_down, home(2, 0, 0, share), weight_sems.at[1]),
    ]
    loads += [
        pltpu.make_async_copy(far_gate.at[i], home(0, 2 + i, 0, begun), weight_sems.at[2 + i])
        for i in range(2)
    ]
    near_copies = [
        remote_copy(own_in, buf.at[0:2, pl.ds(share, share)], shard_sems.at[0, 0, 0],
                    shard_sems.at[0, 0, 1], "wshard", near),
        remote_copy(own_down, home(2, 1, 0, share), shard_sems.at[0, 1, 0],
                    shard_sems.at[0, 1, 1], "wshard", near),
    ]
    rest = ((0, begun, share - begun), (1, 0, share), (2, 0, share))

    def far_copy(c):
        _, first, count = rest[c]
        source = own_down if c == 2 else own_in.at[c]
        return remote_copy(source.at[pl.ds(first, count)], home(c, 2, first, count),
                           shard_sems.at[1, c, 0], shard_sems.at[1, c, 1], "wshard", far)

    def onward_copy(c):
        _, first, count = rest[c]
        return remote_copy(home(c, 2, first, count), home(c, 3, first, count),
                           shard_sems.at[2, c, 0], shard_sems.at[2, c, 1], "wshard", near)

    far_copy(0).start()
    far_copy(1).start()
    for copy in loads + near_copies:
        copy.start()
    for copy in own:
        copy.wait()

    def hidden_part(pair, base):
        spot = pl.ds(pl.multiple_of(pair * both, both), both)
        two = pl.ds(2 * pair, 2)
        these = rows[two].reshape(both, width)
        outers = low_outer[spot, :]
        for first in range(0, part_size, chunk):
            last = min(first + chunk, part_size)
            part, lanes = slice(base + first, base + last), slice(first, last)
            gate, up = dot_nt(these, buf[0, part, :]), dot_nt(these, buf[1, part, :])
            act_grad = dot_nt(outers, buf[2, part, :])
            square = gate * gate
            inner = gate * (0.7978845608028654 + (0.7978845608028654 * 0.044715) * square)
            rise = 0.5 + 0.5 * jnp.tanh(inner)
            bent = gate * rise
            act[spot, lanes] = (bent * up).astype(BF16)
            slope = rise + bent * (1.0 - rise) * (
                2 * 0.7978845608028654 + (6 * 0.7978845608028654 * 0.044715) * square
            )
            low[0, spot, lanes] = (act_grad * up * slope).astype(BF16)
            low[1, spot, lanes] = (act_grad * bent).astype(BF16)
        whole = slice(base, base + part_size)
        result = dot_nn(act[spot, :], buf[2, whole, :])
        back = dot_nn(low[0, spot, :], buf[0, whole, :]) + dot_nn(low[1, spot, :], buf[1, whole, :])
        return spot, result, back

    def near_step(step, carry):
        pair = flip(my_pair, step, pairs)
        first = 2 * pair

        @pl.when(step == 1)
        def _():
            send_rows(turns[1])

        @pl.when(step == pairs // 2)
        def _():
            for c in range(2):
                far_copy(c).wait()
                onward_copy(c).start()
            far_copy(2).start()

        @pl.when(step == 0)
        def _():
            peer = flip(me, 1, size)
            for copy in forth(me, peer, peer):
                copy.wait_recv()

        @pl.when(step > 0)
        def _():
            for which in range(2):
                for copy in forth(me, first + which, first + which):
                    copy.wait_recv()

        for which in range(2):
            gate = column_of(gates[first + which, 0:1, :], capacity)
            spot = pl.ds(pl.multiple_of((first + which) * capacity, capacity), capacity)
            low_outer[spot, :] = (outer[first + which].astype(F32) * gate).astype(BF16)
        spot, result, back = hidden_part(pair, 0)
        made_sum[spot, :] = result
        back_sum[spot, :] = back
        return carry

    def sent_all(copies):
        for remote_one, copy in copies:
            if remote_one:
                copy.wait_send()
            else:
                copy.wait()

    def weight_grads(half):
        every = rows[...].reshape(size * capacity, width)
        outers = low_outer[...]
        count = 0
        base = half * part_size
        waiting = {}
        for c in range(3):
            left = act if c == 2 else low.at[c]
            for first in range(0, part_size, 2 * chunk):
                last = min(first + 2 * chunk, part_size)
                slot = count % 2
                sent_all(waiting.pop(slot, ()))
                piece = dot_tn(left[:, first:last], outers if c == 2 else every)
                grad_stage[slot, : last - first, :] = piece.astype(BF16)
                copies = []
                begin = base + first
                while begin < base + last:
                    group = begin // share
                    end = min(base + last, (group + 1) * share)
                    source = grad_stage.at[slot, pl.ds(begin - base - first, end - begin)]
                    spot = pl.ds(begin - group * share, end - begin)
                    sem = grad_sems.at[slot, len(copies)]
                    if group % 2:
                        target = moved_out.at[group // 2, c, spot]
                        copies.append((True, remote_copy(source, target, sem, moved_sem, "wshard", near)))
                    else:
                        target = grad_out.at[group // 2, c, spot]
                        copies.append((False, pltpu.make_async_copy(source, target, sem)))
                    begin = end
                for _, copy in copies:
                    copy.start()
                waiting[slot] = copies
                count += 1
        for copies in waiting.values():
            sent_all(copies)

    for copy in loads[:2]:
        copy.wait()
    for copy in near_copies:
        copy.wait_recv()
    lax.fori_loop(0, pairs, near_step, 0)
    weight_grads(0)

    def far_step(step, carry):
        pair = flip(my_pair, pairs - 1 - step, pairs)
        first = 2 * pair
        spot, result, back = hidden_part(pair, part_size)
        result = (made_sum[spot, :] + result).astype(BF16)
        back = (back_sum[spot, :] + back).astype(BF16)
        two = pl.ds(first, 2)
        made[two] = result.reshape(2, capacity, width)
        stage[two] = back.reshape(2, capacity, width)
        for which in range(2):
            grads = outer[first + which].astype(F32) * made[first + which].astype(F32)
            line = row_of(jnp.sum(grads, -1, keepdims=True), extra_stage.shape[2])
            extra_stage[first + which] = jnp.broadcast_to(line, extra_stage.shape[1:])
        pltpu.make_async_copy(made.at[two], made_out.at[two], save_sems.at[step]).start()

        @pl.when(step < pairs - 1)
        def _():
            for which in range(2):
                for copy in back_copies(first + which, me, first + which):
                    copy.start()

        @pl.when(step == pairs - 1)
        def _():
            peer = flip(me, 1, size)
            for copy in back_copies(peer, me, peer):
                copy.start()
            for copy in own_back:
                copy.start()

        return carry

    far_copy(2).wait()
    onward_copy(2).start()
    for copy in loads[2:]:
        copy.wait()
    for c in range(3):
        onward_copy(c).wait_recv()
    lax.fori_loop(0, pairs, far_step, 0)
    weight_grads(1)
    remote_copy(moved_out, moved_out, moved_sem, moved_sem, "wshard", near).wait_recv()

    corner = (pl.ds(0, share), pl.ds(0, width))
    rooms = ((low.at[0], act), (low.at[1], low_outer))
    pieces = [(g, c) for g in (1, 0) for c in range(3)]

    def fetch(i):
        slot = i % 2
        return [
            pltpu.make_async_copy(source.at[pieces[i]], room.at[corner], sum_sems.at[slot, k])
            for k, (source, room) in enumerate(zip((grad_out, moved_out), rooms[slot]))
        ]

    def put(i):
        slot = i % 2
        return pltpu.make_async_copy(
            rooms[slot][0].at[corner], grad_out.at[pieces[i]], sum_sems.at[slot, 2]
        )

    for i in range(2):
        for copy in fetch(i):
            copy.start()
    for i in range(len(pieces)):
        for copy in fetch(i):
            copy.wait()
        one, other = rooms[i % 2]

        def add_rows(block, carry):
            spot = (pl.ds(pl.multiple_of(block * 64, 64), 64), slice(0, width))
            one[spot] = (one[spot].astype(F32) + other[spot].astype(F32)).astype(BF16)
            return carry

        lax.fori_loop(0, share // 64, add_rows, 0)
        put(i).start()
        if i + 2 < len(pieces):
            put(i).wait()
            for copy in fetch(i + 2):
                copy.start()
    for i in range(len(pieces) - 2, len(pieces)):
        put(i).wait()
    for copy in own_back:
        copy.wait()
    for copy in near_copies:
        copy.wait_send()
    for c in range(3):
        onward_copy(c).wait_send()
    for step in range(pairs):
        two = pl.ds(2 * flip(my_pair, pairs - 1 - step, pairs), 2)
        pltpu.make_async_copy(made.at[two], made_out.at[two], save_sems.at[step]).wait()
    for step in range(1, size):
        peer = flip(me, step, size)
        for copy in forth(peer, me, peer):
            copy.wait_send()
        for copy in back_copies(peer, me, peer):
            copy.wait_send()
        for copy in back_copies(me, peer, peer):
            copy.wait_recv()


def moe(sent, gates, outer, own_in, own_down, far_gate, chunk=256):
    size, capacity, width = sent.shape
    groups = lax.axis_size("wshard")
    share = own_down.shape[0]
    part = share * groups // 2
    total = size * capacity
    extra = gates.shape[1:]
    dma = pltpu.SemaphoreType.DMA
    result = pl.pallas_call(
        functools.partial(moe_body, size, groups, chunk),
        out_shape=(
            shape_of((size, capacity, width), BF16),
            shape_of((size, *extra), F32),
            shape_of((size, capacity, width), BF16),
        )
        + (shape_of((2, 3, share, width), BF16),) * 2,
        in_specs=[ANY] * 6,
        out_specs=(ANY,) * 5,
        scratch_shapes=[
            pltpu.VMEM((3, share * groups, width), BF16),
            pltpu.VMEM((size, capacity, width), BF16),
            pltpu.VMEM((size, *extra), F32),
            pltpu.VMEM((size, capacity, width), BF16),
            pltpu.VMEM((total, width), BF16),
            pltpu.VMEM((total, width), F32),
            pltpu.VMEM((total, width), F32),
            pltpu.VMEM((total, part), BF16),
            pltpu.VMEM((2, total, part), BF16),
            pltpu.VMEM((size, capacity, width), BF16),
            pltpu.VMEM((size, *extra), F32),
            pltpu.VMEM((size, capacity, width), BF16),
            pltpu.VMEM((2, 2 * chunk, width), BF16),
            dma((4,)),
            dma((3, 3, 2)),
            dma((size, 2)),
            dma((size, 2)),
            dma((size, 2)),
            dma((size, 2)),
            dma((5,)),
            dma((size // 2,)),
            dma((2, 3)),
            dma,
            dma((2, 3)),
        ],
        cost_estimate=pl.CostEstimate(flops=LIGHT, bytes_accessed=LIGHT, transcendentals=0),
        compiler_params=pltpu.CompilerParams(
            collective_id=0, has_side_effects=True, vmem_limit_bytes=66_000_000
        ),
        name="experts",
    )(sent, gates, outer, own_in, own_down, far_gate)
    return result[:4]


def expert_body(groups, chunk, rows_ref, outer_ref, gate_ref, *refs):
    in_refs, down_refs = refs[:groups], refs[groups : 2 * groups]
    made_ref, back_ref, outer_out_ref, gate_grad_ref = refs[2 * groups : 2 * groups + 4]
    act_ref, low_ref, buf_ref, sems = refs[2 * groups + 4 :]
    share = down_refs[0].shape[0]
    hidden = share * groups

    def copies(group):
        spot = pl.ds(group * share, share)
        return (
            pltpu.make_async_copy(in_refs[group], buf_ref.at[0:2, spot], sems.at[2 * group]),
            pltpu.make_async_copy(down_refs[group], buf_ref.at[2, spot], sems.at[2 * group + 1]),
        )

    @pl.when(pl.program_id(0) == 0)
    def _():
        for group in range(groups):
            for copy in copies(group):
                copy.start()

    rows = rows_ref[...]
    low_outer = (outer_ref[...].astype(F32) * gate_ref[...]).astype(BF16)
    outer_out_ref[...] = low_outer

    @pl.when(pl.program_id(0) == 0)
    def _():
        for group in range(groups):
            for copy in copies(group):
                copy.wait()

    for first in range(0, hidden, chunk):
        part = slice(first, first + chunk)
        gate, up = dot_nt(rows, buf_ref[0, part, :]), dot_nt(rows, buf_ref[1, part, :])
        act_grad = dot_nt(low_outer, buf_ref[2, part, :])
        square = gate * gate
        inner = gate * (0.7978845608028654 + (0.7978845608028654 * 0.044715) * square)
        rise = 0.5 + 0.5 * jnp.tanh(inner)
        bent = gate * rise
        act_ref[:, part] = (bent * up).astype(BF16)
        slope = rise + bent * (1.0 - rise) * (
            2 * 0.7978845608028654 + (6 * 0.7978845608028654 * 0.044715) * square
        )
        low_ref[0, :, part] = (act_grad * up * slope).astype(BF16)
        low_ref[1, :, part] = (act_grad * bent).astype(BF16)
    made = dot_nn(act_ref[...], buf_ref[2]).astype(BF16)
    made_ref[...] = made
    back = dot_nn(low_ref[0], buf_ref[0]) + dot_nn(low_ref[1], buf_ref[1])
    back_ref[...] = back.astype(BF16)
    gate_grad_ref[...] = jnp.sum(
        outer_ref[...].astype(F32) * made.astype(F32), -1, keepdims=True
    )


def experts_pass(rows, outer, gate_column, in_weights, down_weights, block=320, chunk=256):
    total, width = rows.shape
    groups = len(in_weights)
    hidden = down_weights[0].shape[0] * groups
    row_spec = pl.BlockSpec((block, width), lambda i: (i, 0))
    column = pl.BlockSpec((block, 1), lambda i: (i, 0))
    wide = pl.BlockSpec((block, hidden), lambda i: (i, 0))
    both = pl.BlockSpec((2, block, hidden), lambda i: (0, i, 0))
    return pl.pallas_call(
        functools.partial(expert_body, groups, chunk),
        grid=(total // block,),
        out_shape=(
            shape_of((total, width), BF16),
            shape_of((total, width), BF16),
            shape_of((total, width), BF16),
            shape_of((total, 1), F32),
            shape_of((total, hidden), BF16),
            shape_of((2, total, hidden), BF16),
        ),
        in_specs=[row_spec, row_spec, column] + [ANY] * (2 * groups),
        out_specs=(row_spec, row_spec, row_spec, column, wide, both),
        scratch_shapes=[
            pltpu.VMEM((3, hidden, width), BF16),
            pltpu.SemaphoreType.DMA((2 * groups,)),
        ],
        cost_estimate=pl.CostEstimate(flops=LIGHT, bytes_accessed=LIGHT, transcendentals=0),
        name="experts",
    )(rows, outer, gate_column, *in_weights, *down_weights)


def moe_plain(sent, gates, outer, own_in, own_down, far_gate):
    in_weights, down_weights = [own_in], [own_down]
    for bit in (1, 2):
        in_weights += [swap(w, "wshard", bit) for w in in_weights]
        down_weights += [swap(w, "wshard", bit) for w in down_weights]
    size, capacity, width = sent.shape
    total = size * capacity
    rows = exchange(sent.reshape(total, width), "dp").reshape(total, width)
    gate_column = lax.all_to_all(gates, "dp", 0, 0, tiled=True)[:, 0, :capacity].reshape(total, 1)
    made, back, outer_low, gate_grads, act, low = experts_pass(
        rows, outer.reshape(total, width), gate_column, in_weights, down_weights
    )
    extra = jnp.pad(gate_grads.reshape(size, 1, capacity), ((0, 0), (0, EXTRA - 1), (0, 0)))
    extra = lax.all_to_all(extra, "dp", 0, 0, tiled=True)
    share = down_weights[0].shape[0]
    grads = []
    for group in range(len(in_weights)):
        part = slice(group * share, (group + 1) * share)
        pieces = [dot_tn(low[c, :, part], rows) for c in range(2)]
        grads.append(jnp.stack(pieces + [dot_tn(act[:, part], outer_low)]).astype(BF16))
    shape = (size, capacity, width)
    moved = jnp.stack([swap(grads[g], "wshard", 1) for g in (1, 3)])
    sums = (jnp.stack(grads[::2]).astype(F32) + moved.astype(F32)).astype(BF16)
    return exchange(back, "dp"), extra, made.reshape(shape), sums


def rear_body(
    size, groups, head_size, remote_made, span_ref, gain_ref, table_ref, ones_ref, router_ref, col_ref, gate_ref,
    extra_ref, tok_hbm, cot_hbm, hidden_hbm, norm_hbm, mixed_hbm, rows_hbm, made_hbm, outw_hbm,
    qkvw_hbm, qkv_hbm, far_hbm,
    output_ref, grad_ref, gains_out, table_out, router_out, sum_out, sum_out_two, far_out,
    tok, cot, hidden, norm, mixed, rows, made, outw, qkvw, qkv, norm_t, mask, grad_hidden,
    grads, probs_ref, scores_ref, diag_sums, wo, wo_got, wg, wg_got, total,
    total_got, sum_ref, early_ref, early_got, late_ref, late_got, diag_ref,
    load_sems, weight_sems, made_send, made_got, part_sems, total_sems, small_sems, far_sems,
):
    me, place = lax.axis_index("dp"), lax.axis_index("wshard")
    near, far = flip(place, 1, groups), flip(place, 2, groups)
    dp_bits, shard_bits = bits_below(size), bits_below(groups)
    peers = [("dp", flip(me, step, size)) for step in range(1, size)]
    greet(peers + [("wshard", near), ("wshard", far)])
    count, width = tok.shape
    blocks = count // TILE
    experts = size
    capacity = rows.shape[0] // experts
    cols = outw.shape[2]
    two_heads = 2 * head_size
    branch, mixgrad, norm_grad = cot, norm, hidden

    loads = [
        pltpu.make_async_copy(source, target, load_sems.at[i])
        for i, (source, target) in enumerate(
            (
                (rows_hbm, rows), (norm_hbm, norm), (hidden_hbm, hidden), (cot_hbm, cot),
                (mixed_hbm, mixed), (outw_hbm, outw), (tok_hbm, tok), (qkv_hbm, qkv),
                (made_hbm.at[me], made.at[me]) if remote_made else (made_hbm, rows),
            )
        )
    ]
    for copy in loads[: 9 if remote_made else 8]:
        copy.start()

    def far_copy(piece):
        return remote_copy(
            far_hbm.at[1, piece], far_out.at[piece], far_sems.at[piece, 0], far_sems.at[piece, 1],
            "wshard", far,
        )

    far_copy(0).start()

    def weight_load(step):
        slot = lax.rem(step, 2)
        return pltpu.make_async_copy(
            qkvw_hbm.at[groups - 1 - step], qkvw.at[slot], weight_sems.at[slot]
        )

    hidden_again = pltpu.make_async_copy(hidden_hbm, hidden, load_sems.at[9])

    def made_copy(source, target, peer):
        return remote_copy(
            made_hbm.at[source], made.at[target], made_send.at[source], made_got.at[target], "dp",
            peer,
        )

    turns = turns_of(size)

    def send_made(turn):
        if remote_made:
            for step in turns[turn]:
                peer = flip(me, step, size)
                made_copy(peer, me, peer).start()

    send_made(0)

    exchanges = [("wshard", place, bit, groups) for bit in shard_bits]
    exchanges += [("dp", me, bit, size) for bit in dp_bits]

    def small_copy(kind, ref, got, step):
        axis, index, bit, length = exchanges[step]
        return remote_copy(
            ref, got.at[step], small_sems.at[kind, step, 0], small_sems.at[kind, step, 1], axis,
            flip(index, bit, length),
        )

    def small_step(kind, ref, got, step):
        now, before = step % 2, (step + 1) % 2
        if step > 0:
            small_copy(kind, ref.at[before], got, step - 1).wait()
            ref[now] = ref[before] + got[step - 1]
        if step < len(exchanges):
            small_copy(kind, ref.at[now], got, step).start()

    slots = [col_ref[:, k : k + 1] for k in range(2)]
    gates = [gate_ref[:, k : k + 1] for k in range(2)]
    lane = iota((count, extra_ref.shape[2]), 1)
    picked = [0.0, 0.0]
    for copy in loads[:1]:
        copy.wait()
    grads_in = 0.0
    for expert in range(experts):
        label = jnp.where(lane < capacity, lane + expert * capacity, -1)
        for k in range(2):
            picked[k] = picked[k] + jnp.where(label == slots[k], extra_ref[expert, 0:1, :], 0.0)
    gate_grads = [jnp.sum(p, -1, keepdims=True) for p in picked]
    mean = gates[0] * gate_grads[0] + gates[1] * gate_grads[1]
    lane = iota((count, 3 * experts), 1)
    part = (lane >= experts).astype(I32) + (lane >= 2 * experts).astype(I32)
    label = lane - part * experts
    logit_grads = 0.0
    for k in range(2):
        own = (label * capacity <= slots[k]) & (slots[k] < (label + 1) * capacity)
        logit_grads = logit_grads + jnp.where(own, gates[k] * (gate_grads[k] - mean), 0.0)
    high, middle, low = split_three(logit_grads)
    split = jnp.where(part == 0, high, jnp.where(part == 1, middle, low)).astype(BF16)
    hits = [onehot_columns(slots[k], 0, experts * capacity) for k in range(2)]
    hits = (hits[0] | hits[1]).astype(F32).astype(BF16)
    for copy in loads[1:4]:
        copy.wait()
    normed_grad = dot_nn(hits, rows[...])
    normed_grad = normed_grad + dot_nn(split, router_ref[...])
    router_grad = dot_tn(split, norm[...])
    early_ref[0, :experts, :] = (
        router_grad[:experts] + router_grad[experts : 2 * experts] + router_grad[2 * experts :]
    )
    unit, recip = unit_norm(hidden[...])
    early_ref[0, experts:, :] = jnp.broadcast_to(
        jnp.sum(normed_grad * unit, 0, keepdims=True), (EXTRA, width)
    )
    small_step(0, early_ref, early_got, 0)
    scaled = normed_grad * gain_ref[1:2, :]
    back = recip * (scaled - unit * jnp.mean(scaled * unit, -1, keepdims=True))
    grad_hidden[...] = cot[...].astype(F32) + back
    branch[...] = grad_hidden[...].astype(BF16)
    for copy in loads[4:6]:
        copy.wait()
    mixed_t = mixed[...].T
    result = 0.0

    def part_copy(item, source, target, kind, axis, peer):
        return remote_copy(
            source, target, part_sems.at[item, kind, 0], part_sems.at[item, kind, 1], axis, peer
        )

    def out_copy(kind):
        return part_copy(
            0, wo.at[(3, 1, 2)[kind]], wo_got.at[kind], kind, "wshard", far if kind == 2 else near
        )

    def qkv_copy(kind):
        return part_copy(
            1, wg.at[(2, 0, 1)[kind]], wg_got.at[kind], kind, "wshard", far if kind == 2 else near
        )

    for group in reversed(range(groups)):
        lanes = pl.ds(pl.multiple_of(flip(place, group, groups) * cols, cols), cols)
        piece = branch[:, lanes]
        result = result + dot_nt(piece, outw[group])
        wo[group] = dot_nn(mixed_t, piece).astype(BF16)
        if group == 3:
            out_copy(0).start()
        if group == 1:
            out_copy(1).start()
    mixgrad[...] = result.astype(BF16)
    for copy in loads[6:8]:
        copy.wait()
    weight_load(0).start()
    unit, _ = unit_norm(tok[...].astype(F32))
    norm_t[...] = (unit * gain_ref[0:1, :]).astype(BF16).T
    fill_mask(mask, span_ref[0])
    diag_ref[...] = spread_bias(table_ref, ones_ref)
    norm_grad[...] = jnp.zeros_like(norm_grad)

    def attend_group(step):
        group = groups - 1 - step
        slot = lax.rem(step, 2)
        weight_load(step).wait()

        @pl.when(step < groups - 1)
        def _():
            weight_load(step + 1).start()

        owner = flip(place, group, groups)
        heads = cols // head_size

        def pair(p, carry):
            offset = pl.multiple_of(p * two_heads, two_heads)
            lanes = pl.ds(offset, two_heads)
            query, keys, value = (qkv[group, c, :, lanes] for c in range(3))
            outer = mixgrad[:, pl.ds(pl.multiple_of(owner * cols + offset, two_heads), two_heads)]
            query_sum, key_sum, value_sum = [None] * blocks, None, None
            for which in range(2):
                head = owner * heads + 2 * p + which
                own = head_lanes(which, head_size)
                own_query, own_key, own_outer = query * own, keys * own, outer * own
                shrunk = own_query * 0.125
                tiles, far_bias = bias_tiles(diag_ref[pl.ds(head, 1), :])
                near_sums, far_sums = [None] * 3, [None] * 2
                for block in range(blocks):
                    piece = slice(block * TILE, (block + 1) * TILE)
                    probs = softmax_tiles(
                        score_tiles(block, shrunk[piece], keys, tiles, far_bias, mask)
                    )
                    prob_grads = dot_nt(own_outer[piece], value)
                    prob_grads = [prob_grads[:, j * TILE : (j + 1) * TILE] for j in range(blocks)]
                    delta = functools.reduce(jnp.add, [a * b for a, b in zip(probs, prob_grads)])
                    delta = jnp.sum(delta, -1, keepdims=True)
                    lows = [(a * (b - delta)).astype(BF16) for a, b in zip(probs, prob_grads)]
                    for other in range(blocks):
                        step = block - other
                        wide = lows[other].astype(F32)
                        if abs(step) >= 2:
                            side = 0 if step > 0 else 1
                            old = far_sums[side]
                            far_sums[side] = wide if old is None else old + wide
                        else:
                            old = near_sums[step + 1]
                            near_sums[step + 1] = wide if old is None else old + wide
                    probs_ref[which, piece, :] = jnp.concatenate([t.astype(BF16) for t in probs], 1)
                    lows = jnp.concatenate(lows, 1)
                    scores_ref[which, piece, :] = lows
                    more = dot_nn(lows, own_key)
                    query_sum[block] = more if which == 0 else query_sum[block] + more
                more = dot_tn(scores_ref[which], own_query)
                key_sum = more if which == 0 else key_sum + more
                more = dot_tn(probs_ref[which], own_outer)
                value_sum = more if which == 0 else value_sum + more
                for step in range(3):
                    wide = jnp.concatenate([near_sums[step], jnp.zeros((TILE, TILE), F32)], 1)
                    half = TILE // 2
                    while half:
                        turned = pltpu.roll(wide[half:], 2 * TILE - half, 1)
                        wide = wide[:half] + turned
                        half //= 2
                    for side in range(2):
                        spot = 2 * step + side
                        diag_sums[head, spot : spot + 1, :] = wide[:, TILE * side : TILE * (side + 1)]
                for side in range(2):
                    diag_sums[head, 6 + side : 7 + side, :] = jnp.sum(far_sums[side], 0, keepdims=True)
            for block in range(blocks):
                piece = slice(block * TILE, (block + 1) * TILE)
                grads[0, piece, lanes] = (query_sum[block] * 0.125).astype(BF16)
            grads[1, :, lanes] = (key_sum * 0.125).astype(BF16)
            grads[2, :, lanes] = value_sum.astype(BF16)
            return carry

        lax.fori_loop(0, cols // two_heads, pair, 0)
        for c in range(3):
            weight_grad = dot_nn(norm_t[...], grads[c]).astype(BF16)

            @pl.when(group > 0)
            def _():
                wg[group - 1, c] = weight_grad

            @pl.when(group == 0)
            def _():
                total[c * width : (c + 1) * width, :] = weight_grad

            norm_grad[...] += dot_nt(grads[c], qkvw[slot, c])

    def add_into(target, *others):
        for first in range(0, target.shape[0], 256):
            spot = slice(first, first + 256)
            value = target[spot].astype(F32)
            for other in others:
                value = value + other[spot].astype(F32)
            target[spot] = value.astype(BF16)

    third = outw.shape[1]
    parts = 4
    length = total.shape[0] // parts
    stages = len(dp_bits)

    def bit_of(step):
        return lax.rem(lax.div(me, dp_bits[step]), 2)

    def segment(part, step):
        first, size_of = part * length, length
        for s in range(step):
            size_of //= 2
            first = first + bit_of(s) * size_of
        return first, size_of

    def halving(part, step):
        first, size_of = segment(part, step)
        half = size_of // 2
        away = pl.multiple_of(first + (1 - bit_of(step)) * half, half)
        return remote_copy(
            total.at[pl.ds(away, half)],
            total_got.at[pl.ds(part * length + length - size_of, half)],
            total_sems.at[part, 0, step, 0], total_sems.at[part, 0, step, 1], "dp",
            flip(me, dp_bits[step], size),
        )

    def add_half(part, step):
        first, half = segment(part, step + 1)
        first = pl.multiple_of(first, half)
        got = part * length + length - 2 * half
        value = total[pl.ds(first, half), :].astype(F32) + total_got[got : got + half, :].astype(F32)
        total[pl.ds(first, half), :] = value.astype(BF16)
        if step == stages - 1:
            sum_ref[pl.ds(first, half), :] = value.astype(BF16)

    def doubling(part, step):
        first, size_of = segment(part, step + 1)
        spot = pl.ds(pl.multiple_of(first, size_of), size_of)
        return remote_copy(
            sum_ref.at[spot], sum_ref.at[spot],
            total_sems.at[part, 1, step, 0], total_sems.at[part, 1, step, 1], "dp",
            flip(me, dp_bits[step], size),
        )

    def sum_stage(part, stage):
        if 0 < stage <= stages:
            halving(part, stage - 1).wait()
            add_half(part, stage - 1)
        elif stage > stages:
            doubling(part, 2 * stages - stage).wait()
        if stage < stages:
            halving(part, stage).start()
        elif stage < 2 * stages:
            doubling(part, 2 * stages - 1 - stage).start()

    def group_step(step, carry):
        @pl.when(step == groups - 1)
        def _():
            far_copy(1).start()

        attend_group(step)

        @pl.when(step == 0)
        def _():
            send_made(1)
            qkv_copy(0).start()
            small_step(0, early_ref, early_got, 1)
            out_copy(0).wait_recv()
            add_into(wo.at[2], wo_got.at[0])
            out_copy(2).start()

        @pl.when(step == 1)
        def _():
            send_made(2)
            qkv_copy(0).wait_recv()
            for c in range(3):
                add_into(wg.at[1, c], wg_got.at[0, c])
            qkv_copy(2).start()
            small_step(0, early_ref, early_got, 2)

        @pl.when(step == 2)
        def _():
            qkv_copy(1).start()
            small_step(0, early_ref, early_got, 3)
            out_copy(1).wait_recv()
            out_copy(2).wait_recv()
            add_into(wo.at[0], wo_got.at[1], wo_got.at[2])
            total[3 * third :, :] = wo[0]
            sum_stage(3, 0)

        return carry

    lax.fori_loop(0, groups, group_step, 0)
    sum_stage(3, 1)

    small_step(0, early_ref, early_got, 4)
    unit, recip = unit_norm(tok[...].astype(F32))
    gain_grad = jnp.sum(norm_grad[...] * unit, 0, keepdims=True)
    table_grad = 0.0
    for k in range(8):
        for piece in split_three(diag_sums[:, k, :]):
            table_grad = table_grad + dot_nt(piece.astype(BF16), ones_ref[:, k * TILE : (k + 1) * TILE])
    late_ref[0] = jnp.zeros(late_ref.shape[1:], F32)
    for k in range(width // TILE):
        late_ref[0, k : k + 1, :] = gain_grad[:, k * TILE : (k + 1) * TILE]
    heads, buckets = table_grad.shape
    late_ref[0, 8 : 8 + heads, :buckets] = table_grad
    small_step(1, late_ref, late_got, 0)

    qkv_copy(1).wait_recv()
    qkv_copy(2).wait()
    def finish_tokens():
        scaled = norm_grad[...] * gain_ref[0:1, :]
        back = recip * (scaled - unit * jnp.mean(scaled * unit, -1, keepdims=True))
        grad_ref[...] = (grad_hidden[...] + back).astype(BF16)
        hidden_again.start()
        if not remote_made:
            loads[8].start()

    def finish_output():
        loads[8].wait()
        hidden_again.wait()
        if remote_made:
            for _, peer in peers:
                made_copy(me, peer, peer).wait_recv()
        values = made[...].reshape(experts * capacity, width) if remote_made else rows[...]
        for first in range(0, count, 256):
            spot = slice(first, first + 256)
            value = hidden[spot, :]
            for k in range(2):
                hit = onehot_columns(slots[k][spot], 0, experts * capacity)
                value = value + gates[k][spot] * dot_nn(hit.astype(F32).astype(BF16), values)
            output_ref[spot, :] = value.astype(BF16)

    rest_early = list(range(groups + 1, len(exchanges) + 1))
    rest_late = list(range(1, len(exchanges) + 1))

    def next_small():
        if rest_early:
            small_step(0, early_ref, early_got, rest_early.pop(0))
        if rest_late:
            small_step(1, late_ref, late_got, rest_late.pop(0))

    for time in range(3 + 2 * stages):
        for part in range(min(3, time + 1)):
            if time == part:
                add_into(
                    total.at[part * third : (part + 1) * third], wg_got.at[1, part], wg_got.at[2, part]
                )
            if time - part <= 2 * stages:
                sum_stage(part, time - part)
        if time + 2 <= 2 * stages:
            sum_stage(3, time + 2)
        if time == 0:
            finish_tokens()
        elif time == 1:
            finish_output()
        elif time == 2:
            far_copy(1).wait()
            far_copy(2).start()
        next_small()
    while rest_early or rest_late:
        next_small()
    saves = [
        pltpu.make_async_copy(sum_ref.at[pl.ds(0, 3 * third)], sum_out, load_sems.at[10]),
        pltpu.make_async_copy(sum_ref.at[pl.ds(3 * third, third)], sum_out_two, load_sems.at[11]),
    ]
    for copy in saves:
        copy.start()
    last = len(exchanges) % 2
    router_out[...] = early_ref[last, :experts, :]
    gains_out[1:2, :] = early_ref[last, experts : experts + 1, :]
    for k in range(width // TILE):
        gains_out[0:1, k * TILE : (k + 1) * TILE] = late_ref[last, k : k + 1, :]
    table_out[...] = late_ref[last, 8 : 8 + heads, :buckets]
    for copy in saves:
        copy.wait()
    far_copy(0).wait()
    far_copy(2).wait()
    if remote_made:
        for _, peer in peers:
            made_copy(peer, me, peer).wait_send()
    for kind in range(3):
        out_copy(kind).wait_send()
    for kind in range(2):
        qkv_copy(kind).wait_send()


def bits_below(size):
    return [1 << b for b in range(size.bit_length() - 1)]


def rear(
    span, gains, table_t, ones, router_t3, slots_col, gates, extra, tokens, cotangent, hidden, normed,
    mixed, rows, made, out_weights, qkv_weights, qkv, expert_sums, head_size,
):
    count, width = tokens.shape
    size, groups = lax.axis_size("dp"), lax.axis_size("wshard")
    heads, buckets = width // head_size, ones.shape[0]
    experts = router_t3.shape[0] // 3
    cols = out_weights.shape[2]
    exchanges = len(bits_below(size)) + len(bits_below(groups))
    dma = pltpu.SemaphoreType.DMA
    wide, small = (count, width), (experts + EXTRA, width)
    late = (8 + heads, TILE)
    total = (4 * width, cols)
    vmem = pltpu.VMEM
    return pl.pallas_call(
        functools.partial(rear_body, size, groups, head_size, made.ndim == 3),
        out_shape=(
            shape_of(wide, BF16),
            shape_of(wide, BF16),
            shape_of((2, width), F32),
            shape_of((heads, buckets), F32),
            shape_of((experts, width), F32),
            shape_of((3 * width, cols), BF16),
            shape_of((width, cols), BF16),
            shape_of(expert_sums.shape[1:], BF16),
        ),
        in_specs=[SMEM] + [VMEM] * 7 + [ANY] * 11,
        out_specs=(VMEM,) * 5 + (ANY,) * 3,
        scratch_shapes=[
            vmem(wide, BF16),
            vmem(wide, BF16),
            vmem(wide, F32),
            vmem(wide, BF16),
            vmem(wide, BF16),
            vmem(rows.shape, BF16),
            vmem(made.shape if made.ndim == 3 else (16, TILE), BF16),
            vmem(out_weights.shape, BF16),
            vmem((2, *qkv_weights.shape[1:]), BF16),
            vmem(qkv.shape, BF16),
            vmem((width, count), BF16),
            vmem((count, count), F32),
            vmem(wide, F32),
            vmem((3, count, cols), BF16),
            vmem((2, count, count), BF16),
            vmem((2, count, count), BF16),
            vmem((heads, 8, TILE), F32),
            vmem((groups, width, cols), BF16),
            vmem((3, width, cols), BF16),
            vmem((groups - 1, 3, width, cols), BF16),
            vmem((3, 3, width, cols), BF16),
            vmem(total, BF16),
            vmem(total, BF16),
            vmem(total, BF16),
            vmem((2, *small), F32),
            vmem((exchanges, *small), F32),
            vmem((2, *late), F32),
            vmem((exchanges, *late), F32),
            vmem((heads, ones.shape[1]), F32),
            dma((12,)),
            dma((2,)),
            dma((size,)),
            dma((size,)),
            dma((2, 3, 2)),
            dma((4, 2, len(bits_below(size)), 2)),
            dma((2, exchanges, 2)),
            dma((3, 2)),
        ],
        cost_estimate=pl.CostEstimate(flops=LIGHT, bytes_accessed=LIGHT, transcendentals=0),
        compiler_params=pltpu.CompilerParams(
            collective_id=2, has_side_effects=True, vmem_limit_bytes=66_000_000
        ),
        name="rear",
    )(
        span, gains, table_t, ones, router_t3, slots_col, gates, extra, tokens, cotangent, hidden,
        normed, mixed, rows, made, out_weights, qkv_weights, qkv, expert_sums,
    )


def result_body(
    in_ref, far_in_ref, down_ref, far_down_ref, qkv_ref, out_ref, output_ref, tokens_ref, gains_ref,
    table_ref, router_ref,
    in_out, down_out, qkv_out, out_out, output_out, tokens_out, gains_out, table_out, router_out,
):
    for c in range(2):
        in_out[c] = in_ref[0, c].astype(F32) + far_in_ref[c].astype(F32)
    down_out[...] = down_ref[0, 0].astype(F32) + far_down_ref[0].astype(F32)
    qkv_out[...] = qkv_ref[...].astype(F32)
    out_out[...] = out_ref[...].astype(F32)
    output_out[...] = output_ref[...]
    tokens_out[...] = tokens_ref[...]
    gains_out[...] = gains_ref[...]
    table_out[...] = table_ref[...]
    router_out[...] = router_ref[...]


def results(expert_sums, far_got, qkv_sum, out_sum, output, grad_tokens, *small, steps=2):
    share, width = far_got.shape[1:]
    part = share // steps

    def rows_of(array):
        return pl.BlockSpec((array.shape[0] // steps, array.shape[1]), lambda i: (i, 0))

    def whole(array):
        return pl.BlockSpec(array.shape, lambda i: (0, 0))

    tall = (qkv_sum, out_sum, output, grad_tokens)
    return pl.pallas_call(
        result_body,
        grid=(steps,),
        out_shape=(
            shape_of((2, share, width), F32),
            shape_of((share, width), F32),
            shape_of(qkv_sum.shape, F32),
            shape_of(out_sum.shape, F32),
            shape_of(output.shape, BF16),
            shape_of(grad_tokens.shape, BF16),
        )
        + tuple(shape_of(a.shape, F32) for a in small),
        in_specs=[
            pl.BlockSpec((1, 2, part, width), lambda i: (0, 0, i, 0)),
            pl.BlockSpec((2, part, width), lambda i: (0, i, 0)),
            pl.BlockSpec((1, 1, part, width), lambda i: (0, 2, i, 0)),
            pl.BlockSpec((1, part, width), lambda i: (2, i, 0)),
        ]
        + [rows_of(a) for a in tall]
        + [whole(a) for a in small],
        out_specs=(
            pl.BlockSpec((2, part, width), lambda i: (0, i, 0)),
            pl.BlockSpec((part, width), lambda i: (i, 0)),
        )
        + tuple(rows_of(a) for a in tall)
        + tuple(whole(a) for a in small),
        cost_estimate=pl.CostEstimate(flops=LIGHT, bytes_accessed=LIGHT, transcendentals=0),
        name="results",
    )(expert_sums, far_got, expert_sums, far_got, *tall, *small)


def swap(value, axis, bit):
    size = lax.axis_size(axis)
    return lax.ppermute(value, axis, [(i, i ^ bit) for i in range(size)])


def bits_of(axis):
    size = lax.axis_size(axis)
    return [1 << b for b in range(size.bit_length() - 1)]


def after(value, *others):
    return lax.optimization_barrier((value, *others))[0]


def exchange(rows, axis):
    size = lax.axis_size(axis)
    total, width = rows.shape
    blocks = rows.reshape(size, total // size, width)
    return lax.all_to_all(blocks, axis, 0, 0, tiled=True)


def per_device(
    tokens,
    cotangent,
    span_starts,
    routes,
    norm_gains,
    bias_table,
    router,
    attn_qkv,
    attn_out,
    expert_in,
    expert_down,
):
    assert span_starts.shape[0] == 1
    tok_count, model_width = tokens.shape
    buckets, head_count = bias_table.shape
    head_size = model_width // head_count
    experts = router.shape[1]
    capacity = (10 * tok_count + 4 * experts - 1) // (4 * experts)
    total = experts * capacity
    place = lax.axis_index("wshard")
    where = jnp.stack([place.astype(I32), span_starts[0]])
    ones = jnp.asarray(diagonal_ones(buckets), BF16)
    table_t = bias_table.T
    router_t = router.T
    expert_in = jnp.swapaxes(expert_in[0], 1, 2)
    expert_down = expert_down[0]

    shards = (attn_qkv, attn_out, expert_in)
    (
        slots_col, gates, sent_gates, qkv_all, out_all, qkv, mixed, hidden, normed_two, sent,
        outer_rows, far_gate,
    ) = front(
        span_starts, routes, norm_gains, table_t, ones, router_t, tokens, cotangent, shards, head_size,
        capacity,
    )
    groups = out_all.shape[0]
    through = moe if capacity % 16 == 0 else moe_plain
    back_rows, back_extra, made, expert_grads = through(
        sent, sent_gates, outer_rows, expert_in, expert_down, far_gate
    )
    if through is moe_plain:
        made = exchange(made.reshape(total, model_width), "dp").reshape(total, model_width)

    output, grad_tokens, grad_gains, table_grad, router_grad, qkv_sum, out_sum, far_got = rear(
        span_starts, norm_gains, table_t, ones, jnp.concatenate([router_t] * 3, 0),
        slots_col, gates, back_extra, tokens, cotangent, hidden, normed_two,
        mixed, back_rows.reshape(total, model_width), made, out_all, qkv_all, qkv, expert_grads,
        head_size,
    )

    (
        in_grad, down_grad, qkv_sum, out_sum, output, grad_tokens, grad_gains, table_grad, router_grad,
    ) = results(
        expert_grads, far_got, qkv_sum, out_sum, output, grad_tokens, grad_gains, table_grad,
        router_grad,
    )
    return (
        output,
        grad_tokens,
        grad_gains,
        table_grad.T,
        router_grad.T,
        qkv_sum.reshape(3, model_width, out_sum.shape[1]),
        out_sum,
        jnp.swapaxes(in_grad, 1, 2)[None],
        down_grad[None],
    )


def solution(mesh):
    return jax.shard_map(
        per_device,
        mesh=mesh,
        in_specs=(
            P(("dp", "wshard"), None),
            P(("dp", "wshard"), None),
            P(("dp", "wshard")),
            P(("dp", "wshard"), None),
            P(),
            P(),
            P(),
            P(None, None, "wshard"),
            P(None, "wshard"),
            P("dp", None, None, "wshard"),
            P("dp", "wshard", None),
        ),
        out_specs=(
            P(("dp", "wshard"), None),
            P(("dp", "wshard"), None),
            P(),
            P(),
            P(),
            P(None, None, "wshard"),
            P(None, "wshard"),
            P("dp", None, None, "wshard"),
            P("dp", "wshard", None),
        ),
        check_vma=False,
    )
```
